32 devices in a mesh: wide: 8 (over z, x), narrow: 4 (over y, core).
Axes of the slice: x: 2, y: 2, z: 4, core: 2. Of those that a mesh axis runs over, the one named last changes fastest.
Arguments:
- large_in: bfloat16 [128, 196, 384], P(('wide', 'narrow')), may hold values from -6 to 6
- small_in: bfloat16 [384, 36, 384], P(('wide', 'narrow')), may hold values from -6 to 6
- large_cot: bfloat16 [128, 196, 384], P(('wide', 'narrow')), may hold values from -6 to 6
- small_cot: bfloat16 [384, 36, 384], P(('wide', 'narrow')), may hold values from -6 to 6
- filters: bfloat16 [2, 86016], P(None, ('wide', 'narrow')), may hold values from -4 to 4
- w_in: bfloat16 [2, 385, 1536], P(None, None, ('wide', 'narrow')), may hold values from -0.3125 to 0.3125
- w_out: bfloat16 [2, 1536, 384], P(None, ('wide', 'narrow')), may hold values from -0.15625 to 0.15625
- gains: float32 [2, 2, 384], replicated, may hold values from 0.5 to 1.5
- biases: float32 [2, 3, 384], replicated, may hold values from -2 to 2
Outputs:
- out_large: bfloat16 [128, 196, 384], P(('wide', 'narrow'))
- out_small: bfloat16 [384, 36, 384], P(('wide', 'narrow'))
- grad_large: float32 [128, 196, 384], P(('wide', 'narrow'))
- grad_small: float32 [384, 36, 384], P(('wide', 'narrow'))
- grad_filters: float32 [2, 86016], P(None, ('wide', 'narrow'))
- grad_w_in: float32 [2, 385, 1536], P(None, None, ('wide', 'narrow'))
- grad_w_out: float32 [2, 1536, 384], P(None, ('wide', 'narrow'))
- grad_gains: float32 [2, 2, 384], replicated
- grad_biases: float32 [2, 3, 384], replicated
The draws below stay inside these ranges and needn't reach their ends.
All inputs are finite; a program needn't handle non-finite values.
Results may differ from the reference program's by a relative error of at most 0.0062.
Values may be sent and summed in bfloat16 or wider, within the bound.
A program may use at most 192 MiB of HBM per device.

```python
import math
import jax
import jax.numpy as jnp
from jax import lax

D = 384
FF = 1536
GL = 14
GS = 6
BLOCKS = 2
MICRO = 2
LCROP = 2
PL = 196
PS = 36
FL = 112
FS = 24
LARGE = 128
SMALL = 384


def level_of(rng, dims, split, least, largest):
    def one(position, blocks):
        heights = jax.random.uniform(jax.random.fold_in(jax.random.fold_in(rng, 6), position), (blocks,), jnp.float32, least / len(split), largest / len(split))
        return jnp.repeat(jnp.exp(heights), dims[position] // blocks).reshape((-1,) + (1,) * (len(dims) - position - 1))

    loudness = one(*split[0])
    for cut in split[1:]:
        loudness = loudness * one(*cut)
    return loudness


def normal_values(own_key, extent, scale, bound, pieces=(), held_as=jnp.bfloat16):
    values = jax.random.normal(own_key, extent, jnp.float32) * scale
    if len(pieces) > 0:
        values = level_of(own_key, extent, pieces, -0.22, 0.18) * values
    return jnp.clip(values, min=-bound, max=bound).astype(held_as)


def setup_inputs(seed: int = 0) -> dict:
    streams_of = jax.random.split(jax.random.key(seed), 10)
    return {
        "large_in": normal_values(streams_of[0], (LARGE, PL, D), 1.0, 6.0, ((0, 32),)),
        "small_in": normal_values(streams_of[1], (SMALL, PS, D), 1.0, 6.0, ((0, 32),)),
        "large_cot": normal_values(streams_of[2], (LARGE, PL, D), 1.0, 6.0, ((0, 32),)),
        "small_cot": normal_values(streams_of[3], (SMALL, PS, D), 1.0, 6.0, ((0, 32),)),
        "filters": normal_values(streams_of[4], (BLOCKS, 2 * FL * D), 0.7, 4.0, ((1, 32),)),
        "w_in": normal_values(streams_of[5], (BLOCKS, D + 1, FF), D ** -0.5, 0.3125, ((2, 32),)),
        "w_out": normal_values(streams_of[6], (BLOCKS, FF, D), FF ** -0.5, 0.15625, ((1, 32),)),
        "gains": jnp.clip(1.0 + 0.1 * jax.random.normal(streams_of[7], (BLOCKS, 2, D), jnp.float32), 0.5, 1.5),
        "biases": normal_values(streams_of[8], (BLOCKS, 3, D), 0.3, 2.0, (), jnp.float32),
    }


precise = lax.Precision.HIGHEST
epsilon = 1e-06

@jax.custom_vjp
def low(v):
    return lax.optimization_barrier(v.astype(jnp.bfloat16)).astype(jnp.float32)

@jax.custom_vjp
def low_back(v):
    return v

def low_keep(v):
    return (low(v), None)

def low_pass(kept, grad):
    return (grad,)

def back_keep(v):
    return (v, None)

def back_low(kept, grad):
    return (low(grad),)
low.defvjp(low_keep, low_pass)
low_back.defvjp(back_keep, back_low)

def dft_tables(grid_cells):
    half_count = grid_cells // 2 + 1
    places = jnp.arange(grid_cells * grid_cells, dtype=jnp.int32)
    place_row = places // grid_cells
    place_col = places % grid_cells
    modes = jnp.arange(grid_cells * half_count, dtype=jnp.int32)
    mode_row = modes // half_count
    mode_col = modes % half_count
    phases = (mode_row[:, None] * place_row[None, :] + mode_col[:, None] * place_col[None, :]) % grid_cells
    angles = phases.astype(jnp.float32) * (2.0 * math.pi / grid_cells)
    forward_re = jnp.cos(angles) / grid_cells
    forward_im = -jnp.sin(angles) / grid_cells
    doubling = jnp.where((mode_col == 0) | (2 * mode_col == grid_cells), 1.0, 2.0).astype(jnp.float32)
    inverse_re = jnp.transpose(forward_re * doubling[:, None])
    inverse_im = jnp.transpose(forward_im * doubling[:, None])
    return (forward_re, forward_im, inverse_re, inverse_im)

def linear_map(size_out, size_in):
    rows_out = jnp.arange(size_out, dtype=jnp.int32)
    spans = rows_out * (size_in - 1)
    lower = spans // (size_out - 1)
    fraction = (spans - lower * (size_out - 1)).astype(jnp.float32) / (size_out - 1)
    columns = jnp.arange(size_in, dtype=jnp.int32)
    first = jnp.where(columns[None, :] == lower[:, None], 1.0 - fraction[:, None], 0.0)
    second = jnp.where(columns[None, :] == lower[:, None] + 1, fraction[:, None], 0.0)
    return (first + second).astype(jnp.float32)

def shrink_map():
    along_rows = linear_map(GS, GL)
    along_cols = linear_map(GS // 2 + 1, GL // 2 + 1)
    return (along_rows[:, None, :, None] * along_cols[None, :, None, :]).reshape(FS, FL)

def filter_grid(patches, tables, filt_re, filt_im):
    forward_re, forward_im, inverse_re, inverse_im = tables
    spec_re = jnp.einsum('fp,bpd->bfd', forward_re, patches, precision=precise)
    spec_im = jnp.einsum('fp,bpd->bfd', forward_im, patches, precision=precise)
    out_re = spec_re * filt_re - spec_im * filt_im
    out_im = spec_re * filt_im + spec_im * filt_re
    back_re = jnp.einsum('pf,bfd->bpd', inverse_re, out_re, precision=precise)
    back_im = jnp.einsum('pf,bfd->bpd', inverse_im, out_im, precision=precise)
    return back_re + back_im

def spectral(normed, large_rows, filt_re, filt_im):
    width = normed.shape[-1]
    shrink = shrink_map()
    small_re = jnp.dot(shrink, filt_re, precision=precise, preferred_element_type=jnp.float32)
    small_im = jnp.dot(shrink, filt_im, precision=precise, preferred_element_type=jnp.float32)
    part_large = filter_grid(normed[:large_rows].reshape(-1, GL * GL, width), dft_tables(GL), filt_re, filt_im)
    part_small = filter_grid(normed[large_rows:].reshape(-1, GS * GS, width), dft_tables(GS), small_re, small_im)
    return jnp.concatenate([part_large.reshape(-1, width), part_small.reshape(-1, width)], 0)

def layer_norm(stream, gain, shift):
    centre = stream - lax.optimization_barrier(jnp.mean(stream, axis=-1, keepdims=True))
    spread = lax.optimization_barrier(jnp.mean(centre * centre, axis=-1, keepdims=True))
    return centre * lax.rsqrt(spread + epsilon) * gain + shift

def network(large_part, small_part, filters, w_in, w_out, gains, biases):
    large_rows = large_part.shape[0] * PL
    stream = jnp.concatenate([large_part.reshape(-1, D), small_part.reshape(-1, D)], 0)
    for layer_index in range(BLOCKS):
        halves = filters[layer_index].reshape(2, FL, D)
        normed = layer_norm(stream, gains[layer_index, 0], biases[layer_index, 0])
        mixed = stream + spectral(normed, large_rows, halves[0], halves[1])
        second = low(layer_norm(mixed, gains[layer_index, 1], biases[layer_index, 1]))
        product = jnp.dot(second, w_in[layer_index, :D], precision=precise, preferred_element_type=jnp.float32)
        pre_act = low_back(product) + w_in[layer_index, D]
        active = low(jax.nn.gelu(pre_act, approximate=False))
        branch = jnp.dot(active, w_out[layer_index], precision=precise, preferred_element_type=jnp.float32)
        stream = mixed + low_back(branch) + biases[layer_index, 2]
    return stream

def reference(large_in, small_in, large_cot, small_cot, filters, w_in, w_out, gains, biases):
    groups = large_in.shape[0] // (LCROP * MICRO)
    large_groups = large_in.reshape(groups, -1, PL, D).astype(jnp.float32)
    small_groups = small_in.reshape(groups, -1, PS, D).astype(jnp.float32)
    large_cots = large_cot.reshape(groups, -1, PL, D).astype(jnp.float32)
    small_cots = small_cot.reshape(groups, -1, PS, D).astype(jnp.float32)
    params = (filters.astype(jnp.float32), w_in.astype(jnp.float32), w_out.astype(jnp.float32), gains, biases)

    def one_group(totals, item):
        large_part, small_part, large_back, small_back = item
        result, pullback = jax.vjp(network, large_part, small_part, *params)
        cotangent = jnp.concatenate([large_back.reshape(-1, D), small_back.reshape(-1, D)], 0)
        grads = pullback(cotangent)
        totals = jax.tree.map(jnp.add, totals, tuple(grads[2:]))
        large_rows = large_part.shape[0] * PL
        out_big = result[:large_rows].reshape(large_part.shape).astype(jnp.bfloat16)
        out_little = result[large_rows:].reshape(small_part.shape).astype(jnp.bfloat16)
        return (totals, (out_big, out_little, grads[0], grads[1]))
    zeros = tuple((jnp.zeros_like(param) for param in params))
    totals, stacked = lax.scan(one_group, zeros, (large_groups, small_groups, large_cots, small_cots))
    out_large = stacked[0].reshape(LARGE, PL, D)
    out_small = stacked[1].reshape(SMALL, PS, D)
    grad_large = stacked[2].reshape(LARGE, PL, D)
    grad_small = stacked[3].reshape(SMALL, PS, D)
    return (out_large, out_small, grad_large, grad_small, totals[0], totals[1], totals[2], totals[3], totals[4])
```

```python
from functools import partial
import math

import jax
import jax.numpy as jnp
import ml_dtypes
import numpy as np
from jax import lax
from jax.experimental import pallas as pl
from jax.experimental.pallas import tpu as pltpu
from jax.sharding import PartitionSpec as P

FF = 1536
GL = 14
GS = 6
BLOCKS = 2
MICRO = 2
PL = 196
FL = 112
FS = 24


precise = lax.Precision.HIGHEST
epsilon = 1e-06


def dft_tables(grid_cells):
    half_count = grid_cells // 2 + 1
    places = jnp.arange(grid_cells * grid_cells, dtype=jnp.int32)
    place_row = places // grid_cells
    place_col = places % grid_cells
    modes = jnp.arange(grid_cells * half_count, dtype=jnp.int32)
    mode_row = modes // half_count
    mode_col = modes % half_count
    phases = (
        mode_row[:, None] * place_row[None, :] + mode_col[:, None] * place_col[None, :]
    ) % grid_cells
    angles = phases.astype(jnp.float32) * (2.0 * math.pi / grid_cells)
    forward_re = jnp.cos(angles) / grid_cells
    forward_im = -jnp.sin(angles) / grid_cells
    doubling = jnp.where((mode_col == 0) | (2 * mode_col == grid_cells), 1.0, 2.0).astype(
        jnp.float32
    )
    inverse_re = jnp.transpose(forward_re * doubling[:, None])
    inverse_im = jnp.transpose(forward_im * doubling[:, None])
    return (forward_re, forward_im, inverse_re, inverse_im)


def linear_map(size_out, size_in):
    rows_out = jnp.arange(size_out, dtype=jnp.int32)
    spans = rows_out * (size_in - 1)
    lower = spans // (size_out - 1)
    fraction = (spans - lower * (size_out - 1)).astype(jnp.float32) / (size_out - 1)
    columns = jnp.arange(size_in, dtype=jnp.int32)
    first = jnp.where(columns[None, :] == lower[:, None], 1.0 - fraction[:, None], 0.0)
    second = jnp.where(columns[None, :] == lower[:, None] + 1, fraction[:, None], 0.0)
    return first + second


def shrink_map():
    along_rows = linear_map(GS, GL)
    along_cols = linear_map(GS // 2 + 1, GL // 2 + 1)
    return (along_rows[:, None, :, None] * along_cols[None, :, None, :]).reshape(FS, FL)


def filter_grid(patches, tables, filt_re, filt_im):
    forward_re, forward_im, inverse_re, inverse_im = tables
    spec_re = jnp.einsum("fp,bpd->bfd", forward_re, patches, precision=precise)
    spec_im = jnp.einsum("fp,bpd->bfd", forward_im, patches, precision=precise)
    out_re = spec_re * filt_re - spec_im * filt_im
    out_im = spec_re * filt_im + spec_im * filt_re
    back_re = jnp.einsum("pf,bfd->bpd", inverse_re, out_re, precision=precise)
    back_im = jnp.einsum("pf,bfd->bpd", inverse_im, out_im, precision=precise)
    return back_re + back_im


def spectral(normed, large_rows, filt_re, filt_im):
    width = normed.shape[-1]
    shrink = shrink_map()
    small_re = jnp.dot(shrink, filt_re, precision=precise, preferred_element_type=jnp.float32)
    small_im = jnp.dot(shrink, filt_im, precision=precise, preferred_element_type=jnp.float32)
    part_large = filter_grid(
        normed[:large_rows].reshape(-1, GL * GL, width), dft_tables(GL), filt_re, filt_im
    )
    part_small = filter_grid(
        normed[large_rows:].reshape(-1, GS * GS, width), dft_tables(GS), small_re, small_im
    )
    return jnp.concatenate([part_large.reshape(-1, width), part_small.reshape(-1, width)], 0)


def layer_norm(stream, gain, shift):
    centre = stream - jnp.mean(stream, axis=-1, keepdims=True)
    spread = jnp.mean(centre * centre, axis=-1, keepdims=True)
    return centre * lax.rsqrt(spread + epsilon) * gain + shift


def per_device(large_in, small_in, large_cot, small_cot, filters, w_in, w_out, gains, biases):
    width = large_in.shape[-1]
    micro_large = large_in.shape[0] // MICRO
    micro_small = small_in.shape[0] // MICRO
    large_rows = micro_large * PL
    exact_gelu = partial(jax.nn.gelu, approximate=False)

    def fetch(layer_index, forward):
        if forward:
            return (
                lax.all_gather(filters[layer_index], ("wide", "narrow"), axis=0, tiled=True),
                lax.all_gather(w_in[layer_index], ("wide", "narrow"), axis=1, tiled=True),
                lax.all_gather(w_out[layer_index], ("wide", "narrow"), axis=0, tiled=True),
            )
        return (
            lax.all_gather(filters[layer_index], ("wide", "narrow"), axis=0, tiled=True),
            lax.all_gather(w_in[layer_index], ("wide", "narrow"), axis=1, tiled=True),
            lax.all_gather(w_out[layer_index], ("wide", "narrow"), axis=0, tiled=True),
        )

    def branch_first(stream, gain, shift, filt_re, filt_im):
        return spectral(layer_norm(stream, gain, shift), large_rows, filt_re, filt_im)

    acc_filter = [jnp.zeros((2, FL, width), jnp.float32) for layer_index in range(BLOCKS)]
    acc_in = [jnp.zeros((width, FF), jnp.float32) for layer_index in range(BLOCKS)]
    acc_in_bias = [jnp.zeros((FF,), jnp.float32) for layer_index in range(BLOCKS)]
    acc_out = [jnp.zeros((FF, width), jnp.float32) for layer_index in range(BLOCKS)]
    acc_gain = [jnp.zeros((2, width), jnp.float32) for layer_index in range(BLOCKS)]
    acc_shift = [jnp.zeros((3, width), jnp.float32) for layer_index in range(BLOCKS)]
    outs_large, outs_small, grads_large, grads_small = ([], [], [], [])
    for micro_step in range(MICRO):
        large_part = large_in[micro_step * micro_large : (micro_step + 1) * micro_large]
        small_part = small_in[micro_step * micro_small : (micro_step + 1) * micro_small]
        stream = jnp.concatenate(
            [large_part.reshape(-1, width), small_part.reshape(-1, width)], 0
        ).astype(jnp.float32)
        saved = []
        for layer_index in range(BLOCKS):
            filt_full, in_full, out_full = fetch(layer_index, True)
            halves = filt_full.reshape(2, FL, width).astype(jnp.float32)
            mixed = stream + branch_first(
                stream, gains[layer_index, 0], biases[layer_index, 0], halves[0], halves[1]
            )
            second = layer_norm(mixed, gains[layer_index, 1], biases[layer_index, 1]).astype(
                jnp.bfloat16
            )
            pre_act = jnp.dot(
                second, in_full[:width], preferred_element_type=jnp.float32
            ) + in_full[width].astype(jnp.float32)
            active = exact_gelu(pre_act).astype(jnp.bfloat16)
            saved.append((stream, mixed, second, pre_act))
            stream = (
                mixed
                + jnp.dot(active, out_full, preferred_element_type=jnp.float32)
                + biases[layer_index, 2]
            )
        outs_large.append(stream[:large_rows].reshape(large_part.shape).astype(jnp.bfloat16))
        outs_small.append(stream[large_rows:].reshape(small_part.shape).astype(jnp.bfloat16))
        large_back = large_cot[micro_step * micro_large : (micro_step + 1) * micro_large]
        small_back = small_cot[micro_step * micro_small : (micro_step + 1) * micro_small]
        grad = jnp.concatenate(
            [large_back.reshape(-1, width), small_back.reshape(-1, width)], 0
        ).astype(jnp.float32)
        for layer_index in reversed(range(BLOCKS)):
            block_input, mixed, second, pre_act = saved[layer_index]
            filt_full, in_full, out_full = fetch(layer_index, False)
            halves = filt_full.reshape(2, FL, width).astype(jnp.float32)
            grad_low = grad.astype(jnp.bfloat16)
            active, gelu_back = jax.vjp(exact_gelu, pre_act)
            active = active.astype(jnp.bfloat16)
            acc_out[layer_index] = acc_out[layer_index] + jnp.einsum(
                "tf,td->fd", active, grad_low, preferred_element_type=jnp.float32
            )
            bias_out_grad = jnp.sum(grad, axis=0)
            active_grad = jnp.einsum(
                "td,fd->tf", grad_low, out_full, preferred_element_type=jnp.float32
            )
            pre_grad = gelu_back(active_grad)[0]
            pre_low = pre_grad.astype(jnp.bfloat16)
            acc_in[layer_index] = acc_in[layer_index] + jnp.einsum(
                "td,tf->df", second, pre_low, preferred_element_type=jnp.float32
            )
            acc_in_bias[layer_index] = acc_in_bias[layer_index] + jnp.sum(pre_grad, axis=0)
            second_grad = jnp.einsum(
                "tf,df->td", pre_low, in_full[:width], preferred_element_type=jnp.float32
            )
            unused, norm_back = jax.vjp(
                layer_norm, mixed, gains[layer_index, 1], biases[layer_index, 1]
            )
            mixed_part, gain_two, shift_two = norm_back(second_grad)
            mixed_grad = grad + mixed_part
            unused, first_back = jax.vjp(
                branch_first,
                block_input,
                gains[layer_index, 0],
                biases[layer_index, 0],
                halves[0],
                halves[1],
            )
            input_part, gain_one, shift_one, filt_re_grad, filt_im_grad = first_back(mixed_grad)
            grad = mixed_grad + input_part
            acc_filter[layer_index] = acc_filter[layer_index] + jnp.stack(
                [filt_re_grad, filt_im_grad], 0
            )
            acc_gain[layer_index] = acc_gain[layer_index] + jnp.stack([gain_one, gain_two], 0)
            acc_shift[layer_index] = acc_shift[layer_index] + jnp.stack(
                [shift_one, shift_two, bias_out_grad], 0
            )
        grads_large.append(grad[:large_rows].reshape(large_part.shape))
        grads_small.append(grad[large_rows:].reshape(small_part.shape))
    filter_shards, in_shards, out_shards = ([], [], [])
    for layer_index in range(BLOCKS):
        in_whole = jnp.concatenate([acc_in[layer_index], acc_in_bias[layer_index][None, :]], 0)
        filter_piece, in_piece, out_piece = (
            lax.psum_scatter(
                acc_filter[layer_index].reshape(-1),
                ("wide", "narrow"),
                scatter_dimension=0,
                tiled=True,
            ),
            lax.psum_scatter(in_whole, ("wide", "narrow"), scatter_dimension=1, tiled=True),
            lax.psum_scatter(
                acc_out[layer_index], ("wide", "narrow"), scatter_dimension=0, tiled=True
            ),
        )
        filter_shards.append(filter_piece)
        in_shards.append(in_piece)
        out_shards.append(out_piece)
    gain_total, shift_total = lax.psum(
        (jnp.stack(acc_gain, 0), jnp.stack(acc_shift, 0)), ("wide", "narrow")
    )
    return (
        jnp.concatenate(outs_large, 0),
        jnp.concatenate(outs_small, 0),
        jnp.concatenate(grads_large, 0),
        jnp.concatenate(grads_small, 0),
        jnp.stack(filter_shards, 0),
        jnp.stack(in_shards, 0),
        jnp.stack(out_shards, 0),
        gain_total,
        shift_total,
    )


MESH_ID = pl.DeviceIdType.MESH
bf16, f32 = jnp.bfloat16, jnp.float32
D, PS, EPS = 384, 36, 1e-6
LP = 208
Q = 4
SR = Q * PS
TILE = 256
HID = 48
FLP = 128
SPEC = 2 * FLP
QF = Q * FS


def dft_arrays(n):
    half = n // 2 + 1
    places, modes = np.arange(n * n), np.arange(n * half)
    phase = ((modes // half)[:, None] * (places // n)[None] + (modes % half)[:, None] * (places % n)[None]) % n
    theta = phase * (2 * math.pi / n)
    fwd_re, fwd_im = np.cos(theta) / n, -np.sin(theta) / n
    weight = np.where((modes % half == 0) | (2 * (modes % half) == n), 1.0, 2.0)
    return fwd_re, fwd_im, fwd_re * weight[:, None], fwd_im * weight[:, None]


def interpolation(rows, cols):
    span = np.arange(rows) * (cols - 1)
    low = span // (rows - 1)
    part = (span - low * (rows - 1)) / (rows - 1)
    at = np.arange(cols)[None]
    return np.where(at == low[:, None], 1 - part[:, None], 0.0) + np.where(at == low[:, None] + 1, part[:, None], 0.0)


def two_terms(table):
    table = np.asarray(table, np.float32)
    high = table.astype(ml_dtypes.bfloat16)
    low = (table - high.astype(np.float32)).astype(ml_dtypes.bfloat16)
    return np.concatenate([high, low], 0)


def constant_tables():
    pos = np.arange(FL) // 7 * 8 + np.arange(FL) % 7
    rows = np.concatenate([pos, FLP + pos])
    fr, fi, ir, ii = dft_arrays(GL)
    fwd, inv = np.zeros((SPEC, LP)), np.zeros((SPEC, LP))
    fwd[rows, :PL], inv[rows, :PL] = np.concatenate([fr, fi]), np.concatenate([ir, ii])
    fr, fi, ir, ii = dft_arrays(GS)
    sfwd, sinv = np.zeros((2 * QF, SR)), np.zeros((2 * QF, SR))
    for q in range(Q):
        at = slice(q * PS, (q + 1) * PS)
        for half, a, b in ((0, fr, ir), (1, fi, ii)):
            to = slice(half * QF + q * FS, half * QF + (q + 1) * FS)
            sfwd[to, at], sinv[to, at] = a, b
    shrink = np.zeros((FS, FLP))
    shrink[:, pos] = (
        interpolation(GS, GL)[:, None, :, None] * interpolation(GS // 2 + 1, GL // 2 + 1)[None, :, None, :]
    ).reshape(FS, FL)
    pick = np.zeros((32, SPEC))
    pick[np.arange(32), 8 * np.arange(32) + 7] = 1
    spread = np.arange(FF)[None] % HID == np.arange(128)[:, None]
    plain = lambda t: np.asarray(t, np.float32).astype(ml_dtypes.bfloat16)
    return [two_terms(t) for t in (fwd, inv.T, inv, fwd.T, sfwd, sinv.T, sinv, sfwd.T, shrink, shrink.T)] + [
        plain(pick), plain(pick.T), plain(spread), plain(spread.T)]


def mm(a, b):
    return lax.dot_general(a, b, (((1,), (0,)), ((), ())), preferred_element_type=f32)


def mm_nt(a, b):
    return lax.dot_general(a, b, (((1,), (1,)), ((), ())), preferred_element_type=f32)


def mm_tn(a, b):
    return lax.dot_general(a, b, (((0,), (0,)), ((), ())), preferred_element_type=f32)


def halves(v):
    high = v.astype(bf16)
    return high, (v - high.astype(f32)).astype(bf16)


def apply_table(table, v):
    rows = table.shape[0] // 2
    high, low = halves(v)
    both = mm(table, high)
    return both[:rows] + both[rows:] + mm(table[:rows], low)


def standardize(v):
    centre = v - jnp.sum(v, -1, keepdims=True) * (1.0 / D)
    r = lax.rsqrt(jnp.sum(centre * centre, -1, keepdims=True) * (1.0 / D) + EPS)
    return centre * r, r


def norm_back(vh, r, q):
    mean_q = jnp.sum(q, -1, keepdims=True) * (1.0 / D)
    mean_qv = jnp.sum(q * vh, -1, keepdims=True) * (1.0 / D)
    return r * (q - mean_q - vh * mean_qv)


def fold(v):
    return jnp.sum(v.reshape(v.shape[0] // 8, 8, v.shape[1]), 0)


def aligned(v, m):
    return v if isinstance(v, int) else pl.multiple_of(v, m)


N_SEND = 256
VMEM_BYTES = 62 << 20


def fused_kernel(large, small, *refs):
    (large_in, small_in, large_cot, small_cot, own_in, own_out, own_pack, gains, biases,
     t_fwd, t_inv, t_inv_t, t_fwd_t, t_sfwd, t_sinv, t_sinv_t, t_sfwd_t, t_shrink, t_shrink_t,
     t_pick, t_pick_t, t_spread, t_spread_t,
     out_large, out_small, grad_large, grad_small, g_pack, g_in, g_out, g_vec,
     xs, vh1, r1, vh2, r2, second, active, slope, sv_large, sv_small, grad_low, back,
     w_in, w_out, pack, filt, filt_s, b_in, facc, sacc, bacc, vacc,
     whole, kept, s_core, s_one, s_two, s_z, r_core, r_one, r_two, r_z,
     f_core, f_keep, f_xy, f_z, v_send, v_core, v_xy, v_z,
     send_sem, recv_sem) = refs
    rows = xs.shape[0]
    groups = small // Q
    base = large * LP
    wide, narrow = lax.axis_index("wide"), lax.axis_index("narrow")
    z, x, y, c = lax.div(wide, 2), lax.rem(wide, 2), lax.div(narrow, 2), lax.rem(narrow, 2)
    other = {"x": 1 - x, "y": 1 - y, "c": 1 - c}
    at = lambda zz, xx, yy, cc: (zz * 2 + xx, yy * 2 + cc)
    z_of = lambda k: lax.rem(z + k, 4)
    z_from = lambda k: lax.rem(z + 4 - k, 4)
    peer = {"x": at(z, 1 - x, y, c), "y": at(z, x, 1 - y, c), "xy": at(z, 1 - x, 1 - y, c), "c": at(z, x, y, 1 - c)}
    for k in (1, 2, 3):
        peer[k] = at(z_of(k), x, y, c)

    ids, started = {}, {}

    def copy(key, src, dst, to):
        i = ids.setdefault(key, len(ids))
        return pltpu.make_async_remote_copy(
            src_ref=src, dst_ref=dst, send_sem=send_sem.at[i], recv_sem=recv_sem.at[i],
            device_id=peer[to], device_id_type=MESH_ID)

    def send(key, src, dst, to):
        d = copy(key, src, dst, to)
        d.start()
        started[key] = d

    def sent(key):
        if key in started:
            started.pop(key).wait_send()

    def gather_ops(j, name):
        ref, own = (w_in, own_in) if name == "in" else (w_out, own_out)
        first, second_axis = ("x", "y") if name == "in" else ("y", "x")

        def z_send():
            ref[j, z, x, y, c] = own[j]
            for k in (1, 3, 2):
                send(("z", j, name, k), own.at[j], ref.at[j, z, x, y, c], k)

        def first_send(k):
            zz = z_from(k)
            if k:
                slot = ref.at[j, zz, x, y, c]
                copy(("z", j, name, k), own.at[j], slot, k).wait_recv()
            piece = ref.at[j, zz, x, y, c]
            send(("1", j, name, k), piece, piece, first)

        def second_send(k):
            zz = z_from(k)
            got = ref.at[j, zz, 1 - x, y, c] if first == "x" else ref.at[j, zz, x, 1 - y, c]
            copy(("1", j, name, k), got, got, first).wait_recv()
            piece = ref.at[j, zz, :, y, c] if first == "x" else ref.at[j, zz, x, :, c]
            send(("2", j, name, k), piece, piece, second_axis)

        def core_send(k):
            zz = z_from(k)
            got = ref.at[j, zz, :, 1 - y, c] if first == "x" else ref.at[j, zz, 1 - x, :, c]
            copy(("2", j, name, k), got, got, second_axis).wait_recv()
            piece = ref.at[j, zz, :, :, c]
            send(("c", j, name, k), piece, piece, "c")

        def core_wait(k):
            got = ref.at[j, z_from(k), :, :, 1 - c]
            copy(("c", j, name, k), got, got, "c").wait_recv()

        return z_send, first_send, second_send, core_send, core_wait

    ORDER = (0, 1, 3, 2)

    def pack_z():
        pack[z, x, y, c] = own_pack[...]
        for k in (1, 3, 2):
            send(("pz", k), own_pack, pack.at[z, x, y, c], k)

    PLANE = (("x", lambda: (1 - x, y)), ("y", lambda: (x, 1 - y)), ("xy", lambda: (1 - x, 1 - y)))

    def pack_xy():
        for k in (1, 3, 2):
            copy(("pz", k), own_pack, pack.at[z_from(k), x, y, c], k).wait_recv()
        for to, _ in PLANE:
            piece = pack.at[:, x, y, c]
            send(("pp", to), piece, piece, to)

    def pack_core():
        for to, where in PLANE:
            xx, yy = where()
            got = pack.at[:, xx, yy, c]
            copy(("pp", to), got, got, to).wait_recv()
        piece = pack.at[:, :, :, c]
        send(("pc",), piece, piece, "c")

    def pack_wait():
        got = pack.at[:, :, :, 1 - c]
        copy(("pc",), got, got, "c").wait_recv()

    def reduce_core(j, a, k, value):
        whole[...] = value.reshape(4, 2, HID, D)
        sent(("rc", 1, a, k))
        for i in range(2):
            for l in range(2):
                kept[a, k, i, l] = whole[2 * i + l, c]
                s_core[a, k, i, l] = whole[2 * i + l, 1 - c].astype(bf16)
        send(("rc", j, a, k), s_core.at[a, k], r_core.at[j, a, k], "c")

    def reduce_one(j, a, k):
        copy(("rc", j, a, k), s_core.at[a, k], r_core.at[j, a, k], "c").wait_recv()
        sent(("r1", 1, a, k))
        for i in range(2):
            if a == 0:
                s_one[a, k, i] = (kept[a, k, i, 1 - y] + r_core[j, a, k, i, 1 - y].astype(f32)).astype(bf16)
            else:
                s_one[a, k, i] = (kept[a, k, 1 - x, i] + r_core[j, a, k, 1 - x, i].astype(f32)).astype(bf16)
        send(("r1", j, a, k), s_one.at[a, k], r_one.at[j, a, k], "y" if a == 0 else "x")

    def reduce_two(j, a, k):
        copy(("r1", j, a, k), s_one.at[a, k], r_one.at[j, a, k], "y" if a == 0 else "x").wait_recv()
        if a == 0:
            s = kept[a, k, 1 - x, y] + r_core[j, a, k, 1 - x, y].astype(f32) + r_one[j, a, k, 1 - x].astype(f32)
        else:
            s = kept[a, k, x, 1 - y] + r_core[j, a, k, x, 1 - y].astype(f32) + r_one[j, a, k, 1 - y].astype(f32)
        sent(("r2", 1, a, k))
        s_two[a, k] = s.astype(bf16)
        send(("r2", j, a, k), s_two.at[a, k], r_two.at[j, a, k], "x" if a == 0 else "y")

    def reduce_z(j, a, k):
        copy(("r2", j, a, k), s_two.at[a, k], r_two.at[j, a, k], "x" if a == 0 else "y").wait_recv()
        one = r_one[j, a, k, x] if a == 0 else r_one[j, a, k, y]
        s = kept[a, k, x, y] + r_core[j, a, k, x, y].astype(f32) + one.astype(f32) + r_two[j, a, k].astype(f32)
        if k:
            sent(("rz", 1, a, k))
            s_z[a, k - 1] = s.astype(bf16)
            send(("rz", j, a, k), s_z.at[a, k - 1], r_z.at[j, a, k - 1], k)
        else:
            dst = g_in if a == 0 else g_out
            dst[j] = s

    def reduce_end(j, a):
        dst = g_in if a == 0 else g_out
        for k in (1, 2, 3):
            copy(("rz", j, a, k), s_z.at[a, k - 1], r_z.at[j, a, k - 1], k).wait_recv()
        dst[j] = dst[j] + r_z[j, a, 0].astype(f32) + r_z[j, a, 1].astype(f32) + r_z[j, a, 2].astype(f32)

    def small_core(j):
        send(("fc", j), facc.at[j, :, :, :, 1 - c], f_core.at[j], "c")
        if j == 0:
            v_send[...] = jnp.concatenate([jnp.sum(vacc[i], 0, keepdims=True) for i in range(10)] + [jnp.zeros((6, D), f32)], 0)
            send(("vc",), v_send, v_core, "c")

    def small_xy(j):
        copy(("fc", j), f_core.at[j], f_core.at[j], "c").wait_recv()
        for zz in range(4):
            for i in range(2):
                for l in range(2):
                    f_keep[j, i, l, zz] = facc[j, zz, i, l, c] + f_core[j, zz, i, l]
        for n, (to, where) in enumerate(PLANE):
            xx, yy = where()
            send(("fp", j, to), f_keep.at[j, xx, yy], f_xy.at[j, n], to)
        if j == 0:
            copy(("vc",), v_core, v_core, "c").wait_recv()
            v_xy[x, y] = v_send[...] + v_core[...]
            for to, where in PLANE:
                send(("vp", to), v_xy.at[x, y], v_xy.at[x, y], to)

    def small_z(j):
        for n, (to, where) in enumerate(PLANE):
            copy(("fp", j, to), f_xy.at[j, n], f_xy.at[j, n], to).wait_recv()
        for zz in range(4):
            f_keep[j, x, y, zz] = f_keep[j, x, y, zz] + f_xy[j, 0, zz] + f_xy[j, 1, zz] + f_xy[j, 2, zz]
        for k in (1, 3, 2):
            send(("fz", j, k), f_keep.at[j, x, y, z_of(k)], f_z.at[j, k - 1], k)
        if j == 0:
            for to, where in PLANE:
                xx, yy = where()
                got = v_xy.at[xx, yy]
                copy(("vp", to), got, got, to).wait_recv()
            v_z[z] = v_xy[0, 0] + v_xy[0, 1] + v_xy[1, 0] + v_xy[1, 1]
            for k in (1, 3, 2):
                send(("vz", k), v_z.at[z], v_z.at[z], k)

    def small_end(j):
        for k in (1, 2, 3):
            copy(("fz", j, k), f_z.at[j, k - 1], f_z.at[j, k - 1], k).wait_recv()
        g_pack[j] = f_keep[j, x, y, z] + f_z[j, 0] + f_z[j, 1] + f_z[j, 2]
        if j == 0:
            for k in (1, 2, 3):
                got = v_z.at[z_from(k)]
                copy(("vz", k), got, got, k).wait_recv()
            g_vec[...] = v_z[0] + v_z[1] + v_z[2] + v_z[3]

    def load_rows(a, b):
        def one(i, _):
            xs[pl.ds(aligned(i * LP + LP - 16, 16), 16), :] = jnp.zeros((16, D), f32)
            xs[pl.ds(aligned(i * LP, 16), PL), :] = a[i].astype(f32)
            return 0
        lax.fori_loop(0, large, one, 0)
        for i in range(small):
            xs[base + i * PS : base + (i + 1) * PS, :] = b[i].astype(f32)
        xs[base + small * PS :, :] = jnp.zeros((rows - base - small * PS, D), f32)

    def store_rows(a, b):
        def one(i, _):
            a[i] = xs[pl.ds(aligned(i * LP, 16), PL), :].astype(a.dtype)
            return 0
        lax.fori_loop(0, large, one, 0)
        for i in range(small):
            b[i] = xs[base + i * PS : base + (i + 1) * PS, :].astype(b.dtype)

    def spread_rows(r):
        return jnp.broadcast_to(r, (r.shape[0], 128))

    def wide_rows(r):
        return jnp.concatenate([r, r, r], -1)

    def mean_row(n_rows, period, scale):
        row = lax.broadcasted_iota(jnp.int32, (n_rows, 1), 0)
        hit = row == 0
        for q in range(1, period):
            hit = hit | (row == q * FS)
        return jnp.where(hit, scale, 0.0).astype(f32)

    def crop_loops(body):
        def big(i, _):
            body(pl.ds(aligned(i * LP, 16), LP), i, True)
            return 0
        def little(i, _):
            body(pl.ds(aligned(base + i * SR, 16), SR), i, False)
            return 0
        lax.fori_loop(0, large, big, 0)
        lax.fori_loop(0, groups, little, 0)

    def to_spectrum(j):
        def body(o, i, big):
            vh, r = standardize(xs[o, :])
            vh1[j, o, :] = vh.astype(bf16)
            r1[j, o, :] = spread_rows(r)
            if big:
                sv_large[j, i] = apply_table(t_fwd[...], vh)
            else:
                sv_small[j, i] = apply_table(t_sfwd[...], vh)
        crop_loops(body)

    def unpack_filters(j):
        f = pack[:, :, :, :, j].reshape(SPEC, D)
        filt[j] = f.astype(f32)
        for h in range(2):
            s = mm(t_shrink[...], f[h * FLP : (h + 1) * FLP])
            s = s[:FS] + s[FS:]
            filt_s[j, h * QF : (h + 1) * QF] = jnp.concatenate([s] * Q, 0)
        bias = mm(t_pick[...], f[:, :128]).astype(bf16)
        bias = mm(bias, t_spread[...])
        mine = lax.div(lax.broadcasted_iota(jnp.int32, (32, FF), 1), HID) == lax.broadcasted_iota(jnp.int32, (32, FF), 0)
        b_in[j] = jnp.sum(jnp.where(mine, bias, 0.0), 0, keepdims=True)

    def spectrum_of(j, i, big):
        sv = sv_large[j, i] if big else sv_small[j, i]
        h = FLP if big else QF
        dc = mean_row(h, 1, float(GL)) if big else mean_row(h, Q, float(GS))
        re = sv[:h] * gains[j, 0:1, :] + dc * biases[j, 0:1, :]
        im = sv[h:] * gains[j, 0:1, :]
        f = filt[j] if big else filt_s[j]
        return sv, re, im, f[:h], f[h:], dc

    def from_spectrum(j):
        def body(o, i, big):
            _, re, im, fr, fi, _ = spectrum_of(j, i, big)
            out = jnp.concatenate([re * fr - im * fi, re * fi + im * fr], 0)
            xs[o, :] = xs[o, :] + apply_table(t_inv[...] if big else t_sinv[...], out)
        crop_loops(body)

    def tiles(body):
        def one(t, _):
            body(pl.ds(aligned(t * TILE, TILE), TILE))
            return 0
        lax.fori_loop(0, rows // TILE, one, 0)

    def expand(j):
        def body(o):
            vh, r = standardize(xs[o, :])
            vh2[j, o, :] = vh
            r2[j, o, :] = spread_rows(r)
            s = (vh * gains[j, 1:2, :] + biases[j, 1:2, :]).astype(bf16)
            second[j, o, :] = s
            for h in range(2):
                w = w_in[j, 2 * h : 2 * h + 2].reshape(FF // 2, D)
                pre = mm_nt(s, w) + b_in[j, :, h * (FF // 2) : (h + 1) * (FF // 2)]
                phi = 0.5 + 0.5 * lax.erf(pre * (1 / math.sqrt(2)))
                active[j, h, o, :] = (pre * phi).astype(bf16)
                slope[j, h, o, :] = (phi + pre * (jnp.exp(-0.5 * pre * pre) * (1 / math.sqrt(2 * math.pi)))).astype(bf16)
        tiles(body)

    def contract(j):
        def body(o):
            s = xs[o, :] + biases[j, 2:3, :]
            for h in range(2):
                s = s + mm(active[j, h, o, :], w_out[j, 2 * h : 2 * h + 2].reshape(FF // 2, D))
            xs[o, :] = s
        tiles(body)

    def z_offset(k):
        zz = z_of(k)
        return lax.div(zz, 2), pl.ds(aligned(lax.rem(zz, 2) * (FF // 4), 128), FF // 4)

    def back_hidden(j, h, last):
        def body(o):
            w = w_out[j, pl.ds(2 * h, 2)].reshape(FF // 2, D)
            pg = mm_nt(grad_low[o, :], w) * slope[j, h, o, :].astype(f32)
            bacc[j, h] += fold(pg)
            p = pg.astype(bf16)
            slope[j, h, o, :] = p
            sg = mm(p, w_in[j, pl.ds(2 * h, 2)].reshape(FF // 2, D))
            if not last:
                back[o, :] = sg
            else:
                sg = sg + back[o, :]
                vh = vh2[j, o, :]
                vacc[2 * j + 1] += fold(sg * vh)
                vacc[4 + 3 * j + 1] += fold(sg)
                xs[o, :] = xs[o, :] + norm_back(vh, wide_rows(r2[j, o, :]), sg * gains[j, 1:2, :])
        tiles(body)

    def weight_in(j, k):
        h, lanes = z_offset(k)
        return mm_tn(slope[j, h, :, lanes], second[j])

    def weight_out(j, k):
        h, lanes = z_offset(k)
        return mm_tn(active[j, h, :, lanes], grad_low[...])

    def back_spectrum(j):
        sacc[...] = jnp.zeros_like(sacc)
        facc[j] = jnp.zeros(facc.shape[1:], f32)
        def body(o, i, big):
            sv, re, im, fr, fi, dc = spectrum_of(j, i, big)
            h = FLP if big else QF
            sg = apply_table(t_inv_t[...] if big else t_sinv_t[...], xs[o, :])
            gr, gi = sg[:h], sg[h:]
            d_re, d_im = re * gr + im * gi, re * gi - im * gr
            if big:
                facc[j] += jnp.concatenate([d_re, d_im], 0).reshape(4, 2, 2, 2, 8, D)
            else:
                sacc[...] += jnp.concatenate([d_re, d_im], 0)
            n_re, n_im = gr * fr + gi * fi, gi * fr - gr * fi
            vacc[2 * j] += fold(n_re * sv[:h]) + fold(n_im * sv[h:])
            vacc[4 + 3 * j] += fold(n_re * dc)
            n = jnp.concatenate([n_re, n_im], 0)
            if big:
                sv_large[j, i] = n
            else:
                sv_small[j, i] = n
        crop_loops(body)
        for h in range(2):
            s = sacc[h * QF : (h + 1) * QF]
            s = s[:FS] + s[FS : 2 * FS] + s[2 * FS : 3 * FS] + s[3 * FS :]
            facc[j, 2 * h : 2 * h + 2] += apply_table(t_shrink_t[...], s).reshape(2, 2, 2, 2, 8, D)
        mine = lax.div(lax.broadcasted_iota(jnp.int32, (32, FF), 1), HID) == lax.broadcasted_iota(jnp.int32, (32, FF), 0)
        row = jnp.sum(jnp.concatenate([bacc[j, 0], bacc[j, 1]], -1), 0, keepdims=True)
        high, low = halves(jnp.where(mine, row, 0.0))
        row = mm(high, t_spread_t[...]) + mm(low, t_spread_t[...])
        high, low = halves(row)
        row = mm(t_pick_t[...], high) + mm(t_pick_t[...], low)
        facc[j] += jnp.concatenate([row, jnp.zeros((SPEC, D - 128), f32)], -1).reshape(4, 2, 2, 2, 8, D)

    def back_rows(j):
        def body(o, i, big):
            n = sv_large[j, i] if big else sv_small[j, i]
            ng = apply_table(t_fwd_t[...] if big else t_sfwd_t[...], n)
            xs[o, :] = xs[o, :] + norm_back(vh1[j, o, :].astype(f32), wide_rows(r1[j, o, :]), ng * gains[j, 0:1, :])
        crop_loops(body)

    barrier = pltpu.get_barrier_semaphore()
    for to in peer.values():
        pl.semaphore_signal(barrier, 1, device_id=to, device_id_type=MESH_ID)
    load_rows(large_in, small_in)
    bacc[...] = jnp.zeros_like(bacc)
    vacc[...] = jnp.zeros_like(vacc)
    pl.semaphore_wait(barrier, len(peer))

    i0, o0, i1, o1 = gather_ops(0, "in"), gather_ops(0, "out"), gather_ops(1, "in"), gather_ops(1, "out")
    pack_z()
    i0[0](); i0[1](0)
    o0[0](); o0[1](0)
    to_spectrum(0)
    pack_xy()
    for k in ORDER[1:]:
        i0[1](k)
        o0[1](k)
    pack_core()
    for k in ORDER:
        i0[2](k)
        o0[2](k)
    pack_wait()
    unpack_filters(0)
    unpack_filters(1)
    from_spectrum(0)
    for k in ORDER:
        i0[3](k)
    for k in ORDER:
        i0[4](k)
    expand(0)
    for k in ORDER:
        o0[3](k)
    i1[0](); i1[1](0)
    o1[0](); o1[1](0)
    for k in ORDER:
        o0[4](k)
    contract(0)
    for k in ORDER[1:]:
        i1[1](k)
        o1[1](k)
    to_spectrum(1)
    for k in ORDER:
        i1[2](k)
        o1[2](k)
    from_spectrum(1)
    for k in ORDER:
        i1[3](k)
        o1[3](k)
    for k in ORDER:
        i1[4](k)
    expand(1)
    for k in ORDER:
        o1[4](k)
    contract(1)
    store_rows(out_large, out_small)
    load_rows(large_cot, small_cot)

    half_z = lax.div(z, 2)
    queue = []

    def advance():
        for item in list(queue):
            stage, j, a, k = item
            (reduce_one, reduce_two, reduce_z)[stage](j, a, k)
            queue.remove(item)
            if stage < 2:
                queue.append((stage + 1, j, a, k))

    for j in (1, 0):
        def low(o):
            g = xs[o, :]
            vacc[4 + 3 * j + 2] += fold(g)
            grad_low[o, :] = g.astype(bf16)
        tiles(low)
        for k in (1, 2, 3, 0):
            reduce_core(j, 1, k, weight_out(j, k))
            advance()
            queue.append((0, j, 1, k))
        back_hidden(j, 1 - half_z, False)
        advance()
        back_hidden(j, half_z, True)
        for k in (1, 2, 3, 0):
            reduce_core(j, 0, k, weight_in(j, k))
            advance()
            queue.append((0, j, 0, k))
        back_spectrum(j)
        small_core(j)
        advance()
        back_rows(j)
        advance()
        small_xy(j)
        if j == 1:
            while queue:
                advance()
            small_z(1)
    while queue:
        advance()
    small_z(0)
    store_rows(grad_large, grad_small)
    for j in (1, 0):
        for a in (1, 0):
            reduce_end(j, a)
        small_end(j)
    for key in list(started):
        sent(key)
    assert len(ids) <= N_SEND


def fused(large_in, small_in, large_cot, small_cot, filters, w_in, w_out, gains, biases):
    large, small = large_in.shape[0], small_in.shape[0]
    rows = -(-(large * LP + small * PS) // TILE) * TILE
    own_in = jnp.swapaxes(w_in[:, :D], 1, 2)
    bias = jnp.pad(w_in[:, D:, :], ((0, 0), (0, 0), (0, D - HID)))
    own_pack = jnp.concatenate([filters.reshape(BLOCKS, 7, D), bias], 1)
    V = pltpu.VMEM
    outs = [(large_in.shape, bf16), (small_in.shape, bf16), (large_in.shape, f32), (small_in.shape, f32),
            ((BLOCKS, 8, D), f32), ((BLOCKS, HID, D), f32), ((BLOCKS, HID, D), f32), ((16, D), f32)]
    grid8 = (4, 2, 2, 2)
    scratch = [
        V((rows, D), f32), V((BLOCKS, rows, D), bf16), V((BLOCKS, rows, 128), f32), V((BLOCKS, rows, D), f32),
        V((BLOCKS, rows, 128), f32), V((BLOCKS, rows, D), bf16), V((BLOCKS, 2, rows, FF // 2), bf16),
        V((BLOCKS, 2, rows, FF // 2), bf16), V((BLOCKS, large, SPEC, D), f32), V((BLOCKS, small // Q, 2 * QF, D), f32),
        V((rows, D), bf16), V((rows, D), f32),
        V((BLOCKS, *grid8, HID, D), bf16), V((BLOCKS, *grid8, HID, D), bf16), V((*grid8, BLOCKS, 8, D), bf16),
        V((BLOCKS, SPEC, D), f32), V((BLOCKS, 2 * QF, D), f32), V((BLOCKS, 1, FF), f32),
        V((BLOCKS, *grid8, 8, D), f32), V((2 * QF, D), f32), V((BLOCKS, 2, 8, FF // 2), f32), V((10, 8, D), f32),
        V((4, 2, HID, D), f32), V((2, 4, 2, 2, HID, D), f32),
        V((2, 4, 2, 2, HID, D), bf16), V((2, 4, 2, HID, D), bf16), V((2, 4, HID, D), bf16), V((2, 3, HID, D), bf16),
        V((BLOCKS, 2, 4, 2, 2, HID, D), bf16), V((BLOCKS, 2, 4, 2, HID, D), bf16), V((BLOCKS, 2, 4, HID, D), bf16),
        V((BLOCKS, 2, 3, HID, D), bf16),
        V((BLOCKS, 4, 2, 2, 8, D), f32), V((BLOCKS, 2, 2, 4, 8, D), f32), V((BLOCKS, 3, 4, 8, D), f32), V((BLOCKS, 3, 8, D), f32),
        V((16, D), f32), V((16, D), f32), V((2, 2, 16, D), f32), V((4, 16, D), f32),
        pltpu.SemaphoreType.DMA((N_SEND,)), pltpu.SemaphoreType.DMA((N_SEND,)),
    ]
    tables = [jnp.asarray(t) for t in constant_tables()]
    vmem = pl.BlockSpec(memory_space=pltpu.VMEM)
    result = pl.pallas_call(
        partial(fused_kernel, large, small),
        out_shape=[jax.ShapeDtypeStruct(s, d) for s, d in outs],
        in_specs=[vmem] * (9 + len(tables)),
        out_specs=[vmem] * len(outs),
        scratch_shapes=scratch,
        compiler_params=pltpu.CompilerParams(collective_id=0, has_side_effects=True, vmem_limit_bytes=VMEM_BYTES),
        name="gfnet_step",
    )(large_in, small_in, large_cot, small_cot, own_in, w_out, own_pack, gains, biases, *tables)
    out_large, out_small, grad_large, grad_small, g_pack, g_in, g_out, g_vec = result
    grad_in = jnp.concatenate([jnp.swapaxes(g_in, 1, 2), g_pack[:, 7:8, :HID]], 1)
    return (out_large, out_small, grad_large, grad_small, g_pack[:, :7].reshape(BLOCKS, -1), grad_in, g_out,
            g_vec[:4].reshape(BLOCKS, 2, D), g_vec[4:10].reshape(BLOCKS, 3, D))


def solution(mesh):
    in_specs = (
        P(("wide", "narrow"), None, None),
        P(("wide", "narrow"), None, None),
        P(("wide", "narrow"), None, None),
        P(("wide", "narrow"), None, None),
        P(None, ("wide", "narrow")),
        P(None, None, ("wide", "narrow")),
        P(None, ("wide", "narrow"), None),
        P(),
        P(),
    )
    out_specs = (
        P(("wide", "narrow"), None, None),
        P(("wide", "narrow"), None, None),
        P(("wide", "narrow"), None, None),
        P(("wide", "narrow"), None, None),
        P(None, ("wide", "narrow")),
        P(None, None, ("wide", "narrow")),
        P(None, ("wide", "narrow"), None),
        P(),
        P(),
    )
    body = fused if dict(mesh.shape) == {"wide": 8, "narrow": 4} else per_device
    return jax.shard_map(
        body, mesh=mesh, in_specs=in_specs, out_specs=out_specs, check_vma=False
    )
```

```python
from functools import partial
import math

import jax
import jax.numpy as jnp
import ml_dtypes
import numpy as np
from jax import lax
from jax.experimental import pallas as pl
from jax.experimental.pallas import tpu as pltpu
from jax.sharding import PartitionSpec as P

FF = 1536
GL = 14
GS = 6
BLOCKS = 2
MICRO = 2
PL = 196
FL = 112
FS = 24


precise = lax.Precision.HIGHEST
epsilon = 1e-06


def dft_tables(grid_cells):
    half_count = grid_cells // 2 + 1
    places = jnp.arange(grid_cells * grid_cells, dtype=jnp.int32)
    place_row = places // grid_cells
    place_col = places % grid_cells
    modes = jnp.arange(grid_cells * half_count, dtype=jnp.int32)
    mode_row = modes // half_count
    mode_col = modes % half_count
    phases = (
        mode_row[:, None] * place_row[None, :] + mode_col[:, None] * place_col[None, :]
    ) % grid_cells
    angles = phases.astype(jnp.float32) * (2.0 * math.pi / grid_cells)
    forward_re = jnp.cos(angles) / grid_cells
    forward_im = -jnp.sin(angles) / grid_cells
    doubling = jnp.where((mode_col == 0) | (2 * mode_col == grid_cells), 1.0, 2.0).astype(
        jnp.float32
    )
    inverse_re = jnp.transpose(forward_re * doubling[:, None])
    inverse_im = jnp.transpose(forward_im * doubling[:, None])
    return (forward_re, forward_im, inverse_re, inverse_im)


def linear_map(size_out, size_in):
    rows_out = jnp.arange(size_out, dtype=jnp.int32)
    spans = rows_out * (size_in - 1)
    lower = spans // (size_out - 1)
    fraction = (spans - lower * (size_out - 1)).astype(jnp.float32) / (size_out - 1)
    columns = jnp.arange(size_in, dtype=jnp.int32)
    first = jnp.where(columns[None, :] == lower[:, None], 1.0 - fraction[:, None], 0.0)
    second = jnp.where(columns[None, :] == lower[:, None] + 1, fraction[:, None], 0.0)
    return first + second


def shrink_map():
    along_rows = linear_map(GS, GL)
    along_cols = linear_map(GS // 2 + 1, GL // 2 + 1)
    return (along_rows[:, None, :, None] * along_cols[None, :, None, :]).reshape(FS, FL)


def filter_grid(patches, tables, filt_re, filt_im):
    forward_re, forward_im, inverse_re, inverse_im = tables
    spec_re = jnp.einsum("fp,bpd->bfd", forward_re, patches, precision=precise)
    spec_im = jnp.einsum("fp,bpd->bfd", forward_im, patches, precision=precise)
    out_re = spec_re * filt_re - spec_im * filt_im
    out_im = spec_re * filt_im + spec_im * filt_re
    back_re = jnp.einsum("pf,bfd->bpd", inverse_re, out_re, precision=precise)
    back_im = jnp.einsum("pf,bfd->bpd", inverse_im, out_im, precision=precise)
    return back_re + back_im


def spectral(normed, large_rows, filt_re, filt_im):
    width = normed.shape[-1]
    shrink = shrink_map()
    small_re = jnp.dot(shrink, filt_re, precision=precise, preferred_element_type=jnp.float32)
    small_im = jnp.dot(shrink, filt_im, precision=precise, preferred_element_type=jnp.float32)
    part_large = filter_grid(
        normed[:large_rows].reshape(-1, GL * GL, width), dft_tables(GL), filt_re, filt_im
    )
    part_small = filter_grid(
        normed[large_rows:].reshape(-1, GS * GS, width), dft_tables(GS), small_re, small_im
    )
    return jnp.concatenate([part_large.reshape(-1, width), part_small.reshape(-1, width)], 0)


def layer_norm(stream, gain, shift):
    centre = stream - jnp.mean(stream, axis=-1, keepdims=True)
    spread = jnp.mean(centre * centre, axis=-1, keepdims=True)
    return centre * lax.rsqrt(spread + epsilon) * gain + shift


def per_device(large_in, small_in, large_cot, small_cot, filters, w_in, w_out, gains, biases):
    width = large_in.shape[-1]
    micro_large = large_in.shape[0] // MICRO
    micro_small = small_in.shape[0] // MICRO
    large_rows = micro_large * PL
    exact_gelu = partial(jax.nn.gelu, approximate=False)

    def fetch(layer_index, forward):
        if forward:
            return (
                lax.all_gather(filters[layer_index], ("wide", "narrow"), axis=0, tiled=True),
                lax.all_gather(w_in[layer_index], ("wide", "narrow"), axis=1, tiled=True),
                lax.all_gather(w_out[layer_index], ("wide", "narrow"), axis=0, tiled=True),
            )
        return (
            lax.all_gather(filters[layer_index], ("wide", "narrow"), axis=0, tiled=True),
            lax.all_gather(w_in[layer_index], ("wide", "narrow"), axis=1, tiled=True),
            lax.all_gather(w_out[layer_index], ("wide", "narrow"), axis=0, tiled=True),
        )

    def branch_first(stream, gain, shift, filt_re, filt_im):
        return spectral(layer_norm(stream, gain, shift), large_rows, filt_re, filt_im)

    acc_filter = [jnp.zeros((2, FL, width), jnp.float32) for layer_index in range(BLOCKS)]
    acc_in = [jnp.zeros((width, FF), jnp.float32) for layer_index in range(BLOCKS)]
    acc_in_bias = [jnp.zeros((FF,), jnp.float32) for layer_index in range(BLOCKS)]
    acc_out = [jnp.zeros((FF, width), jnp.float32) for layer_index in range(BLOCKS)]
    acc_gain = [jnp.zeros((2, width), jnp.float32) for layer_index in range(BLOCKS)]
    acc_shift = [jnp.zeros((3, width), jnp.float32) for layer_index in range(BLOCKS)]
    outs_large, outs_small, grads_large, grads_small = ([], [], [], [])
    for micro_step in range(MICRO):
        large_part = large_in[micro_step * micro_large : (micro_step + 1) * micro_large]
        small_part = small_in[micro_step * micro_small : (micro_step + 1) * micro_small]
        stream = jnp.concatenate(
            [large_part.reshape(-1, width), small_part.reshape(-1, width)], 0
        ).astype(jnp.float32)
        saved = []
        for layer_index in range(BLOCKS):
            filt_full, in_full, out_full = fetch(layer_index, True)
            halves = filt_full.reshape(2, FL, width).astype(jnp.float32)
            mixed = stream + branch_first(
                stream, gains[layer_index, 0], biases[layer_index, 0], halves[0], halves[1]
            )
            second = layer_norm(mixed, gains[layer_index, 1], biases[layer_index, 1]).astype(
                jnp.bfloat16
            )
            pre_act = jnp.dot(
                second, in_full[:width], preferred_element_type=jnp.float32
            ) + in_full[width].astype(jnp.float32)
            active = exact_gelu(pre_act).astype(jnp.bfloat16)
            saved.append((stream, mixed, second, pre_act))
            stream = (
                mixed
                + jnp.dot(active, out_full, preferred_element_type=jnp.float32)
                + biases[layer_index, 2]
            )
        outs_large.append(stream[:large_rows].reshape(large_part.shape).astype(jnp.bfloat16))
        outs_small.append(stream[large_rows:].reshape(small_part.shape).astype(jnp.bfloat16))
        large_back = large_cot[micro_step * micro_large : (micro_step + 1) * micro_large]
        small_back = small_cot[micro_step * micro_small : (micro_step + 1) * micro_small]
        grad = jnp.concatenate(
            [large_back.reshape(-1, width), small_back.reshape(-1, width)], 0
        ).astype(jnp.float32)
        for layer_index in reversed(range(BLOCKS)):
            block_input, mixed, second, pre_act = saved[layer_index]
            filt_full, in_full, out_full = fetch(layer_index, False)
            halves = filt_full.reshape(2, FL, width).astype(jnp.float32)
            grad_low = grad.astype(jnp.bfloat16)
            active, gelu_back = jax.vjp(exact_gelu, pre_act)
            active = active.astype(jnp.bfloat16)
            acc_out[layer_index] = acc_out[layer_index] + jnp.einsum(
                "tf,td->fd", active, grad_low, preferred_element_type=jnp.float32
            )
            bias_out_grad = jnp.sum(grad, axis=0)
            active_grad = jnp.einsum(
                "td,fd->tf", grad_low, out_full, preferred_element_type=jnp.float32
            )
            pre_grad = gelu_back(active_grad)[0]
            pre_low = pre_grad.astype(jnp.bfloat16)
            acc_in[layer_index] = acc_in[layer_index] + jnp.einsum(
                "td,tf->df", second, pre_low, preferred_element_type=jnp.float32
            )
            acc_in_bias[layer_index] = acc_in_bias[layer_index] + jnp.sum(pre_grad, axis=0)
            second_grad = jnp.einsum(
                "tf,df->td", pre_low, in_full[:width], preferred_element_type=jnp.float32
            )
            unused, norm_back = jax.vjp(
                layer_norm, mixed, gains[layer_index, 1], biases[layer_index, 1]
            )
            mixed_part, gain_two, shift_two = norm_back(second_grad)
            mixed_grad = grad + mixed_part
            unused, first_back = jax.vjp(
                branch_first,
                block_input,
                gains[layer_index, 0],
                biases[layer_index, 0],
                halves[0],
                halves[1],
            )
            input_part, gain_one, shift_one, filt_re_grad, filt_im_grad = first_back(mixed_grad)
            grad = mixed_grad + input_part
            acc_filter[layer_index] = acc_filter[layer_index] + jnp.stack(
                [filt_re_grad, filt_im_grad], 0
            )
            acc_gain[layer_index] = acc_gain[layer_index] + jnp.stack([gain_one, gain_two], 0)
            acc_shift[layer_index] = acc_shift[layer_index] + jnp.stack(
                [shift_one, shift_two, bias_out_grad], 0
            )
        grads_large.append(grad[:large_rows].reshape(large_part.shape))
        grads_small.append(grad[large_rows:].reshape(small_part.shape))
    filter_shards, in_shards, out_shards = ([], [], [])
    for layer_index in range(BLOCKS):
        in_whole = jnp.concatenate([acc_in[layer_index], acc_in_bias[layer_index][None, :]], 0)
        filter_piece, in_piece, out_piece = (
            lax.psum_scatter(
                acc_filter[layer_index].reshape(-1),
                ("wide", "narrow"),
                scatter_dimension=0,
                tiled=True,
            ),
            lax.psum_scatter(in_whole, ("wide", "narrow"), scatter_dimension=1, tiled=True),
            lax.psum_scatter(
                acc_out[layer_index], ("wide", "narrow"), scatter_dimension=0, tiled=True
            ),
        )
        filter_shards.append(filter_piece)
        in_shards.append(in_piece)
        out_shards.append(out_piece)
    gain_total, shift_total = lax.psum(
        (jnp.stack(acc_gain, 0), jnp.stack(acc_shift, 0)), ("wide", "narrow")
    )
    return (
        jnp.concatenate(outs_large, 0),
        jnp.concatenate(outs_small, 0),
        jnp.concatenate(grads_large, 0),
        jnp.concatenate(grads_small, 0),
        jnp.stack(filter_shards, 0),
        jnp.stack(in_shards, 0),
        jnp.stack(out_shards, 0),
        gain_total,
        shift_total,
    )


MESH_ID = pl.DeviceIdType.MESH
bf16, f32 = jnp.bfloat16, jnp.float32
D, PS, EPS = 384, 36, 1e-6
LP = 208
Q = 4
SR = Q * PS
TILE = 256
BOTH = ("big", "small")
HID = 48
FLP = 128
SPEC = 2 * FLP
QF = Q * FS


def dft_arrays(n):
    half = n // 2 + 1
    places, modes = np.arange(n * n), np.arange(n * half)
    phase = ((modes // half)[:, None] * (places // n)[None] + (modes % half)[:, None] * (places % n)[None]) % n
    theta = phase * (2 * math.pi / n)
    fwd_re, fwd_im = np.cos(theta) / n, -np.sin(theta) / n
    weight = np.where((modes % half == 0) | (2 * (modes % half) == n), 1.0, 2.0)
    return fwd_re, fwd_im, fwd_re * weight[:, None], fwd_im * weight[:, None]


def interpolation(rows, cols):
    span = np.arange(rows) * (cols - 1)
    low = span // (rows - 1)
    part = (span - low * (rows - 1)) / (rows - 1)
    at = np.arange(cols)[None]
    return np.where(at == low[:, None], 1 - part[:, None], 0.0) + np.where(at == low[:, None] + 1, part[:, None], 0.0)


def two_terms(table):
    table = np.asarray(table, np.float32)
    high = table.astype(ml_dtypes.bfloat16)
    low = (table - high.astype(np.float32)).astype(ml_dtypes.bfloat16)
    return np.concatenate([high, low], 0)


def constant_tables():
    pos = np.arange(FL) // 7 * 8 + np.arange(FL) % 7
    rows = np.concatenate([pos, FLP + pos])
    fr, fi, ir, ii = dft_arrays(GL)
    fwd, inv = np.zeros((SPEC, LP)), np.zeros((SPEC, LP))
    fwd[rows, :PL], inv[rows, :PL] = np.concatenate([fr, fi]), np.concatenate([ir, ii])
    fr, fi, ir, ii = dft_arrays(GS)
    sfwd, sinv = np.zeros((2 * QF, SR)), np.zeros((2 * QF, SR))
    for q in range(Q):
        at = slice(q * PS, (q + 1) * PS)
        for half, a, b in ((0, fr, ir), (1, fi, ii)):
            to = slice(half * QF + q * FS, half * QF + (q + 1) * FS)
            sfwd[to, at], sinv[to, at] = a, b
    shrink = np.zeros((FS, FLP))
    shrink[:, pos] = (
        interpolation(GS, GL)[:, None, :, None] * interpolation(GS // 2 + 1, GL // 2 + 1)[None, :, None, :]
    ).reshape(FS, FL)
    pick = np.zeros((32, SPEC))
    pick[np.arange(32), 8 * np.arange(32) + 7] = 1
    spread = np.arange(FF)[None] % HID == np.arange(128)[:, None]
    plain = lambda t: np.asarray(t, np.float32).astype(ml_dtypes.bfloat16)
    return [two_terms(t) for t in (fwd, inv.T, inv, fwd.T, sfwd, sinv.T, sinv, sfwd.T, shrink, shrink.T)] + [
        plain(pick), plain(pick.T), plain(spread), plain(spread.T)]


def mm(a, b):
    return lax.dot_general(a, b, (((1,), (0,)), ((), ())), preferred_element_type=f32)


def mm_nt(a, b):
    return lax.dot_general(a, b, (((1,), (1,)), ((), ())), preferred_element_type=f32)


def mm_tn(a, b):
    return lax.dot_general(a, b, (((0,), (0,)), ((), ())), preferred_element_type=f32)


def halves(v):
    high = v.astype(bf16)
    return high, (v - high.astype(f32)).astype(bf16)


def apply_table(table, v):
    rows = table.shape[0] // 2
    high, low = halves(v)
    both = mm(table, high)
    return both[:rows] + both[rows:] + mm(table[:rows], low)


def standardize(v):
    centre = v - jnp.sum(v, -1, keepdims=True) * (1.0 / D)
    r = lax.rsqrt(jnp.sum(centre * centre, -1, keepdims=True) * (1.0 / D) + EPS)
    return centre * r, r


def norm_back(vh, r, q):
    mean_q = jnp.sum(q, -1, keepdims=True) * (1.0 / D)
    mean_qv = jnp.sum(q * vh, -1, keepdims=True) * (1.0 / D)
    return r * (q - mean_q - vh * mean_qv)


def fold(v):
    return jnp.sum(v.reshape(v.shape[0] // 8, 8, v.shape[1]), 0)


def aligned(v, m):
    return v if isinstance(v, int) else pl.multiple_of(v, m)


N_SEND = 256
VMEM_BYTES = 62 << 20


def fused_kernel(large, small, *refs):
    (large_in, small_in, large_cot, small_cot, own_in, own_out, own_pack, gains, biases,
     t_fwd, t_inv, t_inv_t, t_fwd_t, t_sfwd, t_sinv, t_sinv_t, t_sfwd_t, t_shrink, t_shrink_t,
     t_pick, t_pick_t, t_spread, t_spread_t,
     out_large, out_small, grad_large, grad_small, g_pack, g_in, g_out, g_vec,
     xs, vh1, r1, vh2, r2, second, active, slope, sv_large, sv_small, grad_low, back,
     w_in, w_out, pack, filt, filt_s, b_in, facc, sacc, bacc, vacc,
     whole, kept, s_core, s_one, s_two, s_z, r_core, r_one, r_two, r_z,
     f_core, f_keep, f_xy, f_z, v_send, v_core, v_xy, v_z,
     send_sem, recv_sem) = refs
    rows = xs.shape[0]
    groups = small // Q
    base = large * LP
    wide, narrow = lax.axis_index("wide"), lax.axis_index("narrow")
    z, x, y, c = lax.div(wide, 2), lax.rem(wide, 2), lax.div(narrow, 2), lax.rem(narrow, 2)
    other = {"x": 1 - x, "y": 1 - y, "c": 1 - c}
    at = lambda zz, xx, yy, cc: (zz * 2 + xx, yy * 2 + cc)
    z_pair = {0: z, 1: z + 1 - 2 * lax.rem(z, 2), 2: lax.rem(z + 2, 4), 3: 3 - z}
    z_of = z_from = lambda k: z_pair[k]
    peer = {"x": at(z, 1 - x, y, c), "y": at(z, x, 1 - y, c), "xy": at(z, 1 - x, 1 - y, c), "c": at(z, x, y, 1 - c)}
    for k in (1, 2, 3):
        peer[k] = at(z_of(k), x, y, c)

    ids, started = {}, {}

    def copy(key, src, dst, to):
        i = ids.setdefault(key, len(ids))
        return pltpu.make_async_remote_copy(
            src_ref=src, dst_ref=dst, send_sem=send_sem.at[i], recv_sem=recv_sem.at[i],
            device_id=peer[to], device_id_type=MESH_ID)

    def send(key, src, dst, to):
        d = copy(key, src, dst, to)
        d.start()
        started[key] = d

    def sent(key):
        if key in started:
            started.pop(key).wait_send()

    PLANE = (("x", lambda: (1 - x, y)), ("y", lambda: (x, 1 - y)), ("xy", lambda: (1 - x, 1 - y)))

    def gather_ops(j, name, plane=False):
        ref, own = (w_in, own_in) if name == "in" else (w_out, own_out)
        first, second_axis = ("x", "y") if name == "in" else ("y", "x")

        def z_send():
            ref[j, z, x, y, c] = own[j]
            for k in (1, 2, 3):
                send(("z", j, name, k), own.at[j], ref.at[j, z, x, y, c], k)

        def first_send(k):
            zz = z_from(k)
            if k:
                slot = ref.at[j, zz, x, y, c]
                copy(("z", j, name, k), own.at[j], slot, k).wait_recv()
            piece = ref.at[j, zz, x, y, c]
            send(("1", j, name, k), piece, piece, first)

        def second_send(k):
            zz = z_from(k)
            got = ref.at[j, zz, 1 - x, y, c] if first == "x" else ref.at[j, zz, x, 1 - y, c]
            copy(("1", j, name, k), got, got, first).wait_recv()
            piece = ref.at[j, zz, :, y, c] if first == "x" else ref.at[j, zz, x, :, c]
            send(("2", j, name, k), piece, piece, second_axis)

        def plane_send(k):
            zz = z_from(k)
            piece = ref.at[j, zz, x, y, c]
            if k:
                copy(("z", j, name, k), own.at[j], piece, k).wait_recv()
            for to in ("xy", "x", "y"):
                send(("p" + to, j, name, k), piece, piece, to)

        def core_send(k):
            zz = z_from(k)
            if plane:
                for to, where in PLANE:
                    xx, yy = where()
                    got = ref.at[j, zz, xx, yy, c]
                    copy(("p" + to, j, name, k), got, got, to).wait_recv()
            else:
                got = ref.at[j, zz, :, 1 - y, c] if first == "x" else ref.at[j, zz, 1 - x, :, c]
                copy(("2", j, name, k), got, got, second_axis).wait_recv()
            piece = ref.at[j, zz, :, :, c]
            send(("c", j, name, k), piece, piece, "c")

        def core_wait(k):
            got = ref.at[j, z_from(k), :, :, 1 - c]
            copy(("c", j, name, k), got, got, "c").wait_recv()

        return z_send, plane_send if plane else first_send, second_send, core_send, core_wait

    ORDER = (0, 1, 2, 3)

    def pack_z():
        pack[z, x, y, c] = own_pack[...]
        for k in (1, 2, 3):
            send(("pz", k), own_pack, pack.at[z, x, y, c], k)

    def pack_xy():
        for k in (1, 2, 3):
            copy(("pz", k), own_pack, pack.at[z_from(k), x, y, c], k).wait_recv()
        for to, _ in PLANE:
            piece = pack.at[:, x, y, c]
            send(("pp", to), piece, piece, to)

    def pack_core():
        for to, where in PLANE:
            xx, yy = where()
            got = pack.at[:, xx, yy, c]
            copy(("pp", to), got, got, to).wait_recv()
        piece = pack.at[:, :, :, c]
        send(("pc",), piece, piece, "c")

    def pack_wait():
        got = pack.at[:, :, :, 1 - c]
        copy(("pc",), got, got, "c").wait_recv()

    def reduce_core(j, a, k, value):
        whole[...] = value.reshape(4, 2, HID, D)
        sent(("rc", 1, a, k))
        for i in range(2):
            for l in range(2):
                kept[a, k, i, l] = whole[2 * i + l, c]
                s_core[a, k, i, l] = whole[2 * i + l, 1 - c].astype(bf16)
        send(("rc", j, a, k), s_core.at[a, k], r_core.at[j, a, k], "c")

    def x_first(a, k):
        return (a + k) % 2 == 1

    def reduce_one(j, a, k):
        copy(("rc", j, a, k), s_core.at[a, k], r_core.at[j, a, k], "c").wait_recv()
        sent(("r1", 1, a, k))
        for i in range(2):
            if x_first(a, k):
                s_one[a, k, i] = (kept[a, k, 1 - x, i] + r_core[j, a, k, 1 - x, i].astype(f32)).astype(bf16)
            else:
                s_one[a, k, i] = (kept[a, k, i, 1 - y] + r_core[j, a, k, i, 1 - y].astype(f32)).astype(bf16)
        send(("r1", j, a, k), s_one.at[a, k], r_one.at[j, a, k], "x" if x_first(a, k) else "y")

    def reduce_two(j, a, k):
        copy(("r1", j, a, k), s_one.at[a, k], r_one.at[j, a, k], "x" if x_first(a, k) else "y").wait_recv()
        if x_first(a, k):
            s = kept[a, k, x, 1 - y] + r_core[j, a, k, x, 1 - y].astype(f32) + r_one[j, a, k, 1 - y].astype(f32)
        else:
            s = kept[a, k, 1 - x, y] + r_core[j, a, k, 1 - x, y].astype(f32) + r_one[j, a, k, 1 - x].astype(f32)
        sent(("r2", 1, a, k))
        s_two[a, k] = s.astype(bf16)
        send(("r2", j, a, k), s_two.at[a, k], r_two.at[j, a, k], "y" if x_first(a, k) else "x")

    def reduce_z(j, a, k):
        copy(("r2", j, a, k), s_two.at[a, k], r_two.at[j, a, k], "y" if x_first(a, k) else "x").wait_recv()
        one = r_one[j, a, k, y] if x_first(a, k) else r_one[j, a, k, x]
        s = kept[a, k, x, y] + r_core[j, a, k, x, y].astype(f32) + one.astype(f32) + r_two[j, a, k].astype(f32)
        if k:
            sent(("rz", 1, a, k))
            s_z[a, k - 1] = s.astype(bf16)
            send(("rz", j, a, k), s_z.at[a, k - 1], r_z.at[j, a, k - 1], k)
        else:
            dst = g_in if a == 0 else g_out
            dst[j] = s

    def reduce_end(j, a):
        dst = g_in if a == 0 else g_out
        for k in (1, 2, 3):
            copy(("rz", j, a, k), s_z.at[a, k - 1], r_z.at[j, a, k - 1], k).wait_recv()
        dst[j] = dst[j] + r_z[j, a, 0].astype(f32) + r_z[j, a, 1].astype(f32) + r_z[j, a, 2].astype(f32)

    def small_core(j):
        send(("fc", j), facc.at[j, :, :, :, 1 - c], f_core.at[j], "c")
        if j == 0:
            v_send[...] = jnp.concatenate([jnp.sum(vacc[i], 0, keepdims=True) for i in range(10)] + [jnp.zeros((6, D), f32)], 0)
            send(("vc",), v_send, v_core, "c")

    def small_xy(j):
        copy(("fc", j), f_core.at[j], f_core.at[j], "c").wait_recv()
        for zz in range(4):
            for i in range(2):
                for l in range(2):
                    f_keep[j, i, l, zz] = facc[j, zz, i, l, c] + f_core[j, zz, i, l]
        for n, (to, where) in enumerate(PLANE):
            xx, yy = where()
            send(("fp", j, to), f_keep.at[j, xx, yy], f_xy.at[j, n], to)
        if j == 0:
            copy(("vc",), v_core, v_core, "c").wait_recv()
            v_xy[x, y] = v_send[...] + v_core[...]
            for to, where in PLANE:
                send(("vp", to), v_xy.at[x, y], v_xy.at[x, y], to)

    def small_z(j):
        for n, (to, where) in enumerate(PLANE):
            copy(("fp", j, to), f_xy.at[j, n], f_xy.at[j, n], to).wait_recv()
        for zz in range(4):
            f_keep[j, x, y, zz] = f_keep[j, x, y, zz] + f_xy[j, 0, zz] + f_xy[j, 1, zz] + f_xy[j, 2, zz]
        for k in (1, 2, 3):
            send(("fz", j, k), f_keep.at[j, x, y, z_of(k)], f_z.at[j, k - 1], k)
        if j == 0:
            for to, where in PLANE:
                xx, yy = where()
                got = v_xy.at[xx, yy]
                copy(("vp", to), got, got, to).wait_recv()
            v_z[z] = v_xy[0, 0] + v_xy[0, 1] + v_xy[1, 0] + v_xy[1, 1]
            for k in (1, 2, 3):
                send(("vz", k), v_z.at[z], v_z.at[z], k)

    def small_end(j):
        for k in (1, 2, 3):
            copy(("fz", j, k), f_z.at[j, k - 1], f_z.at[j, k - 1], k).wait_recv()
        g_pack[j] = f_keep[j, x, y, z] + f_z[j, 0] + f_z[j, 1] + f_z[j, 2]
        if j == 0:
            for k in (1, 2, 3):
                got = v_z.at[z_from(k)]
                copy(("vz", k), got, got, k).wait_recv()
            g_vec[...] = v_z[0] + v_z[1] + v_z[2] + v_z[3]

    def load_rows(a, b):
        def one(i, _):
            xs[pl.ds(aligned(i * LP + LP - 16, 16), 16), :] = jnp.zeros((16, D), f32)
            xs[pl.ds(aligned(i * LP, 16), PL), :] = a[i].astype(f32)
            return 0
        lax.fori_loop(0, large, one, 0)
        for i in range(small):
            xs[base + i * PS : base + (i + 1) * PS, :] = b[i].astype(f32)
        xs[base + small * PS :, :] = jnp.zeros((rows - base - small * PS, D), f32)

    def store_rows(a, b):
        def one(i, _):
            a[i] = xs[pl.ds(aligned(i * LP, 16), PL), :].astype(a.dtype)
            return 0
        lax.fori_loop(0, large, one, 0)
        for i in range(small):
            b[i] = xs[base + i * PS : base + (i + 1) * PS, :].astype(b.dtype)

    def spread_rows(r):
        return jnp.broadcast_to(r, (r.shape[0], 128))

    def wide_rows(r):
        return jnp.concatenate([r, r, r], -1)

    def mean_row(n_rows, period, scale):
        row = lax.broadcasted_iota(jnp.int32, (n_rows, 1), 0)
        hit = row == 0
        for q in range(1, period):
            hit = hit | (row == q * FS)
        return jnp.where(hit, scale, 0.0).astype(f32)

    def crop_loops(body, which):
        def big(i, _):
            body(pl.ds(aligned(i * LP, 16), LP), i, True)
            return 0
        def little(i, _):
            body(pl.ds(aligned(base + i * SR, 16), SR), i, False)
            return 0
        if "big" in which:
            lax.fori_loop(0, large, big, 0)
        if "small" in which:
            lax.fori_loop(0, groups, little, 0)

    def to_spectrum(j, which=BOTH):
        def body(o, i, big):
            vh, r = standardize(xs[o, :])
            vh1[j, o, :] = vh.astype(bf16)
            r1[j, o, :] = spread_rows(r)
            if big:
                sv_large[j, i] = apply_table(t_fwd[...], vh)
            else:
                sv_small[j, i] = apply_table(t_sfwd[...], vh)
        crop_loops(body, which)

    def unpack_filters(j):
        f = pack[:, :, :, :, j].reshape(SPEC, D)
        filt[j] = f.astype(f32)
        for h in range(2):
            s = mm(t_shrink[...], f[h * FLP : (h + 1) * FLP])
            s = s[:FS] + s[FS:]
            filt_s[j, h * QF : (h + 1) * QF] = jnp.concatenate([s] * Q, 0)
        bias = mm(t_pick[...], f[:, :128]).astype(bf16)
        bias = mm(bias, t_spread[...])
        mine = lax.div(lax.broadcasted_iota(jnp.int32, (32, FF), 1), HID) == lax.broadcasted_iota(jnp.int32, (32, FF), 0)
        b_in[j] = jnp.sum(jnp.where(mine, bias, 0.0), 0, keepdims=True)

    def spectrum_of(j, i, big):
        sv = sv_large[j, i] if big else sv_small[j, i]
        h = FLP if big else QF
        dc = mean_row(h, 1, float(GL)) if big else mean_row(h, Q, float(GS))
        re = sv[:h] * gains[j, 0:1, :] + dc * biases[j, 0:1, :]
        im = sv[h:] * gains[j, 0:1, :]
        f = filt[j] if big else filt_s[j]
        return sv, re, im, f[:h], f[h:], dc

    def from_spectrum(j, which=BOTH):
        def body(o, i, big):
            _, re, im, fr, fi, _ = spectrum_of(j, i, big)
            out = jnp.concatenate([re * fr - im * fi, re * fi + im * fr], 0)
            xs[o, :] = xs[o, :] + apply_table(t_inv[...] if big else t_sinv[...], out)
        crop_loops(body, which)

    def tiles(body, start=0, stop=None):
        def one(t, _):
            body(pl.ds(aligned(t * TILE, TILE), TILE))
            return 0
        lax.fori_loop(start, rows // TILE if stop is None else stop, one, 0)

    def expand(j, start, stop):
        def body(o):
            vh, r = standardize(xs[o, :])
            vh2[j, o, :] = vh
            r2[j, o, :] = spread_rows(r)
            s = (vh * gains[j, 1:2, :] + biases[j, 1:2, :]).astype(bf16)
            second[j, o, :] = s
            for h in range(2):
                w = w_in[j, 2 * h : 2 * h + 2].reshape(FF // 2, D)
                pre = mm_nt(s, w) + b_in[j, :, h * (FF // 2) : (h + 1) * (FF // 2)]
                phi = 0.5 + 0.5 * lax.erf(pre * (1 / math.sqrt(2)))
                active[j, h, o, :] = (pre * phi).astype(bf16)
                slope[j, h, o, :] = (phi + pre * (jnp.exp(-0.5 * pre * pre) * (1 / math.sqrt(2 * math.pi)))).astype(bf16)
        tiles(body, start, stop)

    def contract(j):
        def body(o):
            s = xs[o, :] + biases[j, 2:3, :]
            for h in range(2):
                s = s + mm(active[j, h, o, :], w_out[j, 2 * h : 2 * h + 2].reshape(FF // 2, D))
            xs[o, :] = s
        tiles(body)

    def z_offset(k):
        zz = z_of(k)
        return lax.div(zz, 2), pl.ds(aligned(lax.rem(zz, 2) * (FF // 4), 128), FF // 4)

    def back_hidden(j, h, last):
        def body(o):
            w = w_out[j, pl.ds(2 * h, 2)].reshape(FF // 2, D)
            pg = mm_nt(grad_low[o, :], w) * slope[j, h, o, :].astype(f32)
            bacc[j, h] += fold(pg)
            p = pg.astype(bf16)
            slope[j, h, o, :] = p
            sg = mm(p, w_in[j, pl.ds(2 * h, 2)].reshape(FF // 2, D))
            if not last:
                back[o, :] = sg
            else:
                sg = sg + back[o, :]
                vh = vh2[j, o, :]
                vacc[2 * j + 1] += fold(sg * vh)
                vacc[4 + 3 * j + 1] += fold(sg)
                xs[o, :] = xs[o, :] + norm_back(vh, wide_rows(r2[j, o, :]), sg * gains[j, 1:2, :])
        tiles(body)

    def weight_in(j, k):
        h, lanes = z_offset(k)
        return mm_tn(slope[j, h, :, lanes], second[j])

    def weight_out(j, k):
        h, lanes = z_offset(k)
        return mm_tn(active[j, h, :, lanes], grad_low[...])

    def back_spectrum(j, which):
        if which == ("small",):
            sacc[...] = jnp.zeros_like(sacc)
        else:
            facc[j] = jnp.zeros(facc.shape[1:], f32)

        def body(o, i, big):
            sv, re, im, fr, fi, dc = spectrum_of(j, i, big)
            h = FLP if big else QF
            sg = apply_table(t_inv_t[...] if big else t_sinv_t[...], xs[o, :])
            gr, gi = sg[:h], sg[h:]
            d_re, d_im = re * gr + im * gi, re * gi - im * gr
            if big:
                facc[j] += jnp.concatenate([d_re, d_im], 0).reshape(4, 2, 2, 2, 8, D)
            else:
                sacc[...] += jnp.concatenate([d_re, d_im], 0)
            n_re, n_im = gr * fr + gi * fi, gi * fr - gr * fi
            vacc[2 * j] += fold(n_re * sv[:h]) + fold(n_im * sv[h:])
            vacc[4 + 3 * j] += fold(n_re * dc)
            n = jnp.concatenate([n_re, n_im], 0)
            if big:
                sv_large[j, i] = n
            else:
                sv_small[j, i] = n
        crop_loops(body, which)

    def back_filters(j):
        for h in range(2):
            s = sacc[h * QF : (h + 1) * QF]
            s = s[:FS] + s[FS : 2 * FS] + s[2 * FS : 3 * FS] + s[3 * FS :]
            facc[j, 2 * h : 2 * h + 2] += apply_table(t_shrink_t[...], s).reshape(2, 2, 2, 2, 8, D)
        mine = lax.div(lax.broadcasted_iota(jnp.int32, (32, FF), 1), HID) == lax.broadcasted_iota(jnp.int32, (32, FF), 0)
        row = jnp.sum(jnp.concatenate([bacc[j, 0], bacc[j, 1]], -1), 0, keepdims=True)
        high, low = halves(jnp.where(mine, row, 0.0))
        row = mm(high, t_spread_t[...]) + mm(low, t_spread_t[...])
        high, low = halves(row)
        row = mm(t_pick_t[...], high) + mm(t_pick_t[...], low)
        facc[j] += jnp.concatenate([row, jnp.zeros((SPEC, D - 128), f32)], -1).reshape(4, 2, 2, 2, 8, D)

    def back_rows(j, which=BOTH):
        def body(o, i, big):
            n = sv_large[j, i] if big else sv_small[j, i]
            ng = apply_table(t_fwd_t[...] if big else t_sfwd_t[...], n)
            xs[o, :] = xs[o, :] + norm_back(vh1[j, o, :].astype(f32), wide_rows(r1[j, o, :]), ng * gains[j, 0:1, :])
        crop_loops(body, which)

    i0, o0 = gather_ops(0, "in", True), gather_ops(0, "out")
    i1, o1 = gather_ops(1, "in"), gather_ops(1, "out")
    far = ORDER[1:]

    def steps(ops, which, order=ORDER):
        for k in order:
            ops[which](k)

    run = lambda name, f, *a: jax.named_scope(name)(f)(*a)
    barrier = pltpu.get_barrier_semaphore()
    for to in peer.values():
        pl.semaphore_signal(barrier, 1, device_id=to, device_id_type=MESH_ID)
    load_rows(large_in, small_in)
    bacc[...] = jnp.zeros_like(bacc)
    vacc[...] = jnp.zeros_like(vacc)
    run("barrier", pl.semaphore_wait, barrier, len(peer))

    pack_z()
    i0[0]()
    i0[1](0)
    run("to_spectrum", to_spectrum, 0, ("big",))
    run("pack_xy", pack_xy)
    run("i0_1", steps, i0, 1, far)
    o0[0]()
    o0[1](0)
    run("to_spectrum", to_spectrum, 0, ("small",))
    run("pack_core", pack_core)
    run("i0_3", steps, i0, 3, (0,))
    run("pack_wait", pack_wait)
    run("unpack", unpack_filters, 0)
    run("from_spectrum", from_spectrum, 0, ("big",))
    run("o0_1", steps, o0, 1, far)
    run("i0_3", steps, i0, 3, far)
    run("from_spectrum", from_spectrum, 0, ("small",))
    run("o0_2", steps, o0, 2, (0,))
    run("i0_4", steps, i0, 4)
    run("expand", expand, 0, 0, 2)
    run("o0_2", steps, o0, 2, far)
    i1[0]()
    i1[1](0)
    run("expand", expand, 0, 2, None)
    run("o0_3", steps, o0, 3)
    run("i1_1", steps, i1, 1, far)
    o1[0]()
    o1[1](0)
    run("unpack", unpack_filters, 1)
    run("o0_4", steps, o0, 4)
    run("contract", contract, 0)
    run("i1_2", steps, i1, 2)
    run("o1_1", steps, o1, 1, far)
    run("to_spectrum", to_spectrum, 1)
    run("i1_3", steps, i1, 3)
    run("o1_2", steps, o1, 2)
    run("from_spectrum", from_spectrum, 1)
    run("i1_4", steps, i1, 4)
    run("expand", expand, 1, 0, 3)
    run("o1_3", steps, o1, 3)
    run("expand", expand, 1, 3, None)
    run("o1_4", steps, o1, 4)
    run("contract", contract, 1)
    store_rows(out_large, out_small)
    load_rows(large_cot, small_cot)

    half_z = lax.div(z, 2)

    def batch(name, f, j, a, ks):
        with jax.named_scope(name):
            for k in ks:
                f(j, a, k)

    def weights(j, a, ks):
        with jax.named_scope("weights"):
            for k in ks:
                reduce_core(j, a, k, (weight_out if a else weight_in)(j, k))

    ALL, FIRST, LAST = (2, 3, 1, 0), (2, 3), (1, 0)
    for j in (1, 0):
        def low(o):
            g = xs[o, :]
            vacc[4 + 3 * j + 2] += fold(g)
            grad_low[o, :] = g.astype(bf16)
        tiles(low)
        weights(j, 1, ALL)
        if j == 0:
            batch("z", reduce_z, 1, 0, FIRST)
        run("back_hidden", back_hidden, j, 1 - half_z, False)
        batch("one", reduce_one, j, 1, ALL)
        weights(j, 0, FIRST)
        if j == 0:
            batch("two", reduce_two, 1, 0, LAST)
            run("small_z", small_z, 1)
        run("back_hidden", back_hidden, j, half_z, True)
        batch("one", reduce_one, j, 0, FIRST)
        if j == 0:
            batch("z", reduce_z, 1, 0, LAST)
        weights(j, 0, LAST)
        batch("two", reduce_two, j, 1, ALL)
        run("back_spectrum", back_spectrum, j, ("small",))
        batch("one", reduce_one, j, 0, LAST)
        run("back_spectrum", back_spectrum, j, ("big",))
        back_filters(j)
        small_core(j)
        batch("two", reduce_two, j, 0, FIRST)
        run("back_rows", back_rows, j, ("small",))
        batch("z", reduce_z, j, 1, ALL)
        if j == 0:
            run("small_xy", small_xy, j)
            batch("two", reduce_two, j, 0, LAST)
        run("back_rows", back_rows, j, ("big",))
        if j == 1:
            run("small_xy", small_xy, j)
    batch("z", reduce_z, 0, 0, ALL)
    run("small_z", small_z, 0)
    store_rows(grad_large, grad_small)
    for j in (1, 0):
        for a in (1, 0):
            run("reduce_end", reduce_end, j, a)
        run("small_end", small_end, j)
    for key in list(started):
        sent(key)
    assert len(ids) <= N_SEND


def fused(large_in, small_in, large_cot, small_cot, filters, w_in, w_out, gains, biases):
    large, small = large_in.shape[0], small_in.shape[0]
    rows = -(-(large * LP + small * PS) // TILE) * TILE
    own_in = jnp.swapaxes(w_in[:, :D], 1, 2)
    bias = jnp.pad(w_in[:, D:, :], ((0, 0), (0, 0), (0, D - HID)))
    own_pack = jnp.concatenate([filters.reshape(BLOCKS, 7, D), bias], 1)
    V = pltpu.VMEM
    outs = [(large_in.shape, bf16), (small_in.shape, bf16), (large_in.shape, f32), (small_in.shape, f32),
            ((BLOCKS, 8, D), f32), ((BLOCKS, HID, D), f32), ((BLOCKS, HID, D), f32), ((16, D), f32)]
    grid8 = (4, 2, 2, 2)
    scratch = [
        V((rows, D), f32), V((BLOCKS, rows, D), bf16), V((BLOCKS, rows, 128), f32), V((BLOCKS, rows, D), f32),
        V((BLOCKS, rows, 128), f32), V((BLOCKS, rows, D), bf16), V((BLOCKS, 2, rows, FF // 2), bf16),
        V((BLOCKS, 2, rows, FF // 2), bf16), V((BLOCKS, large, SPEC, D), f32), V((BLOCKS, small // Q, 2 * QF, D), f32),
        V((rows, D), bf16), V((rows, D), f32),
        V((BLOCKS, *grid8, HID, D), bf16), V((BLOCKS, *grid8, HID, D), bf16), V((*grid8, BLOCKS, 8, D), bf16),
        V((BLOCKS, SPEC, D), f32), V((BLOCKS, 2 * QF, D), f32), V((BLOCKS, 1, FF), f32),
        V((BLOCKS, *grid8, 8, D), f32), V((2 * QF, D), f32), V((BLOCKS, 2, 8, FF // 2), f32), V((10, 8, D), f32),
        V((4, 2, HID, D), f32), V((2, 4, 2, 2, HID, D), f32),
        V((2, 4, 2, 2, HID, D), bf16), V((2, 4, 2, HID, D), bf16), V((2, 4, HID, D), bf16), V((2, 3, HID, D), bf16),
        V((BLOCKS, 2, 4, 2, 2, HID, D), bf16), V((BLOCKS, 2, 4, 2, HID, D), bf16), V((BLOCKS, 2, 4, HID, D), bf16),
        V((BLOCKS, 2, 3, HID, D), bf16),
        V((BLOCKS, 4, 2, 2, 8, D), f32), V((BLOCKS, 2, 2, 4, 8, D), f32), V((BLOCKS, 3, 4, 8, D), f32), V((BLOCKS, 3, 8, D), f32),
        V((16, D), f32), V((16, D), f32), V((2, 2, 16, D), f32), V((4, 16, D), f32),
        pltpu.SemaphoreType.DMA((N_SEND,)), pltpu.SemaphoreType.DMA((N_SEND,)),
    ]
    tables = [jnp.asarray(t) for t in constant_tables()]
    vmem = pl.BlockSpec(memory_space=pltpu.VMEM)
    result = pl.pallas_call(
        partial(fused_kernel, large, small),
        out_shape=[jax.ShapeDtypeStruct(s, d) for s, d in outs],
        in_specs=[vmem] * (9 + len(tables)),
        out_specs=[vmem] * len(outs),
        scratch_shapes=scratch,
        compiler_params=pltpu.CompilerParams(collective_id=0, has_side_effects=True, vmem_limit_bytes=VMEM_BYTES),
        name="gfnet_step",
    )(large_in, small_in, large_cot, small_cot, own_in, w_out, own_pack, gains, biases, *tables)
    out_large, out_small, grad_large, grad_small, g_pack, g_in, g_out, g_vec = result
    grad_in = jnp.concatenate([jnp.swapaxes(g_in, 1, 2), g_pack[:, 7:8, :HID]], 1)
    return (out_large, out_small, grad_large, grad_small, g_pack[:, :7].reshape(BLOCKS, -1), grad_in, g_out,
            g_vec[:4].reshape(BLOCKS, 2, D), g_vec[4:10].reshape(BLOCKS, 3, D))


def solution(mesh):
    in_specs = (
        P(("wide", "narrow"), None, None),
        P(("wide", "narrow"), None, None),
        P(("wide", "narrow"), None, None),
        P(("wide", "narrow"), None, None),
        P(None, ("wide", "narrow")),
        P(None, None, ("wide", "narrow")),
        P(None, ("wide", "narrow"), None),
        P(),
        P(),
    )
    out_specs = (
        P(("wide", "narrow"), None, None),
        P(("wide", "narrow"), None, None),
        P(("wide", "narrow"), None, None),
        P(("wide", "narrow"), None, None),
        P(None, ("wide", "narrow")),
        P(None, None, ("wide", "narrow")),
        P(None, ("wide", "narrow"), None),
        P(),
        P(),
    )
    body = fused if dict(mesh.shape) == {"wide": 8, "narrow": 4} else per_device
    return jax.shard_map(
        body, mesh=mesh, in_specs=in_specs, out_specs=out_specs, check_vma=False
    )
```

```python
from functools import partial
import math

import jax
import jax.numpy as jnp
import ml_dtypes
import numpy as np
from jax import lax
from jax.experimental import pallas as pl
from jax.experimental.pallas import tpu as pltpu
from jax.sharding import PartitionSpec as P

FF = 1536
GL = 14
GS = 6
BLOCKS = 2
MICRO = 2
PL = 196
FL = 112
FS = 24


precise = lax.Precision.HIGHEST
epsilon = 1e-06


def dft_tables(grid_cells):
    half_count = grid_cells // 2 + 1
    places = jnp.arange(grid_cells * grid_cells, dtype=jnp.int32)
    place_row = places // grid_cells
    place_col = places % grid_cells
    modes = jnp.arange(grid_cells * half_count, dtype=jnp.int32)
    mode_row = modes // half_count
    mode_col = modes % half_count
    phases = (
        mode_row[:, None] * place_row[None, :] + mode_col[:, None] * place_col[None, :]
    ) % grid_cells
    angles = phases.astype(jnp.float32) * (2.0 * math.pi / grid_cells)
    forward_re = jnp.cos(angles) / grid_cells
    forward_im = -jnp.sin(angles) / grid_cells
    doubling = jnp.where((mode_col == 0) | (2 * mode_col == grid_cells), 1.0, 2.0).astype(
        jnp.float32
    )
    inverse_re = jnp.transpose(forward_re * doubling[:, None])
    inverse_im = jnp.transpose(forward_im * doubling[:, None])
    return (forward_re, forward_im, inverse_re, inverse_im)


def linear_map(size_out, size_in):
    rows_out = jnp.arange(size_out, dtype=jnp.int32)
    spans = rows_out * (size_in - 1)
    lower = spans // (size_out - 1)
    fraction = (spans - lower * (size_out - 1)).astype(jnp.float32) / (size_out - 1)
    columns = jnp.arange(size_in, dtype=jnp.int32)
    first = jnp.where(columns[None, :] == lower[:, None], 1.0 - fraction[:, None], 0.0)
    second = jnp.where(columns[None, :] == lower[:, None] + 1, fraction[:, None], 0.0)
    return first + second


def shrink_map():
    along_rows = linear_map(GS, GL)
    along_cols = linear_map(GS // 2 + 1, GL // 2 + 1)
    return (along_rows[:, None, :, None] * along_cols[None, :, None, :]).reshape(FS, FL)


def filter_grid(patches, tables, filt_re, filt_im):
    forward_re, forward_im, inverse_re, inverse_im = tables
    spec_re = jnp.einsum("fp,bpd->bfd", forward_re, patches, precision=precise)
    spec_im = jnp.einsum("fp,bpd->bfd", forward_im, patches, precision=precise)
    out_re = spec_re * filt_re - spec_im * filt_im
    out_im = spec_re * filt_im + spec_im * filt_re
    back_re = jnp.einsum("pf,bfd->bpd", inverse_re, out_re, precision=precise)
    back_im = jnp.einsum("pf,bfd->bpd", inverse_im, out_im, precision=precise)
    return back_re + back_im


def spectral(normed, large_rows, filt_re, filt_im):
    width = normed.shape[-1]
    shrink = shrink_map()
    small_re = jnp.dot(shrink, filt_re, precision=precise, preferred_element_type=jnp.float32)
    small_im = jnp.dot(shrink, filt_im, precision=precise, preferred_element_type=jnp.float32)
    part_large = filter_grid(
        normed[:large_rows].reshape(-1, GL * GL, width), dft_tables(GL), filt_re, filt_im
    )
    part_small = filter_grid(
        normed[large_rows:].reshape(-1, GS * GS, width), dft_tables(GS), small_re, small_im
    )
    return jnp.concatenate([part_large.reshape(-1, width), part_small.reshape(-1, width)], 0)


def layer_norm(stream, gain, shift):
    centre = stream - jnp.mean(stream, axis=-1, keepdims=True)
    spread = jnp.mean(centre * centre, axis=-1, keepdims=True)
    return centre * lax.rsqrt(spread + epsilon) * gain + shift


def per_device(large_in, small_in, large_cot, small_cot, filters, w_in, w_out, gains, biases):
    width = large_in.shape[-1]
    micro_large = large_in.shape[0] // MICRO
    micro_small = small_in.shape[0] // MICRO
    large_rows = micro_large * PL
    exact_gelu = partial(jax.nn.gelu, approximate=False)

    def fetch(layer_index, forward):
        if forward:
            return (
                lax.all_gather(filters[layer_index], ("wide", "narrow"), axis=0, tiled=True),
                lax.all_gather(w_in[layer_index], ("wide", "narrow"), axis=1, tiled=True),
                lax.all_gather(w_out[layer_index], ("wide", "narrow"), axis=0, tiled=True),
            )
        return (
            lax.all_gather(filters[layer_index], ("wide", "narrow"), axis=0, tiled=True),
            lax.all_gather(w_in[layer_index], ("wide", "narrow"), axis=1, tiled=True),
            lax.all_gather(w_out[layer_index], ("wide", "narrow"), axis=0, tiled=True),
        )

    def branch_first(stream, gain, shift, filt_re, filt_im):
        return spectral(layer_norm(stream, gain, shift), large_rows, filt_re, filt_im)

    acc_filter = [jnp.zeros((2, FL, width), jnp.float32) for layer_index in range(BLOCKS)]
    acc_in = [jnp.zeros((width, FF), jnp.float32) for layer_index in range(BLOCKS)]
    acc_in_bias = [jnp.zeros((FF,), jnp.float32) for layer_index in range(BLOCKS)]
    acc_out = [jnp.zeros((FF, width), jnp.float32) for layer_index in range(BLOCKS)]
    acc_gain = [jnp.zeros((2, width), jnp.float32) for layer_index in range(BLOCKS)]
    acc_shift = [jnp.zeros((3, width), jnp.float32) for layer_index in range(BLOCKS)]
    outs_large, outs_small, grads_large, grads_small = ([], [], [], [])
    for micro_step in range(MICRO):
        large_part = large_in[micro_step * micro_large : (micro_step + 1) * micro_large]
        small_part = small_in[micro_step * micro_small : (micro_step + 1) * micro_small]
        stream = jnp.concatenate(
            [large_part.reshape(-1, width), small_part.reshape(-1, width)], 0
        ).astype(jnp.float32)
        saved = []
        for layer_index in range(BLOCKS):
            filt_full, in_full, out_full = fetch(layer_index, True)
            halves = filt_full.reshape(2, FL, width).astype(jnp.float32)
            mixed = stream + branch_first(
                stream, gains[layer_index, 0], biases[layer_index, 0], halves[0], halves[1]
            )
            second = layer_norm(mixed, gains[layer_index, 1], biases[layer_index, 1]).astype(
                jnp.bfloat16
            )
            pre_act = jnp.dot(
                second, in_full[:width], preferred_element_type=jnp.float32
            ) + in_full[width].astype(jnp.float32)
            active = exact_gelu(pre_act).astype(jnp.bfloat16)
            saved.append((stream, mixed, second, pre_act))
            stream = (
                mixed
                + jnp.dot(active, out_full, preferred_element_type=jnp.float32)
                + biases[layer_index, 2]
            )
        outs_large.append(stream[:large_rows].reshape(large_part.shape).astype(jnp.bfloat16))
        outs_small.append(stream[large_rows:].reshape(small_part.shape).astype(jnp.bfloat16))
        large_back = large_cot[micro_step * micro_large : (micro_step + 1) * micro_large]
        small_back = small_cot[micro_step * micro_small : (micro_step + 1) * micro_small]
        grad = jnp.concatenate(
            [large_back.reshape(-1, width), small_back.reshape(-1, width)], 0
        ).astype(jnp.float32)
        for layer_index in reversed(range(BLOCKS)):
            block_input, mixed, second, pre_act = saved[layer_index]
            filt_full, in_full, out_full = fetch(layer_index, False)
            halves = filt_full.reshape(2, FL, width).astype(jnp.float32)
            grad_low = grad.astype(jnp.bfloat16)
            active, gelu_back = jax.vjp(exact_gelu, pre_act)
            active = active.astype(jnp.bfloat16)
            acc_out[layer_index] = acc_out[layer_index] + jnp.einsum(
                "tf,td->fd", active, grad_low, preferred_element_type=jnp.float32
            )
            bias_out_grad = jnp.sum(grad, axis=0)
            active_grad = jnp.einsum(
                "td,fd->tf", grad_low, out_full, preferred_element_type=jnp.float32
            )
            pre_grad = gelu_back(active_grad)[0]
            pre_low = pre_grad.astype(jnp.bfloat16)
            acc_in[layer_index] = acc_in[layer_index] + jnp.einsum(
                "td,tf->df", second, pre_low, preferred_element_type=jnp.float32
            )
            acc_in_bias[layer_index] = acc_in_bias[layer_index] + jnp.sum(pre_grad, axis=0)
            second_grad = jnp.einsum(
                "tf,df->td", pre_low, in_full[:width], preferred_element_type=jnp.float32
            )
            unused, norm_back = jax.vjp(
                layer_norm, mixed, gains[layer_index, 1], biases[layer_index, 1]
            )
            mixed_part, gain_two, shift_two = norm_back(second_grad)
            mixed_grad = grad + mixed_part
            unused, first_back = jax.vjp(
                branch_first,
                block_input,
                gains[layer_index, 0],
                biases[layer_index, 0],
                halves[0],
                halves[1],
            )
            input_part, gain_one, shift_one, filt_re_grad, filt_im_grad = first_back(mixed_grad)
            grad = mixed_grad + input_part
            acc_filter[layer_index] = acc_filter[layer_index] + jnp.stack(
                [filt_re_grad, filt_im_grad], 0
            )
            acc_gain[layer_index] = acc_gain[layer_index] + jnp.stack([gain_one, gain_two], 0)
            acc_shift[layer_index] = acc_shift[layer_index] + jnp.stack(
                [shift_one, shift_two, bias_out_grad], 0
            )
        grads_large.append(grad[:large_rows].reshape(large_part.shape))
        grads_small.append(grad[large_rows:].reshape(small_part.shape))
    filter_shards, in_shards, out_shards = ([], [], [])
    for layer_index in range(BLOCKS):
        in_whole = jnp.concatenate([acc_in[layer_index], acc_in_bias[layer_index][None, :]], 0)
        filter_piece, in_piece, out_piece = (
            lax.psum_scatter(
                acc_filter[layer_index].reshape(-1),
                ("wide", "narrow"),
                scatter_dimension=0,
                tiled=True,
            ),
            lax.psum_scatter(in_whole, ("wide", "narrow"), scatter_dimension=1, tiled=True),
            lax.psum_scatter(
                acc_out[layer_index], ("wide", "narrow"), scatter_dimension=0, tiled=True
            ),
        )
        filter_shards.append(filter_piece)
        in_shards.append(in_piece)
        out_shards.append(out_piece)
    gain_total, shift_total = lax.psum(
        (jnp.stack(acc_gain, 0), jnp.stack(acc_shift, 0)), ("wide", "narrow")
    )
    return (
        jnp.concatenate(outs_large, 0),
        jnp.concatenate(outs_small, 0),
        jnp.concatenate(grads_large, 0),
        jnp.concatenate(grads_small, 0),
        jnp.stack(filter_shards, 0),
        jnp.stack(in_shards, 0),
        jnp.stack(out_shards, 0),
        gain_total,
        shift_total,
    )


MESH_ID = pl.DeviceIdType.MESH
bf16, f32 = jnp.bfloat16, jnp.float32
D, PS, EPS = 384, 36, 1e-6
LP = 208
Q = 4
SR = Q * PS
TILE = 256
BOTH = ("big", "small")
HID = 48
FLP = 128
SPEC = 2 * FLP
QF = Q * FS


def dft_arrays(n):
    half = n // 2 + 1
    places, modes = np.arange(n * n), np.arange(n * half)
    phase = ((modes // half)[:, None] * (places // n)[None] + (modes % half)[:, None] * (places % n)[None]) % n
    theta = phase * (2 * math.pi / n)
    fwd_re, fwd_im = np.cos(theta) / n, -np.sin(theta) / n
    weight = np.where((modes % half == 0) | (2 * (modes % half) == n), 1.0, 2.0)
    return fwd_re, fwd_im, fwd_re * weight[:, None], fwd_im * weight[:, None]


def interpolation(rows, cols):
    span = np.arange(rows) * (cols - 1)
    low = span // (rows - 1)
    part = (span - low * (rows - 1)) / (rows - 1)
    at = np.arange(cols)[None]
    return np.where(at == low[:, None], 1 - part[:, None], 0.0) + np.where(at == low[:, None] + 1, part[:, None], 0.0)


def two_terms(table):
    table = np.asarray(table, np.float32)
    high = table.astype(ml_dtypes.bfloat16)
    low = (table - high.astype(np.float32)).astype(ml_dtypes.bfloat16)
    return np.concatenate([high, low], 0)


def constant_tables():
    pos = np.arange(FL) // 7 * 8 + np.arange(FL) % 7
    rows = np.concatenate([pos, FLP + pos])
    fr, fi, ir, ii = dft_arrays(GL)
    fwd, inv = np.zeros((SPEC, LP)), np.zeros((SPEC, LP))
    fwd[rows, :PL], inv[rows, :PL] = np.concatenate([fr, fi]), np.concatenate([ir, ii])
    fr, fi, ir, ii = dft_arrays(GS)
    sfwd, sinv = np.zeros((2 * QF, SR)), np.zeros((2 * QF, SR))
    for q in range(Q):
        at = slice(q * PS, (q + 1) * PS)
        for half, a, b in ((0, fr, ir), (1, fi, ii)):
            to = slice(half * QF + q * FS, half * QF + (q + 1) * FS)
            sfwd[to, at], sinv[to, at] = a, b
    shrink = np.zeros((FS, FLP))
    shrink[:, pos] = (
        interpolation(GS, GL)[:, None, :, None] * interpolation(GS // 2 + 1, GL // 2 + 1)[None, :, None, :]
    ).reshape(FS, FL)
    pick = np.zeros((32, SPEC))
    pick[np.arange(32), 8 * np.arange(32) + 7] = 1
    spread = np.arange(FF)[None] % HID == np.arange(128)[:, None]
    plain = lambda t: np.asarray(t, np.float32).astype(ml_dtypes.bfloat16)
    return [two_terms(t) for t in (fwd, inv.T, inv, fwd.T, sfwd, sinv.T, sinv, sfwd.T, shrink, shrink.T)] + [
        plain(pick), plain(pick.T), plain(spread), plain(spread.T)]


def mm(a, b):
    return lax.dot_general(a, b, (((1,), (0,)), ((), ())), preferred_element_type=f32)


def mm_nt(a, b):
    return lax.dot_general(a, b, (((1,), (1,)), ((), ())), preferred_element_type=f32)


def mm_tn(a, b):
    return lax.dot_general(a, b, (((0,), (0,)), ((), ())), preferred_element_type=f32)


def halves(v):
    high = v.astype(bf16)
    return high, (v - high.astype(f32)).astype(bf16)


def apply_table(table, v):
    rows = table.shape[0] // 2
    high, low = halves(v)
    both = mm(table, high)
    return both[:rows] + both[rows:] + mm(table[:rows], low)


def standardize(v):
    centre = v - jnp.sum(v, -1, keepdims=True) * (1.0 / D)
    r = lax.rsqrt(jnp.sum(centre * centre, -1, keepdims=True) * (1.0 / D) + EPS)
    return centre * r, r


def norm_back(vh, r, q):
    mean_q = jnp.sum(q, -1, keepdims=True) * (1.0 / D)
    mean_qv = jnp.sum(q * vh, -1, keepdims=True) * (1.0 / D)
    return r * (q - mean_q - vh * mean_qv)


def fold(v):
    return jnp.sum(v.reshape(v.shape[0] // 8, 8, v.shape[1]), 0)


def aligned(v, m):
    return v if isinstance(v, int) else pl.multiple_of(v, m)


N_SEND = 256
VMEM_BYTES = 62 << 20


N_IN, N_OUT = 23, 9


def fused_kernel(large, small, *refs):
    given, made, refs = refs[:N_IN], refs[N_IN : N_IN + N_OUT], refs[N_IN + N_OUT :]
    held, refs = refs[:N_IN], refs[N_IN:]
    (small_rows, large_rows, raw_in, raw_out, raw_filters, gains, biases, cot_large, cot_small,
     t_fwd, t_inv, t_inv_t, t_fwd_t, t_sfwd, t_sinv, t_sinv_t, t_sfwd_t, t_shrink, t_shrink_t,
     t_pick, t_pick_t, t_spread, t_spread_t) = held
    (grad_large, grad_small, g_filters, g_w_in, g_w_out, g_gains, g_biases, g_in, g_out,
     xs, vh1, r1, vh2, r2, second, active, slope, sv_large, sv_small, grad_low, back,
     w_in, w_out, pack, filt, filt_s, b_in, facc, sacc, bacc, vacc,
     whole, kept, s_core, s_one, s_two, s_z, r_core, r_one, r_two, r_z,
     f_core, f_keep, f_xy, f_z, v_send, v_core, v_xy, v_z,
     send_sem, recv_sem, in_sem, out_sem) = refs
    rows = xs.shape[0]
    groups = small // Q
    base = large * LP
    wide, narrow = lax.axis_index("wide"), lax.axis_index("narrow")
    z, x, y, c = lax.div(wide, 2), lax.rem(wide, 2), lax.div(narrow, 2), lax.rem(narrow, 2)
    other = {"x": 1 - x, "y": 1 - y, "c": 1 - c}
    at = lambda zz, xx, yy, cc: (zz * 2 + xx, yy * 2 + cc)
    z_pair = {0: z, 1: z + 1 - 2 * lax.rem(z, 2), 2: lax.rem(z + 2, 4), 3: 3 - z}
    z_of = z_from = lambda k: z_pair[k]
    peer = {"x": at(z, 1 - x, y, c), "y": at(z, x, 1 - y, c), "xy": at(z, 1 - x, 1 - y, c), "c": at(z, x, y, 1 - c)}
    for k in (1, 2, 3):
        peer[k] = at(z_of(k), x, y, c)

    ids, started = {}, {}

    def copy(key, src, dst, to):
        i = ids.setdefault(key, len(ids))
        return pltpu.make_async_remote_copy(
            src_ref=src, dst_ref=dst, send_sem=send_sem.at[i], recv_sem=recv_sem.at[i],
            device_id=peer[to], device_id_type=MESH_ID)

    def send(key, src, dst, to):
        d = copy(key, src, dst, to)
        d.start()
        started[key] = d

    def sent(key):
        if key in started:
            started.pop(key).wait_send()

    PLANE = (("x", lambda: (1 - x, y)), ("y", lambda: (x, 1 - y)), ("xy", lambda: (1 - x, 1 - y)))

    def gather_ops(j, name, plane=False):
        ref = w_in if name == "in" else w_out
        first, second_axis = ("x", "y") if name == "in" else ("y", "x")

        def z_send():
            mine = ref.at[j, z, x, y, c]
            for k in (1, 2, 3):
                send(("z", j, name, k), mine, mine, k)

        def first_send(k):
            zz = z_from(k)
            if k:
                slot = ref.at[j, zz, x, y, c]
                copy(("z", j, name, k), slot, slot, k).wait_recv()
            piece = ref.at[j, zz, x, y, c]
            send(("1", j, name, k), piece, piece, first)

        def second_send(k):
            zz = z_from(k)
            got = ref.at[j, zz, 1 - x, y, c] if first == "x" else ref.at[j, zz, x, 1 - y, c]
            copy(("1", j, name, k), got, got, first).wait_recv()
            piece = ref.at[j, zz, :, y, c] if first == "x" else ref.at[j, zz, x, :, c]
            send(("2", j, name, k), piece, piece, second_axis)

        def plane_send(k):
            zz = z_from(k)
            piece = ref.at[j, zz, x, y, c]
            if k:
                copy(("z", j, name, k), piece, piece, k).wait_recv()
            for to in ("xy", "x", "y"):
                send(("p" + to, j, name, k), piece, piece, to)

        def core_send(k):
            zz = z_from(k)
            if plane:
                for to, where in PLANE:
                    xx, yy = where()
                    got = ref.at[j, zz, xx, yy, c]
                    copy(("p" + to, j, name, k), got, got, to).wait_recv()
            else:
                got = ref.at[j, zz, :, 1 - y, c] if first == "x" else ref.at[j, zz, 1 - x, :, c]
                copy(("2", j, name, k), got, got, second_axis).wait_recv()
            piece = ref.at[j, zz, :, :, c]
            send(("c", j, name, k), piece, piece, "c")

        def core_wait(k):
            got = ref.at[j, z_from(k), :, :, 1 - c]
            copy(("c", j, name, k), got, got, "c").wait_recv()

        return z_send, plane_send if plane else first_send, second_send, core_send, core_wait

    ORDER = (0, 1, 2, 3)

    def pack_z():
        mine = pack.at[z, x, y, c]
        for k in (1, 2, 3):
            send(("pz", k), mine, mine, k)

    def pack_xy():
        for k in (1, 2, 3):
            got = pack.at[z_from(k), x, y, c]
            copy(("pz", k), got, got, k).wait_recv()
        for to, _ in PLANE:
            piece = pack.at[:, x, y, c]
            send(("pp", to), piece, piece, to)

    def pack_core():
        for to, where in PLANE:
            xx, yy = where()
            got = pack.at[:, xx, yy, c]
            copy(("pp", to), got, got, to).wait_recv()
        piece = pack.at[:, :, :, c]
        send(("pc",), piece, piece, "c")

    def pack_wait():
        got = pack.at[:, :, :, 1 - c]
        copy(("pc",), got, got, "c").wait_recv()

    def reduce_core(j, a, k, value):
        whole[...] = value.reshape(4, 2, HID, D)
        sent(("rc", 1, a, k))
        for i in range(2):
            for l in range(2):
                kept[a, k, i, l] = whole[2 * i + l, c]
                s_core[a, k, i, l] = whole[2 * i + l, 1 - c].astype(bf16)
        send(("rc", j, a, k), s_core.at[a, k], r_core.at[j, a, k], "c")

    def x_first(a, k):
        return (a + k) % 2 == 1

    def reduce_one(j, a, k):
        copy(("rc", j, a, k), s_core.at[a, k], r_core.at[j, a, k], "c").wait_recv()
        sent(("r1", 1, a, k))
        for i in range(2):
            if x_first(a, k):
                s_one[a, k, i] = (kept[a, k, 1 - x, i] + r_core[j, a, k, 1 - x, i].astype(f32)).astype(bf16)
            else:
                s_one[a, k, i] = (kept[a, k, i, 1 - y] + r_core[j, a, k, i, 1 - y].astype(f32)).astype(bf16)
        send(("r1", j, a, k), s_one.at[a, k], r_one.at[j, a, k], "x" if x_first(a, k) else "y")

    def reduce_two(j, a, k):
        copy(("r1", j, a, k), s_one.at[a, k], r_one.at[j, a, k], "x" if x_first(a, k) else "y").wait_recv()
        if x_first(a, k):
            s = kept[a, k, x, 1 - y] + r_core[j, a, k, x, 1 - y].astype(f32) + r_one[j, a, k, 1 - y].astype(f32)
        else:
            s = kept[a, k, 1 - x, y] + r_core[j, a, k, 1 - x, y].astype(f32) + r_one[j, a, k, 1 - x].astype(f32)
        sent(("r2", 1, a, k))
        s_two[a, k] = s.astype(bf16)
        send(("r2", j, a, k), s_two.at[a, k], r_two.at[j, a, k], "y" if x_first(a, k) else "x")

    def reduce_z(j, a, k):
        copy(("r2", j, a, k), s_two.at[a, k], r_two.at[j, a, k], "y" if x_first(a, k) else "x").wait_recv()
        one = r_one[j, a, k, y] if x_first(a, k) else r_one[j, a, k, x]
        s = kept[a, k, x, y] + r_core[j, a, k, x, y].astype(f32) + one.astype(f32) + r_two[j, a, k].astype(f32)
        if k:
            sent(("rz", 1, a, k))
            s_z[a, k - 1] = s.astype(bf16)
            send(("rz", j, a, k), s_z.at[a, k - 1], r_z.at[j, a, k - 1], k)
        else:
            dst = g_in if a == 0 else g_out
            dst[j] = s

    def reduce_end(j, a):
        dst = g_in if a == 0 else g_out
        for k in (1, 2, 3):
            copy(("rz", j, a, k), s_z.at[a, k - 1], r_z.at[j, a, k - 1], k).wait_recv()
        s = dst[j] + r_z[j, a, 0].astype(f32) + r_z[j, a, 1].astype(f32) + r_z[j, a, 2].astype(f32)
        if a == 0:
            g_w_in[j, :, :D] = s
        else:
            g_w_out[j] = s

    def small_core(j):
        send(("fc", j), facc.at[j, :, :, :, 1 - c], f_core.at[j], "c")
        if j == 0:
            v_send[...] = jnp.concatenate([jnp.sum(vacc[i], 0, keepdims=True) for i in range(10)] + [jnp.zeros((6, D), f32)], 0)
            send(("vc",), v_send, v_core, "c")

    def small_xy(j):
        copy(("fc", j), f_core.at[j], f_core.at[j], "c").wait_recv()
        for zz in range(4):
            for i in range(2):
                for l in range(2):
                    f_keep[j, i, l, zz] = facc[j, zz, i, l, c] + f_core[j, zz, i, l]
        for n, (to, where) in enumerate(PLANE):
            xx, yy = where()
            send(("fp", j, to), f_keep.at[j, xx, yy], f_xy.at[j, n], to)
        if j == 0:
            copy(("vc",), v_core, v_core, "c").wait_recv()
            v_xy[x, y] = v_send[...] + v_core[...]
            for to, where in PLANE:
                send(("vp", to), v_xy.at[x, y], v_xy.at[x, y], to)

    def small_z(j):
        for n, (to, where) in enumerate(PLANE):
            copy(("fp", j, to), f_xy.at[j, n], f_xy.at[j, n], to).wait_recv()
        for zz in range(4):
            f_keep[j, x, y, zz] = f_keep[j, x, y, zz] + f_xy[j, 0, zz] + f_xy[j, 1, zz] + f_xy[j, 2, zz]
        for k in (1, 2, 3):
            send(("fz", j, k), f_keep.at[j, x, y, z_of(k)], f_z.at[j, k - 1], k)
        if j == 0:
            for to, where in PLANE:
                xx, yy = where()
                got = v_xy.at[xx, yy]
                copy(("vp", to), got, got, to).wait_recv()
            v_z[z] = v_xy[0, 0] + v_xy[0, 1] + v_xy[1, 0] + v_xy[1, 1]
            for k in (1, 2, 3):
                send(("vz", k), v_z.at[z], v_z.at[z], k)

    def small_end(j):
        for k in (1, 2, 3):
            copy(("fz", j, k), f_z.at[j, k - 1], f_z.at[j, k - 1], k).wait_recv()
        s = f_keep[j, x, y, z] + f_z[j, 0] + f_z[j, 1] + f_z[j, 2]
        for r in range(7):
            g_filters[j : j + 1, r * D : (r + 1) * D] = s[r : r + 1]
        g_w_in[j, :, D:] = jnp.sum(jnp.where(diagonal(), s[7:8, :128], 0.0), 1, keepdims=True)
        if j == 0:
            for k in (1, 2, 3):
                got = v_z.at[z_from(k)]
                copy(("vz", k), got, got, k).wait_recv()
            v = v_z[0] + v_z[1] + v_z[2] + v_z[3]
            for i in range(2):
                g_gains[i] = v[2 * i : 2 * i + 2]
                for l in range(3):
                    g_biases[l, i : i + 1] = v[4 + 3 * i + l : 5 + 3 * i + l]

    def diagonal():
        shape = (HID, 128)
        return lax.broadcasted_iota(jnp.int32, shape, 0) == lax.broadcasted_iota(jnp.int32, shape, 1)

    def load_rows(a, b):
        v = jnp.swapaxes(a[...], 0, 1).astype(f32)
        for i in range(large):
            xs[i * LP + LP - 16 : (i + 1) * LP, :] = jnp.zeros((16, D), f32)
            xs[i * LP : i * LP + PL, :] = v[i]
        for i in range(small):
            xs[base + i * PS : base + (i + 1) * PS, :] = b[i].astype(f32)
        xs[base + small * PS :, :] = jnp.zeros((rows - base - small * PS, D), f32)

    def store_large(a):
        v = jnp.concatenate([xs[i * LP : i * LP + PL, :][None] for i in range(large)], 0)
        a[...] = jnp.swapaxes(v, 0, 1).astype(a.dtype)

    def store_small(b):
        for i in range(small):
            b[i] = xs[base + i * PS : base + (i + 1) * PS, :].astype(b.dtype)

    def own_pieces():
        for j in range(BLOCKS):
            w_in[j, z, x, y, c] = raw_in[j, :, :D]
            w_out[j, z, x, y, c] = raw_out[j]
            bias = jnp.sum(jnp.where(diagonal(), raw_in[j, :, D:].astype(f32), 0.0), 0, keepdims=True)
            row = raw_filters[j : j + 1, :].astype(f32)
            parts = [row[:, r * D : (r + 1) * D] for r in range(7)]
            parts.append(jnp.concatenate([bias, jnp.zeros((1, D - 128), f32)], 1))
            pack[z, x, y, c, j] = jnp.concatenate(parts, 0).astype(bf16)

    fetches = [pltpu.make_async_copy(a, b, in_sem.at[n]) for n, (a, b) in enumerate(zip(given, held))]
    stores = []

    def fetched(*which):
        for n in which:
            fetches[n].wait()

    def put(n, value):
        d = pltpu.make_async_copy(value, made[n], out_sem.at[n])
        d.start()
        stores.append(d)

    def spread_rows(r):
        return jnp.broadcast_to(r, (r.shape[0], 128))

    def wide_rows(r):
        return jnp.concatenate([r, r, r], -1)

    def mean_row(n_rows, period, scale):
        row = lax.broadcasted_iota(jnp.int32, (n_rows, 1), 0)
        hit = row == 0
        for q in range(1, period):
            hit = hit | (row == q * FS)
        return jnp.where(hit, scale, 0.0).astype(f32)

    def crop_loops(body, which):
        def big(i, _):
            body(pl.ds(aligned(i * LP, 16), LP), i, True)
            return 0
        def little(i, _):
            body(pl.ds(aligned(base + i * SR, 16), SR), i, False)
            return 0
        if "big" in which:
            lax.fori_loop(0, large, big, 0)
        if "small" in which:
            lax.fori_loop(0, groups, little, 0)

    def to_spectrum(j, which=BOTH):
        def body(o, i, big):
            vh, r = standardize(xs[o, :])
            vh1[j, o, :] = vh.astype(bf16)
            r1[j, o, :] = spread_rows(r)
            if big:
                sv_large[j, i] = apply_table(t_fwd[...], vh)
            else:
                sv_small[j, i] = apply_table(t_sfwd[...], vh)
        crop_loops(body, which)

    def unpack_filters(j):
        f = pack[:, :, :, :, j].reshape(SPEC, D)
        filt[j] = f.astype(f32)
        for h in range(2):
            s = mm(t_shrink[...], f[h * FLP : (h + 1) * FLP])
            s = s[:FS] + s[FS:]
            filt_s[j, h * QF : (h + 1) * QF] = jnp.concatenate([s] * Q, 0)
        bias = mm(t_pick[...], f[:, :128]).astype(bf16)
        bias = mm(bias, t_spread[...])
        mine = lax.div(lax.broadcasted_iota(jnp.int32, (32, FF), 1), HID) == lax.broadcasted_iota(jnp.int32, (32, FF), 0)
        b_in[j] = jnp.sum(jnp.where(mine, bias, 0.0), 0, keepdims=True)

    def spectrum_of(j, i, big):
        sv = sv_large[j, i] if big else sv_small[j, i]
        h = FLP if big else QF
        dc = mean_row(h, 1, float(GL)) if big else mean_row(h, Q, float(GS))
        re = sv[:h] * gains[j, 0:1, :] + dc * biases[0, j : j + 1, :]
        im = sv[h:] * gains[j, 0:1, :]
        f = filt[j] if big else filt_s[j]
        return sv, re, im, f[:h], f[h:], dc

    def from_spectrum(j, which=BOTH):
        def body(o, i, big):
            _, re, im, fr, fi, _ = spectrum_of(j, i, big)
            out = jnp.concatenate([re * fr - im * fi, re * fi + im * fr], 0)
            xs[o, :] = xs[o, :] + apply_table(t_inv[...] if big else t_sinv[...], out)
        crop_loops(body, which)

    def tiles(body, start=0, stop=None):
        def one(t, _):
            body(pl.ds(aligned(t * TILE, TILE), TILE))
            return 0
        lax.fori_loop(start, rows // TILE if stop is None else stop, one, 0)

    def expand(j, start, stop):
        def body(o):
            vh, r = standardize(xs[o, :])
            vh2[j, o, :] = vh
            r2[j, o, :] = spread_rows(r)
            s = (vh * gains[j, 1:2, :] + biases[1, j : j + 1, :]).astype(bf16)
            second[j, o, :] = s
            for h in range(2):
                w = w_in[j, 2 * h : 2 * h + 2].reshape(FF // 2, D)
                pre = mm_nt(s, w) + b_in[j, :, h * (FF // 2) : (h + 1) * (FF // 2)]
                phi = 0.5 + 0.5 * lax.erf(pre * (1 / math.sqrt(2)))
                active[j, h, o, :] = (pre * phi).astype(bf16)
                slope[j, h, o, :] = (phi + pre * (jnp.exp(-0.5 * pre * pre) * (1 / math.sqrt(2 * math.pi)))).astype(bf16)
        tiles(body, start, stop)

    def contract(j):
        def body(o):
            s = xs[o, :] + biases[2, j : j + 1, :]
            for h in range(2):
                s = s + mm(active[j, h, o, :], w_out[j, 2 * h : 2 * h + 2].reshape(FF // 2, D))
            xs[o, :] = s
        tiles(body)

    def z_offset(k):
        zz = z_of(k)
        return lax.div(zz, 2), pl.ds(aligned(lax.rem(zz, 2) * (FF // 4), 128), FF // 4)

    def back_hidden(j, h, last):
        def body(o):
            w = w_out[j, pl.ds(2 * h, 2)].reshape(FF // 2, D)
            pg = mm_nt(grad_low[o, :], w) * slope[j, h, o, :].astype(f32)
            bacc[j, h] += fold(pg)
            p = pg.astype(bf16)
            slope[j, h, o, :] = p
            sg = mm(p, w_in[j, pl.ds(2 * h, 2)].reshape(FF // 2, D))
            if not last:
                back[o, :] = sg
            else:
                sg = sg + back[o, :]
                vh = vh2[j, o, :]
                vacc[2 * j + 1] += fold(sg * vh)
                vacc[4 + 3 * j + 1] += fold(sg)
                xs[o, :] = xs[o, :] + norm_back(vh, wide_rows(r2[j, o, :]), sg * gains[j, 1:2, :])
        tiles(body)

    def weight_in(j, k):
        h, lanes = z_offset(k)
        return mm_tn(slope[j, h, :, lanes], second[j])

    def weight_out(j, k):
        h, lanes = z_offset(k)
        return mm_tn(active[j, h, :, lanes], grad_low[...])

    def back_spectrum(j, which):
        if which == ("small",):
            sacc[...] = jnp.zeros_like(sacc)
        else:
            facc[j] = jnp.zeros(facc.shape[1:], f32)

        def body(o, i, big):
            sv, re, im, fr, fi, dc = spectrum_of(j, i, big)
            h = FLP if big else QF
            sg = apply_table(t_inv_t[...] if big else t_sinv_t[...], xs[o, :])
            gr, gi = sg[:h], sg[h:]
            d_re, d_im = re * gr + im * gi, re * gi - im * gr
            if big:
                facc[j] += jnp.concatenate([d_re, d_im], 0).reshape(4, 2, 2, 2, 8, D)
            else:
                sacc[...] += jnp.concatenate([d_re, d_im], 0)
            n_re, n_im = gr * fr + gi * fi, gi * fr - gr * fi
            vacc[2 * j] += fold(n_re * sv[:h]) + fold(n_im * sv[h:])
            vacc[4 + 3 * j] += fold(n_re * dc)
            n = jnp.concatenate([n_re, n_im], 0)
            if big:
                sv_large[j, i] = n
            else:
                sv_small[j, i] = n
        crop_loops(body, which)

    def back_filters(j):
        for h in range(2):
            s = sacc[h * QF : (h + 1) * QF]
            s = s[:FS] + s[FS : 2 * FS] + s[2 * FS : 3 * FS] + s[3 * FS :]
            facc[j, 2 * h : 2 * h + 2] += apply_table(t_shrink_t[...], s).reshape(2, 2, 2, 2, 8, D)
        mine = lax.div(lax.broadcasted_iota(jnp.int32, (32, FF), 1), HID) == lax.broadcasted_iota(jnp.int32, (32, FF), 0)
        row = jnp.sum(jnp.concatenate([bacc[j, 0], bacc[j, 1]], -1), 0, keepdims=True)
        high, low = halves(jnp.where(mine, row, 0.0))
        row = mm(high, t_spread_t[...]) + mm(low, t_spread_t[...])
        high, low = halves(row)
        row = mm(t_pick_t[...], high) + mm(t_pick_t[...], low)
        facc[j] += jnp.concatenate([row, jnp.zeros((SPEC, D - 128), f32)], -1).reshape(4, 2, 2, 2, 8, D)

    def back_rows(j, which=BOTH):
        def body(o, i, big):
            n = sv_large[j, i] if big else sv_small[j, i]
            ng = apply_table(t_fwd_t[...] if big else t_sfwd_t[...], n)
            xs[o, :] = xs[o, :] + norm_back(vh1[j, o, :].astype(f32), wide_rows(r1[j, o, :]), ng * gains[j, 0:1, :])
        crop_loops(body, which)

    i0, o0 = gather_ops(0, "in", True), gather_ops(0, "out")
    i1, o1 = gather_ops(1, "in"), gather_ops(1, "out")
    far = ORDER[1:]

    def steps(ops, which, order=ORDER):
        for k in order:
            ops[which](k)

    run = lambda name, f, *a: jax.named_scope(name)(f)(*a)
    barrier = pltpu.get_barrier_semaphore()
    for to in peer.values():
        pl.semaphore_signal(barrier, 1, device_id=to, device_id_type=MESH_ID)
    for d in fetches:
        d.start()
    fetched(0, 1, 2, 3, 4)
    own_pieces()
    bacc[...] = jnp.zeros_like(bacc)
    vacc[...] = jnp.zeros_like(vacc)
    run("barrier", pl.semaphore_wait, barrier, len(peer))

    pack_z()
    i0[0]()
    i0[1](0)
    run("load_rows", load_rows, large_rows, small_rows)
    fetched(*range(5, N_IN))
    run("to_spectrum", to_spectrum, 0, ("big",))
    run("pack_xy", pack_xy)
    run("i0_1", steps, i0, 1, far)
    o0[0]()
    o0[1](0)
    run("to_spectrum", to_spectrum, 0, ("small",))
    run("pack_core", pack_core)
    run("i0_3", steps, i0, 3, (0,))
    run("pack_wait", pack_wait)
    run("unpack", unpack_filters, 0)
    run("from_spectrum", from_spectrum, 0, ("big",))
    run("o0_1", steps, o0, 1, far)
    run("i0_3", steps, i0, 3, far)
    run("from_spectrum", from_spectrum, 0, ("small",))
    run("o0_2", steps, o0, 2, (0,))
    run("i0_4", steps, i0, 4)
    run("expand", expand, 0, 0, 2)
    run("o0_2", steps, o0, 2, far)
    i1[0]()
    i1[1](0)
    run("expand", expand, 0, 2, None)
    run("o0_3", steps, o0, 3)
    run("i1_1", steps, i1, 1, far)
    o1[0]()
    o1[1](0)
    run("unpack", unpack_filters, 1)
    run("o0_4", steps, o0, 4)
    run("contract", contract, 0)
    run("i1_2", steps, i1, 2)
    run("o1_1", steps, o1, 1, far)
    run("to_spectrum", to_spectrum, 1)
    run("i1_3", steps, i1, 3)
    run("o1_2", steps, o1, 2)
    run("from_spectrum", from_spectrum, 1)
    run("i1_4", steps, i1, 4)
    run("expand", expand, 1, 0, 3)
    run("o1_3", steps, o1, 3)
    run("expand", expand, 1, 3, None)
    run("o1_4", steps, o1, 4)
    run("contract", contract, 1)
    store_large(large_rows)
    put(0, large_rows)
    store_small(small_rows)
    put(1, small_rows)
    load_rows(cot_large, cot_small)

    half_z = lax.div(z, 2)

    def batch(name, f, j, a, ks):
        with jax.named_scope(name):
            for k in ks:
                f(j, a, k)

    def weights(j, a, ks):
        with jax.named_scope("weights"):
            for k in ks:
                reduce_core(j, a, k, (weight_out if a else weight_in)(j, k))

    ALL, FIRST, LAST = (2, 3, 1, 0), (2, 3), (1, 0)
    for j in (1, 0):
        def low(o):
            g = xs[o, :]
            vacc[4 + 3 * j + 2] += fold(g)
            grad_low[o, :] = g.astype(bf16)
        tiles(low)
        weights(j, 1, ALL)
        if j == 0:
            batch("z", reduce_z, 1, 0, FIRST)
        run("back_hidden", back_hidden, j, 1 - half_z, False)
        batch("one", reduce_one, j, 1, ALL)
        weights(j, 0, FIRST)
        if j == 0:
            batch("two", reduce_two, 1, 0, LAST)
            run("small_z", small_z, 1)
        run("back_hidden", back_hidden, j, half_z, True)
        batch("one", reduce_one, j, 0, FIRST)
        if j == 0:
            batch("z", reduce_z, 1, 0, LAST)
        weights(j, 0, LAST)
        batch("two", reduce_two, j, 1, ALL)
        run("back_spectrum", back_spectrum, j, ("small",))
        batch("one", reduce_one, j, 0, LAST)
        run("back_spectrum", back_spectrum, j, ("big",))
        back_filters(j)
        small_core(j)
        batch("two", reduce_two, j, 0, FIRST)
        run("back_rows", back_rows, j, ("small",))
        if j == 0:
            store_small(grad_small)
            put(3, grad_small)
        batch("z", reduce_z, j, 1, ALL)
        if j == 0:
            run("small_xy", small_xy, j)
            batch("two", reduce_two, j, 0, LAST)
        run("back_rows", back_rows, j, ("big",))
        if j == 0:
            store_large(grad_large)
            put(2, grad_large)
        if j == 1:
            run("small_xy", small_xy, j)
    batch("z", reduce_z, 0, 0, ALL)
    run("small_z", small_z, 0)
    for j in (1, 0):
        for a in (1, 0):
            run("reduce_end", reduce_end, j, a)
    put(6, g_w_out)
    for j in (1, 0):
        run("small_end", small_end, j)
    put(4, g_filters)
    put(5, g_w_in)
    put(7, g_gains)
    put(8, g_biases)
    for d in stores:
        d.wait()
    for key in list(started):
        sent(key)
    assert len(ids) <= N_SEND


def hand_over_kernel(*refs):
    sources, targets, between = refs[:N_OUT], refs[N_OUT : 2 * N_OUT], refs[2 * N_OUT : 3 * N_OUT]
    in_sem, out_sem = refs[3 * N_OUT :]
    ins = [pltpu.make_async_copy(a, b, in_sem.at[n]) for n, (a, b) in enumerate(zip(sources, between))]
    outs = [pltpu.make_async_copy(a, b, out_sem.at[n]) for n, (a, b) in enumerate(zip(between, targets))]
    for d in ins:
        d.start()
    for a, b in zip(ins, outs):
        a.wait()
        b.start()
    for d in outs:
        d.wait()


def fused(large_in, small_in, large_cot, small_cot, filters, w_in, w_out, gains, biases):
    large, small = large_in.shape[0], small_in.shape[0]
    rows = -(-(large * LP + small * PS) // TILE) * TILE
    tables = [jnp.asarray(t) for t in constant_tables()]
    args = [small_in, jnp.swapaxes(large_in, 0, 1), jnp.swapaxes(w_in, 1, 2), w_out, filters, gains,
            jnp.swapaxes(biases, 0, 1), jnp.swapaxes(large_cot, 0, 1), small_cot, *tables]
    V = pltpu.VMEM
    patch_major = (large_in.shape[1], large, D)
    outs = [(patch_major, bf16), (small_in.shape, bf16), (patch_major, f32), (small_in.shape, f32), (filters.shape, f32),
            ((BLOCKS, HID, D + 1), f32), ((BLOCKS, HID, D), f32), (gains.shape, f32), ((3, BLOCKS, D), f32)]
    grid8 = (4, 2, 2, 2)
    scratch = [V(a.shape, a.dtype) for a in args] + [V(shape, dtype) for shape, dtype in outs[2:]] + [
        V((BLOCKS, HID, D), f32), V((BLOCKS, HID, D), f32),
        V((rows, D), f32), V((BLOCKS, rows, D), bf16), V((BLOCKS, rows, 128), f32), V((BLOCKS, rows, D), f32),
        V((BLOCKS, rows, 128), f32), V((BLOCKS, rows, D), bf16), V((BLOCKS, 2, rows, FF // 2), bf16),
        V((BLOCKS, 2, rows, FF // 2), bf16), V((BLOCKS, large, SPEC, D), f32), V((BLOCKS, small // Q, 2 * QF, D), f32),
        V((rows, D), bf16), V((rows, D), f32),
        V((BLOCKS, *grid8, HID, D), bf16), V((BLOCKS, *grid8, HID, D), bf16), V((*grid8, BLOCKS, 8, D), bf16),
        V((BLOCKS, SPEC, D), f32), V((BLOCKS, 2 * QF, D), f32), V((BLOCKS, 1, FF), f32),
        V((BLOCKS, *grid8, 8, D), f32), V((2 * QF, D), f32), V((BLOCKS, 2, 8, FF // 2), f32), V((10, 8, D), f32),
        V((4, 2, HID, D), f32), V((2, 4, 2, 2, HID, D), f32),
        V((2, 4, 2, 2, HID, D), bf16), V((2, 4, 2, HID, D), bf16), V((2, 4, HID, D), bf16), V((2, 3, HID, D), bf16),
        V((BLOCKS, 2, 4, 2, 2, HID, D), bf16), V((BLOCKS, 2, 4, 2, HID, D), bf16), V((BLOCKS, 2, 4, HID, D), bf16),
        V((BLOCKS, 2, 3, HID, D), bf16),
        V((BLOCKS, 4, 2, 2, 8, D), f32), V((BLOCKS, 2, 2, 4, 8, D), f32), V((BLOCKS, 3, 4, 8, D), f32), V((BLOCKS, 3, 8, D), f32),
        V((16, D), f32), V((16, D), f32), V((2, 2, 16, D), f32), V((4, 16, D), f32),
        pltpu.SemaphoreType.DMA((N_SEND,)), pltpu.SemaphoreType.DMA((N_SEND,)),
        pltpu.SemaphoreType.DMA((N_IN,)), pltpu.SemaphoreType.DMA((N_OUT,)),
    ]
    anywhere = pl.BlockSpec(memory_space=pl.ANY)
    out_shape = [jax.ShapeDtypeStruct(shape, dtype) for shape, dtype in outs]
    result = pl.pallas_call(
        partial(fused_kernel, large, small),
        out_shape=out_shape,
        in_specs=[anywhere] * N_IN,
        out_specs=[anywhere] * N_OUT,
        scratch_shapes=scratch,
        compiler_params=pltpu.CompilerParams(collective_id=0, has_side_effects=True, vmem_limit_bytes=VMEM_BYTES),
        name="gfnet_step",
    )(*args)
    out_large, out_small, grad_large, grad_small, g_filters, g_in, g_out, g_gains, g_biases = pl.pallas_call(
        hand_over_kernel,
        out_shape=out_shape,
        in_specs=[anywhere] * N_OUT,
        out_specs=[anywhere] * N_OUT,
        scratch_shapes=[V(shape, dtype) for shape, dtype in outs] + [pltpu.SemaphoreType.DMA((N_OUT,))] * 2,
        compiler_params=pltpu.CompilerParams(vmem_limit_bytes=VMEM_BYTES),
        name="hand_over",
    )(*result)
    return (jnp.swapaxes(out_large, 0, 1), out_small, jnp.swapaxes(grad_large, 0, 1), grad_small, g_filters,
            jnp.swapaxes(g_in, 1, 2), g_out, g_gains, jnp.swapaxes(g_biases, 0, 1))


def solution(mesh):
    in_specs = (
        P(("wide", "narrow"), None, None),
        P(("wide", "narrow"), None, None),
        P(("wide", "narrow"), None, None),
        P(("wide", "narrow"), None, None),
        P(None, ("wide", "narrow")),
        P(None, None, ("wide", "narrow")),
        P(None, ("wide", "narrow"), None),
        P(),
        P(),
    )
    out_specs = (
        P(("wide", "narrow"), None, None),
        P(("wide", "narrow"), None, None),
        P(("wide", "narrow"), None, None),
        P(("wide", "narrow"), None, None),
        P(None, ("wide", "narrow")),
        P(None, None, ("wide", "narrow")),
        P(None, ("wide", "narrow"), None),
        P(),
        P(),
    )
    body = fused if dict(mesh.shape) == {"wide": 8, "narrow": 4} else per_device
    return jax.shard_map(
        body, mesh=mesh, in_specs=in_specs, out_specs=out_specs, check_vma=False
    )
```

```python
from functools import partial
import math

import jax
import jax.numpy as jnp
import ml_dtypes
import numpy as np
from jax import lax
from jax.experimental import pallas as pl
from jax.experimental.pallas import tpu as pltpu
from jax.sharding import PartitionSpec as P

FF = 1536
GL = 14
GS = 6
BLOCKS = 2
MICRO = 2
PL = 196
FL = 112
FS = 24


precise = lax.Precision.HIGHEST
epsilon = 1e-06


def dft_tables(grid_cells):
    half_count = grid_cells // 2 + 1
    places = jnp.arange(grid_cells * grid_cells, dtype=jnp.int32)
    place_row = places // grid_cells
    place_col = places % grid_cells
    modes = jnp.arange(grid_cells * half_count, dtype=jnp.int32)
    mode_row = modes // half_count
    mode_col = modes % half_count
    phases = (
        mode_row[:, None] * place_row[None, :] + mode_col[:, None] * place_col[None, :]
    ) % grid_cells
    angles = phases.astype(jnp.float32) * (2.0 * math.pi / grid_cells)
    forward_re = jnp.cos(angles) / grid_cells
    forward_im = -jnp.sin(angles) / grid_cells
    doubling = jnp.where((mode_col == 0) | (2 * mode_col == grid_cells), 1.0, 2.0).astype(
        jnp.float32
    )
    inverse_re = jnp.transpose(forward_re * doubling[:, None])
    inverse_im = jnp.transpose(forward_im * doubling[:, None])
    return (forward_re, forward_im, inverse_re, inverse_im)


def linear_map(size_out, size_in):
    rows_out = jnp.arange(size_out, dtype=jnp.int32)
    spans = rows_out * (size_in - 1)
    lower = spans // (size_out - 1)
    fraction = (spans - lower * (size_out - 1)).astype(jnp.float32) / (size_out - 1)
    columns = jnp.arange(size_in, dtype=jnp.int32)
    first = jnp.where(columns[None, :] == lower[:, None], 1.0 - fraction[:, None], 0.0)
    second = jnp.where(columns[None, :] == lower[:, None] + 1, fraction[:, None], 0.0)
    return first + second


def shrink_map():
    along_rows = linear_map(GS, GL)
    along_cols = linear_map(GS // 2 + 1, GL // 2 + 1)
    return (along_rows[:, None, :, None] * along_cols[None, :, None, :]).reshape(FS, FL)


def filter_grid(patches, tables, filt_re, filt_im):
    forward_re, forward_im, inverse_re, inverse_im = tables
    spec_re = jnp.einsum("fp,bpd->bfd", forward_re, patches, precision=precise)
    spec_im = jnp.einsum("fp,bpd->bfd", forward_im, patches, precision=precise)
    out_re = spec_re * filt_re - spec_im * filt_im
    out_im = spec_re * filt_im + spec_im * filt_re
    back_re = jnp.einsum("pf,bfd->bpd", inverse_re, out_re, precision=precise)
    back_im = jnp.einsum("pf,bfd->bpd", inverse_im, out_im, precision=precise)
    return back_re + back_im


def spectral(normed, large_rows, filt_re, filt_im):
    width = normed.shape[-1]
    shrink = shrink_map()
    small_re = jnp.dot(shrink, filt_re, precision=precise, preferred_element_type=jnp.float32)
    small_im = jnp.dot(shrink, filt_im, precision=precise, preferred_element_type=jnp.float32)
    part_large = filter_grid(
        normed[:large_rows].reshape(-1, GL * GL, width), dft_tables(GL), filt_re, filt_im
    )
    part_small = filter_grid(
        normed[large_rows:].reshape(-1, GS * GS, width), dft_tables(GS), small_re, small_im
    )
    return jnp.concatenate([part_large.reshape(-1, width), part_small.reshape(-1, width)], 0)


def layer_norm(stream, gain, shift):
    centre = stream - jnp.mean(stream, axis=-1, keepdims=True)
    spread = jnp.mean(centre * centre, axis=-1, keepdims=True)
    return centre * lax.rsqrt(spread + epsilon) * gain + shift


def per_device(large_in, small_in, large_cot, small_cot, filters, w_in, w_out, gains, biases):
    width = large_in.shape[-1]
    micro_large = large_in.shape[0] // MICRO
    micro_small = small_in.shape[0] // MICRO
    large_rows = micro_large * PL
    exact_gelu = partial(jax.nn.gelu, approximate=False)

    def fetch(layer_index, forward):
        if forward:
            return (
                lax.all_gather(filters[layer_index], ("wide", "narrow"), axis=0, tiled=True),
                lax.all_gather(w_in[layer_index], ("wide", "narrow"), axis=1, tiled=True),
                lax.all_gather(w_out[layer_index], ("wide", "narrow"), axis=0, tiled=True),
            )
        return (
            lax.all_gather(filters[layer_index], ("wide", "narrow"), axis=0, tiled=True),
            lax.all_gather(w_in[layer_index], ("wide", "narrow"), axis=1, tiled=True),
            lax.all_gather(w_out[layer_index], ("wide", "narrow"), axis=0, tiled=True),
        )

    def branch_first(stream, gain, shift, filt_re, filt_im):
        return spectral(layer_norm(stream, gain, shift), large_rows, filt_re, filt_im)

    acc_filter = [jnp.zeros((2, FL, width), jnp.float32) for layer_index in range(BLOCKS)]
    acc_in = [jnp.zeros((width, FF), jnp.float32) for layer_index in range(BLOCKS)]
    acc_in_bias = [jnp.zeros((FF,), jnp.float32) for layer_index in range(BLOCKS)]
    acc_out = [jnp.zeros((FF, width), jnp.float32) for layer_index in range(BLOCKS)]
    acc_gain = [jnp.zeros((2, width), jnp.float32) for layer_index in range(BLOCKS)]
    acc_shift = [jnp.zeros((3, width), jnp.float32) for layer_index in range(BLOCKS)]
    outs_large, outs_small, grads_large, grads_small = ([], [], [], [])
    for micro_step in range(MICRO):
        large_part = large_in[micro_step * micro_large : (micro_step + 1) * micro_large]
        small_part = small_in[micro_step * micro_small : (micro_step + 1) * micro_small]
        stream = jnp.concatenate(
            [large_part.reshape(-1, width), small_part.reshape(-1, width)], 0
        ).astype(jnp.float32)
        saved = []
        for layer_index in range(BLOCKS):
            filt_full, in_full, out_full = fetch(layer_index, True)
            halves = filt_full.reshape(2, FL, width).astype(jnp.float32)
            mixed = stream + branch_first(
                stream, gains[layer_index, 0], biases[layer_index, 0], halves[0], halves[1]
            )
            second = layer_norm(mixed, gains[layer_index, 1], biases[layer_index, 1]).astype(
                jnp.bfloat16
            )
            pre_act = jnp.dot(
                second, in_full[:width], preferred_element_type=jnp.float32
            ) + in_full[width].astype(jnp.float32)
            active = exact_gelu(pre_act).astype(jnp.bfloat16)
            saved.append((stream, mixed, second, pre_act))
            stream = (
                mixed
                + jnp.dot(active, out_full, preferred_element_type=jnp.float32)
                + biases[layer_index, 2]
            )
        outs_large.append(stream[:large_rows].reshape(large_part.shape).astype(jnp.bfloat16))
        outs_small.append(stream[large_rows:].reshape(small_part.shape).astype(jnp.bfloat16))
        large_back = large_cot[micro_step * micro_large : (micro_step + 1) * micro_large]
        small_back = small_cot[micro_step * micro_small : (micro_step + 1) * micro_small]
        grad = jnp.concatenate(
            [large_back.reshape(-1, width), small_back.reshape(-1, width)], 0
        ).astype(jnp.float32)
        for layer_index in reversed(range(BLOCKS)):
            block_input, mixed, second, pre_act = saved[layer_index]
            filt_full, in_full, out_full = fetch(layer_index, False)
            halves = filt_full.reshape(2, FL, width).astype(jnp.float32)
            grad_low = grad.astype(jnp.bfloat16)
            active, gelu_back = jax.vjp(exact_gelu, pre_act)
            active = active.astype(jnp.bfloat16)
            acc_out[layer_index] = acc_out[layer_index] + jnp.einsum(
                "tf,td->fd", active, grad_low, preferred_element_type=jnp.float32
            )
            bias_out_grad = jnp.sum(grad, axis=0)
            active_grad = jnp.einsum(
                "td,fd->tf", grad_low, out_full, preferred_element_type=jnp.float32
            )
            pre_grad = gelu_back(active_grad)[0]
            pre_low = pre_grad.astype(jnp.bfloat16)
            acc_in[layer_index] = acc_in[layer_index] + jnp.einsum(
                "td,tf->df", second, pre_low, preferred_element_type=jnp.float32
            )
            acc_in_bias[layer_index] = acc_in_bias[layer_index] + jnp.sum(pre_grad, axis=0)
            second_grad = jnp.einsum(
                "tf,df->td", pre_low, in_full[:width], preferred_element_type=jnp.float32
            )
            unused, norm_back = jax.vjp(
                layer_norm, mixed, gains[layer_index, 1], biases[layer_index, 1]
            )
            mixed_part, gain_two, shift_two = norm_back(second_grad)
            mixed_grad = grad + mixed_part
            unused, first_back = jax.vjp(
                branch_first,
                block_input,
                gains[layer_index, 0],
                biases[layer_index, 0],
                halves[0],
                halves[1],
            )
            input_part, gain_one, shift_one, filt_re_grad, filt_im_grad = first_back(mixed_grad)
            grad = mixed_grad + input_part
            acc_filter[layer_index] = acc_filter[layer_index] + jnp.stack(
                [filt_re_grad, filt_im_grad], 0
            )
            acc_gain[layer_index] = acc_gain[layer_index] + jnp.stack([gain_one, gain_two], 0)
            acc_shift[layer_index] = acc_shift[layer_index] + jnp.stack(
                [shift_one, shift_two, bias_out_grad], 0
            )
        grads_large.append(grad[:large_rows].reshape(large_part.shape))
        grads_small.append(grad[large_rows:].reshape(small_part.shape))
    filter_shards, in_shards, out_shards = ([], [], [])
    for layer_index in range(BLOCKS):
        in_whole = jnp.concatenate([acc_in[layer_index], acc_in_bias[layer_index][None, :]], 0)
        filter_piece, in_piece, out_piece = (
            lax.psum_scatter(
                acc_filter[layer_index].reshape(-1),
                ("wide", "narrow"),
                scatter_dimension=0,
                tiled=True,
            ),
            lax.psum_scatter(in_whole, ("wide", "narrow"), scatter_dimension=1, tiled=True),
            lax.psum_scatter(
                acc_out[layer_index], ("wide", "narrow"), scatter_dimension=0, tiled=True
            ),
        )
        filter_shards.append(filter_piece)
        in_shards.append(in_piece)
        out_shards.append(out_piece)
    gain_total, shift_total = lax.psum(
        (jnp.stack(acc_gain, 0), jnp.stack(acc_shift, 0)), ("wide", "narrow")
    )
    return (
        jnp.concatenate(outs_large, 0),
        jnp.concatenate(outs_small, 0),
        jnp.concatenate(grads_large, 0),
        jnp.concatenate(grads_small, 0),
        jnp.stack(filter_shards, 0),
        jnp.stack(in_shards, 0),
        jnp.stack(out_shards, 0),
        gain_total,
        shift_total,
    )


MESH_ID = pl.DeviceIdType.MESH
bf16, f32 = jnp.bfloat16, jnp.float32
D, PS, EPS = 384, 36, 1e-6
LP = 208
Q = 4
SR = Q * PS
TILE = 256
BOTH = ("big", "small")
HID = 48
FLP = 128
SPEC = 2 * FLP
QF = Q * FS


def dft_arrays(n):
    half = n // 2 + 1
    places, modes = np.arange(n * n), np.arange(n * half)
    phase = ((modes // half)[:, None] * (places // n)[None] + (modes % half)[:, None] * (places % n)[None]) % n
    theta = phase * (2 * math.pi / n)
    fwd_re, fwd_im = np.cos(theta) / n, -np.sin(theta) / n
    weight = np.where((modes % half == 0) | (2 * (modes % half) == n), 1.0, 2.0)
    return fwd_re, fwd_im, fwd_re * weight[:, None], fwd_im * weight[:, None]


def interpolation(rows, cols):
    span = np.arange(rows) * (cols - 1)
    low = span // (rows - 1)
    part = (span - low * (rows - 1)) / (rows - 1)
    at = np.arange(cols)[None]
    return np.where(at == low[:, None], 1 - part[:, None], 0.0) + np.where(at == low[:, None] + 1, part[:, None], 0.0)


def two_terms(table):
    table = np.asarray(table, np.float32)
    high = table.astype(ml_dtypes.bfloat16)
    low = (table - high.astype(np.float32)).astype(ml_dtypes.bfloat16)
    return np.concatenate([high, low], 0)


def constant_tables():
    pos = np.arange(FL) // 7 * 8 + np.arange(FL) % 7
    rows = np.concatenate([pos, FLP + pos])
    fr, fi, ir, ii = dft_arrays(GL)
    fwd, inv = np.zeros((SPEC, LP)), np.zeros((SPEC, LP))
    fwd[rows, :PL], inv[rows, :PL] = np.concatenate([fr, fi]), np.concatenate([ir, ii])
    fr, fi, ir, ii = dft_arrays(GS)
    sfwd, sinv = np.zeros((2 * QF, SR)), np.zeros((2 * QF, SR))
    for q in range(Q):
        at = slice(q * PS, (q + 1) * PS)
        for half, a, b in ((0, fr, ir), (1, fi, ii)):
            to = slice(half * QF + q * FS, half * QF + (q + 1) * FS)
            sfwd[to, at], sinv[to, at] = a, b
    shrink = np.zeros((FS, FLP))
    shrink[:, pos] = (
        interpolation(GS, GL)[:, None, :, None] * interpolation(GS // 2 + 1, GL // 2 + 1)[None, :, None, :]
    ).reshape(FS, FL)
    pick = np.zeros((32, SPEC))
    pick[np.arange(32), 8 * np.arange(32) + 7] = 1
    spread = np.arange(FF)[None] % HID == np.arange(128)[:, None]
    plain = lambda t: np.asarray(t, np.float32).astype(ml_dtypes.bfloat16)
    return ([two_terms(t) for t in (fwd, sfwd)],
            [two_terms(shrink), plain(pick), plain(spread)]
            + [two_terms(t) for t in (inv.T, sinv.T, inv, sinv, shrink.T)]
            + [plain(spread.T), plain(pick.T), two_terms(fwd.T), two_terms(sfwd.T)])


def mm(a, b):
    return lax.dot_general(a, b, (((1,), (0,)), ((), ())), preferred_element_type=f32)


def mm_nt(a, b):
    return lax.dot_general(a, b, (((1,), (1,)), ((), ())), preferred_element_type=f32)


def mm_tn(a, b):
    return lax.dot_general(a, b, (((0,), (0,)), ((), ())), preferred_element_type=f32)


def halves(v):
    high = v.astype(bf16)
    return high, (v - high.astype(f32)).astype(bf16)


def apply_table(table, v):
    rows = table.shape[0] // 2
    high, low = halves(v)
    both = mm(table, high)
    return both[:rows] + both[rows:] + mm(table[:rows], low)


def standardize(v):
    centre = v - jnp.sum(v, -1, keepdims=True) * (1.0 / D)
    r = lax.rsqrt(jnp.sum(centre * centre, -1, keepdims=True) * (1.0 / D) + EPS)
    return centre * r, r


def norm_back(vh, r, q):
    mean_q = jnp.sum(q, -1, keepdims=True) * (1.0 / D)
    mean_qv = jnp.sum(q * vh, -1, keepdims=True) * (1.0 / D)
    return r * (q - mean_q - vh * mean_qv)


def fold(v):
    return jnp.sum(v.reshape(v.shape[0] // 8, 8, v.shape[1]), 0)


def aligned(v, m):
    return v if isinstance(v, int) else pl.multiple_of(v, m)


N_SEND = 256
VMEM_BYTES = 63 << 20


N_IN, N_OUT = 23, 9


def fused_kernel(large, small, *refs):
    given, made, refs = refs[:N_IN], refs[N_IN : N_IN + N_OUT], refs[N_IN + N_OUT :]
    held, refs = refs[:N_IN], refs[N_IN:]
    (raw_in, raw_out, raw_filters, small_rows, large_rows, t_fwd, t_sfwd, cot_large, cot_small, gains, biases,
     t_shrink, t_pick, t_spread, t_inv, t_sinv, t_inv_t, t_sinv_t, t_shrink_t, t_spread_t, t_pick_t, t_fwd_t, t_sfwd_t) = held
    (grad_large, grad_small, g_filters, g_w_in, g_w_out, g_gains, g_biases,
     xs, vh1, r1, vh2, r2, second, active, slope, sv_large, sv_small, grad_low, back,
     w_in, w_out, pack, filt_s, b_in, facc, sacc, bacc, vacc,
     whole, kept, s_core, s_plane, s_z, r_core, r_plane, r_z,
     f_own, f_core, f_keep, f_send, f_xy, f_z_send, f_z, v_send, v_core, v_xy, v_z,
     send_sem, recv_sem, in_sem, out_sem) = refs
    rows = xs.shape[0]
    groups = small // Q
    base = large * LP
    wide, narrow = lax.axis_index("wide"), lax.axis_index("narrow")
    z, x, y, c = lax.div(wide, 2), lax.rem(wide, 2), lax.div(narrow, 2), lax.rem(narrow, 2)
    other = {"x": 1 - x, "y": 1 - y, "c": 1 - c}
    at = lambda zz, xx, yy, cc: (zz * 2 + xx, yy * 2 + cc)
    z_pair = {0: z, 1: z + 1 - 2 * lax.rem(z, 2), 2: lax.rem(z + 2, 4), 3: 3 - z}
    z_of = z_from = lambda k: z_pair[k]
    peer = {"x": at(z, 1 - x, y, c), "y": at(z, x, 1 - y, c), "xy": at(z, 1 - x, 1 - y, c), "c": at(z, x, y, 1 - c)}
    for k in (1, 2, 3):
        peer[k] = at(z_of(k), x, y, c)

    ids, started = {}, {}

    def copy(key, src, dst, to):
        i = ids.setdefault(key, len(ids))
        return pltpu.make_async_remote_copy(
            src_ref=src, dst_ref=dst, send_sem=send_sem.at[i], recv_sem=recv_sem.at[i],
            device_id=peer[to], device_id_type=MESH_ID)

    def send(key, src, dst, to):
        d = copy(key, src, dst, to)
        d.start()
        started[key] = d

    def sent(key):
        if key in started:
            started.pop(key).wait_send()

    PLANE = [("xy", 1 - x, 1 - y), ("x", 1 - x, y), ("y", x, 1 - y)]
    ORDER = (0, 1, 2, 3)

    def gather_ops(j, name):
        ref = w_in if name == "in" else w_out

        def z_send():
            mine = ref.at[j, z, x, y, c]
            for k in (1, 2, 3):
                send(("z", j, name, k), mine, mine, k)

        def plane_send(k):
            piece = ref.at[j, z_from(k), x, y, c]
            if k:
                copy(("z", j, name, k), piece, piece, k).wait_recv()
            for to, _, _ in PLANE:
                send(("p" + to, j, name, k), piece, piece, to)

        def core_send(k):
            zz = z_from(k)
            for to, xx, yy in PLANE:
                got = ref.at[j, zz, xx, yy, c]
                copy(("p" + to, j, name, k), got, got, to).wait_recv()
            piece = ref.at[j, zz, :, :, c]
            send(("c", j, name, k), piece, piece, "c")

        def core_wait(k):
            got = ref.at[j, z_from(k), :, :, 1 - c]
            copy(("c", j, name, k), got, got, "c").wait_recv()

        return z_send, plane_send, core_send, core_wait

    def pack_z(j):
        mine = pack.at[j, z, x, y, c]
        for k in (1, 2, 3):
            send(("pz", j, k), mine, mine, k)

    def pack_plane(j):
        for k in (1, 2, 3):
            got = pack.at[j, z_from(k), x, y, c]
            copy(("pz", j, k), got, got, k).wait_recv()
        for to, _, _ in PLANE:
            piece = pack.at[j, :, x, y, c]
            send(("pp", j, to), piece, piece, to)

    def pack_core(j):
        for to, xx, yy in PLANE:
            got = pack.at[j, :, xx, yy, c]
            copy(("pp", j, to), got, got, to).wait_recv()
        piece = pack.at[j, :, :, :, c]
        send(("pc", j), piece, piece, "c")

    def pack_wait(j):
        got = pack.at[j, :, :, :, 1 - c]
        copy(("pc", j), got, got, "c").wait_recv()

    def reduce_core(j, a, k, value):
        whole[...] = value.reshape(4, 2, HID, D)
        sent(("rc", 1, a, k))
        for i in range(2):
            for l in range(2):
                kept[a, k, i, l] = whole[2 * i + l, c]
                s_core[a, k, i, l] = whole[2 * i + l, 1 - c].astype(bf16)
        send(("rc", j, a, k), s_core.at[a, k], r_core.at[j, a, k], "c")

    def reduce_plane(j, a, k):
        copy(("rc", j, a, k), s_core.at[a, k], r_core.at[j, a, k], "c").wait_recv()
        for n, (to, xx, yy) in enumerate(PLANE):
            sent(("rp", 1, a, k, n))
            s_plane[a, k, n] = (kept[a, k, xx, yy] + r_core[j, a, k, xx, yy].astype(f32)).astype(bf16)
            send(("rp", j, a, k, n), s_plane.at[a, k, n], r_plane.at[j, a, k, n], to)

    def reduce_z(j, a, k):
        s = kept[a, k, x, y] + r_core[j, a, k, x, y].astype(f32)
        for n, (to, _, _) in enumerate(PLANE):
            copy(("rp", j, a, k, n), s_plane.at[a, k, n], r_plane.at[j, a, k, n], to).wait_recv()
            s = s + r_plane[j, a, k, n].astype(f32)
        if k:
            sent(("rz", 1, a, k))
            s_z[a, k - 1] = s.astype(bf16)
            send(("rz", j, a, k), s_z.at[a, k - 1], r_z.at[j, a, k - 1], k)
        elif a == 0:
            g_w_in[j, :, :D] = s
        else:
            g_w_out[j] = s

    def reduce_end(j, a):
        for k in (1, 2, 3):
            copy(("rz", j, a, k), s_z.at[a, k - 1], r_z.at[j, a, k - 1], k).wait_recv()
        s = r_z[j, a, 0].astype(f32) + r_z[j, a, 1].astype(f32) + r_z[j, a, 2].astype(f32)
        if a == 0:
            g_w_in[j, :, :D] += s
        else:
            g_w_out[j] += s

    def small_core(j):
        for zz in range(4):
            for i in range(2):
                for l in range(2):
                    f_own[j, zz, i, l] = facc[j, zz, i, l, 1 - c].astype(bf16)
        send(("fc", j), f_own.at[j], f_core.at[j], "c")
        v_send[j] = jnp.concatenate([jnp.sum(vacc[j, i], 0, keepdims=True) for i in range(5)] + [jnp.zeros((3, D), f32)], 0)
        send(("vc", j), v_send.at[j], v_core.at[j], "c")

    def small_plane(j):
        copy(("fc", j), f_own.at[j], f_core.at[j], "c").wait_recv()
        for zz in range(4):
            for i in range(2):
                for l in range(2):
                    f_keep[j, i, l, zz] = facc[j, zz, i, l, c] + f_core[j, zz, i, l].astype(f32)
        for n, (to, xx, yy) in enumerate(PLANE):
            f_send[j, n] = f_keep[j, xx, yy].astype(bf16)
            send(("fp", j, n), f_send.at[j, n], f_xy.at[j, n], to)
        copy(("vc", j), v_core.at[j], v_core.at[j], "c").wait_recv()
        v_xy[j, x, y] = v_send[j] + v_core[j]
        mine = v_xy.at[j, x, y]
        for to, _, _ in PLANE:
            send(("vp", j, to), mine, mine, to)

    def small_z(j):
        s = f_keep[j, x, y]
        for n, (to, _, _) in enumerate(PLANE):
            copy(("fp", j, n), f_send.at[j, n], f_xy.at[j, n], to).wait_recv()
            s = s + f_xy[j, n].astype(f32)
        f_keep[j, x, y] = s
        for k in (1, 2, 3):
            f_z_send[j, k - 1] = f_keep[j, x, y, z_of(k)].astype(bf16)
            send(("fz", j, k), f_z_send.at[j, k - 1], f_z.at[j, k - 1], k)
        for to, xx, yy in PLANE:
            got = v_xy.at[j, xx, yy]
            copy(("vp", j, to), got, got, to).wait_recv()
        v_z[j, z] = v_xy[j, 0, 0] + v_xy[j, 0, 1] + v_xy[j, 1, 0] + v_xy[j, 1, 1]
        mine = v_z.at[j, z]
        for k in (1, 2, 3):
            send(("vz", j, k), mine, mine, k)

    def small_end(j):
        for k in (1, 2, 3):
            copy(("fz", j, k), f_z_send.at[j, k - 1], f_z.at[j, k - 1], k).wait_recv()
        s = f_keep[j, x, y, z] + f_z[j, 0].astype(f32) + f_z[j, 1].astype(f32) + f_z[j, 2].astype(f32)
        for r in range(7):
            g_filters[j : j + 1, r * D : (r + 1) * D] = s[r : r + 1]
        g_w_in[j, :, D:] = jnp.sum(jnp.where(diagonal(), s[7:8, :128], 0.0), 1, keepdims=True)
        for k in (1, 2, 3):
            got = v_z.at[j, z_from(k)]
            copy(("vz", j, k), got, got, k).wait_recv()
        v = v_z[j, 0] + v_z[j, 1] + v_z[j, 2] + v_z[j, 3]
        g_gains[j] = v[0:2]
        for l in range(3):
            g_biases[l, j : j + 1] = v[2 + l : 3 + l]

    def diagonal():
        shape = (HID, 128)
        return lax.broadcasted_iota(jnp.int32, shape, 0) == lax.broadcasted_iota(jnp.int32, shape, 1)

    def load_rows(dst, a, b):
        v = jnp.swapaxes(a[...], 0, 1).astype(dst.dtype)
        for i in range(large):
            dst[i * LP + LP - 16 : (i + 1) * LP, :] = jnp.zeros((16, D), dst.dtype)
            dst[i * LP : i * LP + PL, :] = v[i]
        for i in range(small):
            dst[base + i * PS : base + (i + 1) * PS, :] = b[i].astype(dst.dtype)
        dst[base + small * PS :, :] = jnp.zeros((rows - base - small * PS, D), dst.dtype)

    def store_large(a):
        v = jnp.concatenate([xs[i * LP : i * LP + PL, :][None] for i in range(large)], 0)
        a[...] = jnp.swapaxes(v, 0, 1).astype(a.dtype)

    def store_small(b):
        for i in range(small):
            b[i] = xs[base + i * PS : base + (i + 1) * PS, :].astype(b.dtype)

    def own_pieces():
        for j in range(BLOCKS):
            w_in[j, z, x, y, c] = raw_in[j, :, :D]
            w_out[j, z, x, y, c] = raw_out[j]
            bias = jnp.sum(jnp.where(diagonal(), raw_in[j, :, D:].astype(f32), 0.0), 0, keepdims=True)
            row = raw_filters[j : j + 1, :].astype(f32)
            parts = [row[:, r * D : (r + 1) * D] for r in range(7)]
            parts.append(jnp.concatenate([bias, jnp.zeros((1, D - 128), f32)], 1))
            pack[j, z, x, y, c] = jnp.concatenate(parts, 0).astype(bf16)

    fetches = [pltpu.make_async_copy(a, b, in_sem.at[n]) for n, (a, b) in enumerate(zip(given, held))]
    stores = []

    def fetched(*which):
        for n in which:
            fetches[n].wait()

    def put(n, value):
        d = pltpu.make_async_copy(value, made[n], out_sem.at[n])
        d.start()
        stores.append(d)

    def spread_rows(r):
        return jnp.broadcast_to(r, (r.shape[0], 128))

    def wide_rows(r):
        return jnp.concatenate([r, r, r], -1)

    def mean_row(n_rows, period, scale):
        row = lax.broadcasted_iota(jnp.int32, (n_rows, 1), 0)
        hit = row == 0
        for q in range(1, period):
            hit = hit | (row == q * FS)
        return jnp.where(hit, scale, 0.0).astype(f32)

    def crop_loops(body, which):
        def big(i, _):
            body(pl.ds(aligned(i * LP, 16), LP), i, True)
            return 0
        def little(i, _):
            body(pl.ds(aligned(base + i * SR, 16), SR), i, False)
            return 0
        if "big" in which:
            lax.fori_loop(0, large, big, 0)
        if "small" in which:
            lax.fori_loop(0, groups, little, 0)

    def to_spectrum(j, which=BOTH):
        def body(o, i, big):
            vh, r = standardize(xs[o, :])
            vh1[j, o, :] = vh.astype(bf16)
            r1[j, o, :] = spread_rows(r)
            if big:
                sv_large[j, i] = apply_table(t_fwd[...], vh)
            else:
                sv_small[j, i] = apply_table(t_sfwd[...], vh)
        crop_loops(body, which)

    def unpack_filters(j):
        f = pack[j].reshape(SPEC, D)
        for h in range(2):
            s = mm(t_shrink[...], f[h * FLP : (h + 1) * FLP])
            s = s[:FS] + s[FS:]
            filt_s[j, h * QF : (h + 1) * QF] = jnp.concatenate([s] * Q, 0)
        bias = mm(t_pick[...], f[:, :128]).astype(bf16)
        bias = mm(bias, t_spread[...])
        mine = lax.div(lax.broadcasted_iota(jnp.int32, (32, FF), 1), HID) == lax.broadcasted_iota(jnp.int32, (32, FF), 0)
        bias = jnp.sum(jnp.where(mine, bias, 0.0), 0, keepdims=True)
        for h in range(2):
            b_in[j, h] = bias[:, h * (FF // 2) : (h + 1) * (FF // 2)]

    def spectrum_of(j, i, big):
        sv = sv_large[j, i] if big else sv_small[j, i]
        h = FLP if big else QF
        dc = mean_row(h, 1, float(GL)) if big else mean_row(h, Q, float(GS))
        re = sv[:h] * gains[j, 0:1, :] + dc * biases[0, j : j + 1, :]
        im = sv[h:] * gains[j, 0:1, :]
        f = pack[j].reshape(SPEC, D).astype(f32) if big else filt_s[j]
        return sv, re, im, f[:h], f[h:], dc

    def from_spectrum(j, which=BOTH):
        def body(o, i, big):
            _, re, im, fr, fi, _ = spectrum_of(j, i, big)
            out = jnp.concatenate([re * fr - im * fi, re * fi + im * fr], 0)
            xs[o, :] = xs[o, :] + apply_table(t_inv[...] if big else t_sinv[...], out)
        crop_loops(body, which)

    def tiles(body, start=0, stop=None):
        def one(t, _):
            body(pl.ds(aligned(t * TILE, TILE), TILE))
            return 0
        lax.fori_loop(start, rows // TILE if stop is None else stop, one, 0)

    def expand(j, h, first, start=0, stop=None):
        def body(o):
            if first:
                vh, r = standardize(xs[o, :])
                vh2[j, o, :] = vh
                r2[j, o, :] = spread_rows(r)
                s = (vh * gains[j, 1:2, :] + biases[1, j : j + 1, :]).astype(bf16)
                second[j, o, :] = s
            else:
                s = second[j, o, :]
            pre = mm_nt(s, w_in[j, pl.ds(2 * h, 2)].reshape(FF // 2, D)) + b_in[j, h]
            phi = 0.5 + 0.5 * lax.erf(pre * (1 / math.sqrt(2)))
            active[j, h, o, :] = (pre * phi).astype(bf16)
            slope[j, h, o, :] = (phi + pre * (jnp.exp(-0.5 * pre * pre) * (1 / math.sqrt(2 * math.pi)))).astype(bf16)
        tiles(body, start, stop)

    def contract(j):
        def body(o):
            s = xs[o, :] + biases[2, j : j + 1, :]
            for h in range(2):
                s = s + mm(active[j, h, o, :], w_out[j, 2 * h : 2 * h + 2].reshape(FF // 2, D))
            xs[o, :] = s
        tiles(body)

    def z_offset(k):
        zz = z_of(k)
        return lax.div(zz, 2), pl.ds(aligned(lax.rem(zz, 2) * (FF // 4), 128), FF // 4)

    def back_hidden(j, h, last):
        def body(o):
            w = w_out[j, pl.ds(2 * h, 2)].reshape(FF // 2, D)
            pg = mm_nt(grad_low[o, :], w) * slope[j, h, o, :].astype(f32)
            bacc[j, h] += fold(pg)
            p = pg.astype(bf16)
            slope[j, h, o, :] = p
            sg = mm(p, w_in[j, pl.ds(2 * h, 2)].reshape(FF // 2, D))
            if not last:
                back[o, :] = sg
            else:
                sg = sg + back[o, :]
                vh = vh2[j, o, :]
                vacc[j, 1] += fold(sg * vh)
                vacc[j, 3] += fold(sg)
                g = xs[o, :] if j == 0 else grad_low[o, :].astype(f32)
                xs[o, :] = g + norm_back(vh, wide_rows(r2[j, o, :]), sg * gains[j, 1:2, :])
        tiles(body)

    def weight_in(j, k):
        h, lanes = z_offset(k)
        return mm_tn(slope[j, h, :, lanes], second[j])

    def weight_out(j, k):
        h, lanes = z_offset(k)
        return mm_tn(active[j, h, :, lanes], grad_low[...])

    def back_spectrum(j, which):
        if which == ("small",):
            sacc[...] = jnp.zeros_like(sacc)
        else:
            facc[j] = jnp.zeros(facc.shape[1:], f32)

        def body(o, i, big):
            sv, re, im, fr, fi, dc = spectrum_of(j, i, big)
            h = FLP if big else QF
            sg = apply_table(t_inv_t[...] if big else t_sinv_t[...], xs[o, :])
            gr, gi = sg[:h], sg[h:]
            d_re, d_im = re * gr + im * gi, re * gi - im * gr
            if big:
                facc[j] += jnp.concatenate([d_re, d_im], 0).reshape(4, 2, 2, 2, 8, D)
            else:
                sacc[...] += jnp.concatenate([d_re, d_im], 0)
            n_re, n_im = gr * fr + gi * fi, gi * fr - gr * fi
            vacc[j, 0] += fold(n_re * sv[:h]) + fold(n_im * sv[h:])
            vacc[j, 2] += fold(n_re * dc)
            n = jnp.concatenate([n_re, n_im], 0)
            if big:
                sv_large[j, i] = n
            else:
                sv_small[j, i] = n
        crop_loops(body, which)

    def back_filters(j):
        for h in range(2):
            s = sacc[h * QF : (h + 1) * QF]
            s = s[:FS] + s[FS : 2 * FS] + s[2 * FS : 3 * FS] + s[3 * FS :]
            facc[j, 2 * h : 2 * h + 2] += apply_table(t_shrink_t[...], s).reshape(2, 2, 2, 2, 8, D)
        mine = lax.div(lax.broadcasted_iota(jnp.int32, (32, FF), 1), HID) == lax.broadcasted_iota(jnp.int32, (32, FF), 0)
        row = jnp.sum(jnp.concatenate([bacc[j, 0], bacc[j, 1]], -1), 0, keepdims=True)
        high, low = halves(jnp.where(mine, row, 0.0))
        row = mm(high, t_spread_t[...]) + mm(low, t_spread_t[...])
        high, low = halves(row)
        row = mm(t_pick_t[...], high) + mm(t_pick_t[...], low)
        facc[j] += jnp.concatenate([row, jnp.zeros((SPEC, D - 128), f32)], -1).reshape(4, 2, 2, 2, 8, D)

    def back_rows(j, which=BOTH):
        def body(o, i, big):
            n = sv_large[j, i] if big else sv_small[j, i]
            ng = apply_table(t_fwd_t[...] if big else t_sfwd_t[...], n)
            xs[o, :] = xs[o, :] + norm_back(vh1[j, o, :].astype(f32), wide_rows(r1[j, o, :]), ng * gains[j, 0:1, :])
        crop_loops(body, which)

    i0, o0 = gather_ops(0, "in"), gather_ops(0, "out")
    i1, o1 = gather_ops(1, "in"), gather_ops(1, "out")
    half_z = lax.div(z, 2)

    def steps(ops, which, order=ORDER):
        for k in order:
            ops[which](k)

    run = lambda name, f, *a: jax.named_scope(name)(f)(*a)
    barrier = pltpu.get_barrier_semaphore()
    for to in peer.values():
        pl.semaphore_signal(barrier, 1, device_id=to, device_id_type=MESH_ID)
    for d in fetches:
        d.start()
    fetched(0, 1, 2)
    own_pieces()
    run("barrier", pl.semaphore_wait, barrier, len(peer))

    pack_z(0)
    i0[0]()
    i0[1](0)
    bacc[...] = jnp.zeros_like(bacc)
    vacc[...] = jnp.zeros_like(vacc)
    fetched(3, 4, 5, 6)
    run("load_rows", load_rows, xs, large_rows, small_rows)
    run("to_spectrum", to_spectrum, 0, ("big",))
    run("pack_plane", pack_plane, 0)
    run("i0_plane", steps, i0, 1, (1, 2, 3))
    o0[0]()
    o0[1](0)
    run("to_spectrum", to_spectrum, 0, ("small",))
    fetched(*range(7, N_IN))
    run("load_cot", load_rows, grad_low, cot_large, cot_small)

    def cot_sum(o):
        vacc[1, 4] += fold(grad_low[o, :].astype(f32))
    run("cot_sum", tiles, cot_sum)
    run("pack_core", pack_core, 0)
    run("i0_core", steps, i0, 2, (0, 1))
    run("pack_wait", pack_wait, 0)
    run("unpack", unpack_filters, 0)
    run("from_spectrum", from_spectrum, 0, ("big",))
    run("o0_plane", steps, o0, 1, (1, 2, 3))
    pack_z(1)
    i1[0]()
    i1[1](0)
    run("from_spectrum", from_spectrum, 0, ("small",))
    run("i0_core", steps, i0, 2, (2, 3))
    run("i0_wait", steps, i0, 3, (0, 1))
    run("expand", expand, 0, half_z, True)
    run("i0_wait", steps, i0, 3, (2, 3))
    run("pack_plane", pack_plane, 1)
    run("i1_plane", steps, i1, 1, (1, 2, 3))
    o1[0]()
    o1[1](0)
    run("o0_core", steps, o0, 2, (0, 1))
    run("expand", expand, 0, 1 - half_z, False)
    run("o0_core", steps, o0, 2, (2, 3))
    run("pack_core", pack_core, 1)
    run("o1_plane", steps, o1, 1, (1, 2, 3))
    run("o0_wait", steps, o0, 3)
    run("contract", contract, 0)
    run("pack_wait", pack_wait, 1)
    run("unpack", unpack_filters, 1)
    run("to_spectrum", to_spectrum, 1)
    run("i1_core", steps, i1, 2)
    run("from_spectrum", from_spectrum, 1)
    run("i1_wait", steps, i1, 3)
    run("expand", expand, 1, half_z, True)
    run("o1_core", steps, o1, 2)
    run("expand", expand, 1, 1 - half_z, False)
    run("o1_wait", steps, o1, 3)
    run("contract", contract, 1)
    store_large(large_rows)
    put(0, large_rows)
    store_small(small_rows)
    put(1, small_rows)

    def batch(name, f, j, a, ks):
        with jax.named_scope(name):
            for k in ks:
                f(j, a, k)

    def weights(j, a, ks):
        with jax.named_scope("weights"):
            for k in ks:
                reduce_core(j, a, k, (weight_out if a else weight_in)(j, k))

    ALL, FIRST, LAST = (2, 3, 1, 0), (2, 3), (1, 0)
    for j in (1, 0):
        if j == 0:
            def low(o):
                g = xs[o, :]
                vacc[0, 4] += fold(g)
                grad_low[o, :] = g.astype(bf16)
            run("low", tiles, low)
        weights(j, 1, ALL)
        if j == 0:
            batch("z", reduce_z, 1, 0, FIRST)
            run("small_z", small_z, 1)
        run("back_hidden", back_hidden, j, 1 - half_z, False)
        batch("plane", reduce_plane, j, 1, ALL)
        if j == 0:
            batch("z", reduce_z, 1, 0, LAST)
        weights(j, 0, FIRST)
        run("back_hidden", back_hidden, j, half_z, True)
        batch("plane", reduce_plane, j, 0, FIRST)
        weights(j, 0, (1,))
        batch("z", reduce_z, j, 1, FIRST)
        run("back_spectrum", back_spectrum, j, ("small",))
        batch("plane", reduce_plane, j, 0, (1,))
        batch("z", reduce_z, j, 1, LAST)
        run("back_spectrum", back_spectrum, j, ("big",))
        run("back_filters", back_filters, j)
        run("small_core", small_core, j)
        if j == 0:
            batch("z", reduce_z, 0, 0, FIRST)
        weights(j, 0, (0,))
        run("small_plane", small_plane, j)
        if j == 0:
            batch("z", reduce_z, 0, 0, (1,))
        run("back_rows", back_rows, j, ("small",))
        batch("plane", reduce_plane, j, 0, (0,))
        if j == 0:
            store_small(grad_small)
            put(3, grad_small)
            for a in (1, 0):
                run("reduce_end", reduce_end, 1, a)
            run("small_end", small_end, 1)
        run("back_rows", back_rows, j, ("big",))
    run("small_z", small_z, 0)
    store_large(grad_large)
    put(2, grad_large)
    run("reduce_end", reduce_end, 0, 1)
    put(6, g_w_out)
    batch("z", reduce_z, 0, 0, (0,))
    run("reduce_end", reduce_end, 0, 0)
    run("small_end", small_end, 0)
    put(4, g_filters)
    put(5, g_w_in)
    put(7, g_gains)
    put(8, g_biases)
    for d in stores:
        d.wait()
    for key in list(started):
        sent(key)
    assert len(ids) <= N_SEND


def hand_over_kernel(*refs):
    sources, targets, between = refs[:N_OUT], refs[N_OUT : 2 * N_OUT], refs[2 * N_OUT : 3 * N_OUT]
    in_sem, out_sem = refs[3 * N_OUT :]
    ins = [pltpu.make_async_copy(a, b, in_sem.at[n]) for n, (a, b) in enumerate(zip(sources, between))]
    outs = [pltpu.make_async_copy(a, b, out_sem.at[n]) for n, (a, b) in enumerate(zip(between, targets))]
    for d in ins:
        d.start()
    for a, b in zip(ins, outs):
        a.wait()
        b.start()
    for d in outs:
        d.wait()


def fused(large_in, small_in, large_cot, small_cot, filters, w_in, w_out, gains, biases):
    large, small = large_in.shape[0], small_in.shape[0]
    rows = -(-(large * LP + small * PS) // TILE) * TILE
    early, late = [[jnp.asarray(t) for t in part] for part in constant_tables()]
    args = [jnp.swapaxes(w_in, 1, 2), w_out, filters, small_in, jnp.swapaxes(large_in, 0, 1), *early,
            jnp.swapaxes(large_cot, 0, 1), small_cot, gains, jnp.swapaxes(biases, 0, 1), *late]
    V = pltpu.VMEM
    patch_major = (large_in.shape[1], large, D)
    outs = [(patch_major, bf16), (small_in.shape, bf16), (patch_major, f32), (small_in.shape, f32), (filters.shape, f32),
            ((BLOCKS, HID, D + 1), f32), ((BLOCKS, HID, D), f32), (gains.shape, f32), ((3, BLOCKS, D), f32)]
    grid8 = (4, 2, 2, 2)
    scratch = [V(a.shape, a.dtype) for a in args] + [V(shape, dtype) for shape, dtype in outs[2:]] + [
        V((rows, D), f32), V((BLOCKS, rows, D), bf16), V((BLOCKS, rows, 128), f32), V((BLOCKS, rows, D), f32),
        V((BLOCKS, rows, 128), f32), V((BLOCKS, rows, D), bf16), V((BLOCKS, 2, rows, FF // 2), bf16),
        V((BLOCKS, 2, rows, FF // 2), bf16), V((BLOCKS, large, SPEC, D), f32), V((BLOCKS, small // Q, 2 * QF, D), f32),
        V((rows, D), bf16), V((rows, D), f32),
        V((BLOCKS, *grid8, HID, D), bf16), V((BLOCKS, *grid8, HID, D), bf16), V((BLOCKS, *grid8, 8, D), bf16),
        V((BLOCKS, 2 * QF, D), f32), V((BLOCKS, 2, 1, FF // 2), f32),
        V((BLOCKS, *grid8, 8, D), f32), V((2 * QF, D), f32), V((BLOCKS, 2, 8, FF // 2), f32), V((BLOCKS, 5, 8, D), f32),
        V((4, 2, HID, D), f32), V((2, 4, 2, 2, HID, D), f32),
        V((2, 4, 2, 2, HID, D), bf16), V((2, 4, 3, HID, D), bf16), V((2, 3, HID, D), bf16),
        V((BLOCKS, 2, 4, 2, 2, HID, D), bf16), V((BLOCKS, 2, 4, 3, HID, D), bf16), V((BLOCKS, 2, 3, HID, D), bf16),
        V((BLOCKS, 4, 2, 2, 8, D), bf16), V((BLOCKS, 4, 2, 2, 8, D), bf16), V((BLOCKS, 2, 2, 4, 8, D), f32),
        V((BLOCKS, 3, 4, 8, D), bf16), V((BLOCKS, 3, 4, 8, D), bf16), V((BLOCKS, 3, 8, D), bf16), V((BLOCKS, 3, 8, D), bf16),
        V((BLOCKS, 8, D), f32), V((BLOCKS, 8, D), f32), V((BLOCKS, 2, 2, 8, D), f32), V((BLOCKS, 4, 8, D), f32),
        pltpu.SemaphoreType.DMA((N_SEND,)), pltpu.SemaphoreType.DMA((N_SEND,)),
        pltpu.SemaphoreType.DMA((N_IN,)), pltpu.SemaphoreType.DMA((N_OUT,)),
    ]
    anywhere = pl.BlockSpec(memory_space=pl.ANY)
    out_shape = [jax.ShapeDtypeStruct(shape, dtype) for shape, dtype in outs]
    result = pl.pallas_call(
        partial(fused_kernel, large, small),
        out_shape=out_shape,
        in_specs=[anywhere] * N_IN,
        out_specs=[anywhere] * N_OUT,
        scratch_shapes=scratch,
        compiler_params=pltpu.CompilerParams(collective_id=0, has_side_effects=True, vmem_limit_bytes=VMEM_BYTES),
        name="gfnet_step",
    )(*args)
    out_large, out_small, grad_large, grad_small, g_filters, g_in, g_out, g_gains, g_biases = pl.pallas_call(
        hand_over_kernel,
        out_shape=out_shape,
        in_specs=[anywhere] * N_OUT,
        out_specs=[anywhere] * N_OUT,
        scratch_shapes=[V(shape, dtype) for shape, dtype in outs] + [pltpu.SemaphoreType.DMA((N_OUT,))] * 2,
        compiler_params=pltpu.CompilerParams(vmem_limit_bytes=VMEM_BYTES),
        name="hand_over",
    )(*result)
    return (jnp.swapaxes(out_large, 0, 1), out_small, jnp.swapaxes(grad_large, 0, 1), grad_small, g_filters,
            jnp.swapaxes(g_in, 1, 2), g_out, g_gains, jnp.swapaxes(g_biases, 0, 1))


def solution(mesh):
    in_specs = (
        P(("wide", "narrow"), None, None),
        P(("wide", "narrow"), None, None),
        P(("wide", "narrow"), None, None),
        P(("wide", "narrow"), None, None),
        P(None, ("wide", "narrow")),
        P(None, None, ("wide", "narrow")),
        P(None, ("wide", "narrow"), None),
        P(),
        P(),
    )
    out_specs = (
        P(("wide", "narrow"), None, None),
        P(("wide", "narrow"), None, None),
        P(("wide", "narrow"), None, None),
        P(("wide", "narrow"), None, None),
        P(None, ("wide", "narrow")),
        P(None, None, ("wide", "narrow")),
        P(None, ("wide", "narrow"), None),
        P(),
        P(),
    )
    body = fused if dict(mesh.shape) == {"wide": 8, "narrow": 4} else per_device
    return jax.shard_map(
        body, mesh=mesh, in_specs=in_specs, out_specs=out_specs, check_vma=False
    )
```

```python
from functools import partial
import math

import jax
import jax.numpy as jnp
import ml_dtypes
import numpy as np
from jax import lax
from jax.experimental import pallas as pl
from jax.experimental.pallas import tpu as pltpu
from jax.sharding import PartitionSpec as P

FF = 1536
GL = 14
GS = 6
BLOCKS = 2
MICRO = 2
PL = 196
FL = 112
FS = 24


precise = lax.Precision.HIGHEST
epsilon = 1e-06


def dft_tables(grid_cells):
    half_count = grid_cells // 2 + 1
    places = jnp.arange(grid_cells * grid_cells, dtype=jnp.int32)
    place_row = places // grid_cells
    place_col = places % grid_cells
    modes = jnp.arange(grid_cells * half_count, dtype=jnp.int32)
    mode_row = modes // half_count
    mode_col = modes % half_count
    phases = (
        mode_row[:, None] * place_row[None, :] + mode_col[:, None] * place_col[None, :]
    ) % grid_cells
    angles = phases.astype(jnp.float32) * (2.0 * math.pi / grid_cells)
    forward_re = jnp.cos(angles) / grid_cells
    forward_im = -jnp.sin(angles) / grid_cells
    doubling = jnp.where((mode_col == 0) | (2 * mode_col == grid_cells), 1.0, 2.0).astype(
        jnp.float32
    )
    inverse_re = jnp.transpose(forward_re * doubling[:, None])
    inverse_im = jnp.transpose(forward_im * doubling[:, None])
    return (forward_re, forward_im, inverse_re, inverse_im)


def linear_map(size_out, size_in):
    rows_out = jnp.arange(size_out, dtype=jnp.int32)
    spans = rows_out * (size_in - 1)
    lower = spans // (size_out - 1)
    fraction = (spans - lower * (size_out - 1)).astype(jnp.float32) / (size_out - 1)
    columns = jnp.arange(size_in, dtype=jnp.int32)
    first = jnp.where(columns[None, :] == lower[:, None], 1.0 - fraction[:, None], 0.0)
    second = jnp.where(columns[None, :] == lower[:, None] + 1, fraction[:, None], 0.0)
    return first + second


def shrink_map():
    along_rows = linear_map(GS, GL)
    along_cols = linear_map(GS // 2 + 1, GL // 2 + 1)
    return (along_rows[:, None, :, None] * along_cols[None, :, None, :]).reshape(FS, FL)


def filter_grid(patches, tables, filt_re, filt_im):
    forward_re, forward_im, inverse_re, inverse_im = tables
    spec_re = jnp.einsum("fp,bpd->bfd", forward_re, patches, precision=precise)
    spec_im = jnp.einsum("fp,bpd->bfd", forward_im, patches, precision=precise)
    out_re = spec_re * filt_re - spec_im * filt_im
    out_im = spec_re * filt_im + spec_im * filt_re
    back_re = jnp.einsum("pf,bfd->bpd", inverse_re, out_re, precision=precise)
    back_im = jnp.einsum("pf,bfd->bpd", inverse_im, out_im, precision=precise)
    return back_re + back_im


def spectral(normed, large_rows, filt_re, filt_im):
    width = normed.shape[-1]
    shrink = shrink_map()
    small_re = jnp.dot(shrink, filt_re, precision=precise, preferred_element_type=jnp.float32)
    small_im = jnp.dot(shrink, filt_im, precision=precise, preferred_element_type=jnp.float32)
    part_large = filter_grid(
        normed[:large_rows].reshape(-1, GL * GL, width), dft_tables(GL), filt_re, filt_im
    )
    part_small = filter_grid(
        normed[large_rows:].reshape(-1, GS * GS, width), dft_tables(GS), small_re, small_im
    )
    return jnp.concatenate([part_large.reshape(-1, width), part_small.reshape(-1, width)], 0)


def layer_norm(stream, gain, shift):
    centre = stream - jnp.mean(stream, axis=-1, keepdims=True)
    spread = jnp.mean(centre * centre, axis=-1, keepdims=True)
    return centre * lax.rsqrt(spread + epsilon) * gain + shift


def per_device(large_in, small_in, large_cot, small_cot, filters, w_in, w_out, gains, biases):
    width = large_in.shape[-1]
    micro_large = large_in.shape[0] // MICRO
    micro_small = small_in.shape[0] // MICRO
    large_rows = micro_large * PL
    exact_gelu = partial(jax.nn.gelu, approximate=False)

    def fetch(layer_index, forward):
        if forward:
            return (
                lax.all_gather(filters[layer_index], ("wide", "narrow"), axis=0, tiled=True),
                lax.all_gather(w_in[layer_index], ("wide", "narrow"), axis=1, tiled=True),
                lax.all_gather(w_out[layer_index], ("wide", "narrow"), axis=0, tiled=True),
            )
        return (
            lax.all_gather(filters[layer_index], ("wide", "narrow"), axis=0, tiled=True),
            lax.all_gather(w_in[layer_index], ("wide", "narrow"), axis=1, tiled=True),
            lax.all_gather(w_out[layer_index], ("wide", "narrow"), axis=0, tiled=True),
        )

    def branch_first(stream, gain, shift, filt_re, filt_im):
        return spectral(layer_norm(stream, gain, shift), large_rows, filt_re, filt_im)

    acc_filter = [jnp.zeros((2, FL, width), jnp.float32) for layer_index in range(BLOCKS)]
    acc_in = [jnp.zeros((width, FF), jnp.float32) for layer_index in range(BLOCKS)]
    acc_in_bias = [jnp.zeros((FF,), jnp.float32) for layer_index in range(BLOCKS)]
    acc_out = [jnp.zeros((FF, width), jnp.float32) for layer_index in range(BLOCKS)]
    acc_gain = [jnp.zeros((2, width), jnp.float32) for layer_index in range(BLOCKS)]
    acc_shift = [jnp.zeros((3, width), jnp.float32) for layer_index in range(BLOCKS)]
    outs_large, outs_small, grads_large, grads_small = ([], [], [], [])
    for micro_step in range(MICRO):
        large_part = large_in[micro_step * micro_large : (micro_step + 1) * micro_large]
        small_part = small_in[micro_step * micro_small : (micro_step + 1) * micro_small]
        stream = jnp.concatenate(
            [large_part.reshape(-1, width), small_part.reshape(-1, width)], 0
        ).astype(jnp.float32)
        saved = []
        for layer_index in range(BLOCKS):
            filt_full, in_full, out_full = fetch(layer_index, True)
            halves = filt_full.reshape(2, FL, width).astype(jnp.float32)
            mixed = stream + branch_first(
                stream, gains[layer_index, 0], biases[layer_index, 0], halves[0], halves[1]
            )
            second = layer_norm(mixed, gains[layer_index, 1], biases[layer_index, 1]).astype(
                jnp.bfloat16
            )
            pre_act = jnp.dot(
                second, in_full[:width], preferred_element_type=jnp.float32
            ) + in_full[width].astype(jnp.float32)
            active = exact_gelu(pre_act).astype(jnp.bfloat16)
            saved.append((stream, mixed, second, pre_act))
            stream = (
                mixed
                + jnp.dot(active, out_full, preferred_element_type=jnp.float32)
                + biases[layer_index, 2]
            )
        outs_large.append(stream[:large_rows].reshape(large_part.shape).astype(jnp.bfloat16))
        outs_small.append(stream[large_rows:].reshape(small_part.shape).astype(jnp.bfloat16))
        large_back = large_cot[micro_step * micro_large : (micro_step + 1) * micro_large]
        small_back = small_cot[micro_step * micro_small : (micro_step + 1) * micro_small]
        grad = jnp.concatenate(
            [large_back.reshape(-1, width), small_back.reshape(-1, width)], 0
        ).astype(jnp.float32)
        for layer_index in reversed(range(BLOCKS)):
            block_input, mixed, second, pre_act = saved[layer_index]
            filt_full, in_full, out_full = fetch(layer_index, False)
            halves = filt_full.reshape(2, FL, width).astype(jnp.float32)
            grad_low = grad.astype(jnp.bfloat16)
            active, gelu_back = jax.vjp(exact_gelu, pre_act)
            active = active.astype(jnp.bfloat16)
            acc_out[layer_index] = acc_out[layer_index] + jnp.einsum(
                "tf,td->fd", active, grad_low, preferred_element_type=jnp.float32
            )
            bias_out_grad = jnp.sum(grad, axis=0)
            active_grad = jnp.einsum(
                "td,fd->tf", grad_low, out_full, preferred_element_type=jnp.float32
            )
            pre_grad = gelu_back(active_grad)[0]
            pre_low = pre_grad.astype(jnp.bfloat16)
            acc_in[layer_index] = acc_in[layer_index] + jnp.einsum(
                "td,tf->df", second, pre_low, preferred_element_type=jnp.float32
            )
            acc_in_bias[layer_index] = acc_in_bias[layer_index] + jnp.sum(pre_grad, axis=0)
            second_grad = jnp.einsum(
                "tf,df->td", pre_low, in_full[:width], preferred_element_type=jnp.float32
            )
            unused, norm_back = jax.vjp(
                layer_norm, mixed, gains[layer_index, 1], biases[layer_index, 1]
            )
            mixed_part, gain_two, shift_two = norm_back(second_grad)
            mixed_grad = grad + mixed_part
            unused, first_back = jax.vjp(
                branch_first,
                block_input,
                gains[layer_index, 0],
                biases[layer_index, 0],
                halves[0],
                halves[1],
            )
            input_part, gain_one, shift_one, filt_re_grad, filt_im_grad = first_back(mixed_grad)
            grad = mixed_grad + input_part
            acc_filter[layer_index] = acc_filter[layer_index] + jnp.stack(
                [filt_re_grad, filt_im_grad], 0
            )
            acc_gain[layer_index] = acc_gain[layer_index] + jnp.stack([gain_one, gain_two], 0)
            acc_shift[layer_index] = acc_shift[layer_index] + jnp.stack(
                [shift_one, shift_two, bias_out_grad], 0
            )
        grads_large.append(grad[:large_rows].reshape(large_part.shape))
        grads_small.append(grad[large_rows:].reshape(small_part.shape))
    filter_shards, in_shards, out_shards = ([], [], [])
    for layer_index in range(BLOCKS):
        in_whole = jnp.concatenate([acc_in[layer_index], acc_in_bias[layer_index][None, :]], 0)
        filter_piece, in_piece, out_piece = (
            lax.psum_scatter(
                acc_filter[layer_index].reshape(-1),
                ("wide", "narrow"),
                scatter_dimension=0,
                tiled=True,
            ),
            lax.psum_scatter(in_whole, ("wide", "narrow"), scatter_dimension=1, tiled=True),
            lax.psum_scatter(
                acc_out[layer_index], ("wide", "narrow"), scatter_dimension=0, tiled=True
            ),
        )
        filter_shards.append(filter_piece)
        in_shards.append(in_piece)
        out_shards.append(out_piece)
    gain_total, shift_total = lax.psum(
        (jnp.stack(acc_gain, 0), jnp.stack(acc_shift, 0)), ("wide", "narrow")
    )
    return (
        jnp.concatenate(outs_large, 0),
        jnp.concatenate(outs_small, 0),
        jnp.concatenate(grads_large, 0),
        jnp.concatenate(grads_small, 0),
        jnp.stack(filter_shards, 0),
        jnp.stack(in_shards, 0),
        jnp.stack(out_shards, 0),
        gain_total,
        shift_total,
    )


MESH_ID = pl.DeviceIdType.MESH
bf16, f32 = jnp.bfloat16, jnp.float32
D, PS, EPS = 384, 36, 1e-6
LP = 208
Q = 4
SR = Q * PS
TILE = 256
BOTH = ("big", "small")
HID = 48
FLP = 128
SPEC = 2 * FLP
QF = Q * FS


def dft_arrays(n):
    half = n // 2 + 1
    places, modes = np.arange(n * n), np.arange(n * half)
    phase = ((modes // half)[:, None] * (places // n)[None] + (modes % half)[:, None] * (places % n)[None]) % n
    theta = phase * (2 * math.pi / n)
    fwd_re, fwd_im = np.cos(theta) / n, -np.sin(theta) / n
    weight = np.where((modes % half == 0) | (2 * (modes % half) == n), 1.0, 2.0)
    return fwd_re, fwd_im, fwd_re * weight[:, None], fwd_im * weight[:, None]


def interpolation(rows, cols):
    span = np.arange(rows) * (cols - 1)
    low = span // (rows - 1)
    part = (span - low * (rows - 1)) / (rows - 1)
    at = np.arange(cols)[None]
    return np.where(at == low[:, None], 1 - part[:, None], 0.0) + np.where(at == low[:, None] + 1, part[:, None], 0.0)


def two_terms(table):
    table = np.asarray(table, np.float32)
    high = table.astype(ml_dtypes.bfloat16)
    low = (table - high.astype(np.float32)).astype(ml_dtypes.bfloat16)
    return np.concatenate([high, low], 0)


def constant_tables():
    pos = np.arange(FL) // 7 * 8 + np.arange(FL) % 7
    rows = np.concatenate([pos, FLP + pos])
    fr, fi, ir, ii = dft_arrays(GL)
    fwd, inv = np.zeros((SPEC, LP)), np.zeros((SPEC, LP))
    fwd[rows, :PL], inv[rows, :PL] = np.concatenate([fr, fi]), np.concatenate([ir, ii])
    fr, fi, ir, ii = dft_arrays(GS)
    sfwd, sinv = np.zeros((2 * QF, SR)), np.zeros((2 * QF, SR))
    for q in range(Q):
        at = slice(q * PS, (q + 1) * PS)
        for half, a, b in ((0, fr, ir), (1, fi, ii)):
            to = slice(half * QF + q * FS, half * QF + (q + 1) * FS)
            sfwd[to, at], sinv[to, at] = a, b
    shrink = np.zeros((FS, FLP))
    shrink[:, pos] = (
        interpolation(GS, GL)[:, None, :, None] * interpolation(GS // 2 + 1, GL // 2 + 1)[None, :, None, :]
    ).reshape(FS, FL)
    pick = np.zeros((32, SPEC))
    pick[np.arange(32), 8 * np.arange(32) + 7] = 1
    spread = np.arange(FF)[None] % HID == np.arange(128)[:, None]
    plain = lambda t: np.asarray(t, np.float32).astype(ml_dtypes.bfloat16)
    return ([two_terms(t) for t in (fwd, sfwd)],
            [two_terms(shrink), plain(pick), plain(spread)]
            + [two_terms(t) for t in (inv.T, sinv.T, inv, sinv, shrink.T)]
            + [plain(spread.T), plain(pick.T), two_terms(fwd.T), two_terms(sfwd.T)])


def mm(a, b):
    return lax.dot_general(a, b, (((1,), (0,)), ((), ())), preferred_element_type=f32)


def mm_nt(a, b):
    return lax.dot_general(a, b, (((1,), (1,)), ((), ())), preferred_element_type=f32)


def mm_tn(a, b):
    return lax.dot_general(a, b, (((0,), (0,)), ((), ())), preferred_element_type=f32)


def halves(v):
    high = v.astype(bf16)
    return high, (v - high.astype(f32)).astype(bf16)


def apply_table(table, v):
    rows = table.shape[0] // 2
    high, low = halves(v)
    both = mm(table, high)
    return both[:rows] + both[rows:] + mm(table[:rows], low)


def standardize(v):
    centre = v - jnp.sum(v, -1, keepdims=True) * (1.0 / D)
    r = lax.rsqrt(jnp.sum(centre * centre, -1, keepdims=True) * (1.0 / D) + EPS)
    return centre * r, r


def norm_back(vh, r, q):
    mean_q = jnp.sum(q, -1, keepdims=True) * (1.0 / D)
    mean_qv = jnp.sum(q * vh, -1, keepdims=True) * (1.0 / D)
    return r * (q - mean_q - vh * mean_qv)


def fold(v):
    return jnp.sum(v.reshape(v.shape[0] // 8, 8, v.shape[1]), 0)


def aligned(v, m):
    return v if isinstance(v, int) else pl.multiple_of(v, m)


N_SEND, N_RECEIVE = 44, 90
VMEM_BYTES = 63 << 20


N_IN, N_OUT = 23, 9


def fused_kernel(large, small, *refs):
    given, made, refs = refs[:N_IN], refs[N_IN : N_IN + N_OUT], refs[N_IN + N_OUT :]
    held, refs = refs[:N_IN], refs[N_IN:]
    (raw_in, raw_out, raw_filters, small_rows, large_rows, t_fwd, t_sfwd, cot_large, cot_small, gains, biases,
     t_shrink, t_pick, t_spread, t_inv, t_sinv, t_inv_t, t_sinv_t, t_shrink_t, t_spread_t, t_pick_t, t_fwd_t, t_sfwd_t) = held
    (grad_large, grad_small, g_filters, g_w_in, g_w_out, g_gains, g_biases,
     xs, vh1, r1, vh2, r2, second, active, slope, sv_large, sv_small, grad_low,
     w_in, w_out, pack, filt_s, b_in, facc, sacc, bacc, vacc,
     kept, s_core, s_plane, s_z, r_core, r_plane, r_z,
     f_own, f_core, f_keep, f_send, f_xy, f_z_send, f_z, v_send, v_core, v_xy, v_z,
     send_sem, recv_sem, in_sem, out_sem) = refs
    rows = xs.shape[0]
    groups = small // Q
    base = large * LP
    wide, narrow = lax.axis_index("wide"), lax.axis_index("narrow")
    z, x, y, c = lax.div(wide, 2), lax.rem(wide, 2), lax.div(narrow, 2), lax.rem(narrow, 2)
    other = {"x": 1 - x, "y": 1 - y, "c": 1 - c}
    at = lambda zz, xx, yy, cc: (zz * 2 + xx, yy * 2 + cc)
    z_pair = {0: z, 1: z + 1 - 2 * lax.rem(z, 2), 2: lax.rem(z + 2, 4), 3: 3 - z}
    z_of = lambda k: z_pair[k]
    peer = {"x": at(z, 1 - x, y, c), "y": at(z, x, 1 - y, c), "xy": at(z, 1 - x, 1 - y, c), "c": at(z, x, y, 1 - c)}
    for k in (1, 2, 3):
        peer[k] = at(z_of(k), x, y, c)

    sending, receiving, unsent = {}, {}, {}

    def send(key, src, dst, to, group=None, view=None):
        group = group or key
        out, back = group if isinstance(group, list) else (group, group)
        pltpu.make_async_remote_copy(
            src_ref=src, dst_ref=dst, send_sem=send_sem.at[sending.setdefault(out, len(sending))],
            recv_sem=recv_sem.at[receiving.setdefault(back, len(receiving))],
            device_id=peer[to], device_id_type=MESH_ID).start()
        unsent[out] = src if view is None else view

    def arrived(key, view):
        sem = recv_sem.at[receiving.setdefault(key, len(receiving))]
        pltpu.make_async_copy(view, view, sem).wait()

    def sent(key):
        if key in unsent:
            view = unsent.pop(key)
            pltpu.make_async_copy(view, view, send_sem.at[sending[key]]).wait()

    PLANE = [("xy", 1 - x, 1 - y), ("x", 1 - x, y), ("y", x, 1 - y)]
    half_z = lax.div(z, 2)
    pair = lambda near: pl.ds(2 * (half_z if near else 1 - half_z), 2)

    def gather_ops(j, name):
        ref = w_in if name == "in" else w_out
        three = ref.at[j, 0:3, x, y, c]
        key = lambda stage, *k: (stage, j, name, *k)

        def z_send():
            mine = ref.at[j, z, x, y, c]
            for k in (1, 2, 3):
                send(None, mine, mine, k, key("z"), three)

        def z_wait():
            arrived(key("z"), three)

        def plane_send(*ks):
            for k in ks:
                piece = ref.at[j, z_of(k), x, y, c]
                for to, _, _ in PLANE:
                    send(None, piece, piece, to, [key("p"), key("p", k)], ref.at[j, 0:3, :, :, c])

        def plane_wait(*ks):
            for k in ks:
                arrived(key("p", k), three)

        def first_send(*ks):
            for k in ks:
                piece = ref.at[j, z_of(k), x, y, c]
                send(None, piece, piece, "xy"[k % 2], [key("1"), key("1", k)], ref.at[j, :, x, y, c])

        def second_send(*ks):
            for k in ks:
                zz = z_of(k)
                arrived(key("1", k), ref.at[j, zz, x, y, c])
                piece = ref.at[j, zz, x, :, c] if k % 2 else ref.at[j, zz, :, y, c]
                send(None, piece, piece, "yx"[k % 2], [key("2"), key("2", k)], ref.at[j, :, x, :, c])

        def second_wait(*ks):
            for k in ks:
                arrived(key("2", k), ref.at[j, z_of(k), x, :, c])

        def core_send(near):
            piece = ref.at[j, pair(near), :, :, c]
            send(None, piece, piece, "c", [key("c"), key("c", near)], ref.at[j, :, :, :, c])

        def core_wait(near):
            arrived(key("c", near), ref.at[j, pair(near), :, :, 1 - c])

        return dict(z=z_send, zw=z_wait, p=plane_send, pw=plane_wait, f=first_send, s=second_send, sw=second_wait,
                    c=core_send, cw=core_wait)

    def pack_z(j):
        mine = pack.at[j, z, x, y, c]
        for k in (1, 2, 3):
            send(None, mine, mine, k, ("pz", j), pack.at[j, 0:3, x, y, c])

    def pack_plane(j):
        arrived(("pz", j), pack.at[j, 0:3, x, y, c])
        piece = pack.at[j, :, x, y, c]
        for to, _, _ in PLANE:
            send(None, piece, piece, to, ("pp", j), pack.at[j, 0:3, :, :, c])

    def pack_core(j):
        arrived(("pp", j), pack.at[j, 0:3, :, :, c])
        piece = pack.at[j, :, :, :, c]
        send(("pc", j), piece, piece, "c")

    def pack_wait(j):
        arrived(("pc", j), pack.at[j, :, :, :, 1 - c])

    def reduce_core(j, a, k, value):
        if j == 0:
            sent(("rc", 1, a))
        for n in range(4):
            even, odd = value[2 * n * HID : (2 * n + 1) * HID], value[(2 * n + 1) * HID : (2 * n + 2) * HID]
            kept[a, k, n // 2, n % 2] = jnp.where(c == 0, even, odd)
            s_core[a, k, n // 2, n % 2] = jnp.where(c == 0, odd, even).astype(bf16)
        send(None, s_core.at[a, k], r_core.at[j, a, k], "c", [("rc", j, a), ("rc", j, a, k)], s_core.at[a])

    def reduce_plane(j, a, k):
        arrived(("rc", j, a, k), r_core.at[j, a, k])
        if j == 0:
            sent(("rp", 1, a))
        for n, (to, xx, yy) in enumerate(PLANE):
            s_plane[a, k, n] = (kept[a, k, xx, yy] + r_core[j, a, k, xx, yy].astype(f32)).astype(bf16)
            send(None, s_plane.at[a, k, n], r_plane.at[j, a, k, n], to, [("rp", j, a), ("rp", j, a, k)], s_plane.at[a])

    def reduce_z(j, a, k):
        s = kept[a, k, x, y] + r_core[j, a, k, x, y].astype(f32)
        arrived(("rp", j, a, k), r_plane.at[j, a, k])
        for n in range(3):
            s = s + r_plane[j, a, k, n].astype(f32)
        if k:
            if j == 0:
                sent(("rz", 1, a))
            s_z[a, k - 1] = s.astype(bf16)
            send(None, s_z.at[a, k - 1], r_z.at[j, a, k - 1], k, ("rz", j, a), s_z.at[a])
        elif a == 0:
            g_w_in[j, :, :D] = s
        else:
            g_w_out[j] = s

    def reduce_end(j, a):
        arrived(("rz", j, a), r_z.at[j, a])
        s = r_z[j, a, 0].astype(f32) + r_z[j, a, 1].astype(f32) + r_z[j, a, 2].astype(f32)
        if a == 0:
            g_w_in[j, :, :D] += s
        else:
            g_w_out[j] += s

    def small_core(j):
        for zz in range(4):
            for i in range(2):
                for l in range(2):
                    f_own[j, zz, i, l] = facc[j, zz, i, l, 1 - c].astype(bf16)
        send(("fc", j), f_own.at[j], f_core.at[j], "c")
        v_send[j] = jnp.concatenate([jnp.sum(vacc[j, i], 0, keepdims=True) for i in range(5)] + [jnp.zeros((3, D), f32)], 0)
        send(("vc", j), v_send.at[j], v_core.at[j], "c")

    def small_plane(j):
        arrived(("fc", j), f_core.at[j])
        for zz in range(4):
            for i in range(2):
                for l in range(2):
                    f_keep[j, i, l, zz] = facc[j, zz, i, l, c] + f_core[j, zz, i, l].astype(f32)
        for n, (to, xx, yy) in enumerate(PLANE):
            f_send[j, n] = f_keep[j, xx, yy].astype(bf16)
            send(None, f_send.at[j, n], f_xy.at[j, n], to, ("fp", j), f_send.at[j])
        arrived(("vc", j), v_core.at[j])
        v_xy[j, x, y] = v_send[j] + v_core[j]
        mine = v_xy.at[j, x, y]
        for to, _, _ in PLANE:
            send(None, mine, mine, to, ("vp", j), v_z.at[j, 0:3])

    def small_z(j):
        s = f_keep[j, x, y]
        arrived(("fp", j), f_xy.at[j])
        for n in range(3):
            s = s + f_xy[j, n].astype(f32)
        f_keep[j, x, y] = s
        for k in (1, 2, 3):
            f_z_send[j, k - 1] = f_keep[j, x, y, z_of(k)].astype(bf16)
            send(None, f_z_send.at[j, k - 1], f_z.at[j, k - 1], k, ("fz", j), f_z.at[j])
        arrived(("vp", j), v_z.at[j, 0:3])
        v_z[j, z] = v_xy[j, 0, 0] + v_xy[j, 0, 1] + v_xy[j, 1, 0] + v_xy[j, 1, 1]
        mine = v_z.at[j, z]
        for k in (1, 2, 3):
            send(None, mine, mine, k, ("vz", j), v_z.at[j, 0:3])

    def small_end(j):
        arrived(("fz", j), f_z.at[j])
        s = f_keep[j, x, y, z] + f_z[j, 0].astype(f32) + f_z[j, 1].astype(f32) + f_z[j, 2].astype(f32)
        for r in range(7):
            g_filters[j : j + 1, r * D : (r + 1) * D] = s[r : r + 1]
        g_w_in[j, :, D:] = jnp.sum(jnp.where(diagonal(), s[7:8, :128], 0.0), 1, keepdims=True)
        arrived(("vz", j), v_z.at[j, 0:3])
        v = v_z[j, 0] + v_z[j, 1] + v_z[j, 2] + v_z[j, 3]
        g_gains[j] = v[0:2]
        for l in range(3):
            g_biases[l, j : j + 1] = v[2 + l : 3 + l]

    def diagonal():
        shape = (HID, 128)
        return lax.broadcasted_iota(jnp.int32, shape, 0) == lax.broadcasted_iota(jnp.int32, shape, 1)

    def load_rows(dst, a, b):
        v = jnp.swapaxes(a[...], 0, 1).astype(dst.dtype)
        for i in range(large):
            dst[i * LP + LP - 16 : (i + 1) * LP, :] = jnp.zeros((16, D), dst.dtype)
            dst[i * LP : i * LP + PL, :] = v[i]
        for i in range(small):
            dst[base + i * PS : base + (i + 1) * PS, :] = b[i].astype(dst.dtype)
        dst[base + small * PS :, :] = jnp.zeros((rows - base - small * PS, D), dst.dtype)

    def store_large(a):
        v = jnp.concatenate([xs[i * LP : i * LP + PL, :][None] for i in range(large)], 0)
        a[...] = jnp.swapaxes(v, 0, 1).astype(a.dtype)

    def store_small(b):
        for i in range(small):
            b[i] = xs[base + i * PS : base + (i + 1) * PS, :].astype(b.dtype)

    def own_pieces():
        for j in range(BLOCKS):
            w_in[j, z, x, y, c] = raw_in[j, :, :D]
            w_out[j, z, x, y, c] = raw_out[j]
            bias = jnp.sum(jnp.where(diagonal(), raw_in[j, :, D:].astype(f32), 0.0), 0, keepdims=True)
            row = raw_filters[j : j + 1, :].astype(f32)
            parts = [row[:, r * D : (r + 1) * D] for r in range(7)]
            parts.append(jnp.concatenate([bias, jnp.zeros((1, D - 128), f32)], 1))
            pack[j, z, x, y, c] = jnp.concatenate(parts, 0).astype(bf16)

    fetches = [pltpu.make_async_copy(a, b, in_sem.at[n]) for n, (a, b) in enumerate(zip(given, held))]
    stores = []

    def fetched(*which):
        for n in which:
            fetches[n].wait()

    def put(n, value):
        d = pltpu.make_async_copy(value, made[n], out_sem.at[n])
        d.start()
        stores.append(d)

    def spread_rows(r):
        return jnp.broadcast_to(r, (r.shape[0], 128))

    def wide_rows(r):
        return jnp.concatenate([r, r, r], -1)

    def mean_row(n_rows, period, scale):
        row = lax.broadcasted_iota(jnp.int32, (n_rows, 1), 0)
        hit = row == 0
        for q in range(1, period):
            hit = hit | (row == q * FS)
        return jnp.where(hit, scale, 0.0).astype(f32)

    def crop_loops(body, which):
        def big(i, _):
            body(pl.ds(aligned(i * LP, 16), LP), i, True)
            return 0
        def little(i, _):
            body(pl.ds(aligned(base + i * SR, 16), SR), i, False)
            return 0
        if "big" in which:
            lax.fori_loop(0, large, big, 0, unroll=True)
        if "small" in which:
            lax.fori_loop(0, groups, little, 0, unroll=True)

    def to_spectrum(j, which=BOTH):
        def body(o, i, big):
            vh, r = standardize(xs[o, :])
            vh1[j, o, :] = vh.astype(bf16)
            r1[j, o, :] = spread_rows(r)
            if big:
                sv_large[j, i] = apply_table(t_fwd[...], vh)
            else:
                sv_small[j, i] = apply_table(t_sfwd[...], vh)
        crop_loops(body, which)

    def unpack_filters(j):
        f = pack[j].reshape(SPEC, D)
        for h in range(2):
            s = mm(t_shrink[...], f[h * FLP : (h + 1) * FLP])
            s = s[:FS] + s[FS:]
            filt_s[j, h * QF : (h + 1) * QF] = jnp.concatenate([s] * Q, 0)
        bias = mm(t_pick[...], f[:, :128]).astype(bf16)
        bias = mm(bias, t_spread[...])
        mine = lax.div(lax.broadcasted_iota(jnp.int32, (32, FF), 1), HID) == lax.broadcasted_iota(jnp.int32, (32, FF), 0)
        bias = jnp.sum(jnp.where(mine, bias, 0.0), 0, keepdims=True)
        for h in range(2):
            b_in[j, h] = bias[:, h * (FF // 2) : (h + 1) * (FF // 2)]

    def spectrum_of(j, i, big):
        sv = sv_large[j, i] if big else sv_small[j, i]
        h = FLP if big else QF
        dc = mean_row(h, 1, float(GL)) if big else mean_row(h, Q, float(GS))
        re = sv[:h] * gains[j, 0:1, :] + dc * biases[0, j : j + 1, :]
        im = sv[h:] * gains[j, 0:1, :]
        f = pack[j].reshape(SPEC, D).astype(f32) if big else filt_s[j]
        return sv, re, im, f[:h], f[h:], dc

    def from_spectrum(j, which=BOTH):
        def body(o, i, big):
            _, re, im, fr, fi, _ = spectrum_of(j, i, big)
            out = jnp.concatenate([re * fr - im * fi, re * fi + im * fr], 0)
            xs[o, :] = xs[o, :] + apply_table(t_inv[...] if big else t_sinv[...], out)
        crop_loops(body, which)

    def tiles(body, start=0, stop=None):
        def one(t, _):
            body(pl.ds(aligned(t * TILE, TILE), TILE))
            return 0
        lax.fori_loop(start, rows // TILE if stop is None else stop, one, 0, unroll=True)

    def expand(j, h, first, start=0, stop=None):
        def body(o):
            if first:
                vh, r = standardize(xs[o, :])
                vh2[j, o, :] = vh
                r2[j, o, :] = spread_rows(r)
                s = (vh * gains[j, 1:2, :] + biases[1, j : j + 1, :]).astype(bf16)
                second[j, o, :] = s
            else:
                s = second[j, o, :]
            pre = mm_nt(s, w_in[j, pl.ds(2 * h, 2)].reshape(FF // 2, D)) + b_in[j, h]
            phi = 0.5 + 0.5 * lax.erf(pre * (1 / math.sqrt(2)))
            active[j, h, o, :] = (pre * phi).astype(bf16)
            slope[j, h, o, :] = (phi + pre * (jnp.exp(-0.5 * pre * pre) * (1 / math.sqrt(2 * math.pi)))).astype(bf16)
        tiles(body, start, stop)

    def contract(j):
        def body(o):
            s = xs[o, :] + biases[2, j : j + 1, :]
            for h in range(2):
                s = s + mm(active[j, h, o, :], w_out[j, 2 * h : 2 * h + 2].reshape(FF // 2, D))
            xs[o, :] = s
        tiles(body)

    def z_offset(k):
        zz = z_of(k)
        return lax.div(zz, 2), pl.ds(aligned(lax.rem(zz, 2) * (FF // 4), 128), FF // 4)

    def back_hidden(j, h, last):
        back = xs if j == 1 else vh2.at[1]

        def body(o):
            w = w_out[j, pl.ds(2 * h, 2)].reshape(FF // 2, D)
            pg = mm_nt(grad_low[o, :], w) * slope[j, h, o, :].astype(f32)
            bacc[j, h] += fold(pg)
            p = pg.astype(bf16)
            slope[j, h, o, :] = p
            sg = mm(p, w_in[j, pl.ds(2 * h, 2)].reshape(FF // 2, D))
            if not last:
                back[o, :] = sg
            else:
                sg = sg + back[o, :]
                vh = vh2[j, o, :]
                vacc[j, 1] += fold(sg * vh)
                vacc[j, 3] += fold(sg)
                g = xs[o, :] if j == 0 else grad_low[o, :].astype(f32)
                xs[o, :] = g + norm_back(vh, wide_rows(r2[j, o, :]), sg * gains[j, 1:2, :])
        tiles(body)

    def weight_in(j, k):
        h, lanes = z_offset(k)
        return mm_tn(slope[j, h, :, lanes], second[j])

    def weight_out(j, k):
        h, lanes = z_offset(k)
        return mm_tn(active[j, h, :, lanes], grad_low[...])

    def back_spectrum(j, which):
        if which == ("small",):
            sacc[...] = jnp.zeros_like(sacc)
        else:
            facc[j] = jnp.zeros(facc.shape[1:], f32)

        def body(o, i, big):
            sv, re, im, fr, fi, dc = spectrum_of(j, i, big)
            h = FLP if big else QF
            sg = apply_table(t_inv_t[...] if big else t_sinv_t[...], xs[o, :])
            gr, gi = sg[:h], sg[h:]
            d_re, d_im = re * gr + im * gi, re * gi - im * gr
            if big:
                facc[j] += jnp.concatenate([d_re, d_im], 0).reshape(4, 2, 2, 2, 8, D)
            else:
                sacc[...] += jnp.concatenate([d_re, d_im], 0)
            n_re, n_im = gr * fr + gi * fi, gi * fr - gr * fi
            vacc[j, 0] += fold(n_re * sv[:h]) + fold(n_im * sv[h:])
            vacc[j, 2] += fold(n_re * dc)
            n = jnp.concatenate([n_re, n_im], 0)
            if big:
                sv_large[j, i] = n
            else:
                sv_small[j, i] = n
        crop_loops(body, which)

    def back_filters(j):
        for h in range(2):
            s = sacc[h * QF : (h + 1) * QF]
            s = s[:FS] + s[FS : 2 * FS] + s[2 * FS : 3 * FS] + s[3 * FS :]
            facc[j, 2 * h : 2 * h + 2] += apply_table(t_shrink_t[...], s).reshape(2, 2, 2, 2, 8, D)
        mine = lax.div(lax.broadcasted_iota(jnp.int32, (32, FF), 1), HID) == lax.broadcasted_iota(jnp.int32, (32, FF), 0)
        row = jnp.sum(jnp.concatenate([bacc[j, 0], bacc[j, 1]], -1), 0, keepdims=True)
        high, low = halves(jnp.where(mine, row, 0.0))
        row = mm(high, t_spread_t[...]) + mm(low, t_spread_t[...])
        high, low = halves(row)
        row = mm(t_pick_t[...], high) + mm(t_pick_t[...], low)
        facc[j] += jnp.concatenate([row, jnp.zeros((SPEC, D - 128), f32)], -1).reshape(4, 2, 2, 2, 8, D)

    def back_rows(j, which=BOTH):
        def body(o, i, big):
            n = sv_large[j, i] if big else sv_small[j, i]
            ng = apply_table(t_fwd_t[...] if big else t_sfwd_t[...], n)
            xs[o, :] = xs[o, :] + norm_back(vh1[j, o, :].astype(f32), wide_rows(r1[j, o, :]), ng * gains[j, 0:1, :])
        crop_loops(body, which)

    i0, o0 = gather_ops(0, "in"), gather_ops(0, "out")
    i1, o1 = gather_ops(1, "in"), gather_ops(1, "out")
    barrier = pltpu.get_barrier_semaphore()
    for to in peer.values():
        pl.semaphore_signal(barrier, 1, device_id=to, device_id_type=MESH_ID)
    for d in fetches:
        d.start()
    fetched(0, 1, 2)
    own_pieces()
    pl.semaphore_wait(barrier, len(peer))

    pack_z(0)
    i0["p"](0)
    i0["z"]()
    bacc[...] = jnp.zeros_like(bacc)
    vacc[...] = jnp.zeros_like(vacc)
    fetched(3, 4, 5, 6)
    load_rows(xs, large_rows, small_rows)
    to_spectrum(0, ("big",))
    pack_plane(0)
    i0["zw"]()
    i0["p"](1, 2, 3)
    o0["z"]()
    o0["p"](0)
    pack_z(1)
    to_spectrum(0, ("small",))
    fetched(*range(7, N_IN))
    load_rows(grad_low, cot_large, cot_small)

    def cot_sum(o):
        vacc[1, 4] += fold(grad_low[o, :].astype(f32))
    tiles(cot_sum)
    pack_core(0)
    i1["z"]()
    pack_wait(0)
    unpack_filters(0)
    i0["pw"](0, 1)
    i0["c"](True)
    from_spectrum(0, ("big",))
    o0["zw"]()
    o0["p"](1, 2, 3)
    i1["f"](0)
    pack_plane(1)
    from_spectrum(0, ("small",))
    i0["pw"](2, 3)
    i0["c"](False)
    i0["cw"](True)
    o1["z"]()
    expand(0, half_z, True)
    i0["cw"](False)
    i1["zw"]()
    i1["f"](1, 2, 3)
    o0["pw"](0, 1)
    o0["c"](True)
    expand(0, 1 - half_z, False)
    o0["pw"](2, 3)
    o0["c"](False)
    i1["s"](0, 1)
    o1["f"](0)
    o0["cw"](True)
    o0["cw"](False)
    contract(0)
    i1["s"](2, 3)
    o1["zw"]()
    o1["f"](1, 2, 3)
    pack_core(1)
    to_spectrum(1)
    pack_wait(1)
    unpack_filters(1)
    i1["sw"](0, 1, 2, 3)
    i1["c"](True)
    i1["c"](False)
    o1["s"](0, 1, 2, 3)
    from_spectrum(1)
    i1["cw"](True)
    expand(1, half_z, True)
    o1["sw"](0, 1, 2, 3)
    o1["c"](True)
    o1["c"](False)
    i1["cw"](False)
    expand(1, 1 - half_z, False)
    o1["cw"](True)
    o1["cw"](False)
    contract(1)
    store_large(large_rows)
    put(0, large_rows)
    store_small(small_rows)
    put(1, small_rows)

    def weights(j, a, k):
        reduce_core(j, a, k, (weight_out if a else weight_in)(j, k))

    def plane(j, a, *ks):
        for k in ks:
            reduce_plane(j, a, k)

    def along_z(j, a, *ks):
        for k in ks:
            reduce_z(j, a, k)

    for k in (2, 3):
        weights(1, 1, k)
    plane(1, 1, 2)
    weights(1, 1, 1)
    plane(1, 1, 3)
    weights(1, 1, 0)
    plane(1, 1, 1)
    back_hidden(1, 1 - half_z, False)
    plane(1, 1, 0)
    for k in (2, 3):
        weights(1, 0, k)
    back_hidden(1, half_z, True)
    plane(1, 0, 2, 3)
    weights(1, 0, 1)
    along_z(1, 1, 2, 3)
    back_spectrum(1, ("small",))
    plane(1, 0, 1)
    weights(1, 0, 0)
    back_spectrum(1, ("big",))
    along_z(1, 1, 1, 0)
    back_filters(1)
    small_core(1)
    back_rows(1, ("small",))
    small_plane(1)
    plane(1, 0, 0)
    back_rows(1, ("big",))

    def low(o):
        g = xs[o, :]
        vacc[0, 4] += fold(g)
        grad_low[o, :] = g.astype(bf16)
    tiles(low)
    along_z(1, 0, 2, 3, 1)
    for k in (2, 3):
        weights(0, 1, k)
    plane(0, 1, 2)
    weights(0, 1, 1)
    plane(0, 1, 3)
    along_z(1, 0, 0)
    small_z(1)
    back_hidden(0, 1 - half_z, False)
    plane(0, 1, 1)
    for k in (2, 3):
        weights(0, 0, k)
    along_z(0, 1, 2)
    back_hidden(0, half_z, True)
    plane(0, 0, 2, 3)
    along_z(0, 1, 3, 1)
    small_end(1)
    reduce_end(1, 1)
    reduce_end(1, 0)
    back_spectrum(0, ("small",))
    back_spectrum(0, ("big",))
    back_filters(0)
    small_core(0)
    weights(0, 0, 1)
    small_plane(0)
    weights(0, 1, 0)
    plane(0, 0, 1)
    weights(0, 0, 0)
    plane(0, 1, 0)
    along_z(0, 0, 2, 3)
    back_rows(0, ("small",))
    store_small(grad_small)
    put(3, grad_small)
    plane(0, 0, 0)
    small_z(0)
    along_z(0, 0, 1)
    back_rows(0, ("big",))
    store_large(grad_large)
    put(2, grad_large)
    along_z(0, 1, 0)
    reduce_end(0, 1)
    put(6, g_w_out)
    along_z(0, 0, 0)
    reduce_end(0, 0)
    small_end(0)
    put(4, g_filters)
    put(5, g_w_in)
    put(7, g_gains)
    put(8, g_biases)
    for d in stores:
        d.wait()
    for key in list(unsent):
        sent(key)
    assert len(sending) == N_SEND and len(receiving) == N_RECEIVE, (len(sending), len(receiving))


def hand_over_kernel(*refs):
    sources, targets, between = refs[:N_OUT], refs[N_OUT : 2 * N_OUT], refs[2 * N_OUT : 3 * N_OUT]
    in_sem, out_sem = refs[3 * N_OUT :]
    ins = [pltpu.make_async_copy(a, b, in_sem.at[n]) for n, (a, b) in enumerate(zip(sources, between))]
    outs = [pltpu.make_async_copy(a, b, out_sem.at[n]) for n, (a, b) in enumerate(zip(between, targets))]
    for d in ins:
        d.start()
    for a, b in zip(ins, outs):
        a.wait()
        b.start()
    for d in outs:
        d.wait()


def fused(large_in, small_in, large_cot, small_cot, filters, w_in, w_out, gains, biases):
    large, small = large_in.shape[0], small_in.shape[0]
    rows = -(-(large * LP + small * PS) // TILE) * TILE
    early, late = [[jnp.asarray(t) for t in part] for part in constant_tables()]
    args = [jnp.swapaxes(w_in, 1, 2), w_out, filters, small_in, jnp.swapaxes(large_in, 0, 1), *early,
            jnp.swapaxes(large_cot, 0, 1), small_cot, gains, jnp.swapaxes(biases, 0, 1), *late]
    V = pltpu.VMEM
    patch_major = (large_in.shape[1], large, D)
    outs = [(patch_major, bf16), (small_in.shape, bf16), (patch_major, f32), (small_in.shape, f32), (filters.shape, f32),
            ((BLOCKS, HID, D + 1), f32), ((BLOCKS, HID, D), f32), (gains.shape, f32), ((3, BLOCKS, D), f32)]
    grid8 = (4, 2, 2, 2)
    scratch = [V(a.shape, a.dtype) for a in args] + [V(shape, dtype) for shape, dtype in outs[2:]] + [
        V((rows, D), f32), V((BLOCKS, rows, D), bf16), V((BLOCKS, rows, 128), f32), V((BLOCKS, rows, D), f32),
        V((BLOCKS, rows, 128), f32), V((BLOCKS, rows, D), bf16), V((BLOCKS, 2, rows, FF // 2), bf16),
        V((BLOCKS, 2, rows, FF // 2), bf16), V((BLOCKS, large, SPEC, D), f32), V((BLOCKS, small // Q, 2 * QF, D), f32),
        V((rows, D), bf16),
        V((BLOCKS, *grid8, HID, D), bf16), V((BLOCKS, *grid8, HID, D), bf16), V((BLOCKS, *grid8, 8, D), bf16),
        V((BLOCKS, 2 * QF, D), f32), V((BLOCKS, 2, 1, FF // 2), f32),
        V((BLOCKS, *grid8, 8, D), f32), V((2 * QF, D), f32), V((BLOCKS, 2, 8, FF // 2), f32), V((BLOCKS, 5, 8, D), f32),
        V((2, 4, 2, 2, HID, D), f32),
        V((2, 4, 2, 2, HID, D), bf16), V((2, 4, 3, HID, D), bf16), V((2, 3, HID, D), bf16),
        V((BLOCKS, 2, 4, 2, 2, HID, D), bf16), V((BLOCKS, 2, 4, 3, HID, D), bf16), V((BLOCKS, 2, 3, HID, D), bf16),
        V((BLOCKS, 4, 2, 2, 8, D), bf16), V((BLOCKS, 4, 2, 2, 8, D), bf16), V((BLOCKS, 2, 2, 4, 8, D), f32),
        V((BLOCKS, 3, 4, 8, D), bf16), V((BLOCKS, 3, 4, 8, D), bf16), V((BLOCKS, 3, 8, D), bf16), V((BLOCKS, 3, 8, D), bf16),
        V((BLOCKS, 8, D), f32), V((BLOCKS, 8, D), f32), V((BLOCKS, 2, 2, 8, D), f32), V((BLOCKS, 4, 8, D), f32),
        pltpu.SemaphoreType.DMA((N_SEND,)), pltpu.SemaphoreType.DMA((N_RECEIVE,)),
        pltpu.SemaphoreType.DMA((N_IN,)), pltpu.SemaphoreType.DMA((N_OUT,)),
    ]
    anywhere = pl.BlockSpec(memory_space=pl.ANY)
    out_shape = [jax.ShapeDtypeStruct(shape, dtype) for shape, dtype in outs]
    result = pl.pallas_call(
        partial(fused_kernel, large, small),
        out_shape=out_shape,
        in_specs=[anywhere] * N_IN,
        out_specs=[anywhere] * N_OUT,
        scratch_shapes=scratch,
        compiler_params=pltpu.CompilerParams(collective_id=0, has_side_effects=True, vmem_limit_bytes=VMEM_BYTES),
        name="gfnet_step",
    )(*args)
    out_large, out_small, grad_large, grad_small, g_filters, g_in, g_out, g_gains, g_biases = pl.pallas_call(
        hand_over_kernel,
        out_shape=out_shape,
        in_specs=[anywhere] * N_OUT,
        out_specs=[anywhere] * N_OUT,
        scratch_shapes=[V(shape, dtype) for shape, dtype in outs] + [pltpu.SemaphoreType.DMA((N_OUT,))] * 2,
        compiler_params=pltpu.CompilerParams(vmem_limit_bytes=VMEM_BYTES),
        name="hand_over",
    )(*result)
    return (jnp.swapaxes(out_large, 0, 1), out_small, jnp.swapaxes(grad_large, 0, 1), grad_small, g_filters,
            jnp.swapaxes(g_in, 1, 2), g_out, g_gains, jnp.swapaxes(g_biases, 0, 1))


def solution(mesh):
    in_specs = (
        P(("wide", "narrow"), None, None),
        P(("wide", "narrow"), None, None),
        P(("wide", "narrow"), None, None),
        P(("wide", "narrow"), None, None),
        P(None, ("wide", "narrow")),
        P(None, None, ("wide", "narrow")),
        P(None, ("wide", "narrow"), None),
        P(),
        P(),
    )
    out_specs = (
        P(("wide", "narrow"), None, None),
        P(("wide", "narrow"), None, None),
        P(("wide", "narrow"), None, None),
        P(("wide", "narrow"), None, None),
        P(None, ("wide", "narrow")),
        P(None, None, ("wide", "narrow")),
        P(None, ("wide", "narrow"), None),
        P(),
        P(),
    )
    body = fused if dict(mesh.shape) == {"wide": 8, "narrow": 4} else per_device
    return jax.shard_map(
        body, mesh=mesh, in_specs=in_specs, out_specs=out_specs, check_vma=False
    )
```

```python
from functools import partial
import math

import jax
import jax.numpy as jnp
import ml_dtypes
import numpy as np
from jax import lax
from jax.experimental import pallas as pl
from jax.experimental.pallas import tpu as pltpu
from jax.sharding import PartitionSpec as P

FF = 1536
GL = 14
GS = 6
BLOCKS = 2
MICRO = 2
PL = 196
FL = 112
FS = 24


precise = lax.Precision.HIGHEST
epsilon = 1e-06


def dft_tables(grid_cells):
    half_count = grid_cells // 2 + 1
    places = jnp.arange(grid_cells * grid_cells, dtype=jnp.int32)
    place_row = places // grid_cells
    place_col = places % grid_cells
    modes = jnp.arange(grid_cells * half_count, dtype=jnp.int32)
    mode_row = modes // half_count
    mode_col = modes % half_count
    phases = (
        mode_row[:, None] * place_row[None, :] + mode_col[:, None] * place_col[None, :]
    ) % grid_cells
    angles = phases.astype(jnp.float32) * (2.0 * math.pi / grid_cells)
    forward_re = jnp.cos(angles) / grid_cells
    forward_im = -jnp.sin(angles) / grid_cells
    doubling = jnp.where((mode_col == 0) | (2 * mode_col == grid_cells), 1.0, 2.0).astype(
        jnp.float32
    )
    inverse_re = jnp.transpose(forward_re * doubling[:, None])
    inverse_im = jnp.transpose(forward_im * doubling[:, None])
    return (forward_re, forward_im, inverse_re, inverse_im)


def linear_map(size_out, size_in):
    rows_out = jnp.arange(size_out, dtype=jnp.int32)
    spans = rows_out * (size_in - 1)
    lower = spans // (size_out - 1)
    fraction = (spans - lower * (size_out - 1)).astype(jnp.float32) / (size_out - 1)
    columns = jnp.arange(size_in, dtype=jnp.int32)
    first = jnp.where(columns[None, :] == lower[:, None], 1.0 - fraction[:, None], 0.0)
    second = jnp.where(columns[None, :] == lower[:, None] + 1, fraction[:, None], 0.0)
    return first + second


def shrink_map():
    along_rows = linear_map(GS, GL)
    along_cols = linear_map(GS // 2 + 1, GL // 2 + 1)
    return (along_rows[:, None, :, None] * along_cols[None, :, None, :]).reshape(FS, FL)


def filter_grid(patches, tables, filt_re, filt_im):
    forward_re, forward_im, inverse_re, inverse_im = tables
    spec_re = jnp.einsum("fp,bpd->bfd", forward_re, patches, precision=precise)
    spec_im = jnp.einsum("fp,bpd->bfd", forward_im, patches, precision=precise)
    out_re = spec_re * filt_re - spec_im * filt_im
    out_im = spec_re * filt_im + spec_im * filt_re
    back_re = jnp.einsum("pf,bfd->bpd", inverse_re, out_re, precision=precise)
    back_im = jnp.einsum("pf,bfd->bpd", inverse_im, out_im, precision=precise)
    return back_re + back_im


def spectral(normed, large_rows, filt_re, filt_im):
    width = normed.shape[-1]
    shrink = shrink_map()
    small_re = jnp.dot(shrink, filt_re, precision=precise, preferred_element_type=jnp.float32)
    small_im = jnp.dot(shrink, filt_im, precision=precise, preferred_element_type=jnp.float32)
    part_large = filter_grid(
        normed[:large_rows].reshape(-1, GL * GL, width), dft_tables(GL), filt_re, filt_im
    )
    part_small = filter_grid(
        normed[large_rows:].reshape(-1, GS * GS, width), dft_tables(GS), small_re, small_im
    )
    return jnp.concatenate([part_large.reshape(-1, width), part_small.reshape(-1, width)], 0)


def layer_norm(stream, gain, shift):
    centre = stream - jnp.mean(stream, axis=-1, keepdims=True)
    spread = jnp.mean(centre * centre, axis=-1, keepdims=True)
    return centre * lax.rsqrt(spread + epsilon) * gain + shift


def per_device(large_in, small_in, large_cot, small_cot, filters, w_in, w_out, gains, biases):
    width = large_in.shape[-1]
    micro_large = large_in.shape[0] // MICRO
    micro_small = small_in.shape[0] // MICRO
    large_rows = micro_large * PL
    exact_gelu = partial(jax.nn.gelu, approximate=False)

    def fetch(layer_index, forward):
        if forward:
            return (
                lax.all_gather(filters[layer_index], ("wide", "narrow"), axis=0, tiled=True),
                lax.all_gather(w_in[layer_index], ("wide", "narrow"), axis=1, tiled=True),
                lax.all_gather(w_out[layer_index], ("wide", "narrow"), axis=0, tiled=True),
            )
        return (
            lax.all_gather(filters[layer_index], ("wide", "narrow"), axis=0, tiled=True),
            lax.all_gather(w_in[layer_index], ("wide", "narrow"), axis=1, tiled=True),
            lax.all_gather(w_out[layer_index], ("wide", "narrow"), axis=0, tiled=True),
        )

    def branch_first(stream, gain, shift, filt_re, filt_im):
        return spectral(layer_norm(stream, gain, shift), large_rows, filt_re, filt_im)

    acc_filter = [jnp.zeros((2, FL, width), jnp.float32) for layer_index in range(BLOCKS)]
    acc_in = [jnp.zeros((width, FF), jnp.float32) for layer_index in range(BLOCKS)]
    acc_in_bias = [jnp.zeros((FF,), jnp.float32) for layer_index in range(BLOCKS)]
    acc_out = [jnp.zeros((FF, width), jnp.float32) for layer_index in range(BLOCKS)]
    acc_gain = [jnp.zeros((2, width), jnp.float32) for layer_index in range(BLOCKS)]
    acc_shift = [jnp.zeros((3, width), jnp.float32) for layer_index in range(BLOCKS)]
    outs_large, outs_small, grads_large, grads_small = ([], [], [], [])
    for micro_step in range(MICRO):
        large_part = large_in[micro_step * micro_large : (micro_step + 1) * micro_large]
        small_part = small_in[micro_step * micro_small : (micro_step + 1) * micro_small]
        stream = jnp.concatenate(
            [large_part.reshape(-1, width), small_part.reshape(-1, width)], 0
        ).astype(jnp.float32)
        saved = []
        for layer_index in range(BLOCKS):
            filt_full, in_full, out_full = fetch(layer_index, True)
            halves = filt_full.reshape(2, FL, width).astype(jnp.float32)
            mixed = stream + branch_first(
                stream, gains[layer_index, 0], biases[layer_index, 0], halves[0], halves[1]
            )
            second = layer_norm(mixed, gains[layer_index, 1], biases[layer_index, 1]).astype(
                jnp.bfloat16
            )
            pre_act = jnp.dot(
                second, in_full[:width], preferred_element_type=jnp.float32
            ) + in_full[width].astype(jnp.float32)
            active = exact_gelu(pre_act).astype(jnp.bfloat16)
            saved.append((stream, mixed, second, pre_act))
            stream = (
                mixed
                + jnp.dot(active, out_full, preferred_element_type=jnp.float32)
                + biases[layer_index, 2]
            )
        outs_large.append(stream[:large_rows].reshape(large_part.shape).astype(jnp.bfloat16))
        outs_small.append(stream[large_rows:].reshape(small_part.shape).astype(jnp.bfloat16))
        large_back = large_cot[micro_step * micro_large : (micro_step + 1) * micro_large]
        small_back = small_cot[micro_step * micro_small : (micro_step + 1) * micro_small]
        grad = jnp.concatenate(
            [large_back.reshape(-1, width), small_back.reshape(-1, width)], 0
        ).astype(jnp.float32)
        for layer_index in reversed(range(BLOCKS)):
            block_input, mixed, second, pre_act = saved[layer_index]
            filt_full, in_full, out_full = fetch(layer_index, False)
            halves = filt_full.reshape(2, FL, width).astype(jnp.float32)
            grad_low = grad.astype(jnp.bfloat16)
            active, gelu_back = jax.vjp(exact_gelu, pre_act)
            active = active.astype(jnp.bfloat16)
            acc_out[layer_index] = acc_out[layer_index] + jnp.einsum(
                "tf,td->fd", active, grad_low, preferred_element_type=jnp.float32
            )
            bias_out_grad = jnp.sum(grad, axis=0)
            active_grad = jnp.einsum(
                "td,fd->tf", grad_low, out_full, preferred_element_type=jnp.float32
            )
            pre_grad = gelu_back(active_grad)[0]
            pre_low = pre_grad.astype(jnp.bfloat16)
            acc_in[layer_index] = acc_in[layer_index] + jnp.einsum(
                "td,tf->df", second, pre_low, preferred_element_type=jnp.float32
            )
            acc_in_bias[layer_index] = acc_in_bias[layer_index] + jnp.sum(pre_grad, axis=0)
            second_grad = jnp.einsum(
                "tf,df->td", pre_low, in_full[:width], preferred_element_type=jnp.float32
            )
            unused, norm_back = jax.vjp(
                layer_norm, mixed, gains[layer_index, 1], biases[layer_index, 1]
            )
            mixed_part, gain_two, shift_two = norm_back(second_grad)
            mixed_grad = grad + mixed_part
            unused, first_back = jax.vjp(
                branch_first,
                block_input,
                gains[layer_index, 0],
                biases[layer_index, 0],
                halves[0],
                halves[1],
            )
            input_part, gain_one, shift_one, filt_re_grad, filt_im_grad = first_back(mixed_grad)
            grad = mixed_grad + input_part
            acc_filter[layer_index] = acc_filter[layer_index] + jnp.stack(
                [filt_re_grad, filt_im_grad], 0
            )
            acc_gain[layer_index] = acc_gain[layer_index] + jnp.stack([gain_one, gain_two], 0)
            acc_shift[layer_index] = acc_shift[layer_index] + jnp.stack(
                [shift_one, shift_two, bias_out_grad], 0
            )
        grads_large.append(grad[:large_rows].reshape(large_part.shape))
        grads_small.append(grad[large_rows:].reshape(small_part.shape))
    filter_shards, in_shards, out_shards = ([], [], [])
    for layer_index in range(BLOCKS):
        in_whole = jnp.concatenate([acc_in[layer_index], acc_in_bias[layer_index][None, :]], 0)
        filter_piece, in_piece, out_piece = (
            lax.psum_scatter(
                acc_filter[layer_index].reshape(-1),
                ("wide", "narrow"),
                scatter_dimension=0,
                tiled=True,
            ),
            lax.psum_scatter(in_whole, ("wide", "narrow"), scatter_dimension=1, tiled=True),
            lax.psum_scatter(
                acc_out[layer_index], ("wide", "narrow"), scatter_dimension=0, tiled=True
            ),
        )
        filter_shards.append(filter_piece)
        in_shards.append(in_piece)
        out_shards.append(out_piece)
    gain_total, shift_total = lax.psum(
        (jnp.stack(acc_gain, 0), jnp.stack(acc_shift, 0)), ("wide", "narrow")
    )
    return (
        jnp.concatenate(outs_large, 0),
        jnp.concatenate(outs_small, 0),
        jnp.concatenate(grads_large, 0),
        jnp.concatenate(grads_small, 0),
        jnp.stack(filter_shards, 0),
        jnp.stack(in_shards, 0),
        jnp.stack(out_shards, 0),
        gain_total,
        shift_total,
    )


MESH_ID = pl.DeviceIdType.MESH
bf16, f32 = jnp.bfloat16, jnp.float32
D, PS, EPS = 384, 36, 1e-6
LP = 208
Q = 4
SR = Q * PS
TILE = 256
BOTH = ("big", "small")
HID = 48
FLP = 128
SPEC = 2 * FLP
QF = Q * FS


def dft_arrays(n):
    half = n // 2 + 1
    places, modes = np.arange(n * n), np.arange(n * half)
    phase = ((modes // half)[:, None] * (places // n)[None] + (modes % half)[:, None] * (places % n)[None]) % n
    theta = phase * (2 * math.pi / n)
    fwd_re, fwd_im = np.cos(theta) / n, -np.sin(theta) / n
    weight = np.where((modes % half == 0) | (2 * (modes % half) == n), 1.0, 2.0)
    return fwd_re, fwd_im, fwd_re * weight[:, None], fwd_im * weight[:, None]


def interpolation(rows, cols):
    span = np.arange(rows) * (cols - 1)
    low = span // (rows - 1)
    part = (span - low * (rows - 1)) / (rows - 1)
    at = np.arange(cols)[None]
    return np.where(at == low[:, None], 1 - part[:, None], 0.0) + np.where(at == low[:, None] + 1, part[:, None], 0.0)


def two_terms(table):
    table = np.asarray(table, np.float32)
    high = table.astype(ml_dtypes.bfloat16)
    low = (table - high.astype(np.float32)).astype(ml_dtypes.bfloat16)
    return np.concatenate([high, low], 0)


def constant_tables():
    pos = np.arange(FL) // 7 * 8 + np.arange(FL) % 7
    rows = np.concatenate([pos, FLP + pos])
    fr, fi, ir, ii = dft_arrays(GL)
    fwd, inv = np.zeros((SPEC, LP)), np.zeros((SPEC, LP))
    fwd[rows, :PL], inv[rows, :PL] = np.concatenate([fr, fi]), np.concatenate([ir, ii])
    fr, fi, ir, ii = dft_arrays(GS)
    sfwd, sinv = np.zeros((2 * QF, SR)), np.zeros((2 * QF, SR))
    for q in range(Q):
        at = slice(q * PS, (q + 1) * PS)
        for half, a, b in ((0, fr, ir), (1, fi, ii)):
            to = slice(half * QF + q * FS, half * QF + (q + 1) * FS)
            sfwd[to, at], sinv[to, at] = a, b
    shrink = np.zeros((FS, FLP))
    shrink[:, pos] = (
        interpolation(GS, GL)[:, None, :, None] * interpolation(GS // 2 + 1, GL // 2 + 1)[None, :, None, :]
    ).reshape(FS, FL)
    piece = np.arange(32)
    pick = np.zeros((64, SPEC))
    pick[piece % 8 * 8 + piece // 8, 8 * piece + 7] = 1
    return [two_terms(t) for t in (fwd, sfwd)], [
        two_terms(shrink), pick.astype(ml_dtypes.bfloat16), two_terms(inv.T), two_terms(sinv.T), two_terms(shrink.T)]


def mm(a, b):
    return lax.dot_general(a, b, (((1,), (0,)), ((), ())), preferred_element_type=f32)


def mm_nt(a, b):
    return lax.dot_general(a, b, (((1,), (1,)), ((), ())), preferred_element_type=f32)


def mm_tn(a, b):
    return lax.dot_general(a, b, (((0,), (0,)), ((), ())), preferred_element_type=f32)


def halves(v):
    high = v.astype(bf16)
    return high, (v - high.astype(f32)).astype(bf16)


def apply_table(table, v):
    rows = table.shape[0] // 2
    high, low = halves(v)
    both = mm(table, high)
    return both[:rows] + both[rows:] + mm(table[:rows], low)


def standardize(v):
    centre = v - jnp.sum(v, -1, keepdims=True) * (1.0 / D)
    r = lax.rsqrt(jnp.sum(centre * centre, -1, keepdims=True) * (1.0 / D) + EPS)
    return centre * r, r


def norm_back(vh, r, q):
    mean_q = jnp.sum(q, -1, keepdims=True) * (1.0 / D)
    mean_qv = jnp.sum(q * vh, -1, keepdims=True) * (1.0 / D)
    return r * (q - mean_q - vh * mean_qv)


def fold(v):
    return jnp.sum(v.reshape(v.shape[0] // 8, 8, v.shape[1]), 0)


def aligned(v, m):
    return v if isinstance(v, int) else pl.multiple_of(v, m)


N_SEND, N_RECEIVE = 44, 90
VMEM_BYTES = 63 << 20


N_IN, N_OUT = 16, 9


def fused_kernel(large, small, *refs):
    given, made, refs = refs[:N_IN], refs[N_IN : N_IN + N_OUT], refs[N_IN + N_OUT :]
    held, refs = refs[:N_IN], refs[N_IN:]
    (raw_in, raw_out, raw_filters, small_rows, large_rows, t_fwd, t_sfwd, cot_large, cot_small, gains, biases,
     t_shrink, t_pick, t_inv, t_sinv, t_shrink_t) = held
    (grad_large, grad_small, g_filters, g_w_in, g_w_out, g_gains, g_biases,
     xs, vh1, r1, vh2, r2, second, active, slope, sv_large, sv_small, grad_low,
     w_in, w_out, pack, filt_s, b_in, facc, sacc, gacc, bacc, vacc,
     kept, s_core, s_plane, s_z, r_core, r_plane, r_z,
     f_own, f_core, f_keep, f_send, f_xy, f_z_send, f_z, v_send, v_core, v_xy, v_z,
     send_sem, recv_sem, in_sem, out_sem) = refs
    rows = xs.shape[0]
    groups = small // Q
    base = large * LP
    wide, narrow = lax.axis_index("wide"), lax.axis_index("narrow")
    z, x, y, c = lax.div(wide, 2), lax.rem(wide, 2), lax.div(narrow, 2), lax.rem(narrow, 2)
    other = {"x": 1 - x, "y": 1 - y, "c": 1 - c}
    at = lambda zz, xx, yy, cc: (zz * 2 + xx, yy * 2 + cc)
    z_pair = {0: z, 1: z + 1 - 2 * lax.rem(z, 2), 2: lax.rem(z + 2, 4), 3: 3 - z}
    z_of = lambda k: z_pair[k]
    peer = {"x": at(z, 1 - x, y, c), "y": at(z, x, 1 - y, c), "xy": at(z, 1 - x, 1 - y, c), "c": at(z, x, y, 1 - c)}
    for k in (1, 2, 3):
        peer[k] = at(z_of(k), x, y, c)

    sending, receiving, unsent = {}, {}, {}

    def send(key, src, dst, to, group=None, view=None):
        group = group or key
        out, back = group if isinstance(group, list) else (group, group)
        pltpu.make_async_remote_copy(
            src_ref=src, dst_ref=dst, send_sem=send_sem.at[sending.setdefault(out, len(sending))],
            recv_sem=recv_sem.at[receiving.setdefault(back, len(receiving))],
            device_id=peer[to], device_id_type=MESH_ID).start()
        unsent[out] = src if view is None else view

    def arrived(key, view):
        sem = recv_sem.at[receiving.setdefault(key, len(receiving))]
        pltpu.make_async_copy(view, view, sem).wait()

    def sent(key):
        if key in unsent:
            view = unsent.pop(key)
            pltpu.make_async_copy(view, view, send_sem.at[sending[key]]).wait()

    PLANE = [("xy", 1 - x, 1 - y), ("x", 1 - x, y), ("y", x, 1 - y)]
    half_z = lax.div(z, 2)
    pair = lambda near: pl.ds(2 * (half_z if near else 1 - half_z), 2)

    def gather_ops(j, name):
        ref = w_in if name == "in" else w_out
        three = ref.at[j, 0:3, x, y, c]
        key = lambda stage, *k: (stage, j, name, *k)

        def z_send():
            mine = ref.at[j, z, x, y, c]
            for k in (1, 2, 3):
                send(None, mine, mine, k, key("z"), three)

        def z_wait():
            arrived(key("z"), three)

        def plane_send(*ks):
            for k in ks:
                piece = ref.at[j, z_of(k), x, y, c]
                for to, _, _ in PLANE:
                    send(None, piece, piece, to, [key("p"), key("p", k)], ref.at[j, 0:3, :, :, c])

        def plane_wait(*ks):
            for k in ks:
                arrived(key("p", k), three)

        def first_send(*ks):
            for k in ks:
                piece = ref.at[j, z_of(k), x, y, c]
                send(None, piece, piece, "xy"[k % 2], [key("1"), key("1", k)], ref.at[j, :, x, y, c])

        def second_send(*ks):
            for k in ks:
                zz = z_of(k)
                arrived(key("1", k), ref.at[j, zz, x, y, c])
                piece = ref.at[j, zz, x, :, c] if k % 2 else ref.at[j, zz, :, y, c]
                send(None, piece, piece, "yx"[k % 2], [key("2"), key("2", k)], ref.at[j, :, x, :, c])

        def second_wait(*ks):
            for k in ks:
                arrived(key("2", k), ref.at[j, z_of(k), x, :, c])

        def core_send(near):
            piece = ref.at[j, pair(near), :, :, c]
            send(None, piece, piece, "c", [key("c"), key("c", near)], ref.at[j, :, :, :, c])

        def core_wait(near):
            arrived(key("c", near), ref.at[j, pair(near), :, :, 1 - c])

        return dict(z=z_send, zw=z_wait, p=plane_send, pw=plane_wait, f=first_send, s=second_send, sw=second_wait,
                    c=core_send, cw=core_wait)

    def pack_z(j):
        mine = pack.at[j, z, x, y, c]
        for k in (1, 2, 3):
            send(None, mine, mine, k, ("pz", j), pack.at[j, 0:3, x, y, c])

    def pack_plane(j):
        arrived(("pz", j), pack.at[j, 0:3, x, y, c])
        piece = pack.at[j, :, x, y, c]
        for to, _, _ in PLANE:
            send(None, piece, piece, to, ("pp", j), pack.at[j, 0:3, :, :, c])

    def pack_core(j):
        arrived(("pp", j), pack.at[j, 0:3, :, :, c])
        piece = pack.at[j, :, :, :, c]
        send(("pc", j), piece, piece, "c")

    def pack_wait(j):
        arrived(("pc", j), pack.at[j, :, :, :, 1 - c])

    def reduce_core(j, a, k, value):
        if j == 0:
            sent(("rc", 1, a))
        for n in range(4):
            even, odd = value[2 * n * HID : (2 * n + 1) * HID], value[(2 * n + 1) * HID : (2 * n + 2) * HID]
            kept[a, k, n // 2, n % 2] = jnp.where(c == 0, even, odd)
            s_core[a, k, n // 2, n % 2] = jnp.where(c == 0, odd, even).astype(bf16)
        send(None, s_core.at[a, k], r_core.at[j, a, k], "c", [("rc", j, a), ("rc", j, a, k)], s_core.at[a])

    def reduce_plane(j, a, k):
        arrived(("rc", j, a, k), r_core.at[j, a, k])
        if j == 0:
            sent(("rp", 1, a))
        for n, (to, xx, yy) in enumerate(PLANE):
            s_plane[a, k, n] = (kept[a, k, xx, yy] + r_core[j, a, k, xx, yy].astype(f32)).astype(bf16)
            send(None, s_plane.at[a, k, n], r_plane.at[j, a, k, n], to, [("rp", j, a), ("rp", j, a, k)], s_plane.at[a])

    def reduce_z(j, a, k):
        s = kept[a, k, x, y] + r_core[j, a, k, x, y].astype(f32)
        arrived(("rp", j, a, k), r_plane.at[j, a, k])
        for n in range(3):
            s = s + r_plane[j, a, k, n].astype(f32)
        if k:
            if j == 0:
                sent(("rz", 1, a))
            s_z[a, k - 1] = s.astype(bf16)
            send(None, s_z.at[a, k - 1], r_z.at[j, a, k - 1], k, ("rz", j, a), s_z.at[a])
        elif a == 0:
            g_w_in[j, :, :D] = s
        else:
            g_w_out[j] = s

    def reduce_end(j, a):
        arrived(("rz", j, a), r_z.at[j, a])
        s = r_z[j, a, 0].astype(f32) + r_z[j, a, 1].astype(f32) + r_z[j, a, 2].astype(f32)
        if a == 0:
            g_w_in[j, :, :D] += s
        else:
            g_w_out[j] += s

    def small_core(j):
        for zz in range(4):
            for i in range(2):
                for l in range(2):
                    f_own[j, zz, i, l] = facc[j, zz, i, l, 1 - c].astype(bf16)
        send(("fc", j), f_own.at[j], f_core.at[j], "c")
        v_send[j] = jnp.concatenate([jnp.sum(vacc[j, i], 0, keepdims=True) for i in range(5)] + [jnp.zeros((3, D), f32)], 0)
        send(("vc", j), v_send.at[j], v_core.at[j], "c")

    def small_plane(j):
        arrived(("fc", j), f_core.at[j])
        for zz in range(4):
            for i in range(2):
                for l in range(2):
                    f_keep[j, i, l, zz] = facc[j, zz, i, l, c] + f_core[j, zz, i, l].astype(f32)
        for n, (to, xx, yy) in enumerate(PLANE):
            f_send[j, n] = f_keep[j, xx, yy].astype(bf16)
            send(None, f_send.at[j, n], f_xy.at[j, n], to, ("fp", j), f_send.at[j])
        arrived(("vc", j), v_core.at[j])
        v_xy[j, x, y] = v_send[j] + v_core[j]
        mine = v_xy.at[j, x, y]
        for to, _, _ in PLANE:
            send(None, mine, mine, to, ("vp", j), v_z.at[j, 0:3])

    def small_z(j):
        s = f_keep[j, x, y]
        arrived(("fp", j), f_xy.at[j])
        for n in range(3):
            s = s + f_xy[j, n].astype(f32)
        f_keep[j, x, y] = s
        for k in (1, 2, 3):
            f_z_send[j, k - 1] = f_keep[j, x, y, z_of(k)].astype(bf16)
            send(None, f_z_send.at[j, k - 1], f_z.at[j, k - 1], k, ("fz", j), f_z.at[j])
        arrived(("vp", j), v_z.at[j, 0:3])
        v_z[j, z] = v_xy[j, 0, 0] + v_xy[j, 0, 1] + v_xy[j, 1, 0] + v_xy[j, 1, 1]
        mine = v_z.at[j, z]
        for k in (1, 2, 3):
            send(None, mine, mine, k, ("vz", j), v_z.at[j, 0:3])

    def small_end(j):
        arrived(("fz", j), f_z.at[j])
        s = f_keep[j, x, y, z] + f_z[j, 0].astype(f32) + f_z[j, 1].astype(f32) + f_z[j, 2].astype(f32)
        for r in range(7):
            g_filters[j : j + 1, r * D : (r + 1) * D] = s[r : r + 1]
        g_w_in[j, :, D:] = jnp.sum(jnp.where(diagonal(), s[7:8, :128], 0.0), 1, keepdims=True)
        arrived(("vz", j), v_z.at[j, 0:3])
        v = v_z[j, 0] + v_z[j, 1] + v_z[j, 2] + v_z[j, 3]
        g_gains[j] = v[0:2]
        for l in range(3):
            g_biases[l, j : j + 1] = v[2 + l : 3 + l]

    def diagonal():
        shape = (HID, 128)
        return lax.broadcasted_iota(jnp.int32, shape, 0) == lax.broadcasted_iota(jnp.int32, shape, 1)

    def load_rows(dst, a, b):
        v = jnp.swapaxes(a[...], 0, 1).astype(dst.dtype)
        for i in range(large):
            dst[i * LP + LP - 16 : (i + 1) * LP, :] = jnp.zeros((16, D), dst.dtype)
            dst[i * LP : i * LP + PL, :] = v[i]
        for i in range(small):
            dst[base + i * PS : base + (i + 1) * PS, :] = b[i].astype(dst.dtype)
        dst[base + small * PS :, :] = jnp.zeros((rows - base - small * PS, D), dst.dtype)

    def store_large(a):
        v = jnp.concatenate([xs[i * LP : i * LP + PL, :][None] for i in range(large)], 0)
        a[...] = jnp.swapaxes(v, 0, 1).astype(a.dtype)

    def store_small(b):
        for i in range(small):
            b[i] = xs[base + i * PS : base + (i + 1) * PS, :].astype(b.dtype)

    def own_pieces():
        for j in range(BLOCKS):
            w_in[j, z, x, y, c] = raw_in[j, :, :D]
            w_out[j, z, x, y, c] = raw_out[j]
            bias = jnp.sum(jnp.where(diagonal(), raw_in[j, :, D:].astype(f32), 0.0), 0, keepdims=True)
            row = raw_filters[j : j + 1, :].astype(f32)
            parts = [row[:, r * D : (r + 1) * D] for r in range(7)]
            parts.append(jnp.concatenate([bias, jnp.zeros((1, D - 128), f32)], 1))
            pack[j, z, x, y, c] = jnp.concatenate(parts, 0).astype(bf16)

    fetches = [pltpu.make_async_copy(a, b, in_sem.at[n]) for n, (a, b) in enumerate(zip(given, held))]
    stores = []

    def fetched(*which):
        for n in which:
            fetches[n].wait()

    def put(n, value):
        d = pltpu.make_async_copy(value, made[n], out_sem.at[n])
        d.start()
        stores.append(d)

    def spread_rows(r):
        return jnp.broadcast_to(r, (r.shape[0], 128))

    def wide_rows(r):
        return jnp.concatenate([r, r, r], -1)

    def first_row(scale):
        return jnp.where(lax.broadcasted_iota(jnp.int32, (8, 1), 0) == 0, float(scale), 0.0)

    def column_weights(big):
        row = lax.broadcasted_iota(jnp.int32, (FLP if big else QF, 1), 0)
        column = lax.rem(lax.rem(row, 8) + 16 - lax.div(row, 8), 8) if big else lax.rem(row, 4)
        return jnp.where((column == 0) | (column == (GL if big else GS) // 2), 1.0, 2.0)

    def crop_loops(body, which):
        def big(i, _):
            body(pl.ds(aligned(i * LP, 16), LP), i, True)
            return 0
        def little(i, _):
            body(pl.ds(aligned(base + i * SR, 16), SR), i, False)
            return 0
        if "big" in which:
            lax.fori_loop(0, large, big, 0, unroll=True)
        if "small" in which:
            lax.fori_loop(0, groups, little, 0, unroll=True)

    def to_spectrum(j, which=BOTH):
        def body(o, i, big):
            vh, r = standardize(xs[o, :])
            vh1[j, o, :] = vh.astype(bf16)
            r1[j, o, :] = spread_rows(r)
            if big:
                sv_large[j, i] = apply_table(t_fwd[...], vh)
            else:
                sv_small[j, i] = apply_table(t_sfwd[...], vh)
        crop_loops(body, which)

    def unpack_filters(j):
        f = pack[j].reshape(SPEC, D)
        for h in range(2):
            s = mm(t_shrink[...], f[h * FLP : (h + 1) * FLP])
            s = s[:FS] + s[FS:]
            filt_s[j, h * QF : (h + 1) * QF] = jnp.concatenate([s] * Q, 0)
        bias = mm(t_pick[...], f[:, :128])
        bias = jnp.where(lax.broadcasted_iota(jnp.int32, (64, 128), 1) < HID, bias, 0.0)
        total = jnp.zeros((8, D), f32)
        for i in range(8):
            part = jnp.concatenate([bias[8 * i : 8 * i + 8], jnp.zeros((8, D - 128), f32)], 1)
            total = total + (pltpu.roll(part, HID * i, 1) if i else part)
        for h in range(2):
            b_in[j, h] = jnp.concatenate([total[2 * h : 2 * h + 1], total[2 * h + 1 : 2 * h + 2]], 1)

    def spectrum_of(j, i, big):
        sv = sv_large[j, i] if big else sv_small[j, i]
        h, period = (FLP, FLP) if big else (QF, FS)
        re, im = sv[:h] * gains[j, 0:1, :], sv[h:] * gains[j, 0:1, :]
        mean = first_row(GL if big else GS) * biases[0, j : j + 1, :]
        parts = []
        for n in range(0, h, period):
            parts += [re[n : n + 8] + mean, re[n + 8 : n + period]]
        f = pack[j].reshape(SPEC, D).astype(f32) if big else filt_s[j]
        return sv, jnp.concatenate(parts, 0), im, f[:h], f[h:]

    def from_spectrum(j, which=BOTH):
        def body(o, i, big):
            _, re, im, fr, fi = spectrum_of(j, i, big)
            out = jnp.concatenate([re * fr - im * fi, re * fi + im * fr], 0)
            xs[o, :] = xs[o, :] + apply_table(t_inv[...] if big else t_sinv[...], out)
        crop_loops(body, which)

    def tiles(body, start=0, stop=None):
        def one(t, _):
            body(pl.ds(aligned(t * TILE, TILE), TILE))
            return 0
        lax.fori_loop(start, rows // TILE if stop is None else stop, one, 0, unroll=True)

    def expand(j, h, first, start=0, stop=None):
        def body(o):
            if first:
                vh, r = standardize(xs[o, :])
                vh2[j, o, :] = vh
                r2[j, o, :] = spread_rows(r)
                s = (vh * gains[j, 1:2, :] + biases[1, j : j + 1, :]).astype(bf16)
                second[j, o, :] = s
            else:
                s = second[j, o, :]
            pre = mm_nt(s, w_in[j, pl.ds(2 * h, 2)].reshape(FF // 2, D)) + b_in[j, h]
            phi = 0.5 + 0.5 * lax.erf(pre * (1 / math.sqrt(2)))
            active[j, h, o, :] = (pre * phi).astype(bf16)
            slope[j, h, o, :] = (phi + pre * (jnp.exp(-0.5 * pre * pre) * (1 / math.sqrt(2 * math.pi)))).astype(bf16)
        tiles(body, start, stop)

    def contract(j):
        def body(o):
            s = xs[o, :] + biases[2, j : j + 1, :]
            for h in range(2):
                s = s + mm(active[j, h, o, :], w_out[j, 2 * h : 2 * h + 2].reshape(FF // 2, D))
            xs[o, :] = s
        tiles(body)

    def z_offset(k):
        zz = z_of(k)
        return lax.div(zz, 2), pl.ds(aligned(lax.rem(zz, 2) * (FF // 4), 128), FF // 4)

    def back_hidden(j, h, last):
        back = xs if j == 1 else vh2.at[1]

        def body(o):
            w = w_out[j, pl.ds(2 * h, 2)].reshape(FF // 2, D)
            pg = mm_nt(grad_low[o, :], w) * slope[j, h, o, :].astype(f32)
            bacc[j, h] += fold(pg)
            p = pg.astype(bf16)
            slope[j, h, o, :] = p
            sg = mm(p, w_in[j, pl.ds(2 * h, 2)].reshape(FF // 2, D))
            if not last:
                back[o, :] = sg
            else:
                sg = sg + back[o, :]
                vh = vh2[j, o, :]
                vacc[j, 1] += fold(sg * vh)
                vacc[j, 3] += fold(sg)
                g = xs[o, :] if j == 0 else grad_low[o, :].astype(f32)
                xs[o, :] = g + norm_back(vh, wide_rows(r2[j, o, :]), sg * gains[j, 1:2, :])
        tiles(body)

    def weight_in(j, k):
        h, lanes = z_offset(k)
        return mm_tn(slope[j, h, :, lanes], second[j])

    def weight_out(j, k):
        h, lanes = z_offset(k)
        return mm_tn(active[j, h, :, lanes], grad_low[...])

    def back_spectrum(j, which):
        if which == ("small",):
            sacc[...] = jnp.zeros_like(sacc)
            gacc[...] = jnp.zeros_like(gacc)
        else:
            facc[j] = jnp.zeros(facc.shape[1:], f32)

        def body(o, i, big):
            sv, re, im, fr, fi = spectrum_of(j, i, big)
            h, period = (FLP, FLP) if big else (QF, FS)
            sg = apply_table(t_fwd[...] if big else t_sfwd[...], xs[o, :])
            gr, gi = sg[:h], sg[h:]
            d_re, d_im = re * gr + im * gi, re * gi - im * gr
            if big:
                facc[j] += jnp.concatenate([d_re, d_im], 0).reshape(4, 2, 2, 2, 8, D)
            else:
                sacc[...] += jnp.concatenate([d_re, d_im], 0)
            n_re, n_im = gr * fr + gi * fi, gi * fr - gr * fi
            first = 0 if big else FLP
            gacc[first : first + h] += n_re * sv[:h] + n_im * sv[h:]
            mean = n_re[:8]
            for n in range(period, h, period):
                mean = mean + n_re[n : n + 8]
            vacc[j, 2] += mean * first_row(GL if big else GS)
            n = jnp.concatenate([n_re, n_im], 0)
            if big:
                sv_large[j, i] = n
            else:
                sv_small[j, i] = n
        crop_loops(body, which)

    def back_filters(j):
        w, ws = column_weights(True), column_weights(False)
        vacc[j, 0] = fold(gacc[:FLP] * w) + fold(gacc[FLP:] * ws)
        for h in range(2):
            s = sacc[h * QF : (h + 1) * QF] * ws
            s = s[:FS] + s[FS : 2 * FS] + s[2 * FS : 3 * FS] + s[3 * FS :]
            total = facc[j, 2 * h : 2 * h + 2].reshape(FLP, D) * w + apply_table(t_shrink_t[...], s)
            facc[j, 2 * h : 2 * h + 2] = total.reshape(2, 2, 2, 2, 8, D)
        row = [jnp.sum(bacc[j, h], 0, keepdims=True) for h in range(2)]
        row = jnp.concatenate([row[0][:, :D], row[0][:, D:], row[1][:, :D], row[1][:, D:], jnp.zeros((4, D), f32)], 0)
        mine = lax.broadcasted_iota(jnp.int32, (8, 128), 1) < HID
        for i in range(8):
            part = jnp.where(mine, (pltpu.roll(row, D - HID * i, 1) if i else row)[:, :128], 0.0)
            for g in range(4):
                facc[j, g, i // 4, i // 2 % 2, i % 2, 7:8, :128] = part[g : g + 1]

    def back_rows(j, which=BOTH):
        def body(o, i, big):
            n = sv_large[j, i] if big else sv_small[j, i]
            ng = apply_table(t_inv[...] if big else t_sinv[...], n)
            xs[o, :] = xs[o, :] + norm_back(vh1[j, o, :].astype(f32), wide_rows(r1[j, o, :]), ng * gains[j, 0:1, :])
        crop_loops(body, which)

    i0, o0 = gather_ops(0, "in"), gather_ops(0, "out")
    i1, o1 = gather_ops(1, "in"), gather_ops(1, "out")
    barrier = pltpu.get_barrier_semaphore()
    for to in peer.values():
        pl.semaphore_signal(barrier, 1, device_id=to, device_id_type=MESH_ID)
    for d in fetches:
        d.start()
    fetched(0, 1, 2)
    own_pieces()
    pl.semaphore_wait(barrier, len(peer))

    pack_z(0)
    i0["p"](0)
    i0["z"]()
    bacc[...] = jnp.zeros_like(bacc)
    vacc[...] = jnp.zeros_like(vacc)
    fetched(3, 4, 5, 6)
    load_rows(xs, large_rows, small_rows)
    to_spectrum(0, ("big",))
    pack_plane(0)
    i0["zw"]()
    i0["p"](1, 2, 3)
    o0["z"]()
    o0["p"](0)
    pack_z(1)
    to_spectrum(0, ("small",))
    fetched(*range(7, N_IN))
    load_rows(grad_low, cot_large, cot_small)

    def cot_sum(o):
        vacc[1, 4] += fold(grad_low[o, :].astype(f32))
    tiles(cot_sum)
    pack_core(0)
    i1["z"]()
    pack_wait(0)
    unpack_filters(0)
    i0["pw"](0, 1)
    i0["c"](True)
    from_spectrum(0, ("big",))
    o0["zw"]()
    o0["p"](1, 2, 3)
    i1["f"](0)
    pack_plane(1)
    from_spectrum(0, ("small",))
    i0["pw"](2, 3)
    i0["c"](False)
    i0["cw"](True)
    o1["z"]()
    expand(0, half_z, True)
    i0["cw"](False)
    i1["zw"]()
    i1["f"](1, 2, 3)
    o0["pw"](0, 1)
    o0["c"](True)
    expand(0, 1 - half_z, False)
    o0["pw"](2, 3)
    o0["c"](False)
    i1["s"](0, 1)
    o1["f"](0)
    o0["cw"](True)
    o0["cw"](False)
    contract(0)
    i1["s"](2, 3)
    o1["zw"]()
    o1["f"](1, 2, 3)
    pack_core(1)
    to_spectrum(1)
    pack_wait(1)
    unpack_filters(1)
    i1["sw"](0, 1, 2, 3)
    i1["c"](True)
    i1["c"](False)
    o1["s"](0, 1, 2, 3)
    from_spectrum(1)
    i1["cw"](True)
    expand(1, half_z, True)
    o1["sw"](0, 1, 2, 3)
    o1["c"](True)
    o1["c"](False)
    i1["cw"](False)
    expand(1, 1 - half_z, False)
    o1["cw"](True)
    o1["cw"](False)
    contract(1)
    store_large(large_rows)
    put(0, large_rows)
    store_small(small_rows)
    put(1, small_rows)

    def weights(j, a, k):
        reduce_core(j, a, k, (weight_out if a else weight_in)(j, k))

    def plane(j, a, *ks):
        for k in ks:
            reduce_plane(j, a, k)

    def along_z(j, a, *ks):
        for k in ks:
            reduce_z(j, a, k)

    for k in (2, 3):
        weights(1, 1, k)
    plane(1, 1, 2)
    weights(1, 1, 1)
    plane(1, 1, 3)
    weights(1, 1, 0)
    plane(1, 1, 1)
    back_hidden(1, 1 - half_z, False)
    plane(1, 1, 0)
    for k in (2, 3):
        weights(1, 0, k)
    back_hidden(1, half_z, True)
    plane(1, 0, 2, 3)
    weights(1, 0, 1)
    along_z(1, 1, 2, 3)
    back_spectrum(1, ("small",))
    plane(1, 0, 1)
    weights(1, 0, 0)
    back_spectrum(1, ("big",))
    along_z(1, 1, 1, 0)
    back_filters(1)
    small_core(1)
    back_rows(1, ("small",))
    small_plane(1)
    plane(1, 0, 0)
    back_rows(1, ("big",))

    def low(o):
        g = xs[o, :]
        vacc[0, 4] += fold(g)
        grad_low[o, :] = g.astype(bf16)
    tiles(low)
    along_z(1, 0, 2, 3, 1)
    for k in (2, 3):
        weights(0, 1, k)
    plane(0, 1, 2)
    weights(0, 1, 1)
    plane(0, 1, 3)
    along_z(1, 0, 0)
    small_z(1)
    back_hidden(0, 1 - half_z, False)
    plane(0, 1, 1)
    for k in (2, 3):
        weights(0, 0, k)
    along_z(0, 1, 2)
    back_hidden(0, half_z, True)
    plane(0, 0, 2, 3)
    along_z(0, 1, 3, 1)
    small_end(1)
    reduce_end(1, 1)
    reduce_end(1, 0)
    back_spectrum(0, ("small",))
    back_spectrum(0, ("big",))
    back_filters(0)
    small_core(0)
    weights(0, 0, 1)
    small_plane(0)
    weights(0, 1, 0)
    plane(0, 0, 1)
    weights(0, 0, 0)
    plane(0, 1, 0)
    along_z(0, 0, 2, 3)
    back_rows(0, ("small",))
    store_small(grad_small)
    put(3, grad_small)
    plane(0, 0, 0)
    small_z(0)
    along_z(0, 0, 1)
    back_rows(0, ("big",))
    store_large(grad_large)
    put(2, grad_large)
    along_z(0, 1, 0)
    reduce_end(0, 1)
    put(6, g_w_out)
    along_z(0, 0, 0)
    reduce_end(0, 0)
    small_end(0)
    put(4, g_filters)
    put(5, g_w_in)
    put(7, g_gains)
    put(8, g_biases)
    for d in stores:
        d.wait()
    for key in list(unsent):
        sent(key)
    assert len(sending) == N_SEND and len(receiving) == N_RECEIVE, (len(sending), len(receiving))


def hand_over_kernel(*refs):
    sources, targets, between = refs[:N_OUT], refs[N_OUT : 2 * N_OUT], refs[2 * N_OUT : 3 * N_OUT]
    in_sem, out_sem = refs[3 * N_OUT :]
    ins = [pltpu.make_async_copy(a, b, in_sem.at[n]) for n, (a, b) in enumerate(zip(sources, between))]
    outs = [pltpu.make_async_copy(a, b, out_sem.at[n]) for n, (a, b) in enumerate(zip(between, targets))]
    for d in ins:
        d.start()
    for a, b in zip(ins, outs):
        a.wait()
        b.start()
    for d in outs:
        d.wait()


def fused(large_in, small_in, large_cot, small_cot, filters, w_in, w_out, gains, biases):
    large, small = large_in.shape[0], small_in.shape[0]
    rows = -(-(large * LP + small * PS) // TILE) * TILE
    early, late = [[jnp.asarray(t) for t in part] for part in constant_tables()]
    args = [jnp.swapaxes(w_in, 1, 2), w_out, filters, small_in, jnp.swapaxes(large_in, 0, 1), *early,
            jnp.swapaxes(large_cot, 0, 1), small_cot, gains, jnp.swapaxes(biases, 0, 1), *late]
    V = pltpu.VMEM
    patch_major = (large_in.shape[1], large, D)
    outs = [(patch_major, bf16), (small_in.shape, bf16), (patch_major, f32), (small_in.shape, f32), (filters.shape, f32),
            ((BLOCKS, HID, D + 1), f32), ((BLOCKS, HID, D), f32), (gains.shape, f32), ((3, BLOCKS, D), f32)]
    grid8 = (4, 2, 2, 2)
    scratch = [V(a.shape, a.dtype) for a in args] + [V(shape, dtype) for shape, dtype in outs[2:]] + [
        V((rows, D), f32), V((BLOCKS, rows, D), bf16), V((BLOCKS, rows, 128), f32), V((BLOCKS, rows, D), f32),
        V((BLOCKS, rows, 128), f32), V((BLOCKS, rows, D), bf16), V((BLOCKS, 2, rows, FF // 2), bf16),
        V((BLOCKS, 2, rows, FF // 2), bf16), V((BLOCKS, large, SPEC, D), f32), V((BLOCKS, small // Q, 2 * QF, D), f32),
        V((rows, D), bf16),
        V((BLOCKS, *grid8, HID, D), bf16), V((BLOCKS, *grid8, HID, D), bf16), V((BLOCKS, *grid8, 8, D), bf16),
        V((BLOCKS, 2 * QF, D), f32), V((BLOCKS, 2, 1, FF // 2), f32),
        V((BLOCKS, *grid8, 8, D), f32), V((2 * QF, D), f32), V((FLP + QF, D), f32), V((BLOCKS, 2, 8, FF // 2), f32), V((BLOCKS, 5, 8, D), f32),
        V((2, 4, 2, 2, HID, D), f32),
        V((2, 4, 2, 2, HID, D), bf16), V((2, 4, 3, HID, D), bf16), V((2, 3, HID, D), bf16),
        V((BLOCKS, 2, 4, 2, 2, HID, D), bf16), V((BLOCKS, 2, 4, 3, HID, D), bf16), V((BLOCKS, 2, 3, HID, D), bf16),
        V((BLOCKS, 4, 2, 2, 8, D), bf16), V((BLOCKS, 4, 2, 2, 8, D), bf16), V((BLOCKS, 2, 2, 4, 8, D), f32),
        V((BLOCKS, 3, 4, 8, D), bf16), V((BLOCKS, 3, 4, 8, D), bf16), V((BLOCKS, 3, 8, D), bf16), V((BLOCKS, 3, 8, D), bf16),
        V((BLOCKS, 8, D), f32), V((BLOCKS, 8, D), f32), V((BLOCKS, 2, 2, 8, D), f32), V((BLOCKS, 4, 8, D), f32),
        pltpu.SemaphoreType.DMA((N_SEND,)), pltpu.SemaphoreType.DMA((N_RECEIVE,)),
        pltpu.SemaphoreType.DMA((N_IN,)), pltpu.SemaphoreType.DMA((N_OUT,)),
    ]
    anywhere = pl.BlockSpec(memory_space=pl.ANY)
    out_shape = [jax.ShapeDtypeStruct(shape, dtype) for shape, dtype in outs]
    result = pl.pallas_call(
        partial(fused_kernel, large, small),
        out_shape=out_shape,
        in_specs=[anywhere] * N_IN,
        out_specs=[anywhere] * N_OUT,
        scratch_shapes=scratch,
        compiler_params=pltpu.CompilerParams(collective_id=0, has_side_effects=True, vmem_limit_bytes=VMEM_BYTES),
        name="gfnet_step",
    )(*args)
    out_large, out_small, grad_large, grad_small, g_filters, g_in, g_out, g_gains, g_biases = pl.pallas_call(
        hand_over_kernel,
        out_shape=out_shape,
        in_specs=[anywhere] * N_OUT,
        out_specs=[anywhere] * N_OUT,
        scratch_shapes=[V(shape, dtype) for shape, dtype in outs] + [pltpu.SemaphoreType.DMA((N_OUT,))] * 2,
        compiler_params=pltpu.CompilerParams(vmem_limit_bytes=VMEM_BYTES),
        name="hand_over",
    )(*result)
    return (jnp.swapaxes(out_large, 0, 1), out_small, jnp.swapaxes(grad_large, 0, 1), grad_small, g_filters,
            jnp.swapaxes(g_in, 1, 2), g_out, g_gains, jnp.swapaxes(g_biases, 0, 1))


def solution(mesh):
    in_specs = (
        P(("wide", "narrow"), None, None),
        P(("wide", "narrow"), None, None),
        P(("wide", "narrow"), None, None),
        P(("wide", "narrow"), None, None),
        P(None, ("wide", "narrow")),
        P(None, None, ("wide", "narrow")),
        P(None, ("wide", "narrow"), None),
        P(),
        P(),
    )
    out_specs = (
        P(("wide", "narrow"), None, None),
        P(("wide", "narrow"), None, None),
        P(("wide", "narrow"), None, None),
        P(("wide", "narrow"), None, None),
        P(None, ("wide", "narrow")),
        P(None, None, ("wide", "narrow")),
        P(None, ("wide", "narrow"), None),
        P(),
        P(),
    )
    body = fused if dict(mesh.shape) == {"wide": 8, "narrow": 4} else per_device
    return jax.shard_map(
        body, mesh=mesh, in_specs=in_specs, out_specs=out_specs, check_vma=False
    )
```

```python
from functools import partial
import math

import jax
import jax.numpy as jnp
import ml_dtypes
import numpy as np
from jax import lax
from jax.experimental import pallas as pl
from jax.experimental.pallas import tpu as pltpu
from jax.sharding import PartitionSpec as P

FF = 1536
GL = 14
GS = 6
BLOCKS = 2
MICRO = 2
PL = 196
FL = 112
FS = 24


precise = lax.Precision.HIGHEST
epsilon = 1e-06


def dft_tables(grid_cells):
    half_count = grid_cells // 2 + 1
    places = jnp.arange(grid_cells * grid_cells, dtype=jnp.int32)
    place_row = places // grid_cells
    place_col = places % grid_cells
    modes = jnp.arange(grid_cells * half_count, dtype=jnp.int32)
    mode_row = modes // half_count
    mode_col = modes % half_count
    phases = (
        mode_row[:, None] * place_row[None, :] + mode_col[:, None] * place_col[None, :]
    ) % grid_cells
    angles = phases.astype(jnp.float32) * (2.0 * math.pi / grid_cells)
    forward_re = jnp.cos(angles) / grid_cells
    forward_im = -jnp.sin(angles) / grid_cells
    doubling = jnp.where((mode_col == 0) | (2 * mode_col == grid_cells), 1.0, 2.0).astype(
        jnp.float32
    )
    inverse_re = jnp.transpose(forward_re * doubling[:, None])
    inverse_im = jnp.transpose(forward_im * doubling[:, None])
    return (forward_re, forward_im, inverse_re, inverse_im)


def linear_map(size_out, size_in):
    rows_out = jnp.arange(size_out, dtype=jnp.int32)
    spans = rows_out * (size_in - 1)
    lower = spans // (size_out - 1)
    fraction = (spans - lower * (size_out - 1)).astype(jnp.float32) / (size_out - 1)
    columns = jnp.arange(size_in, dtype=jnp.int32)
    first = jnp.where(columns[None, :] == lower[:, None], 1.0 - fraction[:, None], 0.0)
    second = jnp.where(columns[None, :] == lower[:, None] + 1, fraction[:, None], 0.0)
    return first + second


def shrink_map():
    along_rows = linear_map(GS, GL)
    along_cols = linear_map(GS // 2 + 1, GL // 2 + 1)
    return (along_rows[:, None, :, None] * along_cols[None, :, None, :]).reshape(FS, FL)


def filter_grid(patches, tables, filt_re, filt_im):
    forward_re, forward_im, inverse_re, inverse_im = tables
    spec_re = jnp.einsum("fp,bpd->bfd", forward_re, patches, precision=precise)
    spec_im = jnp.einsum("fp,bpd->bfd", forward_im, patches, precision=precise)
    out_re = spec_re * filt_re - spec_im * filt_im
    out_im = spec_re * filt_im + spec_im * filt_re
    back_re = jnp.einsum("pf,bfd->bpd", inverse_re, out_re, precision=precise)
    back_im = jnp.einsum("pf,bfd->bpd", inverse_im, out_im, precision=precise)
    return back_re + back_im


def spectral(normed, large_rows, filt_re, filt_im):
    width = normed.shape[-1]
    shrink = shrink_map()
    small_re = jnp.dot(shrink, filt_re, precision=precise, preferred_element_type=jnp.float32)
    small_im = jnp.dot(shrink, filt_im, precision=precise, preferred_element_type=jnp.float32)
    part_large = filter_grid(
        normed[:large_rows].reshape(-1, GL * GL, width), dft_tables(GL), filt_re, filt_im
    )
    part_small = filter_grid(
        normed[large_rows:].reshape(-1, GS * GS, width), dft_tables(GS), small_re, small_im
    )
    return jnp.concatenate([part_large.reshape(-1, width), part_small.reshape(-1, width)], 0)


def layer_norm(stream, gain, shift):
    centre = stream - jnp.mean(stream, axis=-1, keepdims=True)
    spread = jnp.mean(centre * centre, axis=-1, keepdims=True)
    return centre * lax.rsqrt(spread + epsilon) * gain + shift


def per_device(large_in, small_in, large_cot, small_cot, filters, w_in, w_out, gains, biases):
    width = large_in.shape[-1]
    micro_large = large_in.shape[0] // MICRO
    micro_small = small_in.shape[0] // MICRO
    large_rows = micro_large * PL
    exact_gelu = partial(jax.nn.gelu, approximate=False)

    def fetch(layer_index, forward):
        if forward:
            return (
                lax.all_gather(filters[layer_index], ("wide", "narrow"), axis=0, tiled=True),
                lax.all_gather(w_in[layer_index], ("wide", "narrow"), axis=1, tiled=True),
                lax.all_gather(w_out[layer_index], ("wide", "narrow"), axis=0, tiled=True),
            )
        return (
            lax.all_gather(filters[layer_index], ("wide", "narrow"), axis=0, tiled=True),
            lax.all_gather(w_in[layer_index], ("wide", "narrow"), axis=1, tiled=True),
            lax.all_gather(w_out[layer_index], ("wide", "narrow"), axis=0, tiled=True),
        )

    def branch_first(stream, gain, shift, filt_re, filt_im):
        return spectral(layer_norm(stream, gain, shift), large_rows, filt_re, filt_im)

    acc_filter = [jnp.zeros((2, FL, width), jnp.float32) for layer_index in range(BLOCKS)]
    acc_in = [jnp.zeros((width, FF), jnp.float32) for layer_index in range(BLOCKS)]
    acc_in_bias = [jnp.zeros((FF,), jnp.float32) for layer_index in range(BLOCKS)]
    acc_out = [jnp.zeros((FF, width), jnp.float32) for layer_index in range(BLOCKS)]
    acc_gain = [jnp.zeros((2, width), jnp.float32) for layer_index in range(BLOCKS)]
    acc_shift = [jnp.zeros((3, width), jnp.float32) for layer_index in range(BLOCKS)]
    outs_large, outs_small, grads_large, grads_small = ([], [], [], [])
    for micro_step in range(MICRO):
        large_part = large_in[micro_step * micro_large : (micro_step + 1) * micro_large]
        small_part = small_in[micro_step * micro_small : (micro_step + 1) * micro_small]
        stream = jnp.concatenate(
            [large_part.reshape(-1, width), small_part.reshape(-1, width)], 0
        ).astype(jnp.float32)
        saved = []
        for layer_index in range(BLOCKS):
            filt_full, in_full, out_full = fetch(layer_index, True)
            halves = filt_full.reshape(2, FL, width).astype(jnp.float32)
            mixed = stream + branch_first(
                stream, gains[layer_index, 0], biases[layer_index, 0], halves[0], halves[1]
            )
            second = layer_norm(mixed, gains[layer_index, 1], biases[layer_index, 1]).astype(
                jnp.bfloat16
            )
            pre_act = jnp.dot(
                second, in_full[:width], preferred_element_type=jnp.float32
            ) + in_full[width].astype(jnp.float32)
            active = exact_gelu(pre_act).astype(jnp.bfloat16)
            saved.append((stream, mixed, second, pre_act))
            stream = (
                mixed
                + jnp.dot(active, out_full, preferred_element_type=jnp.float32)
                + biases[layer_index, 2]
            )
        outs_large.append(stream[:large_rows].reshape(large_part.shape).astype(jnp.bfloat16))
        outs_small.append(stream[large_rows:].reshape(small_part.shape).astype(jnp.bfloat16))
        large_back = large_cot[micro_step * micro_large : (micro_step + 1) * micro_large]
        small_back = small_cot[micro_step * micro_small : (micro_step + 1) * micro_small]
        grad = jnp.concatenate(
            [large_back.reshape(-1, width), small_back.reshape(-1, width)], 0
        ).astype(jnp.float32)
        for layer_index in reversed(range(BLOCKS)):
            block_input, mixed, second, pre_act = saved[layer_index]
            filt_full, in_full, out_full = fetch(layer_index, False)
            halves = filt_full.reshape(2, FL, width).astype(jnp.float32)
            grad_low = grad.astype(jnp.bfloat16)
            active, gelu_back = jax.vjp(exact_gelu, pre_act)
            active = active.astype(jnp.bfloat16)
            acc_out[layer_index] = acc_out[layer_index] + jnp.einsum(
                "tf,td->fd", active, grad_low, preferred_element_type=jnp.float32
            )
            bias_out_grad = jnp.sum(grad, axis=0)
            active_grad = jnp.einsum(
                "td,fd->tf", grad_low, out_full, preferred_element_type=jnp.float32
            )
            pre_grad = gelu_back(active_grad)[0]
            pre_low = pre_grad.astype(jnp.bfloat16)
            acc_in[layer_index] = acc_in[layer_index] + jnp.einsum(
                "td,tf->df", second, pre_low, preferred_element_type=jnp.float32
            )
            acc_in_bias[layer_index] = acc_in_bias[layer_index] + jnp.sum(pre_grad, axis=0)
            second_grad = jnp.einsum(
                "tf,df->td", pre_low, in_full[:width], preferred_element_type=jnp.float32
            )
            unused, norm_back = jax.vjp(
                layer_norm, mixed, gains[layer_index, 1], biases[layer_index, 1]
            )
            mixed_part, gain_two, shift_two = norm_back(second_grad)
            mixed_grad = grad + mixed_part
            unused, first_back = jax.vjp(
                branch_first,
                block_input,
                gains[layer_index, 0],
                biases[layer_index, 0],
                halves[0],
                halves[1],
            )
            input_part, gain_one, shift_one, filt_re_grad, filt_im_grad = first_back(mixed_grad)
            grad = mixed_grad + input_part
            acc_filter[layer_index] = acc_filter[layer_index] + jnp.stack(
                [filt_re_grad, filt_im_grad], 0
            )
            acc_gain[layer_index] = acc_gain[layer_index] + jnp.stack([gain_one, gain_two], 0)
            acc_shift[layer_index] = acc_shift[layer_index] + jnp.stack(
                [shift_one, shift_two, bias_out_grad], 0
            )
        grads_large.append(grad[:large_rows].reshape(large_part.shape))
        grads_small.append(grad[large_rows:].reshape(small_part.shape))
    filter_shards, in_shards, out_shards = ([], [], [])
    for layer_index in range(BLOCKS):
        in_whole = jnp.concatenate([acc_in[layer_index], acc_in_bias[layer_index][None, :]], 0)
        filter_piece, in_piece, out_piece = (
            lax.psum_scatter(
                acc_filter[layer_index].reshape(-1),
                ("wide", "narrow"),
                scatter_dimension=0,
                tiled=True,
            ),
            lax.psum_scatter(in_whole, ("wide", "narrow"), scatter_dimension=1, tiled=True),
            lax.psum_scatter(
                acc_out[layer_index], ("wide", "narrow"), scatter_dimension=0, tiled=True
            ),
        )
        filter_shards.append(filter_piece)
        in_shards.append(in_piece)
        out_shards.append(out_piece)
    gain_total, shift_total = lax.psum(
        (jnp.stack(acc_gain, 0), jnp.stack(acc_shift, 0)), ("wide", "narrow")
    )
    return (
        jnp.concatenate(outs_large, 0),
        jnp.concatenate(outs_small, 0),
        jnp.concatenate(grads_large, 0),
        jnp.concatenate(grads_small, 0),
        jnp.stack(filter_shards, 0),
        jnp.stack(in_shards, 0),
        jnp.stack(out_shards, 0),
        gain_total,
        shift_total,
    )


MESH_ID = pl.DeviceIdType.MESH
bf16, f32 = jnp.bfloat16, jnp.float32
D, PS, EPS = 384, 36, 1e-6
LP = 208
Q = 4
SR = Q * PS
TILE = 256
BOTH = ("big", "small")
HID = 48
FLP = 128
SPEC = 2 * FLP
QF = Q * FS


def dft_arrays(n):
    half = n // 2 + 1
    places, modes = np.arange(n * n), np.arange(n * half)
    phase = ((modes // half)[:, None] * (places // n)[None] + (modes % half)[:, None] * (places % n)[None]) % n
    theta = phase * (2 * math.pi / n)
    fwd_re, fwd_im = np.cos(theta) / n, -np.sin(theta) / n
    weight = np.where((modes % half == 0) | (2 * (modes % half) == n), 1.0, 2.0)
    return fwd_re, fwd_im, fwd_re * weight[:, None], fwd_im * weight[:, None]


def interpolation(rows, cols):
    span = np.arange(rows) * (cols - 1)
    low = span // (rows - 1)
    part = (span - low * (rows - 1)) / (rows - 1)
    at = np.arange(cols)[None]
    return np.where(at == low[:, None], 1 - part[:, None], 0.0) + np.where(at == low[:, None] + 1, part[:, None], 0.0)


def two_terms(table):
    table = np.asarray(table, np.float32)
    high = table.astype(ml_dtypes.bfloat16)
    low = (table - high.astype(np.float32)).astype(ml_dtypes.bfloat16)
    return np.concatenate([high, low], 0)


def constant_tables():
    pos = np.arange(FL) // 7 * 8 + np.arange(FL) % 7
    rows = np.concatenate([pos, FLP + pos])
    fr, fi, ir, ii = dft_arrays(GL)
    fwd, inv = np.zeros((SPEC, LP)), np.zeros((SPEC, LP))
    fwd[rows, :PL], inv[rows, :PL] = np.concatenate([fr, fi]), np.concatenate([ir, ii])
    fr, fi, ir, ii = dft_arrays(GS)
    sfwd, sinv = np.zeros((2 * QF, SR)), np.zeros((2 * QF, SR))
    for q in range(Q):
        at = slice(q * PS, (q + 1) * PS)
        for half, a, b in ((0, fr, ir), (1, fi, ii)):
            to = slice(half * QF + q * FS, half * QF + (q + 1) * FS)
            sfwd[to, at], sinv[to, at] = a, b
    shrink = np.zeros((FS, FLP))
    shrink[:, pos] = (
        interpolation(GS, GL)[:, None, :, None] * interpolation(GS // 2 + 1, GL // 2 + 1)[None, :, None, :]
    ).reshape(FS, FL)
    piece = np.arange(32)
    pick = np.zeros((64, SPEC))
    pick[piece % 8 * 8 + piece // 8, 8 * piece + 7] = 1
    return [two_terms(t) for t in (fwd, sfwd)], [
        two_terms(shrink), pick.astype(ml_dtypes.bfloat16), two_terms(inv.T), two_terms(sinv.T), two_terms(shrink.T)]


def mm(a, b):
    return lax.dot_general(a, b, (((1,), (0,)), ((), ())), preferred_element_type=f32)


def mm_nt(a, b):
    return lax.dot_general(a, b, (((1,), (1,)), ((), ())), preferred_element_type=f32)


def mm_tn(a, b):
    return lax.dot_general(a, b, (((0,), (0,)), ((), ())), preferred_element_type=f32)


def halves(v):
    high = v.astype(bf16)
    return high, (v - high.astype(f32)).astype(bf16)


def apply_table(table, v):
    rows = table.shape[0] // 2
    high, low = halves(v)
    both = mm(table, high)
    return both[:rows] + both[rows:] + mm(table[:rows], low)


def standardize(v):
    centre = v - jnp.sum(v, -1, keepdims=True) * (1.0 / D)
    r = lax.rsqrt(jnp.sum(centre * centre, -1, keepdims=True) * (1.0 / D) + EPS)
    return centre * r, r


def norm_back(vh, r, q):
    mean_q = jnp.sum(q, -1, keepdims=True) * (1.0 / D)
    mean_qv = jnp.sum(q * vh, -1, keepdims=True) * (1.0 / D)
    return r * (q - mean_q - vh * mean_qv)


def fold(v):
    return jnp.sum(v.reshape(v.shape[0] // 8, 8, v.shape[1]), 0)


def aligned(v, m):
    return v if isinstance(v, int) else pl.multiple_of(v, m)


N_SEND, N_RECEIVE = 46, 98
VMEM_BYTES = 63 << 20


N_IN, N_OUT = 16, 9


def fused_kernel(large, small, *refs):
    given, made, refs = refs[:N_IN], refs[N_IN : N_IN + N_OUT], refs[N_IN + N_OUT :]
    held, refs = refs[:N_IN], refs[N_IN:]
    (raw_in, raw_out, raw_filters, small_rows, large_rows, t_fwd, t_sfwd, cot_large, cot_small, gains, biases,
     t_shrink, t_pick, t_inv, t_sinv, t_shrink_t) = held
    (grad_large, grad_small, g_filters, g_w_in, g_w_out, g_gains, g_biases,
     xs, vh1, r1, vh2, r2, second, active, slope, sv_large, sv_small, grad_low,
     w_in, w_out, pack, filt_s, b_in, shift, back, facc, sacc, gacc, bacc, vacc,
     kept, s_core, s_plane, s_z, r_core, r_plane, r_z,
     f_own, f_core, f_keep, f_send, f_xy, f_z_send, f_z, v_send, v_core, v_xy, v_z,
     send_sem, recv_sem, in_sem, out_sem) = refs
    rows = xs.shape[0]
    groups = small // Q
    base = large * LP
    wide, narrow = lax.axis_index("wide"), lax.axis_index("narrow")
    z, x, y, c = lax.div(wide, 2), lax.rem(wide, 2), lax.div(narrow, 2), lax.rem(narrow, 2)
    other = {"x": 1 - x, "y": 1 - y, "c": 1 - c}
    at = lambda zz, xx, yy, cc: (zz * 2 + xx, yy * 2 + cc)
    z_pair = {0: z, 1: z + 1 - 2 * lax.rem(z, 2), 2: lax.rem(z + 2, 4), 3: 3 - z}
    z_of = lambda k: z_pair[k]
    peer = {"x": at(z, 1 - x, y, c), "y": at(z, x, 1 - y, c), "xy": at(z, 1 - x, 1 - y, c), "c": at(z, x, y, 1 - c)}
    for k in (1, 2, 3):
        peer[k] = at(z_of(k), x, y, c)

    sending, receiving = {}, {}

    def send(j, key, src, dst, to, part=None):
        out = 2 * sending.setdefault(key, len(sending)) + j
        back = key if part is None else (key, part)
        pltpu.make_async_remote_copy(
            src_ref=src, dst_ref=dst, send_sem=send_sem.at[out],
            recv_sem=recv_sem.at[2 * receiving.setdefault(back, len(receiving)) + j],
            device_id=peer[to], device_id_type=MESH_ID).start()

    def arrived(j, key, view, part=None):
        back = key if part is None else (key, part)
        sem = recv_sem.at[2 * receiving.setdefault(back, len(receiving)) + j]
        pltpu.make_async_copy(view, view, sem).wait()

    def sent(j, key, view):
        pltpu.make_async_copy(view, view, send_sem.at[2 * sending.setdefault(key, len(sending)) + j]).wait()

    PLANE = [("xy", 1 - x, 1 - y), ("x", 1 - x, y), ("y", x, 1 - y)]
    half_z = lax.div(z, 2)
    pair = lambda near: pl.ds(2 * (half_z if near else 1 - half_z), 2)

    def gather_ops(j, name):
        ref = w_in if name == "in" else w_out
        three = ref.at[j, 0:3, x, y, c]

        def z_send():
            mine = ref.at[j, z, x, y, c]
            for k in (1, 2, 3):
                send(j, name + "z", mine, mine, k)

        def z_wait():
            arrived(j, name + "z", three)

        def plane_send(*ks):
            for k in ks:
                piece = ref.at[j, z_of(k), x, y, c]
                for to, _, _ in PLANE:
                    send(j, name + "p", piece, piece, to, part=k)

        def plane_wait(*ks):
            for k in ks:
                arrived(j, name + "p", three, k)

        def first_send(*ks):
            for k in ks:
                piece = ref.at[j, z_of(k), x, y, c]
                send(j, name + "f", piece, piece, "xy"[k % 2], part=k)

        def second_send(*ks):
            for k in ks:
                zz = z_of(k)
                arrived(j, name + "f", ref.at[j, zz, x, y, c], k)
                piece = ref.at[j, zz, x, :, c] if k % 2 else ref.at[j, zz, :, y, c]
                send(j, name + "p", piece, piece, "yx"[k % 2], part=k)

        def second_wait(*ks):
            for k in ks:
                arrived(j, name + "p", ref.at[j, z_of(k), x, :, c], k)

        def core_send(near):
            piece = ref.at[j, pair(near), :, :, c]
            send(j, name + "c", piece, piece, "c", part=near)

        def core_wait(near):
            arrived(j, name + "c", ref.at[j, pair(near), :, :, 1 - c], near)

        def all_sent():
            sent(j, name + "z", three)
            if j:
                sent(j, name + "f", ref.at[j, :, x, y, c])
                sent(j, name + "p", ref.at[j, :, x, :, c])
            else:
                sent(j, name + "p", ref.at[j, 0:3, :, :, c])
            sent(j, name + "c", ref.at[j, :, :, :, c])

        return dict(z=z_send, zw=z_wait, p=plane_send, pw=plane_wait, f=first_send, s=second_send, sw=second_wait,
                    c=core_send, cw=core_wait, e=all_sent)

    def pack_z(j):
        mine = pack.at[j, z, x, y, c]
        for k in (1, 2, 3):
            send(j, "pz", mine, mine, k)

    def pack_plane(j):
        arrived(j, "pz", pack.at[j, 0:3, x, y, c])
        piece = pack.at[j, :, x, y, c]
        for to, _, _ in PLANE:
            send(j, "pp", piece, piece, to)

    def pack_core(j):
        arrived(j, "pp", pack.at[j, 0:3, :, :, c])
        piece = pack.at[j, :, :, :, c]
        send(j, "pc", piece, piece, "c")

    def pack_wait(j):
        arrived(j, "pc", pack.at[j, :, :, :, 1 - c])

    def pack_sent(j):
        sent(j, "pz", pack.at[j, 0:3, x, y, c])
        sent(j, "pp", pack.at[j, 0:3, :, :, c])
        sent(j, "pc", pack.at[j, :, :, :, c])

    def clear(j, a, k, key, view):
        if k == 2:
            @pl.when(j == 0)
            def _():
                sent(1, key, view)

    def reduce_core(j, a, k, value):
        clear(j, a, k, "rc%d" % a, s_core.at[a])
        for n in range(4):
            even, odd = value[2 * n * HID : (2 * n + 1) * HID], value[(2 * n + 1) * HID : (2 * n + 2) * HID]
            kept[a, k, n // 2, n % 2] = jnp.where(c == 0, even, odd)
            s_core[a, k, n // 2, n % 2] = jnp.where(c == 0, odd, even).astype(bf16)
        send(j, "rc%d" % a, s_core.at[a, k], r_core.at[j, a, k], "c", k)

    def reduce_plane(j, a, k):
        arrived(j, "rc%d" % a, r_core.at[j, a, k], k)
        if not isinstance(j, int):
            clear(j, a, k, "rp%d" % a, s_plane.at[a])
        for n, (to, xx, yy) in enumerate(PLANE):
            s_plane[a, k, n] = (kept[a, k, xx, yy] + r_core[j, a, k, xx, yy].astype(f32)).astype(bf16)
            send(j, "rp%d" % a, s_plane.at[a, k, n], r_plane.at[j, a, k, n], to, k)

    def reduce_z(j, a, k):
        s = kept[a, k, x, y] + r_core[j, a, k, x, y].astype(f32)
        arrived(j, "rp%d" % a, r_plane.at[j, a, k], k)
        for n in range(3):
            s = s + r_plane[j, a, k, n].astype(f32)
        if k:
            if not isinstance(j, int):
                clear(j, a, k, "rz%d" % a, s_z.at[a])
            s_z[a, k - 1] = s.astype(bf16)
            send(j, "rz%d" % a, s_z.at[a, k - 1], r_z.at[j, a, k - 1], k)
        elif a == 0:
            g_w_in[j, :, :D] = s
        else:
            g_w_out[j] = s

    def reduce_end(j, a):
        arrived(j, "rz%d" % a, r_z.at[j, a])
        s = r_z[j, a, 0].astype(f32) + r_z[j, a, 1].astype(f32) + r_z[j, a, 2].astype(f32)
        if a == 0:
            g_w_in[j, :, :D] += s
        else:
            g_w_out[j] += s

    def small_core(j):
        for zz in range(4):
            for i in range(2):
                for l in range(2):
                    f_own[j, zz, i, l] = facc[j, zz, i, l, 1 - c].astype(bf16)
        send(j, "fc", f_own.at[j], f_core.at[j], "c")
        v_send[j] = jnp.concatenate([jnp.sum(vacc[j, i], 0, keepdims=True) for i in range(5)] + [jnp.zeros((3, D), f32)], 0)
        send(j, "vc", v_send.at[j], v_core.at[j], "c")

    def small_plane(j):
        arrived(j, "fc", f_core.at[j])
        for zz in range(4):
            for i in range(2):
                for l in range(2):
                    f_keep[j, i, l, zz] = facc[j, zz, i, l, c] + f_core[j, zz, i, l].astype(f32)
        for n, (to, xx, yy) in enumerate(PLANE):
            f_send[j, n] = f_keep[j, xx, yy].astype(bf16)
            send(j, "fp", f_send.at[j, n], f_xy.at[j, n], to)
        arrived(j, "vc", v_core.at[j])
        v_xy[j, x, y] = v_send[j] + v_core[j]
        mine = v_xy.at[j, x, y]
        for to, _, _ in PLANE:
            send(j, "vp", mine, mine, to)

    def small_z(j):
        s = f_keep[j, x, y]
        arrived(j, "fp", f_xy.at[j])
        for n in range(3):
            s = s + f_xy[j, n].astype(f32)
        f_keep[j, x, y] = s
        for k in (1, 2, 3):
            f_z_send[j, k - 1] = f_keep[j, x, y, z_of(k)].astype(bf16)
            send(j, "fz", f_z_send.at[j, k - 1], f_z.at[j, k - 1], k)
        arrived(j, "vp", v_z.at[j, 0:3])
        v_z[j, z] = v_xy[j, 0, 0] + v_xy[j, 0, 1] + v_xy[j, 1, 0] + v_xy[j, 1, 1]
        mine = v_z.at[j, z]
        for k in (1, 2, 3):
            send(j, "vz", mine, mine, k)

    def small_end(j):
        arrived(j, "fz", f_z.at[j])
        s = f_keep[j, x, y, z] + f_z[j, 0].astype(f32) + f_z[j, 1].astype(f32) + f_z[j, 2].astype(f32)
        for r in range(7):
            g_filters[j : j + 1, r * D : (r + 1) * D] = s[r : r + 1]
        g_w_in[j, :, D:] = jnp.sum(jnp.where(diagonal(), s[7:8, :128], 0.0), 1, keepdims=True)
        arrived(j, "vz", v_z.at[j, 0:3])
        v = v_z[j, 0] + v_z[j, 1] + v_z[j, 2] + v_z[j, 3]
        g_gains[j] = v[0:2]
        for l in range(3):
            g_biases[l, j : j + 1] = v[2 + l : 3 + l]

    def small_sent(j):
        for key, view in (("fc", f_own), ("vc", v_send), ("fp", f_send), ("fz", f_z)):
            sent(j, key, view.at[j])
        for key in ("vp", "vz"):
            sent(j, key, v_z.at[j, 0:3])

    def diagonal():
        shape = (HID, 128)
        return lax.broadcasted_iota(jnp.int32, shape, 0) == lax.broadcasted_iota(jnp.int32, shape, 1)

    def load_rows(dst, a, b):
        v = jnp.swapaxes(a[...], 0, 1).astype(dst.dtype)
        for i in range(large):
            dst[i * LP + LP - 16 : (i + 1) * LP, :] = jnp.zeros((16, D), dst.dtype)
            dst[i * LP : i * LP + PL, :] = v[i]
        for i in range(small):
            dst[base + i * PS : base + (i + 1) * PS, :] = b[i].astype(dst.dtype)
        dst[base + small * PS :, :] = jnp.zeros((rows - base - small * PS, D), dst.dtype)

    def store_large(a):
        v = jnp.concatenate([xs[i * LP : i * LP + PL, :][None] for i in range(large)], 0)
        a[...] = jnp.swapaxes(v, 0, 1).astype(a.dtype)

    def store_small(b):
        for i in range(small):
            b[i] = xs[base + i * PS : base + (i + 1) * PS, :].astype(b.dtype)

    def own_pieces():
        for j in range(BLOCKS):
            w_in[j, z, x, y, c] = raw_in[j, :, :D]
            w_out[j, z, x, y, c] = raw_out[j]
            bias = jnp.sum(jnp.where(diagonal(), raw_in[j, :, D:].astype(f32), 0.0), 0, keepdims=True)
            row = raw_filters[j : j + 1, :].astype(f32)
            parts = [row[:, r * D : (r + 1) * D] for r in range(7)]
            parts.append(jnp.concatenate([bias, jnp.zeros((1, D - 128), f32)], 1))
            pack[j, z, x, y, c] = jnp.concatenate(parts, 0).astype(bf16)

    fetches = [pltpu.make_async_copy(a, b, in_sem.at[n]) for n, (a, b) in enumerate(zip(given, held))]
    stores = {}

    def fetched(*which):
        for n in which:
            fetches[n].wait()

    def put(n, value):
        pltpu.make_async_copy(value, made[n], out_sem.at[n]).start()
        stores[n] = value

    def spread_rows(r):
        return jnp.broadcast_to(r, (r.shape[0], 128))

    def wide_rows(r):
        return jnp.concatenate([r, r, r], -1)

    def first_row(scale):
        return jnp.where(lax.broadcasted_iota(jnp.int32, (8, 1), 0) == 0, float(scale), 0.0)

    def column_weights(big):
        row = lax.broadcasted_iota(jnp.int32, (FLP if big else QF, 1), 0)
        column = lax.rem(lax.rem(row, 8) + 16 - lax.div(row, 8), 8) if big else lax.rem(row, 4)
        return jnp.where((column == 0) | (column == (GL if big else GS) // 2), 1.0, 2.0)

    def crop_loops(body, which):
        if "big" in which:
            for i in range(large):
                body(pl.ds(i * LP, LP), i, True)
        if "small" in which:
            for i in range(groups):
                body(pl.ds(base + i * SR, SR), i, False)

    def to_spectrum(j, which=BOTH):
        def body(o, i, big):
            vh, r = standardize(xs[o, :])
            vh1[j, o, :] = vh.astype(bf16)
            r1[j, o, :] = spread_rows(r)
            if big:
                sv_large[j, i] = apply_table(t_fwd[...], vh)
            else:
                sv_small[j, i] = apply_table(t_sfwd[...], vh)
        crop_loops(body, which)

    def unpack_filters(j):
        f = pack[j].reshape(SPEC, D)
        for h in range(2):
            s = mm(t_shrink[...], f[h * FLP : (h + 1) * FLP])
            s = s[:FS] + s[FS:]
            filt_s[j, h * QF : (h + 1) * QF] = jnp.concatenate([s] * Q, 0)
        bias = mm(t_pick[...], f[:, :128])
        bias = jnp.where(lax.broadcasted_iota(jnp.int32, (64, 128), 1) < HID, bias, 0.0)
        total = jnp.zeros((8, D), f32)
        for i in range(8):
            part = jnp.concatenate([bias[8 * i : 8 * i + 8], jnp.zeros((8, D - 128), f32)], 1)
            total = total + (pltpu.roll(part, HID * i, 1) if i else part)
        for h in range(2):
            b_in[j, h] = jnp.concatenate([total[2 * h : 2 * h + 1], total[2 * h + 1 : 2 * h + 2]], 1)

    def spectrum_of(j, i, big):
        sv = sv_large[j, i] if big else sv_small[j, i]
        h, period = (FLP, FLP) if big else (QF, FS)
        re, im = sv[:h] * gains[j, 0:1, :], sv[h:] * gains[j, 0:1, :]
        mean = first_row(GL if big else GS) * shift[j, 0]
        parts = []
        for n in range(0, h, period):
            parts += [re[n : n + 8] + mean, re[n + 8 : n + period]]
        f = pack[j].reshape(SPEC, D).astype(f32) if big else filt_s[j]
        return sv, jnp.concatenate(parts, 0), im, f[:h], f[h:]

    def from_spectrum(j, which=BOTH):
        def body(o, i, big):
            _, re, im, fr, fi = spectrum_of(j, i, big)
            out = jnp.concatenate([re * fr - im * fi, re * fi + im * fr], 0)
            xs[o, :] = xs[o, :] + apply_table(t_inv[...] if big else t_sinv[...], out)
        crop_loops(body, which)

    def tiles(body):
        for t in range(rows // TILE):
            body(pl.ds(t * TILE, TILE))

    def expand(j, h, first):
        def body(o):
            if first:
                vh, r = standardize(xs[o, :])
                vh2[j, o, :] = vh
                r2[j, o, :] = spread_rows(r)
                s = (vh * gains[j, 1:2, :] + shift[j, 1]).astype(bf16)
                second[j, o, :] = s
            else:
                s = second[j, o, :]
            pre = mm_nt(s, w_in[j, pl.ds(2 * h, 2)].reshape(FF // 2, D)) + b_in[j, h]
            phi = 0.5 + 0.5 * lax.erf(pre * (1 / math.sqrt(2)))
            active[j, h, o, :] = (pre * phi).astype(bf16)
            slope[j, h, o, :] = (phi + pre * (jnp.exp(-0.5 * pre * pre) * (1 / math.sqrt(2 * math.pi)))).astype(bf16)
        tiles(body)

    def contract(j):
        def body(o):
            s = xs[o, :] + shift[j, 2]
            for h in range(2):
                s = s + mm(active[j, h, o, :], w_out[j, 2 * h : 2 * h + 2].reshape(FF // 2, D))
            xs[o, :] = s
        tiles(body)

    def z_offset(k):
        zz = z_of(k)
        return lax.div(zz, 2), pl.ds(aligned(lax.rem(zz, 2) * (FF // 4), 128), FF // 4)

    def back_hidden(j, h, last):
        def body(o):
            w = w_out[j, pl.ds(2 * h, 2)].reshape(FF // 2, D)
            pg = mm_nt(grad_low[o, :], w) * slope[j, h, o, :].astype(f32)
            bacc[j, h] += fold(pg)
            p = pg.astype(bf16)
            slope[j, h, o, :] = p
            sg = mm(p, w_in[j, pl.ds(2 * h, 2)].reshape(FF // 2, D))
            if not last:
                back[o, :] = sg
            else:
                sg = sg + back[o, :]
                vh = vh2[j, o, :]
                vacc[j, 1] += fold(sg * vh)
                vacc[j, 3] += fold(sg)
                xs[o, :] = xs[o, :] + norm_back(vh, wide_rows(r2[j, o, :]), sg * gains[j, 1:2, :])
        tiles(body)

    def weight_in(j, k):
        h, lanes = z_offset(k)
        return mm_tn(slope[j, h, :, lanes], second[j])

    def weight_out(j, k):
        h, lanes = z_offset(k)
        return mm_tn(active[j, h, :, lanes], grad_low[...])

    def back_spectrum(j, which):
        if which == ("small",):
            sacc[...] = jnp.zeros_like(sacc)
            gacc[...] = jnp.zeros_like(gacc)
        else:
            facc[j] = jnp.zeros(facc.shape[1:], f32)

        def body(o, i, big):
            sv, re, im, fr, fi = spectrum_of(j, i, big)
            h, period = (FLP, FLP) if big else (QF, FS)
            sg = apply_table(t_fwd[...] if big else t_sfwd[...], xs[o, :])
            gr, gi = sg[:h], sg[h:]
            d_re, d_im = re * gr + im * gi, re * gi - im * gr
            if big:
                facc[j] += jnp.concatenate([d_re, d_im], 0).reshape(4, 2, 2, 2, 8, D)
            else:
                sacc[...] += jnp.concatenate([d_re, d_im], 0)
            n_re, n_im = gr * fr + gi * fi, gi * fr - gr * fi
            first = 0 if big else FLP
            gacc[first : first + h] += n_re * sv[:h] + n_im * sv[h:]
            mean = n_re[:8]
            for n in range(period, h, period):
                mean = mean + n_re[n : n + 8]
            vacc[j, 2] += mean * first_row(GL if big else GS)
            n = jnp.concatenate([n_re, n_im], 0)
            if big:
                sv_large[j, i] = n
            else:
                sv_small[j, i] = n
        crop_loops(body, which)

    def back_filters(j):
        w, ws = column_weights(True), column_weights(False)
        vacc[j, 0] = fold(gacc[:FLP] * w) + fold(gacc[FLP:] * ws)
        for h in range(2):
            s = sacc[h * QF : (h + 1) * QF] * ws
            s = s[:FS] + s[FS : 2 * FS] + s[2 * FS : 3 * FS] + s[3 * FS :]
            total = facc[j, 2 * h : 2 * h + 2].reshape(FLP, D) * w + apply_table(t_shrink_t[...], s)
            facc[j, 2 * h : 2 * h + 2] = total.reshape(2, 2, 2, 2, 8, D)
        row = [jnp.sum(bacc[j, h], 0, keepdims=True) for h in range(2)]
        row = jnp.concatenate([row[0][:, :D], row[0][:, D:], row[1][:, :D], row[1][:, D:], jnp.zeros((4, D), f32)], 0)
        mine = lax.broadcasted_iota(jnp.int32, (8, 128), 1) < HID
        for i in range(8):
            part = jnp.where(mine, (pltpu.roll(row, D - HID * i, 1) if i else row)[:, :128], 0.0)
            for g in range(4):
                facc[j, g, i // 4, i // 2 % 2, i % 2, 7:8, :128] = part[g : g + 1]

    def back_rows(j, which=BOTH):
        def body(o, i, big):
            n = sv_large[j, i] if big else sv_small[j, i]
            ng = apply_table(t_inv[...] if big else t_sinv[...], n)
            xs[o, :] = xs[o, :] + norm_back(vh1[j, o, :].astype(f32), wide_rows(r1[j, o, :]), ng * gains[j, 0:1, :])
        crop_loops(body, which)

    i0, o0 = gather_ops(0, "in"), gather_ops(0, "out")
    i1, o1 = gather_ops(1, "in"), gather_ops(1, "out")
    barrier = pltpu.get_barrier_semaphore()
    for to in peer.values():
        pl.semaphore_signal(barrier, 1, device_id=to, device_id_type=MESH_ID)
    for d in fetches:
        d.start()
    fetched(0, 1, 2)
    own_pieces()
    pl.semaphore_wait(barrier, len(peer))

    pack_z(0)
    i0["p"](0)
    i0["z"]()
    bacc[...] = jnp.zeros_like(bacc)
    vacc[...] = jnp.zeros_like(vacc)
    fetched(3, 4, 5, 6)
    load_rows(xs, large_rows, small_rows)

    def forward(j, _):
        first, then = (lambda f: pl.when(j == 0)(f)), (lambda f: pl.when(j == 1)(f))
        to_spectrum(j, ("big",))

        @first
        def _():
            pack_plane(0)
            i0["zw"]()
            i0["p"](1, 2, 3)
            o0["z"]()
            o0["p"](0)
            pack_z(1)
        to_spectrum(j, ("small",))

        @first
        def _():
            fetched(*range(7, N_IN))
            for l in range(BLOCKS):
                for i in range(3):
                    shift[l, i] = biases[i, l : l + 1, :]
            load_rows(grad_low, cot_large, cot_small)

            def cot_sum(o):
                vacc[1, 4] += fold(grad_low[o, :].astype(f32))
            tiles(cot_sum)
            pack_core(0)
            i1["z"]()
            pack_wait(0)

        @then
        def _():
            pack_wait(1)
        unpack_filters(j)

        @first
        def _():
            i0["pw"](0, 1)
            i0["c"](True)

        @then
        def _():
            i1["sw"](0, 1, 2, 3)
            i1["c"](True)
            i1["c"](False)
            o1["s"](0, 1)
        from_spectrum(j, ("big",))

        @first
        def _():
            o0["zw"]()
            o0["p"](1, 2, 3)
            i1["f"](0)
            pack_plane(1)
        from_spectrum(j, ("small",))

        @first
        def _():
            i0["pw"](2, 3)
            i0["c"](False)
            i0["cw"](True)
            o1["z"]()

        @then
        def _():
            o1["s"](2, 3)
            i1["cw"](True)
        expand(j, half_z, True)

        @first
        def _():
            i0["cw"](False)
            i1["zw"]()
            i1["f"](1, 2, 3)
            o0["pw"](0, 1)
            o0["c"](True)

        @then
        def _():
            i1["cw"](False)
        expand(j, 1 - half_z, False)

        @first
        def _():
            o0["pw"](2, 3)
            o0["c"](False)
            i1["s"](0, 1)
            o1["f"](0)
            o0["cw"](True)
            o0["cw"](False)

        @then
        def _():
            o1["sw"](0, 1, 2, 3)
            o1["c"](True)
            o1["c"](False)
            o1["cw"](True)
            o1["cw"](False)
        contract(j)

        @first
        def _():
            i1["s"](2, 3)
            o1["zw"]()
            o1["f"](1, 2, 3)
            pack_core(1)
        return 0

    lax.fori_loop(0, BLOCKS, forward, 0)
    store_large(large_rows)
    put(0, large_rows)
    store_small(small_rows)
    put(1, small_rows)

    def weights(j, a, k):
        reduce_core(j, a, k, (weight_out if a else weight_in)(j, k))

    def plane(j, a, *ks):
        for k in ks:
            reduce_plane(j, a, k)

    def along_z(j, a, *ks):
        for k in ks:
            reduce_z(j, a, k)

    def backward(t, _):
        j = BLOCKS - 1 - t
        first, then = (lambda f: pl.when(j == 1)(f)), (lambda f: pl.when(j == 0)(f))

        @first
        def _():
            def start(o):
                xs[o, :] = grad_low[o, :].astype(f32)
            tiles(start)

        @then
        def _():
            def low(o):
                g = xs[o, :]
                vacc[0, 4] += fold(g)
                grad_low[o, :] = g.astype(bf16)
            tiles(low)
            plane(1, 0, 0)
        for k in (2, 3, 1):
            weights(j, 1, k)
        plane(j, 1, 2, 3)

        @then
        def _():
            along_z(1, 0, 1)
        back_hidden(j, 1 - half_z, False)
        plane(j, 1, 1)

        @then
        def _():
            along_z(1, 1, 0)
            small_z(1)
            along_z(1, 0, 0)
        for k in (2, 3):
            weights(j, 0, k)
        along_z(j, 1, 2)
        back_hidden(j, half_z, True)
        plane(j, 0, 2, 3)
        along_z(j, 1, 3, 1)

        @then
        def _():
            small_end(1)
            reduce_end(1, 1)
            reduce_end(1, 0)
        back_spectrum(j, ("small",))
        back_spectrum(j, ("big",))
        back_filters(j)
        small_core(j)
        weights(j, 0, 1)
        small_plane(j)
        weights(j, 1, 0)
        plane(j, 0, 1)
        weights(j, 0, 0)
        plane(j, 1, 0)
        along_z(j, 0, 2, 3)
        back_rows(j, ("small",))

        @then
        def _():
            store_small(grad_small)
            put(3, grad_small)
            plane(0, 0, 0)
        back_rows(j, ("big",))
        return 0

    lax.fori_loop(0, BLOCKS, backward, 0)
    small_z(0)
    along_z(0, 0, 1)
    store_large(grad_large)
    put(2, grad_large)
    along_z(0, 1, 0)
    reduce_end(0, 1)
    put(6, g_w_out)
    along_z(0, 0, 0)
    reduce_end(0, 0)
    small_end(0)
    put(4, g_filters)
    put(5, g_w_in)
    put(7, g_gains)
    put(8, g_biases)
    for n in range(len(made)):
        pltpu.make_async_copy(stores[n], made[n], out_sem.at[n]).wait()
    for ops in (i0, o0, i1, o1):
        ops["e"]()
    for j in range(BLOCKS):
        pack_sent(j)
        small_sent(j)
    for a in range(2):
        for key, view in (("rc%d", s_core), ("rp%d", s_plane), ("rz%d", s_z)):
            sent(0, key % a, view.at[a])
    assert 2 * len(sending) == N_SEND and 2 * len(receiving) == N_RECEIVE, (len(sending), len(receiving))


def hand_over_kernel(*refs):
    sources, targets, between = refs[:N_OUT], refs[N_OUT : 2 * N_OUT], refs[2 * N_OUT : 3 * N_OUT]
    in_sem, out_sem = refs[3 * N_OUT :]
    ins = [pltpu.make_async_copy(a, b, in_sem.at[n]) for n, (a, b) in enumerate(zip(sources, between))]
    outs = [pltpu.make_async_copy(a, b, out_sem.at[n]) for n, (a, b) in enumerate(zip(between, targets))]
    for d in ins:
        d.start()
    for a, b in zip(ins, outs):
        a.wait()
        b.start()
    for d in outs:
        d.wait()


def fused(large_in, small_in, large_cot, small_cot, filters, w_in, w_out, gains, biases):
    large, small = large_in.shape[0], small_in.shape[0]
    rows = -(-(large * LP + small * PS) // TILE) * TILE
    early, late = [[jnp.asarray(t) for t in part] for part in constant_tables()]
    args = [jnp.swapaxes(w_in, 1, 2), w_out, filters, small_in, jnp.swapaxes(large_in, 0, 1), *early,
            jnp.swapaxes(large_cot, 0, 1), small_cot, gains, jnp.swapaxes(biases, 0, 1), *late]
    V = pltpu.VMEM
    patch_major = (large_in.shape[1], large, D)
    outs = [(patch_major, bf16), (small_in.shape, bf16), (patch_major, f32), (small_in.shape, f32), (filters.shape, f32),
            ((BLOCKS, HID, D + 1), f32), ((BLOCKS, HID, D), f32), (gains.shape, f32), ((3, BLOCKS, D), f32)]
    grid8 = (4, 2, 2, 2)
    scratch = [V(a.shape, a.dtype) for a in args] + [V(shape, dtype) for shape, dtype in outs[2:]] + [
        V((rows, D), f32), V((BLOCKS, rows, D), bf16), V((BLOCKS, rows, 128), f32), V((BLOCKS, rows, D), f32),
        V((BLOCKS, rows, 128), f32), V((BLOCKS, rows, D), bf16), V((BLOCKS, 2, rows, FF // 2), bf16),
        V((BLOCKS, 2, rows, FF // 2), bf16), V((BLOCKS, large, SPEC, D), f32), V((BLOCKS, small // Q, 2 * QF, D), f32),
        V((rows, D), bf16),
        V((BLOCKS, *grid8, HID, D), bf16), V((BLOCKS, *grid8, HID, D), bf16), V((BLOCKS, *grid8, 8, D), bf16),
        V((BLOCKS, 2 * QF, D), f32), V((BLOCKS, 2, 1, FF // 2), f32), V((BLOCKS, 3, 1, D), f32), V((rows, D), f32),
        V((BLOCKS, *grid8, 8, D), f32), V((2 * QF, D), f32), V((FLP + QF, D), f32), V((BLOCKS, 2, 8, FF // 2), f32), V((BLOCKS, 5, 8, D), f32),
        V((2, 4, 2, 2, HID, D), f32),
        V((2, 4, 2, 2, HID, D), bf16), V((2, 4, 3, HID, D), bf16), V((2, 3, HID, D), bf16),
        V((BLOCKS, 2, 4, 2, 2, HID, D), bf16), V((BLOCKS, 2, 4, 3, HID, D), bf16), V((BLOCKS, 2, 3, HID, D), bf16),
        V((BLOCKS, 4, 2, 2, 8, D), bf16), V((BLOCKS, 4, 2, 2, 8, D), bf16), V((BLOCKS, 2, 2, 4, 8, D), f32),
        V((BLOCKS, 3, 4, 8, D), bf16), V((BLOCKS, 3, 4, 8, D), bf16), V((BLOCKS, 3, 8, D), bf16), V((BLOCKS, 3, 8, D), bf16),
        V((BLOCKS, 8, D), f32), V((BLOCKS, 8, D), f32), V((BLOCKS, 2, 2, 8, D), f32), V((BLOCKS, 4, 8, D), f32),
        pltpu.SemaphoreType.DMA((N_SEND,)), pltpu.SemaphoreType.DMA((N_RECEIVE,)),
        pltpu.SemaphoreType.DMA((N_IN,)), pltpu.SemaphoreType.DMA((N_OUT,)),
    ]
    anywhere = pl.BlockSpec(memory_space=pl.ANY)
    out_shape = [jax.ShapeDtypeStruct(shape, dtype) for shape, dtype in outs]
    result = pl.pallas_call(
        partial(fused_kernel, large, small),
        out_shape=out_shape,
        in_specs=[anywhere] * N_IN,
        out_specs=[anywhere] * N_OUT,
        scratch_shapes=scratch,
        compiler_params=pltpu.CompilerParams(collective_id=0, has_side_effects=True, vmem_limit_bytes=VMEM_BYTES),
        name="gfnet_step",
    )(*args)
    out_large, out_small, grad_large, grad_small, g_filters, g_in, g_out, g_gains, g_biases = pl.pallas_call(
        hand_over_kernel,
        out_shape=out_shape,
        in_specs=[anywhere] * N_OUT,
        out_specs=[anywhere] * N_OUT,
        scratch_shapes=[V(shape, dtype) for shape, dtype in outs] + [pltpu.SemaphoreType.DMA((N_OUT,))] * 2,
        compiler_params=pltpu.CompilerParams(vmem_limit_bytes=VMEM_BYTES),
        name="hand_over",
    )(*result)
    return (jnp.swapaxes(out_large, 0, 1), out_small, jnp.swapaxes(grad_large, 0, 1), grad_small, g_filters,
            jnp.swapaxes(g_in, 1, 2), g_out, g_gains, jnp.swapaxes(g_biases, 0, 1))


def solution(mesh):
    in_specs = (
        P(("wide", "narrow"), None, None),
        P(("wide", "narrow"), None, None),
        P(("wide", "narrow"), None, None),
        P(("wide", "narrow"), None, None),
        P(None, ("wide", "narrow")),
        P(None, None, ("wide", "narrow")),
        P(None, ("wide", "narrow"), None),
        P(),
        P(),
    )
    out_specs = (
        P(("wide", "narrow"), None, None),
        P(("wide", "narrow"), None, None),
        P(("wide", "narrow"), None, None),
        P(("wide", "narrow"), None, None),
        P(None, ("wide", "narrow")),
        P(None, None, ("wide", "narrow")),
        P(None, ("wide", "narrow"), None),
        P(),
        P(),
    )
    body = fused if dict(mesh.shape) == {"wide": 8, "narrow": 4} else per_device
    return jax.shard_map(
        body, mesh=mesh, in_specs=in_specs, out_specs=out_specs, check_vma=False
    )
```

```python
from functools import partial
import math

import jax
import jax.numpy as jnp
import ml_dtypes
import numpy as np
from jax import lax
from jax.experimental import pallas as pl
from jax.experimental.pallas import tpu as pltpu
from jax.sharding import PartitionSpec as P

FF = 1536
GL = 14
GS = 6
BLOCKS = 2
MICRO = 2
PL = 196
FL = 112
FS = 24


precise = lax.Precision.HIGHEST
epsilon = 1e-06


def dft_tables(grid_cells):
    half_count = grid_cells // 2 + 1
    places = jnp.arange(grid_cells * grid_cells, dtype=jnp.int32)
    place_row = places // grid_cells
    place_col = places % grid_cells
    modes = jnp.arange(grid_cells * half_count, dtype=jnp.int32)
    mode_row = modes // half_count
    mode_col = modes % half_count
    phases = (
        mode_row[:, None] * place_row[None, :] + mode_col[:, None] * place_col[None, :]
    ) % grid_cells
    angles = phases.astype(jnp.float32) * (2.0 * math.pi / grid_cells)
    forward_re = jnp.cos(angles) / grid_cells
    forward_im = -jnp.sin(angles) / grid_cells
    doubling = jnp.where((mode_col == 0) | (2 * mode_col == grid_cells), 1.0, 2.0).astype(
        jnp.float32
    )
    inverse_re = jnp.transpose(forward_re * doubling[:, None])
    inverse_im = jnp.transpose(forward_im * doubling[:, None])
    return (forward_re, forward_im, inverse_re, inverse_im)


def linear_map(size_out, size_in):
    rows_out = jnp.arange(size_out, dtype=jnp.int32)
    spans = rows_out * (size_in - 1)
    lower = spans // (size_out - 1)
    fraction = (spans - lower * (size_out - 1)).astype(jnp.float32) / (size_out - 1)
    columns = jnp.arange(size_in, dtype=jnp.int32)
    first = jnp.where(columns[None, :] == lower[:, None], 1.0 - fraction[:, None], 0.0)
    second = jnp.where(columns[None, :] == lower[:, None] + 1, fraction[:, None], 0.0)
    return first + second


def shrink_map():
    along_rows = linear_map(GS, GL)
    along_cols = linear_map(GS // 2 + 1, GL // 2 + 1)
    return (along_rows[:, None, :, None] * along_cols[None, :, None, :]).reshape(FS, FL)


def filter_grid(patches, tables, filt_re, filt_im):
    forward_re, forward_im, inverse_re, inverse_im = tables
    spec_re = jnp.einsum("fp,bpd->bfd", forward_re, patches, precision=precise)
    spec_im = jnp.einsum("fp,bpd->bfd", forward_im, patches, precision=precise)
    out_re = spec_re * filt_re - spec_im * filt_im
    out_im = spec_re * filt_im + spec_im * filt_re
    back_re = jnp.einsum("pf,bfd->bpd", inverse_re, out_re, precision=precise)
    back_im = jnp.einsum("pf,bfd->bpd", inverse_im, out_im, precision=precise)
    return back_re + back_im


def spectral(normed, large_rows, filt_re, filt_im):
    width = normed.shape[-1]
    shrink = shrink_map()
    small_re = jnp.dot(shrink, filt_re, precision=precise, preferred_element_type=jnp.float32)
    small_im = jnp.dot(shrink, filt_im, precision=precise, preferred_element_type=jnp.float32)
    part_large = filter_grid(
        normed[:large_rows].reshape(-1, GL * GL, width), dft_tables(GL), filt_re, filt_im
    )
    part_small = filter_grid(
        normed[large_rows:].reshape(-1, GS * GS, width), dft_tables(GS), small_re, small_im
    )
    return jnp.concatenate([part_large.reshape(-1, width), part_small.reshape(-1, width)], 0)


def layer_norm(stream, gain, shift):
    centre = stream - jnp.mean(stream, axis=-1, keepdims=True)
    spread = jnp.mean(centre * centre, axis=-1, keepdims=True)
    return centre * lax.rsqrt(spread + epsilon) * gain + shift


def per_device(large_in, small_in, large_cot, small_cot, filters, w_in, w_out, gains, biases):
    width = large_in.shape[-1]
    micro_large = large_in.shape[0] // MICRO
    micro_small = small_in.shape[0] // MICRO
    large_rows = micro_large * PL
    exact_gelu = partial(jax.nn.gelu, approximate=False)

    def fetch(layer_index, forward):
        if forward:
            return (
                lax.all_gather(filters[layer_index], ("wide", "narrow"), axis=0, tiled=True),
                lax.all_gather(w_in[layer_index], ("wide", "narrow"), axis=1, tiled=True),
                lax.all_gather(w_out[layer_index], ("wide", "narrow"), axis=0, tiled=True),
            )
        return (
            lax.all_gather(filters[layer_index], ("wide", "narrow"), axis=0, tiled=True),
            lax.all_gather(w_in[layer_index], ("wide", "narrow"), axis=1, tiled=True),
            lax.all_gather(w_out[layer_index], ("wide", "narrow"), axis=0, tiled=True),
        )

    def branch_first(stream, gain, shift, filt_re, filt_im):
        return spectral(layer_norm(stream, gain, shift), large_rows, filt_re, filt_im)

    acc_filter = [jnp.zeros((2, FL, width), jnp.float32) for layer_index in range(BLOCKS)]
    acc_in = [jnp.zeros((width, FF), jnp.float32) for layer_index in range(BLOCKS)]
    acc_in_bias = [jnp.zeros((FF,), jnp.float32) for layer_index in range(BLOCKS)]
    acc_out = [jnp.zeros((FF, width), jnp.float32) for layer_index in range(BLOCKS)]
    acc_gain = [jnp.zeros((2, width), jnp.float32) for layer_index in range(BLOCKS)]
    acc_shift = [jnp.zeros((3, width), jnp.float32) for layer_index in range(BLOCKS)]
    outs_large, outs_small, grads_large, grads_small = ([], [], [], [])
    for micro_step in range(MICRO):
        large_part = large_in[micro_step * micro_large : (micro_step + 1) * micro_large]
        small_part = small_in[micro_step * micro_small : (micro_step + 1) * micro_small]
        stream = jnp.concatenate(
            [large_part.reshape(-1, width), small_part.reshape(-1, width)], 0
        ).astype(jnp.float32)
        saved = []
        for layer_index in range(BLOCKS):
            filt_full, in_full, out_full = fetch(layer_index, True)
            halves = filt_full.reshape(2, FL, width).astype(jnp.float32)
            mixed = stream + branch_first(
                stream, gains[layer_index, 0], biases[layer_index, 0], halves[0], halves[1]
            )
            second = layer_norm(mixed, gains[layer_index, 1], biases[layer_index, 1]).astype(
                jnp.bfloat16
            )
            pre_act = jnp.dot(
                second, in_full[:width], preferred_element_type=jnp.float32
            ) + in_full[width].astype(jnp.float32)
            active = exact_gelu(pre_act).astype(jnp.bfloat16)
            saved.append((stream, mixed, second, pre_act))
            stream = (
                mixed
                + jnp.dot(active, out_full, preferred_element_type=jnp.float32)
                + biases[layer_index, 2]
            )
        outs_large.append(stream[:large_rows].reshape(large_part.shape).astype(jnp.bfloat16))
        outs_small.append(stream[large_rows:].reshape(small_part.shape).astype(jnp.bfloat16))
        large_back = large_cot[micro_step * micro_large : (micro_step + 1) * micro_large]
        small_back = small_cot[micro_step * micro_small : (micro_step + 1) * micro_small]
        grad = jnp.concatenate(
            [large_back.reshape(-1, width), small_back.reshape(-1, width)], 0
        ).astype(jnp.float32)
        for layer_index in reversed(range(BLOCKS)):
            block_input, mixed, second, pre_act = saved[layer_index]
            filt_full, in_full, out_full = fetch(layer_index, False)
            halves = filt_full.reshape(2, FL, width).astype(jnp.float32)
            grad_low = grad.astype(jnp.bfloat16)
            active, gelu_back = jax.vjp(exact_gelu, pre_act)
            active = active.astype(jnp.bfloat16)
            acc_out[layer_index] = acc_out[layer_index] + jnp.einsum(
                "tf,td->fd", active, grad_low, preferred_element_type=jnp.float32
            )
            bias_out_grad = jnp.sum(grad, axis=0)
            active_grad = jnp.einsum(
                "td,fd->tf", grad_low, out_full, preferred_element_type=jnp.float32
            )
            pre_grad = gelu_back(active_grad)[0]
            pre_low = pre_grad.astype(jnp.bfloat16)
            acc_in[layer_index] = acc_in[layer_index] + jnp.einsum(
                "td,tf->df", second, pre_low, preferred_element_type=jnp.float32
            )
            acc_in_bias[layer_index] = acc_in_bias[layer_index] + jnp.sum(pre_grad, axis=0)
            second_grad = jnp.einsum(
                "tf,df->td", pre_low, in_full[:width], preferred_element_type=jnp.float32
            )
            unused, norm_back = jax.vjp(
                layer_norm, mixed, gains[layer_index, 1], biases[layer_index, 1]
            )
            mixed_part, gain_two, shift_two = norm_back(second_grad)
            mixed_grad = grad + mixed_part
            unused, first_back = jax.vjp(
                branch_first,
                block_input,
                gains[layer_index, 0],
                biases[layer_index, 0],
                halves[0],
                halves[1],
            )
            input_part, gain_one, shift_one, filt_re_grad, filt_im_grad = first_back(mixed_grad)
            grad = mixed_grad + input_part
            acc_filter[layer_index] = acc_filter[layer_index] + jnp.stack(
                [filt_re_grad, filt_im_grad], 0
            )
            acc_gain[layer_index] = acc_gain[layer_index] + jnp.stack([gain_one, gain_two], 0)
            acc_shift[layer_index] = acc_shift[layer_index] + jnp.stack(
                [shift_one, shift_two, bias_out_grad], 0
            )
        grads_large.append(grad[:large_rows].reshape(large_part.shape))
        grads_small.append(grad[large_rows:].reshape(small_part.shape))
    filter_shards, in_shards, out_shards = ([], [], [])
    for layer_index in range(BLOCKS):
        in_whole = jnp.concatenate([acc_in[layer_index], acc_in_bias[layer_index][None, :]], 0)
        filter_piece, in_piece, out_piece = (
            lax.psum_scatter(
                acc_filter[layer_index].reshape(-1),
                ("wide", "narrow"),
                scatter_dimension=0,
                tiled=True,
            ),
            lax.psum_scatter(in_whole, ("wide", "narrow"), scatter_dimension=1, tiled=True),
            lax.psum_scatter(
                acc_out[layer_index], ("wide", "narrow"), scatter_dimension=0, tiled=True
            ),
        )
        filter_shards.append(filter_piece)
        in_shards.append(in_piece)
        out_shards.append(out_piece)
    gain_total, shift_total = lax.psum(
        (jnp.stack(acc_gain, 0), jnp.stack(acc_shift, 0)), ("wide", "narrow")
    )
    return (
        jnp.concatenate(outs_large, 0),
        jnp.concatenate(outs_small, 0),
        jnp.concatenate(grads_large, 0),
        jnp.concatenate(grads_small, 0),
        jnp.stack(filter_shards, 0),
        jnp.stack(in_shards, 0),
        jnp.stack(out_shards, 0),
        gain_total,
        shift_total,
    )


MESH_ID = pl.DeviceIdType.MESH
bf16, f32 = jnp.bfloat16, jnp.float32
D, PS, EPS = 384, 36, 1e-6
LP = 208
Q = 4
SR = Q * PS
TILE = 256
BOTH = ("big", "small")
HID = 48
FLP = 128
SPEC = 2 * FLP
QF = Q * FS


def dft_arrays(n):
    half = n // 2 + 1
    places, modes = np.arange(n * n), np.arange(n * half)
    phase = ((modes // half)[:, None] * (places // n)[None] + (modes % half)[:, None] * (places % n)[None]) % n
    theta = phase * (2 * math.pi / n)
    fwd_re, fwd_im = np.cos(theta) / n, -np.sin(theta) / n
    weight = np.where((modes % half == 0) | (2 * (modes % half) == n), 1.0, 2.0)
    return fwd_re, fwd_im, fwd_re * weight[:, None], fwd_im * weight[:, None]


def interpolation(rows, cols):
    span = np.arange(rows) * (cols - 1)
    low = span // (rows - 1)
    part = (span - low * (rows - 1)) / (rows - 1)
    at = np.arange(cols)[None]
    return np.where(at == low[:, None], 1 - part[:, None], 0.0) + np.where(at == low[:, None] + 1, part[:, None], 0.0)


def two_terms(table):
    table = np.asarray(table, np.float32)
    high = table.astype(ml_dtypes.bfloat16)
    low = (table - high.astype(np.float32)).astype(ml_dtypes.bfloat16)
    return np.concatenate([high, low], 0)


def constant_tables():
    pos = np.arange(FL) // 7 * 8 + np.arange(FL) % 7
    rows = np.concatenate([pos, FLP + pos])
    fr, fi, ir, ii = dft_arrays(GL)
    fwd, inv = np.zeros((SPEC, LP)), np.zeros((SPEC, LP))
    fwd[rows, :PL], inv[rows, :PL] = np.concatenate([fr, fi]), np.concatenate([ir, ii])
    fr, fi, ir, ii = dft_arrays(GS)
    sfwd, sinv = np.zeros((2 * QF, SR)), np.zeros((2 * QF, SR))
    for q in range(Q):
        at = slice(q * PS, (q + 1) * PS)
        for half, a, b in ((0, fr, ir), (1, fi, ii)):
            to = slice(half * QF + q * FS, half * QF + (q + 1) * FS)
            sfwd[to, at], sinv[to, at] = a, b
    shrink = np.zeros((FS, FLP))
    shrink[:, pos] = (
        interpolation(GS, GL)[:, None, :, None] * interpolation(GS // 2 + 1, GL // 2 + 1)[None, :, None, :]
    ).reshape(FS, FL)
    piece = np.arange(32)
    pick = np.zeros((64, SPEC))
    pick[piece % 8 * 8 + piece // 8, 8 * piece + 7] = 1
    return [two_terms(t) for t in (fwd, sfwd)], [
        two_terms(shrink), pick.astype(ml_dtypes.bfloat16), two_terms(inv.T), two_terms(sinv.T), two_terms(shrink.T)]


def mm(a, b):
    return lax.dot_general(a, b, (((1,), (0,)), ((), ())), preferred_element_type=f32)


def mm_nt(a, b):
    return lax.dot_general(a, b, (((1,), (1,)), ((), ())), preferred_element_type=f32)


def mm_tn(a, b):
    return lax.dot_general(a, b, (((0,), (0,)), ((), ())), preferred_element_type=f32)


def halves(v):
    high = v.astype(bf16)
    return high, (v - high.astype(f32)).astype(bf16)


def apply_table(table, v):
    rows = table.shape[0] // 2
    high, low = halves(v)
    both = mm(table, high)
    return both[:rows] + both[rows:] + mm(table[:rows], low)


def standardize(v):
    centre = v - jnp.sum(v, -1, keepdims=True) * (1.0 / D)
    r = lax.rsqrt(jnp.sum(centre * centre, -1, keepdims=True) * (1.0 / D) + EPS)
    return centre * r, r


def norm_back(vh, r, q):
    mean_q = jnp.sum(q, -1, keepdims=True) * (1.0 / D)
    mean_qv = jnp.sum(q * vh, -1, keepdims=True) * (1.0 / D)
    return r * (q - mean_q - vh * mean_qv)


def fold(v):
    return jnp.sum(v.reshape(v.shape[0] // 8, 8, v.shape[1]), 0)


def aligned(v, m):
    return v if isinstance(v, int) else pl.multiple_of(v, m)


N_SEND, N_RECEIVE = 46, 102
VMEM_BYTES = 63 << 20


N_IN, N_OUT = 16, 9


def fused_kernel(large, small, *refs):
    given, made, refs = refs[:N_IN], refs[N_IN : N_IN + N_OUT], refs[N_IN + N_OUT :]
    held, refs = refs[:N_IN], refs[N_IN:]
    (raw_in, raw_out, raw_filters, small_rows, large_rows, t_fwd, t_sfwd, cot_large, cot_small, gains, biases,
     t_shrink, t_pick, t_inv, t_sinv, t_shrink_t) = held
    (grad_large, grad_small, g_filters, g_w_in, g_w_out, g_gains, g_biases,
     xs, vh1, r1, vh2, r2, second, active, slope, sv_large, sv_small, grad_low,
     w_in, w_out, pack, filt_s, b_in, shift, back, facc, sacc, gacc, bacc, vacc,
     kept, s_core, s_plane, s_z, r_core, r_plane, r_z,
     f_own, f_core, f_keep, f_send, f_xy, f_z_send, f_z, v_send, v_core, v_xy, v_z,
     send_sem, recv_sem, in_sem, out_sem) = refs
    rows = xs.shape[0]
    groups = small // Q
    base = large * LP
    wide, narrow = lax.axis_index("wide"), lax.axis_index("narrow")
    z, x, y, c = lax.div(wide, 2), lax.rem(wide, 2), lax.div(narrow, 2), lax.rem(narrow, 2)
    other = {"x": 1 - x, "y": 1 - y, "c": 1 - c}
    at = lambda zz, xx, yy, cc: (zz * 2 + xx, yy * 2 + cc)
    z_pair = {0: z, 1: z + 1 - 2 * lax.rem(z, 2), 2: lax.rem(z + 2, 4), 3: 3 - z}
    z_of = lambda k: z_pair[k]
    peer = {"x": at(z, 1 - x, y, c), "y": at(z, x, 1 - y, c), "xy": at(z, 1 - x, 1 - y, c), "c": at(z, x, y, 1 - c)}
    for k in (1, 2, 3):
        peer[k] = at(z_of(k), x, y, c)

    sending, receiving = {}, {}

    def send(j, key, src, dst, to, part=None):
        out = 2 * sending.setdefault(key, len(sending)) + j
        back = key if part is None else (key, part)
        pltpu.make_async_remote_copy(
            src_ref=src, dst_ref=dst, send_sem=send_sem.at[out],
            recv_sem=recv_sem.at[2 * receiving.setdefault(back, len(receiving)) + j],
            device_id=peer[to], device_id_type=MESH_ID).start()

    def arrived(j, key, view, part=None):
        back = key if part is None else (key, part)
        sem = recv_sem.at[2 * receiving.setdefault(back, len(receiving)) + j]
        pltpu.make_async_copy(view, view, sem).wait()

    def sent(j, key, view):
        pltpu.make_async_copy(view, view, send_sem.at[2 * sending.setdefault(key, len(sending)) + j]).wait()

    PLANE = [("xy", 1 - x, 1 - y), ("x", 1 - x, y), ("y", x, 1 - y)]
    half_z = lax.div(z, 2)
    pair = lambda near: pl.ds(2 * (half_z if near else 1 - half_z), 2)

    def gather_ops(j, name):
        ref = w_in if name == "in" else w_out
        three = ref.at[j, 0:3, x, y, c]

        def z_send():
            mine = ref.at[j, z, x, y, c]
            for k in (1, 2, 3):
                send(j, name + "z", mine, mine, k, part=k == 1)

        def z_wait(near):
            arrived(j, name + "z", ref.at[j, 0 : 1 if near else 2, x, y, c], near)

        def plane_send(*ks):
            for k in ks:
                piece = ref.at[j, z_of(k), x, y, c]
                for to, _, _ in PLANE:
                    send(j, name + "p", piece, piece, to, part=k)

        def plane_wait(*ks):
            for k in ks:
                arrived(j, name + "p", three, k)

        def first_send(*ks):
            for k in ks:
                piece = ref.at[j, z_of(k), x, y, c]
                send(j, name + "f", piece, piece, "xy"[k % 2], part=k)

        def second_send(*ks):
            for k in ks:
                zz = z_of(k)
                arrived(j, name + "f", ref.at[j, zz, x, y, c], k)
                piece = ref.at[j, zz, x, :, c] if k % 2 else ref.at[j, zz, :, y, c]
                send(j, name + "p", piece, piece, "yx"[k % 2], part=k)

        def second_wait(*ks):
            for k in ks:
                arrived(j, name + "p", ref.at[j, z_of(k), x, :, c], k)

        def core_send(near):
            piece = ref.at[j, pair(near), :, :, c]
            send(j, name + "c", piece, piece, "c", part=near)

        def core_wait(near):
            arrived(j, name + "c", ref.at[j, pair(near), :, :, 1 - c], near)

        def all_sent():
            sent(j, name + "z", three)
            if j:
                sent(j, name + "f", ref.at[j, :, x, y, c])
                sent(j, name + "p", ref.at[j, :, x, :, c])
            else:
                sent(j, name + "p", ref.at[j, 0:3, :, :, c])
            sent(j, name + "c", ref.at[j, :, :, :, c])

        return dict(z=z_send, zw=z_wait, p=plane_send, pw=plane_wait, f=first_send, s=second_send, sw=second_wait,
                    c=core_send, cw=core_wait, e=all_sent)

    def pack_z(j):
        mine = pack.at[j, z, x, y, c]
        for k in (1, 2, 3):
            send(j, "pz", mine, mine, k)

    def pack_plane(j):
        arrived(j, "pz", pack.at[j, 0:3, x, y, c])
        piece = pack.at[j, :, x, y, c]
        for to, _, _ in PLANE:
            send(j, "pp", piece, piece, to)

    def pack_core(j):
        arrived(j, "pp", pack.at[j, 0:3, :, :, c])
        piece = pack.at[j, :, :, :, c]
        send(j, "pc", piece, piece, "c")

    def pack_wait(j):
        arrived(j, "pc", pack.at[j, :, :, :, 1 - c])

    def pack_sent(j):
        sent(j, "pz", pack.at[j, 0:3, x, y, c])
        sent(j, "pp", pack.at[j, 0:3, :, :, c])
        sent(j, "pc", pack.at[j, :, :, :, c])

    def clear(j, a, k, key, view):
        if k == 2:
            @pl.when(j == 0)
            def _():
                sent(1, key, view)

    def reduce_core(j, a, k, value):
        clear(j, a, k, "rc%d" % a, s_core.at[a])
        for n in range(4):
            even, odd = value[2 * n * HID : (2 * n + 1) * HID], value[(2 * n + 1) * HID : (2 * n + 2) * HID]
            kept[a, k, n // 2, n % 2] = jnp.where(c == 0, even, odd)
            s_core[a, k, n // 2, n % 2] = jnp.where(c == 0, odd, even).astype(bf16)
        send(j, "rc%d" % a, s_core.at[a, k], r_core.at[j, a, k], "c", k)

    def reduce_plane(j, a, k):
        arrived(j, "rc%d" % a, r_core.at[j, a, k], k)
        if not isinstance(j, int):
            clear(j, a, k, "rp%d" % a, s_plane.at[a])
        for n, (to, xx, yy) in enumerate(PLANE):
            s_plane[a, k, n] = (kept[a, k, xx, yy] + r_core[j, a, k, xx, yy].astype(f32)).astype(bf16)
            send(j, "rp%d" % a, s_plane.at[a, k, n], r_plane.at[j, a, k, n], to, k)

    def reduce_z(j, a, k):
        s = kept[a, k, x, y] + r_core[j, a, k, x, y].astype(f32)
        arrived(j, "rp%d" % a, r_plane.at[j, a, k], k)
        for n in range(3):
            s = s + r_plane[j, a, k, n].astype(f32)
        if k:
            if not isinstance(j, int):
                clear(j, a, k, "rz%d" % a, s_z.at[a])
            s_z[a, k - 1] = s.astype(bf16)
            send(j, "rz%d" % a, s_z.at[a, k - 1], r_z.at[j, a, k - 1], k)
        elif a == 0:
            g_w_in[j, :, :D] = s
        else:
            g_w_out[j] = s

    def reduce_end(j, a):
        arrived(j, "rz%d" % a, r_z.at[j, a])
        s = r_z[j, a, 0].astype(f32) + r_z[j, a, 1].astype(f32) + r_z[j, a, 2].astype(f32)
        if a == 0:
            g_w_in[j, :, :D] += s
        else:
            g_w_out[j] += s

    def small_core(j):
        for zz in range(4):
            for i in range(2):
                for l in range(2):
                    f_own[j, zz, i, l] = facc[j, zz, i, l, 1 - c].astype(bf16)
        send(j, "fc", f_own.at[j], f_core.at[j], "c")
        v_send[j] = jnp.concatenate([jnp.sum(vacc[j, i], 0, keepdims=True) for i in range(5)] + [jnp.zeros((3, D), f32)], 0)
        send(j, "vc", v_send.at[j], v_core.at[j], "c")

    def small_plane(j):
        arrived(j, "fc", f_core.at[j])
        for zz in range(4):
            for i in range(2):
                for l in range(2):
                    f_keep[j, i, l, zz] = facc[j, zz, i, l, c] + f_core[j, zz, i, l].astype(f32)
        for n, (to, xx, yy) in enumerate(PLANE):
            f_send[j, n] = f_keep[j, xx, yy].astype(bf16)
            send(j, "fp", f_send.at[j, n], f_xy.at[j, n], to)
        arrived(j, "vc", v_core.at[j])
        v_xy[j, x, y] = v_send[j] + v_core[j]
        mine = v_xy.at[j, x, y]
        for to, _, _ in PLANE:
            send(j, "vp", mine, mine, to)

    def small_z(j):
        s = f_keep[j, x, y]
        arrived(j, "fp", f_xy.at[j])
        for n in range(3):
            s = s + f_xy[j, n].astype(f32)
        f_keep[j, x, y] = s
        for k in (1, 2, 3):
            f_z_send[j, k - 1] = f_keep[j, x, y, z_of(k)].astype(bf16)
            send(j, "fz", f_z_send.at[j, k - 1], f_z.at[j, k - 1], k)
        arrived(j, "vp", v_z.at[j, 0:3])
        v_z[j, z] = v_xy[j, 0, 0] + v_xy[j, 0, 1] + v_xy[j, 1, 0] + v_xy[j, 1, 1]
        mine = v_z.at[j, z]
        for k in (1, 2, 3):
            send(j, "vz", mine, mine, k)

    def small_end(j):
        arrived(j, "fz", f_z.at[j])
        s = f_keep[j, x, y, z] + f_z[j, 0].astype(f32) + f_z[j, 1].astype(f32) + f_z[j, 2].astype(f32)
        for r in range(7):
            g_filters[j : j + 1, r * D : (r + 1) * D] = s[r : r + 1]
        g_w_in[j, :, D:] = jnp.sum(jnp.where(diagonal(), s[7:8, :128], 0.0), 1, keepdims=True)
        arrived(j, "vz", v_z.at[j, 0:3])
        v = v_z[j, 0] + v_z[j, 1] + v_z[j, 2] + v_z[j, 3]
        g_gains[j] = v[0:2]
        for l in range(3):
            g_biases[l, j : j + 1] = v[2 + l : 3 + l]

    def small_sent(j):
        for key, view in (("fc", f_own), ("vc", v_send), ("fp", f_send), ("fz", f_z)):
            sent(j, key, view.at[j])
        for key in ("vp", "vz"):
            sent(j, key, v_z.at[j, 0:3])

    def diagonal():
        shape = (HID, 128)
        return lax.broadcasted_iota(jnp.int32, shape, 0) == lax.broadcasted_iota(jnp.int32, shape, 1)

    def load_rows(dst, a, b):
        v = jnp.swapaxes(a[...], 0, 1).astype(dst.dtype)
        for i in range(large):
            dst[i * LP + LP - 16 : (i + 1) * LP, :] = jnp.zeros((16, D), dst.dtype)
            dst[i * LP : i * LP + PL, :] = v[i]
        for i in range(small):
            dst[base + i * PS : base + (i + 1) * PS, :] = b[i].astype(dst.dtype)
        dst[base + small * PS :, :] = jnp.zeros((rows - base - small * PS, D), dst.dtype)

    def store_large(a):
        v = jnp.concatenate([xs[i * LP : i * LP + PL, :][None] for i in range(large)], 0)
        a[...] = jnp.swapaxes(v, 0, 1).astype(a.dtype)

    def store_small(b):
        for i in range(small):
            b[i] = xs[base + i * PS : base + (i + 1) * PS, :].astype(b.dtype)

    def own_pieces():
        for j in range(BLOCKS):
            w_in[j, z, x, y, c] = raw_in[j, :, :D]
            w_out[j, z, x, y, c] = raw_out[j]
            bias = jnp.sum(jnp.where(diagonal(), raw_in[j, :, D:].astype(f32), 0.0), 0, keepdims=True)
            row = raw_filters[j : j + 1, :].astype(f32)
            parts = [row[:, r * D : (r + 1) * D] for r in range(7)]
            parts.append(jnp.concatenate([bias, jnp.zeros((1, D - 128), f32)], 1))
            pack[j, z, x, y, c] = jnp.concatenate(parts, 0).astype(bf16)

    fetches = [pltpu.make_async_copy(a, b, in_sem.at[n]) for n, (a, b) in enumerate(zip(given, held))]
    stores = {}

    def fetched(*which):
        for n in which:
            fetches[n].wait()

    def put(n, value):
        pltpu.make_async_copy(value, made[n], out_sem.at[n]).start()
        stores[n] = value

    def spread_rows(r):
        return jnp.broadcast_to(r, (r.shape[0], 128))

    def wide_rows(r):
        return jnp.concatenate([r, r, r], -1)

    def first_row(scale):
        return jnp.where(lax.broadcasted_iota(jnp.int32, (8, 1), 0) == 0, float(scale), 0.0)

    def column_weights(big):
        row = lax.broadcasted_iota(jnp.int32, (FLP if big else QF, 1), 0)
        column = lax.rem(lax.rem(row, 8) + 16 - lax.div(row, 8), 8) if big else lax.rem(row, 4)
        return jnp.where((column == 0) | (column == (GL if big else GS) // 2), 1.0, 2.0)

    def crop_loops(body, which):
        if "big" in which:
            for i in range(large):
                body(pl.ds(i * LP, LP), i, True)
        if "small" in which:
            for i in range(groups):
                body(pl.ds(base + i * SR, SR), i, False)

    def to_spectrum(j, which=BOTH):
        def body(o, i, big):
            vh, r = standardize(xs[o, :])
            vh1[j, o, :] = vh.astype(bf16)
            r1[j, o, :] = spread_rows(r)
            if big:
                sv_large[j, i] = apply_table(t_fwd[...], vh)
            else:
                sv_small[j, i] = apply_table(t_sfwd[...], vh)
        crop_loops(body, which)

    def unpack_filters(j):
        f = pack[j].reshape(SPEC, D)
        for h in range(2):
            s = mm(t_shrink[...], f[h * FLP : (h + 1) * FLP])
            s = s[:FS] + s[FS:]
            filt_s[j, h * QF : (h + 1) * QF] = jnp.concatenate([s] * Q, 0)
        bias = mm(t_pick[...], f[:, :128])
        bias = jnp.where(lax.broadcasted_iota(jnp.int32, (64, 128), 1) < HID, bias, 0.0)
        total = jnp.zeros((8, D), f32)
        for i in range(8):
            part = jnp.concatenate([bias[8 * i : 8 * i + 8], jnp.zeros((8, D - 128), f32)], 1)
            total = total + (pltpu.roll(part, HID * i, 1) if i else part)
        for h in range(2):
            b_in[j, h] = jnp.concatenate([total[2 * h : 2 * h + 1], total[2 * h + 1 : 2 * h + 2]], 1)

    def spectrum_of(j, i, big):
        sv = sv_large[j, i] if big else sv_small[j, i]
        h, period = (FLP, FLP) if big else (QF, FS)
        re, im = sv[:h] * gains[j, 0:1, :], sv[h:] * gains[j, 0:1, :]
        mean = first_row(GL if big else GS) * shift[j, 0]
        parts = []
        for n in range(0, h, period):
            parts += [re[n : n + 8] + mean, re[n + 8 : n + period]]
        f = pack[j].reshape(SPEC, D).astype(f32) if big else filt_s[j]
        return sv, jnp.concatenate(parts, 0), im, f[:h], f[h:]

    def from_spectrum(j, which=BOTH):
        def body(o, i, big):
            _, re, im, fr, fi = spectrum_of(j, i, big)
            out = jnp.concatenate([re * fr - im * fi, re * fi + im * fr], 0)
            xs[o, :] = xs[o, :] + apply_table(t_inv[...] if big else t_sinv[...], out)
        crop_loops(body, which)

    def tiles(body):
        for t in range(rows // TILE):
            body(pl.ds(t * TILE, TILE))

    def expand(j, h, first):
        def body(o):
            if first:
                vh, r = standardize(xs[o, :])
                vh2[j, o, :] = vh
                r2[j, o, :] = spread_rows(r)
                s = (vh * gains[j, 1:2, :] + shift[j, 1]).astype(bf16)
                second[j, o, :] = s
            else:
                s = second[j, o, :]
            pre = mm_nt(s, w_in[j, pl.ds(2 * h, 2)].reshape(FF // 2, D)) + b_in[j, h]
            phi = 0.5 + 0.5 * lax.erf(pre * (1 / math.sqrt(2)))
            active[j, h, o, :] = (pre * phi).astype(bf16)
            slope[j, h, o, :] = (phi + pre * (jnp.exp(-0.5 * pre * pre) * (1 / math.sqrt(2 * math.pi)))).astype(bf16)
        tiles(body)

    def contract(j):
        def body(o):
            s = xs[o, :] + shift[j, 2]
            for h in range(2):
                s = s + mm(active[j, h, o, :], w_out[j, 2 * h : 2 * h + 2].reshape(FF // 2, D))
            xs[o, :] = s
        tiles(body)

    def z_offset(k):
        zz = z_of(k)
        return lax.div(zz, 2), pl.ds(aligned(lax.rem(zz, 2) * (FF // 4), 128), FF // 4)

    def back_hidden(j, h, last):
        def body(o):
            w = w_out[j, pl.ds(2 * h, 2)].reshape(FF // 2, D)
            pg = mm_nt(grad_low[o, :], w) * slope[j, h, o, :].astype(f32)
            bacc[j, h] += fold(pg)
            p = pg.astype(bf16)
            slope[j, h, o, :] = p
            sg = mm(p, w_in[j, pl.ds(2 * h, 2)].reshape(FF // 2, D))
            if not last:
                back[o, :] = sg
            else:
                sg = sg + back[o, :]
                vh = vh2[j, o, :]
                vacc[j, 1] += fold(sg * vh)
                vacc[j, 3] += fold(sg)
                xs[o, :] = xs[o, :] + norm_back(vh, wide_rows(r2[j, o, :]), sg * gains[j, 1:2, :])
        tiles(body)

    def weight_in(j, k):
        h, lanes = z_offset(k)
        return mm_tn(slope[j, h, :, lanes], second[j])

    def weight_out(j, k):
        h, lanes = z_offset(k)
        return mm_tn(active[j, h, :, lanes], grad_low[...])

    def back_spectrum(j, which):
        if which == ("small",):
            sacc[...] = jnp.zeros_like(sacc)
            gacc[...] = jnp.zeros_like(gacc)
        else:
            facc[j] = jnp.zeros(facc.shape[1:], f32)

        def body(o, i, big):
            sv, re, im, fr, fi = spectrum_of(j, i, big)
            h, period = (FLP, FLP) if big else (QF, FS)
            sg = apply_table(t_fwd[...] if big else t_sfwd[...], xs[o, :])
            gr, gi = sg[:h], sg[h:]
            d_re, d_im = re * gr + im * gi, re * gi - im * gr
            if big:
                facc[j] += jnp.concatenate([d_re, d_im], 0).reshape(4, 2, 2, 2, 8, D)
            else:
                sacc[...] += jnp.concatenate([d_re, d_im], 0)
            n_re, n_im = gr * fr + gi * fi, gi * fr - gr * fi
            first = 0 if big else FLP
            gacc[first : first + h] += n_re * sv[:h] + n_im * sv[h:]
            mean = n_re[:8]
            for n in range(period, h, period):
                mean = mean + n_re[n : n + 8]
            vacc[j, 2] += mean * first_row(GL if big else GS)
            n = jnp.concatenate([n_re, n_im], 0)
            if big:
                sv_large[j, i] = n
            else:
                sv_small[j, i] = n
        crop_loops(body, which)

    def back_filters(j):
        w, ws = column_weights(True), column_weights(False)
        vacc[j, 0] = fold(gacc[:FLP] * w) + fold(gacc[FLP:] * ws)
        for h in range(2):
            s = sacc[h * QF : (h + 1) * QF] * ws
            s = s[:FS] + s[FS : 2 * FS] + s[2 * FS : 3 * FS] + s[3 * FS :]
            total = facc[j, 2 * h : 2 * h + 2].reshape(FLP, D) * w + apply_table(t_shrink_t[...], s)
            facc[j, 2 * h : 2 * h + 2] = total.reshape(2, 2, 2, 2, 8, D)
        row = [jnp.sum(bacc[j, h], 0, keepdims=True) for h in range(2)]
        row = jnp.concatenate([row[0][:, :D], row[0][:, D:], row[1][:, :D], row[1][:, D:], jnp.zeros((4, D), f32)], 0)
        mine = lax.broadcasted_iota(jnp.int32, (8, 128), 1) < HID
        for i in range(8):
            part = jnp.where(mine, (pltpu.roll(row, D - HID * i, 1) if i else row)[:, :128], 0.0)
            for g in range(4):
                facc[j, g, i // 4, i // 2 % 2, i % 2, 7:8, :128] = part[g : g + 1]

    def back_rows(j, which=BOTH):
        def body(o, i, big):
            n = sv_large[j, i] if big else sv_small[j, i]
            ng = apply_table(t_inv[...] if big else t_sinv[...], n)
            xs[o, :] = xs[o, :] + norm_back(vh1[j, o, :].astype(f32), wide_rows(r1[j, o, :]), ng * gains[j, 0:1, :])
        crop_loops(body, which)

    i0, o0 = gather_ops(0, "in"), gather_ops(0, "out")
    i1, o1 = gather_ops(1, "in"), gather_ops(1, "out")
    barrier = pltpu.get_barrier_semaphore()
    for to in peer.values():
        pl.semaphore_signal(barrier, 1, device_id=to, device_id_type=MESH_ID)
    for d in fetches:
        d.start()
    fetched(0, 1, 2)
    own_pieces()
    pl.semaphore_wait(barrier, len(peer))

    pack_z(0)
    i0["p"](0)
    i0["z"]()
    bacc[...] = jnp.zeros_like(bacc)
    vacc[...] = jnp.zeros_like(vacc)
    fetched(3, 4, 5, 6)
    load_rows(xs, large_rows, small_rows)

    def forward(j, _):
        first, then = (lambda f: pl.when(j == 0)(f)), (lambda f: pl.when(j == 1)(f))
        to_spectrum(j, ("big",))

        @first
        def _():
            pack_plane(0)
            i0["zw"](True)
            i0["p"](1)
        to_spectrum(j, ("small",))

        @first
        def _():
            i0["zw"](False)
            i0["p"](2, 3)
            o0["z"]()
            o0["p"](0)
            pack_z(1)
            fetched(*range(7, N_IN))
            for l in range(BLOCKS):
                for i in range(3):
                    shift[l, i] = biases[i, l : l + 1, :]
            load_rows(grad_low, cot_large, cot_small)

            def cot_sum(o):
                vacc[1, 4] += fold(grad_low[o, :].astype(f32))
            tiles(cot_sum)
            pack_core(0)
            i1["z"]()
            pack_wait(0)

        @then
        def _():
            pack_wait(1)
        unpack_filters(j)

        @then
        def _():
            i1["sw"](0, 1, 2, 3)
            i1["c"](True)
            i1["c"](False)
            o1["s"](0, 1)
        from_spectrum(j, ("big",))

        @first
        def _():
            i0["pw"](0, 1)
            i0["c"](True)
            o0["zw"](True)
            o0["p"](1)
        from_spectrum(j, ("small",))

        @first
        def _():
            o0["zw"](False)
            o0["p"](2, 3)
            i1["f"](0)
            pack_plane(1)
            o1["z"]()
            i0["cw"](True)

        @then
        def _():
            o1["s"](2, 3)
            i1["cw"](True)
        expand(j, half_z, True)

        @first
        def _():
            i0["pw"](2, 3)
            i0["c"](False)
            i1["zw"](True)
            i1["zw"](False)
            i1["f"](1, 2, 3)
            i0["cw"](False)
            o0["pw"](0, 1)
            o0["c"](True)

        @then
        def _():
            i1["cw"](False)
        expand(j, 1 - half_z, False)

        @first
        def _():
            o0["pw"](2, 3)
            o0["c"](False)
            o1["f"](0)
            o0["cw"](True)
            o0["cw"](False)
            i1["s"](0, 1, 2, 3)

        @then
        def _():
            o1["sw"](0, 1, 2, 3)
            o1["c"](True)
            o1["c"](False)
            o1["cw"](True)
            o1["cw"](False)
        contract(j)

        @first
        def _():
            o1["zw"](True)
            o1["zw"](False)
            o1["f"](1, 2, 3)
            pack_core(1)
        return 0

    lax.fori_loop(0, BLOCKS, forward, 0)
    store_large(large_rows)
    put(0, large_rows)
    store_small(small_rows)
    put(1, small_rows)

    def weights(j, a, k):
        reduce_core(j, a, k, (weight_out if a else weight_in)(j, k))

    def plane(j, a, *ks):
        for k in ks:
            reduce_plane(j, a, k)

    def along_z(j, a, *ks):
        for k in ks:
            reduce_z(j, a, k)

    def backward(t, _):
        j = BLOCKS - 1 - t
        first, then = (lambda f: pl.when(j == 1)(f)), (lambda f: pl.when(j == 0)(f))

        @first
        def _():
            def start(o):
                xs[o, :] = grad_low[o, :].astype(f32)
            tiles(start)

        @then
        def _():
            def low(o):
                g = xs[o, :]
                vacc[0, 4] += fold(g)
                grad_low[o, :] = g.astype(bf16)
            tiles(low)
            plane(1, 0, 0)
        for k in (2, 3, 1):
            weights(j, 1, k)
        plane(j, 1, 2, 3)

        @then
        def _():
            along_z(1, 0, 1)
        back_hidden(j, 1 - half_z, False)
        plane(j, 1, 1)

        @then
        def _():
            along_z(1, 1, 0)
            small_z(1)
            along_z(1, 0, 0)
        for k in (2, 3):
            weights(j, 0, k)
        along_z(j, 1, 2)
        back_hidden(j, half_z, True)
        plane(j, 0, 2, 3)
        along_z(j, 1, 3, 1)

        @then
        def _():
            small_end(1)
            reduce_end(1, 1)
            reduce_end(1, 0)
        back_spectrum(j, ("small",))
        back_spectrum(j, ("big",))
        back_filters(j)
        small_core(j)
        weights(j, 0, 1)
        small_plane(j)
        weights(j, 1, 0)
        plane(j, 0, 1)
        weights(j, 0, 0)
        along_z(j, 0, 2, 3)
        back_rows(j, ("small",))
        plane(j, 1, 0)

        @then
        def _():
            store_small(grad_small)
            put(3, grad_small)
        back_rows(j, ("big",))
        return 0

    lax.fori_loop(0, BLOCKS, backward, 0)
    plane(0, 0, 0)
    small_z(0)
    along_z(0, 0, 1)
    store_large(grad_large)
    put(2, grad_large)
    along_z(0, 1, 0)
    reduce_end(0, 1)
    put(6, g_w_out)
    along_z(0, 0, 0)
    reduce_end(0, 0)
    small_end(0)
    put(4, g_filters)
    put(5, g_w_in)
    put(7, g_gains)
    put(8, g_biases)
    for n in range(len(made)):
        pltpu.make_async_copy(stores[n], made[n], out_sem.at[n]).wait()
    for ops in (i0, o0, i1, o1):
        ops["e"]()
    for j in range(BLOCKS):
        pack_sent(j)
        small_sent(j)
    for a in range(2):
        for key, view in (("rc%d", s_core), ("rp%d", s_plane), ("rz%d", s_z)):
            sent(0, key % a, view.at[a])
    assert 2 * len(sending) == N_SEND and 2 * len(receiving) == N_RECEIVE, (len(sending), len(receiving))


def hand_over_kernel(*refs):
    sources, targets, between = refs[:N_OUT], refs[N_OUT : 2 * N_OUT], refs[2 * N_OUT : 3 * N_OUT]
    in_sem, out_sem = refs[3 * N_OUT :]
    ins = [pltpu.make_async_copy(a, b, in_sem.at[n]) for n, (a, b) in enumerate(zip(sources, between))]
    outs = [pltpu.make_async_copy(a, b, out_sem.at[n]) for n, (a, b) in enumerate(zip(between, targets))]
    for d in ins:
        d.start()
    for a, b in zip(ins, outs):
        a.wait()
        b.start()
    for d in outs:
        d.wait()


def fused(large_in, small_in, large_cot, small_cot, filters, w_in, w_out, gains, biases):
    large, small = large_in.shape[0], small_in.shape[0]
    rows = -(-(large * LP + small * PS) // TILE) * TILE
    early, late = [[jnp.asarray(t) for t in part] for part in constant_tables()]
    args = [jnp.swapaxes(w_in, 1, 2), w_out, filters, small_in, jnp.swapaxes(large_in, 0, 1), *early,
            jnp.swapaxes(large_cot, 0, 1), small_cot, gains, jnp.swapaxes(biases, 0, 1), *late]
    V = pltpu.VMEM
    patch_major = (large_in.shape[1], large, D)
    outs = [(patch_major, bf16), (small_in.shape, bf16), (patch_major, f32), (small_in.shape, f32), (filters.shape, f32),
            ((BLOCKS, HID, D + 1), f32), ((BLOCKS, HID, D), f32), (gains.shape, f32), ((3, BLOCKS, D), f32)]
    grid8 = (4, 2, 2, 2)
    scratch = [V(a.shape, a.dtype) for a in args] + [V(shape, dtype) for shape, dtype in outs[2:]] + [
        V((rows, D), f32), V((BLOCKS, rows, D), bf16), V((BLOCKS, rows, 128), f32), V((BLOCKS, rows, D), f32),
        V((BLOCKS, rows, 128), f32), V((BLOCKS, rows, D), bf16), V((BLOCKS, 2, rows, FF // 2), bf16),
        V((BLOCKS, 2, rows, FF // 2), bf16), V((BLOCKS, large, SPEC, D), f32), V((BLOCKS, small // Q, 2 * QF, D), f32),
        V((rows, D), bf16),
        V((BLOCKS, *grid8, HID, D), bf16), V((BLOCKS, *grid8, HID, D), bf16), V((BLOCKS, *grid8, 8, D), bf16),
        V((BLOCKS, 2 * QF, D), f32), V((BLOCKS, 2, 1, FF // 2), f32), V((BLOCKS, 3, 1, D), f32), V((rows, D), f32),
        V((BLOCKS, *grid8, 8, D), f32), V((2 * QF, D), f32), V((FLP + QF, D), f32), V((BLOCKS, 2, 8, FF // 2), f32), V((BLOCKS, 5, 8, D), f32),
        V((2, 4, 2, 2, HID, D), f32),
        V((2, 4, 2, 2, HID, D), bf16), V((2, 4, 3, HID, D), bf16), V((2, 3, HID, D), bf16),
        V((BLOCKS, 2, 4, 2, 2, HID, D), bf16), V((BLOCKS, 2, 4, 3, HID, D), bf16), V((BLOCKS, 2, 3, HID, D), bf16),
        V((BLOCKS, 4, 2, 2, 8, D), bf16), V((BLOCKS, 4, 2, 2, 8, D), bf16), V((BLOCKS, 2, 2, 4, 8, D), f32),
        V((BLOCKS, 3, 4, 8, D), bf16), V((BLOCKS, 3, 4, 8, D), bf16), V((BLOCKS, 3, 8, D), bf16), V((BLOCKS, 3, 8, D), bf16),
        V((BLOCKS, 8, D), f32), V((BLOCKS, 8, D), f32), V((BLOCKS, 2, 2, 8, D), f32), V((BLOCKS, 4, 8, D), f32),
        pltpu.SemaphoreType.DMA((N_SEND,)), pltpu.SemaphoreType.DMA((N_RECEIVE,)),
        pltpu.SemaphoreType.DMA((N_IN,)), pltpu.SemaphoreType.DMA((N_OUT,)),
    ]
    anywhere = pl.BlockSpec(memory_space=pl.ANY)
    out_shape = [jax.ShapeDtypeStruct(shape, dtype) for shape, dtype in outs]
    result = pl.pallas_call(
        partial(fused_kernel, large, small),
        out_shape=out_shape,
        in_specs=[anywhere] * N_IN,
        out_specs=[anywhere] * N_OUT,
        scratch_shapes=scratch,
        compiler_params=pltpu.CompilerParams(collective_id=0, has_side_effects=True, vmem_limit_bytes=VMEM_BYTES),
        name="gfnet_step",
    )(*args)
    out_large, out_small, grad_large, grad_small, g_filters, g_in, g_out, g_gains, g_biases = pl.pallas_call(
        hand_over_kernel,
        out_shape=out_shape,
        in_specs=[anywhere] * N_OUT,
        out_specs=[anywhere] * N_OUT,
        scratch_shapes=[V(shape, dtype) for shape, dtype in outs] + [pltpu.SemaphoreType.DMA((N_OUT,))] * 2,
        compiler_params=pltpu.CompilerParams(vmem_limit_bytes=VMEM_BYTES),
        name="hand_over",
    )(*result)
    return (jnp.swapaxes(out_large, 0, 1), out_small, jnp.swapaxes(grad_large, 0, 1), grad_small, g_filters,
            jnp.swapaxes(g_in, 1, 2), g_out, g_gains, jnp.swapaxes(g_biases, 0, 1))


def solution(mesh):
    in_specs = (
        P(("wide", "narrow"), None, None),
        P(("wide", "narrow"), None, None),
        P(("wide", "narrow"), None, None),
        P(("wide", "narrow"), None, None),
        P(None, ("wide", "narrow")),
        P(None, None, ("wide", "narrow")),
        P(None, ("wide", "narrow"), None),
        P(),
        P(),
    )
    out_specs = (
        P(("wide", "narrow"), None, None),
        P(("wide", "narrow"), None, None),
        P(("wide", "narrow"), None, None),
        P(("wide", "narrow"), None, None),
        P(None, ("wide", "narrow")),
        P(None, None, ("wide", "narrow")),
        P(None, ("wide", "narrow"), None),
        P(),
        P(),
    )
    body = fused if dict(mesh.shape) == {"wide": 8, "narrow": 4} else per_device
    return jax.shard_map(
        body, mesh=mesh, in_specs=in_specs, out_specs=out_specs, check_vma=False
    )
```

```python
from functools import partial
import math

import jax
import jax.numpy as jnp
import ml_dtypes
import numpy as np
from jax import lax
from jax.experimental import pallas as pl
from jax.experimental.pallas import tpu as pltpu
from jax.sharding import PartitionSpec as P

FF = 1536
GL = 14
GS = 6
BLOCKS = 2
MICRO = 2
PL = 196
FL = 112
FS = 24


precise = lax.Precision.HIGHEST
epsilon = 1e-06


def dft_tables(grid_cells):
    half_count = grid_cells // 2 + 1
    places = jnp.arange(grid_cells * grid_cells, dtype=jnp.int32)
    place_row = places // grid_cells
    place_col = places % grid_cells
    modes = jnp.arange(grid_cells * half_count, dtype=jnp.int32)
    mode_row = modes // half_count
    mode_col = modes % half_count
    phases = (
        mode_row[:, None] * place_row[None, :] + mode_col[:, None] * place_col[None, :]
    ) % grid_cells
    angles = phases.astype(jnp.float32) * (2.0 * math.pi / grid_cells)
    forward_re = jnp.cos(angles) / grid_cells
    forward_im = -jnp.sin(angles) / grid_cells
    doubling = jnp.where((mode_col == 0) | (2 * mode_col == grid_cells), 1.0, 2.0).astype(
        jnp.float32
    )
    inverse_re = jnp.transpose(forward_re * doubling[:, None])
    inverse_im = jnp.transpose(forward_im * doubling[:, None])
    return (forward_re, forward_im, inverse_re, inverse_im)


def linear_map(size_out, size_in):
    rows_out = jnp.arange(size_out, dtype=jnp.int32)
    spans = rows_out * (size_in - 1)
    lower = spans // (size_out - 1)
    fraction = (spans - lower * (size_out - 1)).astype(jnp.float32) / (size_out - 1)
    columns = jnp.arange(size_in, dtype=jnp.int32)
    first = jnp.where(columns[None, :] == lower[:, None], 1.0 - fraction[:, None], 0.0)
    second = jnp.where(columns[None, :] == lower[:, None] + 1, fraction[:, None], 0.0)
    return first + second


def shrink_map():
    along_rows = linear_map(GS, GL)
    along_cols = linear_map(GS // 2 + 1, GL // 2 + 1)
    return (along_rows[:, None, :, None] * along_cols[None, :, None, :]).reshape(FS, FL)


def filter_grid(patches, tables, filt_re, filt_im):
    forward_re, forward_im, inverse_re, inverse_im = tables
    spec_re = jnp.einsum("fp,bpd->bfd", forward_re, patches, precision=precise)
    spec_im = jnp.einsum("fp,bpd->bfd", forward_im, patches, precision=precise)
    out_re = spec_re * filt_re - spec_im * filt_im
    out_im = spec_re * filt_im + spec_im * filt_re
    back_re = jnp.einsum("pf,bfd->bpd", inverse_re, out_re, precision=precise)
    back_im = jnp.einsum("pf,bfd->bpd", inverse_im, out_im, precision=precise)
    return back_re + back_im


def spectral(normed, large_rows, filt_re, filt_im):
    width = normed.shape[-1]
    shrink = shrink_map()
    small_re = jnp.dot(shrink, filt_re, precision=precise, preferred_element_type=jnp.float32)
    small_im = jnp.dot(shrink, filt_im, precision=precise, preferred_element_type=jnp.float32)
    part_large = filter_grid(
        normed[:large_rows].reshape(-1, GL * GL, width), dft_tables(GL), filt_re, filt_im
    )
    part_small = filter_grid(
        normed[large_rows:].reshape(-1, GS * GS, width), dft_tables(GS), small_re, small_im
    )
    return jnp.concatenate([part_large.reshape(-1, width), part_small.reshape(-1, width)], 0)


def layer_norm(stream, gain, shift):
    centre = stream - jnp.mean(stream, axis=-1, keepdims=True)
    spread = jnp.mean(centre * centre, axis=-1, keepdims=True)
    return centre * lax.rsqrt(spread + epsilon) * gain + shift


def per_device(large_in, small_in, large_cot, small_cot, filters, w_in, w_out, gains, biases):
    width = large_in.shape[-1]
    micro_large = large_in.shape[0] // MICRO
    micro_small = small_in.shape[0] // MICRO
    large_rows = micro_large * PL
    exact_gelu = partial(jax.nn.gelu, approximate=False)

    def fetch(layer_index, forward):
        if forward:
            return (
                lax.all_gather(filters[layer_index], ("wide", "narrow"), axis=0, tiled=True),
                lax.all_gather(w_in[layer_index], ("wide", "narrow"), axis=1, tiled=True),
                lax.all_gather(w_out[layer_index], ("wide", "narrow"), axis=0, tiled=True),
            )
        return (
            lax.all_gather(filters[layer_index], ("wide", "narrow"), axis=0, tiled=True),
            lax.all_gather(w_in[layer_index], ("wide", "narrow"), axis=1, tiled=True),
            lax.all_gather(w_out[layer_index], ("wide", "narrow"), axis=0, tiled=True),
        )

    def branch_first(stream, gain, shift, filt_re, filt_im):
        return spectral(layer_norm(stream, gain, shift), large_rows, filt_re, filt_im)

    acc_filter = [jnp.zeros((2, FL, width), jnp.float32) for layer_index in range(BLOCKS)]
    acc_in = [jnp.zeros((width, FF), jnp.float32) for layer_index in range(BLOCKS)]
    acc_in_bias = [jnp.zeros((FF,), jnp.float32) for layer_index in range(BLOCKS)]
    acc_out = [jnp.zeros((FF, width), jnp.float32) for layer_index in range(BLOCKS)]
    acc_gain = [jnp.zeros((2, width), jnp.float32) for layer_index in range(BLOCKS)]
    acc_shift = [jnp.zeros((3, width), jnp.float32) for layer_index in range(BLOCKS)]
    outs_large, outs_small, grads_large, grads_small = ([], [], [], [])
    for micro_step in range(MICRO):
        large_part = large_in[micro_step * micro_large : (micro_step + 1) * micro_large]
        small_part = small_in[micro_step * micro_small : (micro_step + 1) * micro_small]
        stream = jnp.concatenate(
            [large_part.reshape(-1, width), small_part.reshape(-1, width)], 0
        ).astype(jnp.float32)
        saved = []
        for layer_index in range(BLOCKS):
            filt_full, in_full, out_full = fetch(layer_index, True)
            halves = filt_full.reshape(2, FL, width).astype(jnp.float32)
            mixed = stream + branch_first(
                stream, gains[layer_index, 0], biases[layer_index, 0], halves[0], halves[1]
            )
            second = layer_norm(mixed, gains[layer_index, 1], biases[layer_index, 1]).astype(
                jnp.bfloat16
            )
            pre_act = jnp.dot(
                second, in_full[:width], preferred_element_type=jnp.float32
            ) + in_full[width].astype(jnp.float32)
            active = exact_gelu(pre_act).astype(jnp.bfloat16)
            saved.append((stream, mixed, second, pre_act))
            stream = (
                mixed
                + jnp.dot(active, out_full, preferred_element_type=jnp.float32)
                + biases[layer_index, 2]
            )
        outs_large.append(stream[:large_rows].reshape(large_part.shape).astype(jnp.bfloat16))
        outs_small.append(stream[large_rows:].reshape(small_part.shape).astype(jnp.bfloat16))
        large_back = large_cot[micro_step * micro_large : (micro_step + 1) * micro_large]
        small_back = small_cot[micro_step * micro_small : (micro_step + 1) * micro_small]
        grad = jnp.concatenate(
            [large_back.reshape(-1, width), small_back.reshape(-1, width)], 0
        ).astype(jnp.float32)
        for layer_index in reversed(range(BLOCKS)):
            block_input, mixed, second, pre_act = saved[layer_index]
            filt_full, in_full, out_full = fetch(layer_index, False)
            halves = filt_full.reshape(2, FL, width).astype(jnp.float32)
            grad_low = grad.astype(jnp.bfloat16)
            active, gelu_back = jax.vjp(exact_gelu, pre_act)
            active = active.astype(jnp.bfloat16)
            acc_out[layer_index] = acc_out[layer_index] + jnp.einsum(
                "tf,td->fd", active, grad_low, preferred_element_type=jnp.float32
            )
            bias_out_grad = jnp.sum(grad, axis=0)
            active_grad = jnp.einsum(
                "td,fd->tf", grad_low, out_full, preferred_element_type=jnp.float32
            )
            pre_grad = gelu_back(active_grad)[0]
            pre_low = pre_grad.astype(jnp.bfloat16)
            acc_in[layer_index] = acc_in[layer_index] + jnp.einsum(
                "td,tf->df", second, pre_low, preferred_element_type=jnp.float32
            )
            acc_in_bias[layer_index] = acc_in_bias[layer_index] + jnp.sum(pre_grad, axis=0)
            second_grad = jnp.einsum(
                "tf,df->td", pre_low, in_full[:width], preferred_element_type=jnp.float32
            )
            unused, norm_back = jax.vjp(
                layer_norm, mixed, gains[layer_index, 1], biases[layer_index, 1]
            )
            mixed_part, gain_two, shift_two = norm_back(second_grad)
            mixed_grad = grad + mixed_part
            unused, first_back = jax.vjp(
                branch_first,
                block_input,
                gains[layer_index, 0],
                biases[layer_index, 0],
                halves[0],
                halves[1],
            )
            input_part, gain_one, shift_one, filt_re_grad, filt_im_grad = first_back(mixed_grad)
            grad = mixed_grad + input_part
            acc_filter[layer_index] = acc_filter[layer_index] + jnp.stack(
                [filt_re_grad, filt_im_grad], 0
            )
            acc_gain[layer_index] = acc_gain[layer_index] + jnp.stack([gain_one, gain_two], 0)
            acc_shift[layer_index] = acc_shift[layer_index] + jnp.stack(
                [shift_one, shift_two, bias_out_grad], 0
            )
        grads_large.append(grad[:large_rows].reshape(large_part.shape))
        grads_small.append(grad[large_rows:].reshape(small_part.shape))
    filter_shards, in_shards, out_shards = ([], [], [])
    for layer_index in range(BLOCKS):
        in_whole = jnp.concatenate([acc_in[layer_index], acc_in_bias[layer_index][None, :]], 0)
        filter_piece, in_piece, out_piece = (
            lax.psum_scatter(
                acc_filter[layer_index].reshape(-1),
                ("wide", "narrow"),
                scatter_dimension=0,
                tiled=True,
            ),
            lax.psum_scatter(in_whole, ("wide", "narrow"), scatter_dimension=1, tiled=True),
            lax.psum_scatter(
                acc_out[layer_index], ("wide", "narrow"), scatter_dimension=0, tiled=True
            ),
        )
        filter_shards.append(filter_piece)
        in_shards.append(in_piece)
        out_shards.append(out_piece)
    gain_total, shift_total = lax.psum(
        (jnp.stack(acc_gain, 0), jnp.stack(acc_shift, 0)), ("wide", "narrow")
    )
    return (
        jnp.concatenate(outs_large, 0),
        jnp.concatenate(outs_small, 0),
        jnp.concatenate(grads_large, 0),
        jnp.concatenate(grads_small, 0),
        jnp.stack(filter_shards, 0),
        jnp.stack(in_shards, 0),
        jnp.stack(out_shards, 0),
        gain_total,
        shift_total,
    )


MESH_ID = pl.DeviceIdType.MESH
bf16, f32 = jnp.bfloat16, jnp.float32
D, PS, EPS = 384, 36, 1e-6
LP = 208
Q = 4
SR = Q * PS
TILE = 256
BOTH = ("big", "small")
HID = 48
FLP = 128
SPEC = 2 * FLP
QF = Q * FS


def dft_arrays(n):
    half = n // 2 + 1
    places, modes = np.arange(n * n), np.arange(n * half)
    phase = ((modes // half)[:, None] * (places // n)[None] + (modes % half)[:, None] * (places % n)[None]) % n
    theta = phase * (2 * math.pi / n)
    fwd_re, fwd_im = np.cos(theta) / n, -np.sin(theta) / n
    weight = np.where((modes % half == 0) | (2 * (modes % half) == n), 1.0, 2.0)
    return fwd_re, fwd_im, fwd_re * weight[:, None], fwd_im * weight[:, None]


def interpolation(rows, cols):
    span = np.arange(rows) * (cols - 1)
    low = span // (rows - 1)
    part = (span - low * (rows - 1)) / (rows - 1)
    at = np.arange(cols)[None]
    return np.where(at == low[:, None], 1 - part[:, None], 0.0) + np.where(at == low[:, None] + 1, part[:, None], 0.0)


def two_terms(table):
    table = np.asarray(table, np.float32)
    high = table.astype(ml_dtypes.bfloat16)
    low = (table - high.astype(np.float32)).astype(ml_dtypes.bfloat16)
    return np.concatenate([high, low], 0)


def constant_tables():
    pos = np.arange(FL) // 7 * 8 + np.arange(FL) % 7
    rows = np.concatenate([pos, FLP + pos])
    fr, fi, ir, ii = dft_arrays(GL)
    fwd, inv = np.zeros((SPEC, LP)), np.zeros((SPEC, LP))
    fwd[rows, :PL], inv[rows, :PL] = np.concatenate([fr, fi]), np.concatenate([ir, ii])
    fr, fi, ir, ii = dft_arrays(GS)
    sfwd, sinv = np.zeros((2 * QF, SR)), np.zeros((2 * QF, SR))
    for q in range(Q):
        at = slice(q * PS, (q + 1) * PS)
        for half, a, b in ((0, fr, ir), (1, fi, ii)):
            to = slice(half * QF + q * FS, half * QF + (q + 1) * FS)
            sfwd[to, at], sinv[to, at] = a, b
    shrink = np.zeros((FS, FLP))
    shrink[:, pos] = (
        interpolation(GS, GL)[:, None, :, None] * interpolation(GS // 2 + 1, GL // 2 + 1)[None, :, None, :]
    ).reshape(FS, FL)
    piece = np.arange(32)
    pick = np.zeros((64, SPEC))
    pick[piece % 8 * 8 + piece // 8, 8 * piece + 7] = 1
    return [two_terms(t) for t in (fwd, sfwd)], [
        two_terms(shrink), pick.astype(ml_dtypes.bfloat16), two_terms(inv.T), two_terms(sinv.T), two_terms(shrink.T)]


def mm(a, b):
    return lax.dot_general(a, b, (((1,), (0,)), ((), ())), preferred_element_type=f32)


def mm_nt(a, b):
    return lax.dot_general(a, b, (((1,), (1,)), ((), ())), preferred_element_type=f32)


def mm_tn(a, b):
    return lax.dot_general(a, b, (((0,), (0,)), ((), ())), preferred_element_type=f32)


def halves(v):
    high = v.astype(bf16)
    return high, (v - high.astype(f32)).astype(bf16)


def apply_table(table, v):
    rows = table.shape[0] // 2
    high, low = halves(v)
    both = mm(table, high)
    return both[:rows] + both[rows:] + mm(table[:rows], low)


def standardize(v):
    centre = v - jnp.sum(v, -1, keepdims=True) * (1.0 / D)
    r = lax.rsqrt(jnp.sum(centre * centre, -1, keepdims=True) * (1.0 / D) + EPS)
    return centre * r, r


def norm_back(vh, r, q):
    mean_q = jnp.sum(q, -1, keepdims=True) * (1.0 / D)
    mean_qv = jnp.sum(q * vh, -1, keepdims=True) * (1.0 / D)
    return r * (q - mean_q - vh * mean_qv)


def fold(v):
    return jnp.sum(v.reshape(v.shape[0] // 8, 8, v.shape[1]), 0)


def aligned(v, m):
    return v if isinstance(v, int) else pl.multiple_of(v, m)


N_SEND, N_RECEIVE = 46, 102
VMEM_BYTES = 63 << 20


N_IN, N_OUT = 16, 9


def fused_kernel(large, small, *refs):
    given, made, refs = refs[:N_IN], refs[N_IN : N_IN + N_OUT], refs[N_IN + N_OUT :]
    held, refs = refs[:N_IN], refs[N_IN:]
    (raw_in, raw_out, raw_filters, small_rows, large_rows, t_fwd, t_sfwd, cot_large, cot_small, gains, biases,
     t_shrink, t_pick, t_inv, t_sinv, t_shrink_t) = held
    (grad_large, grad_small, g_filters, g_w_in, g_w_out, g_gains, g_biases,
     xs, vh1, r1, vh2, r2, second, active, slope, sv_large, sv_small, grad_low,
     w_in, w_out, pack, filt_s, b_in, shift, back, facc, sacc, gacc, bacc, vacc,
     kept, s_core, s_plane, s_z, r_core, r_plane, r_z,
     f_own, f_core, f_keep, f_send, f_xy, f_z_send, f_z, v_send, v_core, v_xy, v_z,
     send_sem, recv_sem, in_sem, out_sem) = refs
    rows = xs.shape[0]
    groups = small // Q
    base = large * LP
    wide, narrow = lax.axis_index("wide"), lax.axis_index("narrow")
    z, x, y, c = lax.div(wide, 2), lax.rem(wide, 2), lax.div(narrow, 2), lax.rem(narrow, 2)
    other = {"x": 1 - x, "y": 1 - y, "c": 1 - c}
    at = lambda zz, xx, yy, cc: (zz * 2 + xx, yy * 2 + cc)
    z_pair = {0: z, 1: z + 1 - 2 * lax.rem(z, 2), 2: lax.rem(z + 2, 4), 3: 3 - z}
    z_of = lambda k: z_pair[k]
    peer = {"x": at(z, 1 - x, y, c), "y": at(z, x, 1 - y, c), "xy": at(z, 1 - x, 1 - y, c), "c": at(z, x, y, 1 - c)}
    for k in (1, 2, 3):
        peer[k] = at(z_of(k), x, y, c)

    sending, receiving = {}, {}

    def send(j, key, src, dst, to, part=None):
        out = 2 * sending.setdefault(key, len(sending)) + j
        back = key if part is None else (key, part)
        pltpu.make_async_remote_copy(
            src_ref=src, dst_ref=dst, send_sem=send_sem.at[out],
            recv_sem=recv_sem.at[2 * receiving.setdefault(back, len(receiving)) + j],
            device_id=peer[to], device_id_type=MESH_ID).start()

    def arrived(j, key, view, part=None):
        back = key if part is None else (key, part)
        sem = recv_sem.at[2 * receiving.setdefault(back, len(receiving)) + j]
        pltpu.make_async_copy(view, view, sem).wait()

    def sent(j, key, view):
        pltpu.make_async_copy(view, view, send_sem.at[2 * sending.setdefault(key, len(sending)) + j]).wait()

    PLANE = [("xy", 1 - x, 1 - y), ("x", 1 - x, y), ("y", x, 1 - y)]
    half_z = lax.div(z, 2)
    pair = lambda near: pl.ds(2 * (half_z if near else 1 - half_z), 2)

    def gather_ops(j, name):
        ref = w_in if name == "in" else w_out
        three = ref.at[j, 0:3, x, y, c]

        def z_send():
            mine = ref.at[j, z, x, y, c]
            for k in (1, 2, 3):
                send(j, name + "z", mine, mine, k, part=k == 1)

        def z_wait(near):
            arrived(j, name + "z", ref.at[j, 0 : 1 if near else 2, x, y, c], near)

        def plane_send(*ks):
            for k in ks:
                piece = ref.at[j, z_of(k), x, y, c]
                for to, _, _ in PLANE:
                    send(j, name + "p", piece, piece, to, part=k)

        def plane_wait(*ks):
            for k in ks:
                arrived(j, name + "p", three, k)

        def first_send(*ks):
            for k in ks:
                piece = ref.at[j, z_of(k), x, y, c]
                send(j, name + "f", piece, piece, "xy"[k % 2], part=k)

        def second_send(*ks):
            for k in ks:
                zz = z_of(k)
                arrived(j, name + "f", ref.at[j, zz, x, y, c], k)
                piece = ref.at[j, zz, x, :, c] if k % 2 else ref.at[j, zz, :, y, c]
                send(j, name + "p", piece, piece, "yx"[k % 2], part=k)

        def second_wait(*ks):
            for k in ks:
                arrived(j, name + "p", ref.at[j, z_of(k), x, :, c], k)

        def core_send(near):
            piece = ref.at[j, pair(near), :, :, c]
            send(j, name + "c", piece, piece, "c", part=near)

        def core_wait(near):
            arrived(j, name + "c", ref.at[j, pair(near), :, :, 1 - c], near)

        def all_sent():
            sent(j, name + "z", three)
            if j:
                sent(j, name + "f", ref.at[j, :, x, y, c])
                sent(j, name + "p", ref.at[j, :, x, :, c])
            else:
                sent(j, name + "p", ref.at[j, 0:3, :, :, c])
            sent(j, name + "c", ref.at[j, :, :, :, c])

        return dict(z=z_send, zw=z_wait, p=plane_send, pw=plane_wait, f=first_send, s=second_send, sw=second_wait,
                    c=core_send, cw=core_wait, e=all_sent)

    def pack_z(j):
        mine = pack.at[j, z, x, y, c]
        for k in (1, 2, 3):
            send(j, "pz", mine, mine, k)

    def pack_plane(j):
        arrived(j, "pz", pack.at[j, 0:3, x, y, c])
        piece = pack.at[j, :, x, y, c]
        for to, _, _ in PLANE:
            send(j, "pp", piece, piece, to)

    def pack_core(j):
        arrived(j, "pp", pack.at[j, 0:3, :, :, c])
        piece = pack.at[j, :, :, :, c]
        send(j, "pc", piece, piece, "c")

    def pack_wait(j):
        arrived(j, "pc", pack.at[j, :, :, :, 1 - c])

    def pack_sent(j):
        sent(j, "pz", pack.at[j, 0:3, x, y, c])
        sent(j, "pp", pack.at[j, 0:3, :, :, c])
        sent(j, "pc", pack.at[j, :, :, :, c])

    def clear(j, a, k, key, view):
        if k == 2:
            @pl.when(j == 0)
            def _():
                sent(1, key, view)

    def reduce_core(j, a, k, value):
        clear(j, a, k, "rc%d" % a, s_core.at[a])
        for n in range(4):
            even, odd = value[2 * n * HID : (2 * n + 1) * HID], value[(2 * n + 1) * HID : (2 * n + 2) * HID]
            kept[a, k, n // 2, n % 2] = jnp.where(c == 0, even, odd)
            s_core[a, k, n // 2, n % 2] = jnp.where(c == 0, odd, even).astype(bf16)
        send(j, "rc%d" % a, s_core.at[a, k], r_core.at[j, a, k], "c", k)

    def reduce_plane(j, a, k):
        arrived(j, "rc%d" % a, r_core.at[j, a, k], k)
        if not isinstance(j, int):
            clear(j, a, k, "rp%d" % a, s_plane.at[a])
        for n, (to, xx, yy) in enumerate(PLANE):
            s_plane[a, k, n] = (kept[a, k, xx, yy] + r_core[j, a, k, xx, yy].astype(f32)).astype(bf16)
            send(j, "rp%d" % a, s_plane.at[a, k, n], r_plane.at[j, a, k, n], to, k)

    def reduce_z(j, a, k):
        s = kept[a, k, x, y] + r_core[j, a, k, x, y].astype(f32)
        arrived(j, "rp%d" % a, r_plane.at[j, a, k], k)
        for n in range(3):
            s = s + r_plane[j, a, k, n].astype(f32)
        if k:
            if not isinstance(j, int):
                clear(j, a, k, "rz%d" % a, s_z.at[a])
            s_z[a, k - 1] = s.astype(bf16)
            send(j, "rz%d" % a, s_z.at[a, k - 1], r_z.at[j, a, k - 1], k)
        elif a == 0:
            g_w_in[j, :, :D] = s
        else:
            g_w_out[j] = s

    def reduce_end(j, a):
        arrived(j, "rz%d" % a, r_z.at[j, a])
        s = r_z[j, a, 0].astype(f32) + r_z[j, a, 1].astype(f32) + r_z[j, a, 2].astype(f32)
        if a == 0:
            g_w_in[j, :, :D] += s
        else:
            g_w_out[j] += s

    def small_core(j):
        for zz in range(4):
            for i in range(2):
                for l in range(2):
                    f_own[j, zz, i, l] = facc[j, zz, i, l, 1 - c].astype(bf16)
        send(j, "fc", f_own.at[j], f_core.at[j], "c")
        v_send[j] = jnp.concatenate([jnp.sum(vacc[j, i], 0, keepdims=True) for i in range(5)] + [jnp.zeros((3, D), f32)], 0)
        send(j, "vc", v_send.at[j], v_core.at[j], "c")

    def small_plane(j):
        arrived(j, "fc", f_core.at[j])
        for zz in range(4):
            for i in range(2):
                for l in range(2):
                    f_keep[j, i, l, zz] = facc[j, zz, i, l, c] + f_core[j, zz, i, l].astype(f32)
        for n, (to, xx, yy) in enumerate(PLANE):
            f_send[j, n] = f_keep[j, xx, yy].astype(bf16)
            send(j, "fp", f_send.at[j, n], f_xy.at[j, n], to)
        arrived(j, "vc", v_core.at[j])
        v_z[j, z] = v_send[j] + v_core[j]
        mine = v_z.at[j, z]
        for k in (1, 2, 3):
            send(j, "vz", mine, mine, k)

    def small_z(j):
        s = f_keep[j, x, y]
        arrived(j, "fp", f_xy.at[j])
        for n in range(3):
            s = s + f_xy[j, n].astype(f32)
        f_keep[j, x, y] = s
        for k in (1, 2, 3):
            f_z_send[j, k - 1] = f_keep[j, x, y, z_of(k)].astype(bf16)
            send(j, "fz", f_z_send.at[j, k - 1], f_z.at[j, k - 1], k)
        arrived(j, "vz", v_z.at[j, 0:3])
        v_xy[j, x, y] = v_z[j, 0] + v_z[j, 1] + v_z[j, 2] + v_z[j, 3]
        mine = v_xy.at[j, x, y]
        for to, _, _ in PLANE:
            send(j, "vp", mine, mine, to)

    def small_end(j):
        arrived(j, "fz", f_z.at[j])
        s = f_keep[j, x, y, z] + f_z[j, 0].astype(f32) + f_z[j, 1].astype(f32) + f_z[j, 2].astype(f32)
        for r in range(7):
            g_filters[j : j + 1, r * D : (r + 1) * D] = s[r : r + 1]
        g_w_in[j, :, D:] = jnp.sum(jnp.where(diagonal(), s[7:8, :128], 0.0), 1, keepdims=True)
        arrived(j, "vp", v_z.at[j, 0:3])
        v = v_xy[j, 0, 0] + v_xy[j, 0, 1] + v_xy[j, 1, 0] + v_xy[j, 1, 1]
        g_gains[j] = v[0:2]
        for l in range(3):
            g_biases[l, j : j + 1] = v[2 + l : 3 + l]

    def small_sent(j):
        for key, view in (("fc", f_own), ("vc", v_send), ("fp", f_send), ("fz", f_z)):
            sent(j, key, view.at[j])
        for key in ("vp", "vz"):
            sent(j, key, v_z.at[j, 0:3])

    def diagonal():
        shape = (HID, 128)
        return lax.broadcasted_iota(jnp.int32, shape, 0) == lax.broadcasted_iota(jnp.int32, shape, 1)

    def load_rows(dst, a, b):
        v = jnp.swapaxes(a[...], 0, 1).astype(dst.dtype)
        for i in range(large):
            dst[i * LP + LP - 16 : (i + 1) * LP, :] = jnp.zeros((16, D), dst.dtype)
            dst[i * LP : i * LP + PL, :] = v[i]
        for i in range(small):
            dst[base + i * PS : base + (i + 1) * PS, :] = b[i].astype(dst.dtype)
        dst[base + small * PS :, :] = jnp.zeros((rows - base - small * PS, D), dst.dtype)

    def store_large(a):
        v = jnp.concatenate([xs[i * LP : i * LP + PL, :][None] for i in range(large)], 0)
        a[...] = jnp.swapaxes(v, 0, 1).astype(a.dtype)

    def store_small(b):
        for i in range(small):
            b[i] = xs[base + i * PS : base + (i + 1) * PS, :].astype(b.dtype)

    def own_pieces():
        for j in range(BLOCKS):
            w_in[j, z, x, y, c] = raw_in[j, :, :D]
            w_out[j, z, x, y, c] = raw_out[j]
            bias = jnp.sum(jnp.where(diagonal(), raw_in[j, :, D:].astype(f32), 0.0), 0, keepdims=True)
            row = raw_filters[j : j + 1, :].astype(f32)
            parts = [row[:, r * D : (r + 1) * D] for r in range(7)]
            parts.append(jnp.concatenate([bias, jnp.zeros((1, D - 128), f32)], 1))
            pack[j, z, x, y, c] = jnp.concatenate(parts, 0).astype(bf16)

    fetches = [pltpu.make_async_copy(a, b, in_sem.at[n]) for n, (a, b) in enumerate(zip(given, held))]
    stores = {}

    def fetched(*which):
        for n in which:
            fetches[n].wait()

    def put(n, value):
        pltpu.make_async_copy(value, made[n], out_sem.at[n]).start()
        stores[n] = value

    def spread_rows(r):
        return jnp.broadcast_to(r, (r.shape[0], 128))

    def wide_rows(r):
        return jnp.concatenate([r, r, r], -1)

    def first_row(scale):
        return jnp.where(lax.broadcasted_iota(jnp.int32, (8, 1), 0) == 0, float(scale), 0.0)

    def column_weights(big):
        row = lax.broadcasted_iota(jnp.int32, (FLP if big else QF, 1), 0)
        column = lax.rem(lax.rem(row, 8) + 16 - lax.div(row, 8), 8) if big else lax.rem(row, 4)
        return jnp.where((column == 0) | (column == (GL if big else GS) // 2), 1.0, 2.0)

    def crop_loops(body, which):
        if "big" in which:
            for i in range(large):
                body(pl.ds(i * LP, LP), i, True)
        if "small" in which:
            for i in range(groups):
                body(pl.ds(base + i * SR, SR), i, False)

    def to_spectrum(j, which=BOTH):
        def body(o, i, big):
            vh, r = standardize(xs[o, :])
            vh1[j, o, :] = vh.astype(bf16)
            r1[j, o, :] = spread_rows(r)
            if big:
                sv_large[j, i] = apply_table(t_fwd[...], vh)
            else:
                sv_small[j, i] = apply_table(t_sfwd[...], vh)
        crop_loops(body, which)

    def unpack_filters(j):
        f = pack[j].reshape(SPEC, D)
        for h in range(2):
            s = mm(t_shrink[...], f[h * FLP : (h + 1) * FLP])
            s = s[:FS] + s[FS:]
            filt_s[j, h * QF : (h + 1) * QF] = jnp.concatenate([s] * Q, 0)
        bias = mm(t_pick[...], f[:, :128])
        bias = jnp.where(lax.broadcasted_iota(jnp.int32, (64, 128), 1) < HID, bias, 0.0)
        total = jnp.zeros((8, D), f32)
        for i in range(8):
            part = jnp.concatenate([bias[8 * i : 8 * i + 8], jnp.zeros((8, D - 128), f32)], 1)
            total = total + (pltpu.roll(part, HID * i, 1) if i else part)
        for h in range(2):
            b_in[j, h] = jnp.concatenate([total[2 * h : 2 * h + 1], total[2 * h + 1 : 2 * h + 2]], 1)

    def spectrum_of(j, i, big):
        sv = sv_large[j, i] if big else sv_small[j, i]
        h, period = (FLP, FLP) if big else (QF, FS)
        re, im = sv[:h] * gains[j, 0:1, :], sv[h:] * gains[j, 0:1, :]
        mean = first_row(GL if big else GS) * shift[j, 0]
        parts = []
        for n in range(0, h, period):
            parts += [re[n : n + 8] + mean, re[n + 8 : n + period]]
        f = pack[j].reshape(SPEC, D).astype(f32) if big else filt_s[j]
        return sv, jnp.concatenate(parts, 0), im, f[:h], f[h:]

    def from_spectrum(j, which=BOTH):
        def body(o, i, big):
            _, re, im, fr, fi = spectrum_of(j, i, big)
            out = jnp.concatenate([re * fr - im * fi, re * fi + im * fr], 0)
            xs[o, :] = xs[o, :] + apply_table(t_inv[...] if big else t_sinv[...], out)
        crop_loops(body, which)

    def tiles(body):
        for t in range(rows // TILE):
            body(pl.ds(t * TILE, TILE))

    def expand(j, h, first):
        def body(o):
            if first:
                vh, r = standardize(xs[o, :])
                vh2[j, o, :] = vh
                r2[j, o, :] = spread_rows(r)
                s = (vh * gains[j, 1:2, :] + shift[j, 1]).astype(bf16)
                second[j, o, :] = s
            else:
                s = second[j, o, :]
            pre = mm_nt(s, w_in[j, pl.ds(2 * h, 2)].reshape(FF // 2, D)) + b_in[j, h]
            phi = 0.5 + 0.5 * lax.erf(pre * (1 / math.sqrt(2)))
            active[j, h, o, :] = (pre * phi).astype(bf16)
            slope[j, h, o, :] = (phi + pre * (jnp.exp(-0.5 * pre * pre) * (1 / math.sqrt(2 * math.pi)))).astype(bf16)
        tiles(body)

    def contract(j):
        def body(o):
            s = xs[o, :] + shift[j, 2]
            for h in range(2):
                s = s + mm(active[j, h, o, :], w_out[j, 2 * h : 2 * h + 2].reshape(FF // 2, D))
            xs[o, :] = s
        tiles(body)

    def z_offset(k):
        zz = z_of(k)
        return lax.div(zz, 2), pl.ds(aligned(lax.rem(zz, 2) * (FF // 4), 128), FF // 4)

    def back_hidden(j, h, last):
        def body(o):
            w = w_out[j, pl.ds(2 * h, 2)].reshape(FF // 2, D)
            pg = mm_nt(grad_low[o, :], w) * slope[j, h, o, :].astype(f32)
            bacc[j, h] += fold(pg)
            p = pg.astype(bf16)
            slope[j, h, o, :] = p
            sg = mm(p, w_in[j, pl.ds(2 * h, 2)].reshape(FF // 2, D))
            if not last:
                back[o, :] = sg
            else:
                sg = sg + back[o, :]
                vh = vh2[j, o, :]
                vacc[j, 1] += fold(sg * vh)
                vacc[j, 3] += fold(sg)
                xs[o, :] = xs[o, :] + norm_back(vh, wide_rows(r2[j, o, :]), sg * gains[j, 1:2, :])
        tiles(body)

    def weight_in(j, k):
        h, lanes = z_offset(k)
        return mm_tn(slope[j, h, :, lanes], second[j])

    def weight_out(j, k):
        h, lanes = z_offset(k)
        return mm_tn(active[j, h, :, lanes], grad_low[...])

    def back_spectrum(j, which):
        if which == ("small",):
            sacc[...] = jnp.zeros_like(sacc)
            gacc[...] = jnp.zeros_like(gacc)
        else:
            facc[j] = jnp.zeros(facc.shape[1:], f32)

        def body(o, i, big):
            sv, re, im, fr, fi = spectrum_of(j, i, big)
            h, period = (FLP, FLP) if big else (QF, FS)
            sg = apply_table(t_fwd[...] if big else t_sfwd[...], xs[o, :])
            gr, gi = sg[:h], sg[h:]
            d_re, d_im = re * gr + im * gi, re * gi - im * gr
            if big:
                facc[j] += jnp.concatenate([d_re, d_im], 0).reshape(4, 2, 2, 2, 8, D)
            else:
                sacc[...] += jnp.concatenate([d_re, d_im], 0)
            n_re, n_im = gr * fr + gi * fi, gi * fr - gr * fi
            first = 0 if big else FLP
            gacc[first : first + h] += n_re * sv[:h] + n_im * sv[h:]
            mean = n_re[:8]
            for n in range(period, h, period):
                mean = mean + n_re[n : n + 8]
            vacc[j, 2] += mean * first_row(GL if big else GS)
            n = jnp.concatenate([n_re, n_im], 0)
            if big:
                sv_large[j, i] = n
            else:
                sv_small[j, i] = n
        crop_loops(body, which)

    def back_filters(j):
        w, ws = column_weights(True), column_weights(False)
        vacc[j, 0] = fold(gacc[:FLP] * w) + fold(gacc[FLP:] * ws)
        for h in range(2):
            s = sacc[h * QF : (h + 1) * QF] * ws
            s = s[:FS] + s[FS : 2 * FS] + s[2 * FS : 3 * FS] + s[3 * FS :]
            total = facc[j, 2 * h : 2 * h + 2].reshape(FLP, D) * w + apply_table(t_shrink_t[...], s)
            facc[j, 2 * h : 2 * h + 2] = total.reshape(2, 2, 2, 2, 8, D)
        row = [jnp.sum(bacc[j, h], 0, keepdims=True) for h in range(2)]
        row = jnp.concatenate([row[0][:, :D], row[0][:, D:], row[1][:, :D], row[1][:, D:], jnp.zeros((4, D), f32)], 0)
        mine = lax.broadcasted_iota(jnp.int32, (8, 128), 1) < HID
        for i in range(8):
            part = jnp.where(mine, (pltpu.roll(row, D - HID * i, 1) if i else row)[:, :128], 0.0)
            for g in range(4):
                facc[j, g, i // 4, i // 2 % 2, i % 2, 7:8, :128] = part[g : g + 1]

    def back_rows(j, which=BOTH):
        def body(o, i, big):
            n = sv_large[j, i] if big else sv_small[j, i]
            ng = apply_table(t_inv[...] if big else t_sinv[...], n)
            xs[o, :] = xs[o, :] + norm_back(vh1[j, o, :].astype(f32), wide_rows(r1[j, o, :]), ng * gains[j, 0:1, :])
        crop_loops(body, which)

    i0, o0 = gather_ops(0, "in"), gather_ops(0, "out")
    i1, o1 = gather_ops(1, "in"), gather_ops(1, "out")
    barrier = pltpu.get_barrier_semaphore()
    for to in peer.values():
        pl.semaphore_signal(barrier, 1, device_id=to, device_id_type=MESH_ID)
    for d in fetches:
        d.start()
    fetched(0, 1, 2)
    own_pieces()
    pl.semaphore_wait(barrier, len(peer))

    pack_z(0)
    i0["p"](0)
    i0["z"]()
    bacc[...] = jnp.zeros_like(bacc)
    vacc[...] = jnp.zeros_like(vacc)
    fetched(3, 4, 5, 6)
    load_rows(xs, large_rows, small_rows)

    def forward(j, _):
        first, then = (lambda f: pl.when(j == 0)(f)), (lambda f: pl.when(j == 1)(f))
        to_spectrum(j, ("big",))

        @first
        def _():
            pack_plane(0)
            i0["zw"](True)
            i0["p"](1)
            o0["z"]()
        to_spectrum(j, ("small",))

        @first
        def _():
            i0["zw"](False)
            i0["p"](2, 3)
            o0["p"](0)
            pack_z(1)
            fetched(*range(7, N_IN))
            for l in range(BLOCKS):
                for i in range(3):
                    shift[l, i] = biases[i, l : l + 1, :]
            load_rows(grad_low, cot_large, cot_small)

            def cot_sum(o):
                vacc[1, 4] += fold(grad_low[o, :].astype(f32))
            tiles(cot_sum)
            pack_core(0)
            i1["z"]()
            pack_wait(0)

        @then
        def _():
            pack_wait(1)
        unpack_filters(j)

        @then
        def _():
            i1["sw"](0, 1, 2, 3)
            i1["c"](True)
            i1["c"](False)
            o1["s"](0, 1)
        from_spectrum(j, ("big",))

        @first
        def _():
            i0["pw"](0, 1)
            i0["c"](True)
            o0["zw"](True)
            o0["p"](1)
        from_spectrum(j, ("small",))

        @first
        def _():
            o0["zw"](False)
            o0["p"](2, 3)
            i1["f"](0)
            pack_plane(1)
            o1["z"]()
            i0["pw"](2, 3)
            i0["c"](False)
            i0["cw"](True)

        @then
        def _():
            o1["s"](2, 3)
            i1["cw"](True)
        expand(j, half_z, True)

        @first
        def _():
            i1["zw"](True)
            i1["zw"](False)
            i1["f"](1, 2, 3)
            i0["cw"](False)
            o0["pw"](0, 1)
            o0["c"](True)

        @then
        def _():
            i1["cw"](False)
            o1["sw"](0, 1, 2, 3)
            o1["c"](True)
            o1["c"](False)
        expand(j, 1 - half_z, False)

        @first
        def _():
            o0["pw"](2, 3)
            o0["c"](False)
            o1["f"](0)
            o0["cw"](True)
            o0["cw"](False)
            i1["s"](0, 1, 2, 3)

        @then
        def _():
            o1["cw"](True)
            o1["cw"](False)
        contract(j)

        @first
        def _():
            o1["zw"](True)
            o1["zw"](False)
            o1["f"](1, 2, 3)
            pack_core(1)
        return 0

    lax.fori_loop(0, BLOCKS, forward, 0)
    store_large(large_rows)
    put(0, large_rows)
    store_small(small_rows)
    put(1, small_rows)

    def weights(j, a, k):
        reduce_core(j, a, k, (weight_out if a else weight_in)(j, k))

    def plane(j, a, *ks):
        for k in ks:
            reduce_plane(j, a, k)

    def along_z(j, a, *ks):
        for k in ks:
            reduce_z(j, a, k)

    def backward(t, _):
        j = BLOCKS - 1 - t
        first, then = (lambda f: pl.when(j == 1)(f)), (lambda f: pl.when(j == 0)(f))

        @first
        def _():
            def start(o):
                xs[o, :] = grad_low[o, :].astype(f32)
            tiles(start)

        @then
        def _():
            def low(o):
                g = xs[o, :]
                vacc[0, 4] += fold(g)
                grad_low[o, :] = g.astype(bf16)
            tiles(low)
            plane(1, 0, 0)
        for k in (2, 3, 1):
            weights(j, 1, k)
        plane(j, 1, 2, 3)

        @then
        def _():
            along_z(1, 0, 1)
        back_hidden(j, 1 - half_z, False)
        plane(j, 1, 1)

        @then
        def _():
            along_z(1, 1, 0)
            small_z(1)
            along_z(1, 0, 0)
        for k in (2, 3):
            weights(j, 0, k)
        along_z(j, 1, 2)
        back_hidden(j, half_z, True)
        plane(j, 0, 2, 3)
        along_z(j, 1, 3, 1)

        @then
        def _():
            small_end(1)
            reduce_end(1, 1)
            reduce_end(1, 0)
        back_spectrum(j, ("small",))
        back_spectrum(j, ("big",))
        back_filters(j)
        small_core(j)
        weights(j, 0, 1)
        small_plane(j)
        weights(j, 1, 0)
        plane(j, 0, 1)
        weights(j, 0, 0)
        along_z(j, 0, 2, 3)
        back_rows(j, ("small",))
        plane(j, 1, 0)

        @then
        def _():
            store_small(grad_small)
            put(3, grad_small)
        back_rows(j, ("big",))
        return 0

    lax.fori_loop(0, BLOCKS, backward, 0)
    plane(0, 0, 0)
    small_z(0)
    along_z(0, 0, 1)
    store_large(grad_large)
    put(2, grad_large)
    along_z(0, 1, 0)
    reduce_end(0, 1)
    put(6, g_w_out)
    along_z(0, 0, 0)
    reduce_end(0, 0)
    small_end(0)
    put(4, g_filters)
    put(5, g_w_in)
    put(7, g_gains)
    put(8, g_biases)
    for n in range(len(made)):
        pltpu.make_async_copy(stores[n], made[n], out_sem.at[n]).wait()
    for ops in (i0, o0, i1, o1):
        ops["e"]()
    for j in range(BLOCKS):
        pack_sent(j)
        small_sent(j)
    for a in range(2):
        for key, view in (("rc%d", s_core), ("rp%d", s_plane), ("rz%d", s_z)):
            sent(0, key % a, view.at[a])
    assert 2 * len(sending) == N_SEND and 2 * len(receiving) == N_RECEIVE, (len(sending), len(receiving))


def hand_over_kernel(*refs):
    sources, targets, between = refs[:N_OUT], refs[N_OUT : 2 * N_OUT], refs[2 * N_OUT : 3 * N_OUT]
    in_sem, out_sem = refs[3 * N_OUT :]
    ins = [pltpu.make_async_copy(a, b, in_sem.at[n]) for n, (a, b) in enumerate(zip(sources, between))]
    outs = [pltpu.make_async_copy(a, b, out_sem.at[n]) for n, (a, b) in enumerate(zip(between, targets))]
    for d in ins:
        d.start()
    for a, b in zip(ins, outs):
        a.wait()
        b.start()
    for d in outs:
        d.wait()


def fused(large_in, small_in, large_cot, small_cot, filters, w_in, w_out, gains, biases):
    large, small = large_in.shape[0], small_in.shape[0]
    rows = -(-(large * LP + small * PS) // TILE) * TILE
    early, late = [[jnp.asarray(t) for t in part] for part in constant_tables()]
    args = [jnp.swapaxes(w_in, 1, 2), w_out, filters, small_in, jnp.swapaxes(large_in, 0, 1), *early,
            jnp.swapaxes(large_cot, 0, 1), small_cot, gains, jnp.swapaxes(biases, 0, 1), *late]
    V = pltpu.VMEM
    patch_major = (large_in.shape[1], large, D)
    outs = [(patch_major, bf16), (small_in.shape, bf16), (patch_major, f32), (small_in.shape, f32), (filters.shape, f32),
            ((BLOCKS, HID, D + 1), f32), ((BLOCKS, HID, D), f32), (gains.shape, f32), ((3, BLOCKS, D), f32)]
    grid8 = (4, 2, 2, 2)
    scratch = [V(a.shape, a.dtype) for a in args] + [V(shape, dtype) for shape, dtype in outs[2:]] + [
        V((rows, D), f32), V((BLOCKS, rows, D), bf16), V((BLOCKS, rows, 128), f32), V((BLOCKS, rows, D), f32),
        V((BLOCKS, rows, 128), f32), V((BLOCKS, rows, D), bf16), V((BLOCKS, 2, rows, FF // 2), bf16),
        V((BLOCKS, 2, rows, FF // 2), bf16), V((BLOCKS, large, SPEC, D), f32), V((BLOCKS, small // Q, 2 * QF, D), f32),
        V((rows, D), bf16),
        V((BLOCKS, *grid8, HID, D), bf16), V((BLOCKS, *grid8, HID, D), bf16), V((BLOCKS, *grid8, 8, D), bf16),
        V((BLOCKS, 2 * QF, D), f32), V((BLOCKS, 2, 1, FF // 2), f32), V((BLOCKS, 3, 1, D), f32), V((rows, D), f32),
        V((BLOCKS, *grid8, 8, D), f32), V((2 * QF, D), f32), V((FLP + QF, D), f32), V((BLOCKS, 2, 8, FF // 2), f32), V((BLOCKS, 5, 8, D), f32),
        V((2, 4, 2, 2, HID, D), f32),
        V((2, 4, 2, 2, HID, D), bf16), V((2, 4, 3, HID, D), bf16), V((2, 3, HID, D), bf16),
        V((BLOCKS, 2, 4, 2, 2, HID, D), bf16), V((BLOCKS, 2, 4, 3, HID, D), bf16), V((BLOCKS, 2, 3, HID, D), bf16),
        V((BLOCKS, 4, 2, 2, 8, D), bf16), V((BLOCKS, 4, 2, 2, 8, D), bf16), V((BLOCKS, 2, 2, 4, 8, D), f32),
        V((BLOCKS, 3, 4, 8, D), bf16), V((BLOCKS, 3, 4, 8, D), bf16), V((BLOCKS, 3, 8, D), bf16), V((BLOCKS, 3, 8, D), bf16),
        V((BLOCKS, 8, D), f32), V((BLOCKS, 8, D), f32), V((BLOCKS, 2, 2, 8, D), f32), V((BLOCKS, 4, 8, D), f32),
        pltpu.SemaphoreType.DMA((N_SEND,)), pltpu.SemaphoreType.DMA((N_RECEIVE,)),
        pltpu.SemaphoreType.DMA((N_IN,)), pltpu.SemaphoreType.DMA((N_OUT,)),
    ]
    anywhere = pl.BlockSpec(memory_space=pl.ANY)
    out_shape = [jax.ShapeDtypeStruct(shape, dtype) for shape, dtype in outs]
    result = pl.pallas_call(
        partial(fused_kernel, large, small),
        out_shape=out_shape,
        in_specs=[anywhere] * N_IN,
        out_specs=[anywhere] * N_OUT,
        scratch_shapes=scratch,
        compiler_params=pltpu.CompilerParams(collective_id=0, has_side_effects=True, vmem_limit_bytes=VMEM_BYTES),
        name="gfnet_step",
    )(*args)
    out_large, out_small, grad_large, grad_small, g_filters, g_in, g_out, g_gains, g_biases = pl.pallas_call(
        hand_over_kernel,
        out_shape=out_shape,
        in_specs=[anywhere] * N_OUT,
        out_specs=[anywhere] * N_OUT,
        scratch_shapes=[V(shape, dtype) for shape, dtype in outs] + [pltpu.SemaphoreType.DMA((N_OUT,))] * 2,
        compiler_params=pltpu.CompilerParams(vmem_limit_bytes=VMEM_BYTES),
        name="hand_over",
    )(*result)
    return (jnp.swapaxes(out_large, 0, 1), out_small, jnp.swapaxes(grad_large, 0, 1), grad_small, g_filters,
            jnp.swapaxes(g_in, 1, 2), g_out, g_gains, jnp.swapaxes(g_biases, 0, 1))


def solution(mesh):
    in_specs = (
        P(("wide", "narrow"), None, None),
        P(("wide", "narrow"), None, None),
        P(("wide", "narrow"), None, None),
        P(("wide", "narrow"), None, None),
        P(None, ("wide", "narrow")),
        P(None, None, ("wide", "narrow")),
        P(None, ("wide", "narrow"), None),
        P(),
        P(),
    )
    out_specs = (
        P(("wide", "narrow"), None, None),
        P(("wide", "narrow"), None, None),
        P(("wide", "narrow"), None, None),
        P(("wide", "narrow"), None, None),
        P(None, ("wide", "narrow")),
        P(None, None, ("wide", "narrow")),
        P(None, ("wide", "narrow"), None),
        P(),
        P(),
    )
    body = fused if dict(mesh.shape) == {"wide": 8, "narrow": 4} else per_device
    return jax.shard_map(
        body, mesh=mesh, in_specs=in_specs, out_specs=out_specs, check_vma=False
    )
```

```python
from functools import partial
import math

import jax
import jax.numpy as jnp
import ml_dtypes
import numpy as np
from jax import lax
from jax.experimental import pallas as pl
from jax.experimental.pallas import tpu as pltpu
from jax.sharding import PartitionSpec as P

FF = 1536
GL = 14
GS = 6
BLOCKS = 2
MICRO = 2
PL = 196
FL = 112
FS = 24


precise = lax.Precision.HIGHEST
epsilon = 1e-06


def dft_tables(grid_cells):
    half_count = grid_cells // 2 + 1
    places = jnp.arange(grid_cells * grid_cells, dtype=jnp.int32)
    place_row = places // grid_cells
    place_col = places % grid_cells
    modes = jnp.arange(grid_cells * half_count, dtype=jnp.int32)
    mode_row = modes // half_count
    mode_col = modes % half_count
    phases = (
        mode_row[:, None] * place_row[None, :] + mode_col[:, None] * place_col[None, :]
    ) % grid_cells
    angles = phases.astype(jnp.float32) * (2.0 * math.pi / grid_cells)
    forward_re = jnp.cos(angles) / grid_cells
    forward_im = -jnp.sin(angles) / grid_cells
    doubling = jnp.where((mode_col == 0) | (2 * mode_col == grid_cells), 1.0, 2.0).astype(
        jnp.float32
    )
    inverse_re = jnp.transpose(forward_re * doubling[:, None])
    inverse_im = jnp.transpose(forward_im * doubling[:, None])
    return (forward_re, forward_im, inverse_re, inverse_im)


def linear_map(size_out, size_in):
    rows_out = jnp.arange(size_out, dtype=jnp.int32)
    spans = rows_out * (size_in - 1)
    lower = spans // (size_out - 1)
    fraction = (spans - lower * (size_out - 1)).astype(jnp.float32) / (size_out - 1)
    columns = jnp.arange(size_in, dtype=jnp.int32)
    first = jnp.where(columns[None, :] == lower[:, None], 1.0 - fraction[:, None], 0.0)
    second = jnp.where(columns[None, :] == lower[:, None] + 1, fraction[:, None], 0.0)
    return first + second


def shrink_map():
    along_rows = linear_map(GS, GL)
    along_cols = linear_map(GS // 2 + 1, GL // 2 + 1)
    return (along_rows[:, None, :, None] * along_cols[None, :, None, :]).reshape(FS, FL)


def filter_grid(patches, tables, filt_re, filt_im):
    forward_re, forward_im, inverse_re, inverse_im = tables
    spec_re = jnp.einsum("fp,bpd->bfd", forward_re, patches, precision=precise)
    spec_im = jnp.einsum("fp,bpd->bfd", forward_im, patches, precision=precise)
    out_re = spec_re * filt_re - spec_im * filt_im
    out_im = spec_re * filt_im + spec_im * filt_re
    back_re = jnp.einsum("pf,bfd->bpd", inverse_re, out_re, precision=precise)
    back_im = jnp.einsum("pf,bfd->bpd", inverse_im, out_im, precision=precise)
    return back_re + back_im


def spectral(normed, large_rows, filt_re, filt_im):
    width = normed.shape[-1]
    shrink = shrink_map()
    small_re = jnp.dot(shrink, filt_re, precision=precise, preferred_element_type=jnp.float32)
    small_im = jnp.dot(shrink, filt_im, precision=precise, preferred_element_type=jnp.float32)
    part_large = filter_grid(
        normed[:large_rows].reshape(-1, GL * GL, width), dft_tables(GL), filt_re, filt_im
    )
    part_small = filter_grid(
        normed[large_rows:].reshape(-1, GS * GS, width), dft_tables(GS), small_re, small_im
    )
    return jnp.concatenate([part_large.reshape(-1, width), part_small.reshape(-1, width)], 0)


def layer_norm(stream, gain, shift):
    centre = stream - jnp.mean(stream, axis=-1, keepdims=True)
    spread = jnp.mean(centre * centre, axis=-1, keepdims=True)
    return centre * lax.rsqrt(spread + epsilon) * gain + shift


def per_device(large_in, small_in, large_cot, small_cot, filters, w_in, w_out, gains, biases):
    width = large_in.shape[-1]
    micro_large = large_in.shape[0] // MICRO
    micro_small = small_in.shape[0] // MICRO
    large_rows = micro_large * PL
    exact_gelu = partial(jax.nn.gelu, approximate=False)

    def fetch(layer_index, forward):
        if forward:
            return (
                lax.all_gather(filters[layer_index], ("wide", "narrow"), axis=0, tiled=True),
                lax.all_gather(w_in[layer_index], ("wide", "narrow"), axis=1, tiled=True),
                lax.all_gather(w_out[layer_index], ("wide", "narrow"), axis=0, tiled=True),
            )
        return (
            lax.all_gather(filters[layer_index], ("wide", "narrow"), axis=0, tiled=True),
            lax.all_gather(w_in[layer_index], ("wide", "narrow"), axis=1, tiled=True),
            lax.all_gather(w_out[layer_index], ("wide", "narrow"), axis=0, tiled=True),
        )

    def branch_first(stream, gain, shift, filt_re, filt_im):
        return spectral(layer_norm(stream, gain, shift), large_rows, filt_re, filt_im)

    acc_filter = [jnp.zeros((2, FL, width), jnp.float32) for layer_index in range(BLOCKS)]
    acc_in = [jnp.zeros((width, FF), jnp.float32) for layer_index in range(BLOCKS)]
    acc_in_bias = [jnp.zeros((FF,), jnp.float32) for layer_index in range(BLOCKS)]
    acc_out = [jnp.zeros((FF, width), jnp.float32) for layer_index in range(BLOCKS)]
    acc_gain = [jnp.zeros((2, width), jnp.float32) for layer_index in range(BLOCKS)]
    acc_shift = [jnp.zeros((3, width), jnp.float32) for layer_index in range(BLOCKS)]
    outs_large, outs_small, grads_large, grads_small = ([], [], [], [])
    for micro_step in range(MICRO):
        large_part = large_in[micro_step * micro_large : (micro_step + 1) * micro_large]
        small_part = small_in[micro_step * micro_small : (micro_step + 1) * micro_small]
        stream = jnp.concatenate(
            [large_part.reshape(-1, width), small_part.reshape(-1, width)], 0
        ).astype(jnp.float32)
        saved = []
        for layer_index in range(BLOCKS):
            filt_full, in_full, out_full = fetch(layer_index, True)
            halves = filt_full.reshape(2, FL, width).astype(jnp.float32)
            mixed = stream + branch_first(
                stream, gains[layer_index, 0], biases[layer_index, 0], halves[0], halves[1]
            )
            second = layer_norm(mixed, gains[layer_index, 1], biases[layer_index, 1]).astype(
                jnp.bfloat16
            )
            pre_act = jnp.dot(
                second, in_full[:width], preferred_element_type=jnp.float32
            ) + in_full[width].astype(jnp.float32)
            active = exact_gelu(pre_act).astype(jnp.bfloat16)
            saved.append((stream, mixed, second, pre_act))
            stream = (
                mixed
                + jnp.dot(active, out_full, preferred_element_type=jnp.float32)
                + biases[layer_index, 2]
            )
        outs_large.append(stream[:large_rows].reshape(large_part.shape).astype(jnp.bfloat16))
        outs_small.append(stream[large_rows:].reshape(small_part.shape).astype(jnp.bfloat16))
        large_back = large_cot[micro_step * micro_large : (micro_step + 1) * micro_large]
        small_back = small_cot[micro_step * micro_small : (micro_step + 1) * micro_small]
        grad = jnp.concatenate(
            [large_back.reshape(-1, width), small_back.reshape(-1, width)], 0
        ).astype(jnp.float32)
        for layer_index in reversed(range(BLOCKS)):
            block_input, mixed, second, pre_act = saved[layer_index]
            filt_full, in_full, out_full = fetch(layer_index, False)
            halves = filt_full.reshape(2, FL, width).astype(jnp.float32)
            grad_low = grad.astype(jnp.bfloat16)
            active, gelu_back = jax.vjp(exact_gelu, pre_act)
            active = active.astype(jnp.bfloat16)
            acc_out[layer_index] = acc_out[layer_index] + jnp.einsum(
                "tf,td->fd", active, grad_low, preferred_element_type=jnp.float32
            )
            bias_out_grad = jnp.sum(grad, axis=0)
            active_grad = jnp.einsum(
                "td,fd->tf", grad_low, out_full, preferred_element_type=jnp.float32
            )
            pre_grad = gelu_back(active_grad)[0]
            pre_low = pre_grad.astype(jnp.bfloat16)
            acc_in[layer_index] = acc_in[layer_index] + jnp.einsum(
                "td,tf->df", second, pre_low, preferred_element_type=jnp.float32
            )
            acc_in_bias[layer_index] = acc_in_bias[layer_index] + jnp.sum(pre_grad, axis=0)
            second_grad = jnp.einsum(
                "tf,df->td", pre_low, in_full[:width], preferred_element_type=jnp.float32
            )
            unused, norm_back = jax.vjp(
                layer_norm, mixed, gains[layer_index, 1], biases[layer_index, 1]
            )
            mixed_part, gain_two, shift_two = norm_back(second_grad)
            mixed_grad = grad + mixed_part
            unused, first_back = jax.vjp(
                branch_first,
                block_input,
                gains[layer_index, 0],
                biases[layer_index, 0],
                halves[0],
                halves[1],
            )
            input_part, gain_one, shift_one, filt_re_grad, filt_im_grad = first_back(mixed_grad)
            grad = mixed_grad + input_part
            acc_filter[layer_index] = acc_filter[layer_index] + jnp.stack(
                [filt_re_grad, filt_im_grad], 0
            )
            acc_gain[layer_index] = acc_gain[layer_index] + jnp.stack([gain_one, gain_two], 0)
            acc_shift[layer_index] = acc_shift[layer_index] + jnp.stack(
                [shift_one, shift_two, bias_out_grad], 0
            )
        grads_large.append(grad[:large_rows].reshape(large_part.shape))
        grads_small.append(grad[large_rows:].reshape(small_part.shape))
    filter_shards, in_shards, out_shards = ([], [], [])
    for layer_index in range(BLOCKS):
        in_whole = jnp.concatenate([acc_in[layer_index], acc_in_bias[layer_index][None, :]], 0)
        filter_piece, in_piece, out_piece = (
            lax.psum_scatter(
                acc_filter[layer_index].reshape(-1),
                ("wide", "narrow"),
                scatter_dimension=0,
                tiled=True,
            ),
            lax.psum_scatter(in_whole, ("wide", "narrow"), scatter_dimension=1, tiled=True),
            lax.psum_scatter(
                acc_out[layer_index], ("wide", "narrow"), scatter_dimension=0, tiled=True
            ),
        )
        filter_shards.append(filter_piece)
        in_shards.append(in_piece)
        out_shards.append(out_piece)
    gain_total, shift_total = lax.psum(
        (jnp.stack(acc_gain, 0), jnp.stack(acc_shift, 0)), ("wide", "narrow")
    )
    return (
        jnp.concatenate(outs_large, 0),
        jnp.concatenate(outs_small, 0),
        jnp.concatenate(grads_large, 0),
        jnp.concatenate(grads_small, 0),
        jnp.stack(filter_shards, 0),
        jnp.stack(in_shards, 0),
        jnp.stack(out_shards, 0),
        gain_total,
        shift_total,
    )


MESH_ID = pl.DeviceIdType.MESH
bf16, f32 = jnp.bfloat16, jnp.float32
D, PS, EPS = 384, 36, 1e-6
LP = 208
Q = 4
SR = Q * PS
TILE = 256
BOTH = ("big", "small")
HID = 48
FLP = 128
SPEC = 2 * FLP
QF = Q * FS


def dft_arrays(n):
    half = n // 2 + 1
    places, modes = np.arange(n * n), np.arange(n * half)
    phase = ((modes // half)[:, None] * (places // n)[None] + (modes % half)[:, None] * (places % n)[None]) % n
    theta = phase * (2 * math.pi / n)
    fwd_re, fwd_im = np.cos(theta) / n, -np.sin(theta) / n
    weight = np.where((modes % half == 0) | (2 * (modes % half) == n), 1.0, 2.0)
    return fwd_re, fwd_im, fwd_re * weight[:, None], fwd_im * weight[:, None]


def interpolation(rows, cols):
    span = np.arange(rows) * (cols - 1)
    low = span // (rows - 1)
    part = (span - low * (rows - 1)) / (rows - 1)
    at = np.arange(cols)[None]
    return np.where(at == low[:, None], 1 - part[:, None], 0.0) + np.where(at == low[:, None] + 1, part[:, None], 0.0)


def two_terms(table):
    table = np.asarray(table, np.float32)
    high = table.astype(ml_dtypes.bfloat16)
    low = (table - high.astype(np.float32)).astype(ml_dtypes.bfloat16)
    return np.concatenate([high, low], 0)


def constant_tables():
    pos = np.arange(FL) // 7 * 8 + np.arange(FL) % 7
    rows = np.concatenate([pos, FLP + pos])
    fr, fi, ir, ii = dft_arrays(GL)
    fwd, inv = np.zeros((SPEC, LP)), np.zeros((SPEC, LP))
    fwd[rows, :PL], inv[rows, :PL] = np.concatenate([fr, fi]), np.concatenate([ir, ii])
    fr, fi, ir, ii = dft_arrays(GS)
    sfwd, sinv = np.zeros((2 * QF, SR)), np.zeros((2 * QF, SR))
    for q in range(Q):
        at = slice(q * PS, (q + 1) * PS)
        for half, a, b in ((0, fr, ir), (1, fi, ii)):
            to = slice(half * QF + q * FS, half * QF + (q + 1) * FS)
            sfwd[to, at], sinv[to, at] = a, b
    shrink = np.zeros((FS, FLP))
    shrink[:, pos] = (
        interpolation(GS, GL)[:, None, :, None] * interpolation(GS // 2 + 1, GL // 2 + 1)[None, :, None, :]
    ).reshape(FS, FL)
    piece = np.arange(32)
    pick = np.zeros((64, SPEC))
    pick[piece % 8 * 8 + piece // 8, 8 * piece + 7] = 1
    return [two_terms(t) for t in (fwd, sfwd)], [
        two_terms(shrink), pick.astype(ml_dtypes.bfloat16), two_terms(inv.T), two_terms(sinv.T), two_terms(shrink.T)]


def mm(a, b):
    return lax.dot_general(a, b, (((1,), (0,)), ((), ())), preferred_element_type=f32)


def mm_nt(a, b):
    return lax.dot_general(a, b, (((1,), (1,)), ((), ())), preferred_element_type=f32)


def mm_tn(a, b):
    return lax.dot_general(a, b, (((0,), (0,)), ((), ())), preferred_element_type=f32)


def halves(v):
    high = v.astype(bf16)
    return high, (v - high.astype(f32)).astype(bf16)


def apply_table(table, v):
    rows = table.shape[0] // 2
    high, low = halves(v)
    both = mm(table, high)
    return both[:rows] + both[rows:] + mm(table[:rows], low)


def standardize(v):
    centre = v - jnp.sum(v, -1, keepdims=True) * (1.0 / D)
    r = lax.rsqrt(jnp.sum(centre * centre, -1, keepdims=True) * (1.0 / D) + EPS)
    return centre * r, r


def norm_back(vh, r, q):
    mean_q = jnp.sum(q, -1, keepdims=True) * (1.0 / D)
    mean_qv = jnp.sum(q * vh, -1, keepdims=True) * (1.0 / D)
    return r * (q - mean_q - vh * mean_qv)


def fold(v):
    return jnp.sum(v.reshape(v.shape[0] // 8, 8, v.shape[1]), 0)


def aligned(v, m):
    return v if isinstance(v, int) else pl.multiple_of(v, m)


N_SEND, N_RECEIVE = 46, 102
VMEM_BYTES = 63 << 20


N_IN, N_OUT = 16, 9


def fused_kernel(large, small, *refs):
    given, made, refs = refs[:N_IN], refs[N_IN : N_IN + N_OUT], refs[N_IN + N_OUT :]
    held, refs = refs[:N_IN], refs[N_IN:]
    (raw_in, raw_out, raw_filters, small_rows, large_rows, t_fwd, t_sfwd, cot_large, cot_small, gains, biases,
     t_shrink, t_pick, t_inv, t_sinv, t_shrink_t) = held
    (grad_large, grad_small, g_filters, g_w_in, g_w_out, g_gains, g_biases,
     xs, vh1, r1, vh2, r2, second, active, slope, sv_large, sv_small, grad_low,
     w_in, w_out, pack, filt_s, b_in, shift, back, facc, sacc, gacc, bacc, vacc,
     kept, s_core, s_plane, s_z, r_core, r_plane, r_z,
     f_own, f_core, f_keep, f_send, f_xy, f_z_send, f_z, v_send, v_core, v_xy, v_z,
     send_sem, recv_sem, in_sem, out_sem) = refs
    rows = xs.shape[0]
    groups = small // Q
    base = large * LP
    wide, narrow = lax.axis_index("wide"), lax.axis_index("narrow")
    z, x, y, c = lax.div(wide, 2), lax.rem(wide, 2), lax.div(narrow, 2), lax.rem(narrow, 2)
    other = {"x": 1 - x, "y": 1 - y, "c": 1 - c}
    at = lambda zz, xx, yy, cc: (zz * 2 + xx, yy * 2 + cc)
    z_pair = {0: z, 1: z + 1 - 2 * lax.rem(z, 2), 2: lax.rem(z + 2, 4), 3: 3 - z}
    z_of = lambda k: z_pair[k]
    peer = {"x": at(z, 1 - x, y, c), "y": at(z, x, 1 - y, c), "xy": at(z, 1 - x, 1 - y, c), "c": at(z, x, y, 1 - c)}
    for k in (1, 2, 3):
        peer[k] = at(z_of(k), x, y, c)

    sending, receiving = {}, {}

    def send(j, key, src, dst, to, part=None):
        out = 2 * sending.setdefault(key, len(sending)) + j
        back = key if part is None else (key, part)
        pltpu.make_async_remote_copy(
            src_ref=src, dst_ref=dst, send_sem=send_sem.at[out],
            recv_sem=recv_sem.at[2 * receiving.setdefault(back, len(receiving)) + j],
            device_id=peer[to], device_id_type=MESH_ID).start()

    def arrived(j, key, view, part=None):
        back = key if part is None else (key, part)
        sem = recv_sem.at[2 * receiving.setdefault(back, len(receiving)) + j]
        pltpu.make_async_copy(view, view, sem).wait()

    def sent(j, key, view):
        pltpu.make_async_copy(view, view, send_sem.at[2 * sending.setdefault(key, len(sending)) + j]).wait()

    PLANE = [("xy", 1 - x, 1 - y), ("x", 1 - x, y), ("y", x, 1 - y)]
    half_z = lax.div(z, 2)
    pair = lambda near: pl.ds(2 * (half_z if near else 1 - half_z), 2)

    def gather_ops(j, name):
        ref = w_in if name == "in" else w_out
        three = ref.at[j, 0:3, x, y, c]

        def z_send():
            mine = ref.at[j, z, x, y, c]
            for k in (1, 2, 3):
                send(j, name + "z", mine, mine, k, part=k == 1)

        def z_wait(near):
            arrived(j, name + "z", ref.at[j, 0 : 1 if near else 2, x, y, c], near)

        def plane_send(*ks):
            for k in ks:
                piece = ref.at[j, z_of(k), x, y, c]
                for to, _, _ in PLANE:
                    send(j, name + "p", piece, piece, to, part=k)

        def plane_wait(*ks):
            for k in ks:
                arrived(j, name + "p", three, k)

        def first_send(*ks):
            for k in ks:
                piece = ref.at[j, z_of(k), x, y, c]
                send(j, name + "f", piece, piece, "xy"[k % 2], part=k)

        def second_send(*ks):
            for k in ks:
                zz = z_of(k)
                arrived(j, name + "f", ref.at[j, zz, x, y, c], k)
                piece = ref.at[j, zz, x, :, c] if k % 2 else ref.at[j, zz, :, y, c]
                send(j, name + "p", piece, piece, "yx"[k % 2], part=k)

        def second_wait(*ks):
            for k in ks:
                arrived(j, name + "p", ref.at[j, z_of(k), x, :, c], k)

        def core_send(near):
            piece = ref.at[j, pair(near), :, :, c]
            send(j, name + "c", piece, piece, "c", part=near)

        def core_wait(near):
            arrived(j, name + "c", ref.at[j, pair(near), :, :, 1 - c], near)

        def all_sent():
            sent(j, name + "z", three)
            if j:
                sent(j, name + "f", ref.at[j, :, x, y, c])
                sent(j, name + "p", ref.at[j, :, x, :, c])
            else:
                sent(j, name + "p", ref.at[j, 0:3, :, :, c])
            sent(j, name + "c", ref.at[j, :, :, :, c])

        return dict(z=z_send, zw=z_wait, p=plane_send, pw=plane_wait, f=first_send, s=second_send, sw=second_wait,
                    c=core_send, cw=core_wait, e=all_sent)

    def pack_z(j):
        mine = pack.at[j, z, x, y, c]
        for k in (1, 2, 3):
            send(j, "pz", mine, mine, k)

    def pack_plane(j):
        arrived(j, "pz", pack.at[j, 0:3, x, y, c])
        piece = pack.at[j, :, x, y, c]
        for to, _, _ in PLANE:
            send(j, "pp", piece, piece, to)

    def pack_core(j):
        arrived(j, "pp", pack.at[j, 0:3, :, :, c])
        piece = pack.at[j, :, :, :, c]
        send(j, "pc", piece, piece, "c")

    def pack_wait(j):
        arrived(j, "pc", pack.at[j, :, :, :, 1 - c])

    def pack_sent(j):
        sent(j, "pz", pack.at[j, 0:3, x, y, c])
        sent(j, "pp", pack.at[j, 0:3, :, :, c])
        sent(j, "pc", pack.at[j, :, :, :, c])

    def clear(j, a, k, key, view):
        if k == 2:
            @pl.when(j == 0)
            def _():
                sent(1, key, view)

    def reduce_core(j, a, k, value):
        clear(j, a, k, "rc%d" % a, s_core.at[a])
        for n in range(4):
            even, odd = value[2 * n * HID : (2 * n + 1) * HID], value[(2 * n + 1) * HID : (2 * n + 2) * HID]
            kept[a, k, n // 2, n % 2] = jnp.where(c == 0, even, odd)
            s_core[a, k, n // 2, n % 2] = jnp.where(c == 0, odd, even).astype(bf16)
        send(j, "rc%d" % a, s_core.at[a, k], r_core.at[j, a, k], "c", k)

    def reduce_plane(j, a, k):
        arrived(j, "rc%d" % a, r_core.at[j, a, k], k)
        if not isinstance(j, int):
            clear(j, a, k, "rp%d" % a, s_plane.at[a])
        for n, (to, xx, yy) in enumerate(PLANE):
            s_plane[a, k, n] = (kept[a, k, xx, yy] + r_core[j, a, k, xx, yy].astype(f32)).astype(bf16)
            send(j, "rp%d" % a, s_plane.at[a, k, n], r_plane.at[j, a, k, n], to, k)

    def reduce_z(j, a, k):
        s = kept[a, k, x, y] + r_core[j, a, k, x, y].astype(f32)
        arrived(j, "rp%d" % a, r_plane.at[j, a, k], k)
        for n in range(3):
            s = s + r_plane[j, a, k, n].astype(f32)
        if k:
            if not isinstance(j, int):
                clear(j, a, k, "rz%d" % a, s_z.at[a])
            s_z[a, k - 1] = s.astype(bf16)
            send(j, "rz%d" % a, s_z.at[a, k - 1], r_z.at[j, a, k - 1], k)
        elif a == 0:
            g_w_in[j, :, :D] = s
        else:
            g_w_out[j] = s

    def reduce_end(j, a):
        arrived(j, "rz%d" % a, r_z.at[j, a])
        s = r_z[j, a, 0].astype(f32) + r_z[j, a, 1].astype(f32) + r_z[j, a, 2].astype(f32)
        if a == 0:
            g_w_in[j, :, :D] += s
        else:
            g_w_out[j] += s

    def small_core(j):
        for zz in range(4):
            for i in range(2):
                for l in range(2):
                    f_own[j, zz, i, l] = facc[j, zz, i, l, 1 - c].astype(bf16)
        send(j, "fc", f_own.at[j], f_core.at[j], "c")
        v_send[j] = jnp.concatenate([jnp.sum(vacc[j, i], 0, keepdims=True) for i in range(5)] + [jnp.zeros((3, D), f32)], 0)
        send(j, "vc", v_send.at[j], v_core.at[j], "c")

    def small_plane(j):
        arrived(j, "fc", f_core.at[j])
        for zz in range(4):
            for i in range(2):
                for l in range(2):
                    f_keep[j, i, l, zz] = facc[j, zz, i, l, c] + f_core[j, zz, i, l].astype(f32)
        for n, (to, xx, yy) in enumerate(PLANE):
            f_send[j, n] = f_keep[j, xx, yy].astype(bf16)
            send(j, "fp", f_send.at[j, n], f_xy.at[j, n], to)
        arrived(j, "vc", v_core.at[j])
        v_z[j, z] = v_send[j] + v_core[j]
        mine = v_z.at[j, z]
        for k in (1, 2, 3):
            send(j, "vz", mine, mine, k)

    def small_z(j):
        s = f_keep[j, x, y]
        arrived(j, "fp", f_xy.at[j])
        for n in range(3):
            s = s + f_xy[j, n].astype(f32)
        f_keep[j, x, y] = s
        for k in (1, 2, 3):
            f_z_send[j, k - 1] = f_keep[j, x, y, z_of(k)].astype(bf16)
            send(j, "fz", f_z_send.at[j, k - 1], f_z.at[j, k - 1], k)
        arrived(j, "vz", v_z.at[j, 0:3])
        v_xy[j, x, y] = v_z[j, 0] + v_z[j, 1] + v_z[j, 2] + v_z[j, 3]
        mine = v_xy.at[j, x, y]
        for to, _, _ in PLANE:
            send(j, "vp", mine, mine, to)

    def small_end(j):
        arrived(j, "fz", f_z.at[j])
        s = f_keep[j, x, y, z] + f_z[j, 0].astype(f32) + f_z[j, 1].astype(f32) + f_z[j, 2].astype(f32)
        for r in range(7):
            g_filters[j : j + 1, r * D : (r + 1) * D] = s[r : r + 1]
        g_w_in[j, :, D:] = jnp.sum(jnp.where(diagonal(), s[7:8, :128], 0.0), 1, keepdims=True)
        arrived(j, "vp", v_z.at[j, 0:3])
        v = v_xy[j, 0, 0] + v_xy[j, 0, 1] + v_xy[j, 1, 0] + v_xy[j, 1, 1]
        g_gains[j] = v[0:2]
        for l in range(3):
            g_biases[l, j : j + 1] = v[2 + l : 3 + l]

    def small_sent(j):
        for key, view in (("fc", f_own), ("vc", v_send), ("fp", f_send), ("fz", f_z)):
            sent(j, key, view.at[j])
        for key in ("vp", "vz"):
            sent(j, key, v_z.at[j, 0:3])

    def diagonal():
        shape = (HID, 128)
        return lax.broadcasted_iota(jnp.int32, shape, 0) == lax.broadcasted_iota(jnp.int32, shape, 1)

    def load_rows(dst, a, b):
        v = jnp.swapaxes(a[...], 0, 1).astype(dst.dtype)
        for i in range(large):
            dst[i * LP + LP - 16 : (i + 1) * LP, :] = jnp.zeros((16, D), dst.dtype)
            dst[i * LP : i * LP + PL, :] = v[i]
        for i in range(small):
            dst[base + i * PS : base + (i + 1) * PS, :] = b[i].astype(dst.dtype)
        dst[base + small * PS :, :] = jnp.zeros((rows - base - small * PS, D), dst.dtype)

    def store_large(a):
        v = jnp.concatenate([xs[i * LP : i * LP + PL, :][None] for i in range(large)], 0)
        a[...] = jnp.swapaxes(v, 0, 1).astype(a.dtype)

    def store_small(b):
        for i in range(small):
            b[i] = xs[base + i * PS : base + (i + 1) * PS, :].astype(b.dtype)

    def own_pieces():
        for j in range(BLOCKS):
            w_in[j, z, x, y, c] = raw_in[j, :, :D]
            w_out[j, z, x, y, c] = raw_out[j]
            bias = jnp.sum(jnp.where(diagonal(), raw_in[j, :, D:].astype(f32), 0.0), 0, keepdims=True)
            row = raw_filters[j : j + 1, :].astype(f32)
            parts = [row[:, r * D : (r + 1) * D] for r in range(7)]
            parts.append(jnp.concatenate([bias, jnp.zeros((1, D - 128), f32)], 1))
            pack[j, z, x, y, c] = jnp.concatenate(parts, 0).astype(bf16)

    fetches = [pltpu.make_async_copy(a, b, in_sem.at[n]) for n, (a, b) in enumerate(zip(given, held))]
    stores = {}

    def fetched(*which):
        for n in which:
            fetches[n].wait()

    def put(n, value):
        pltpu.make_async_copy(value, made[n], out_sem.at[n]).start()
        stores[n] = value

    def spread_rows(r):
        return jnp.broadcast_to(r, (r.shape[0], 128))

    def wide_rows(r):
        return jnp.concatenate([r, r, r], -1)

    def first_row(scale):
        return jnp.where(lax.broadcasted_iota(jnp.int32, (8, 1), 0) == 0, float(scale), 0.0)

    def column_weights(big):
        row = lax.broadcasted_iota(jnp.int32, (FLP if big else QF, 1), 0)
        column = lax.rem(lax.rem(row, 8) + 16 - lax.div(row, 8), 8) if big else lax.rem(row, 4)
        return jnp.where((column == 0) | (column == (GL if big else GS) // 2), 1.0, 2.0)

    def crop_loops(body, which):
        if "big" in which:
            for i in range(large):
                body(pl.ds(i * LP, LP), i, True)
        if "small" in which:
            for i in range(groups):
                body(pl.ds(base + i * SR, SR), i, False)

    def to_spectrum(j, which=BOTH):
        def body(o, i, big):
            vh, r = standardize(xs[o, :])
            vh1[j, o, :] = vh.astype(bf16)
            r1[j, o, :] = spread_rows(r)
            if big:
                sv_large[j, i] = apply_table(t_fwd[...], vh)
            else:
                sv_small[j, i] = apply_table(t_sfwd[...], vh)
        crop_loops(body, which)

    def unpack_filters(j):
        f = pack[j].reshape(SPEC, D)
        for h in range(2):
            s = mm(t_shrink[...], f[h * FLP : (h + 1) * FLP])
            s = s[:FS] + s[FS:]
            filt_s[j, h * QF : (h + 1) * QF] = jnp.concatenate([s] * Q, 0)
        bias = mm(t_pick[...], f[:, :128])
        bias = jnp.where(lax.broadcasted_iota(jnp.int32, (64, 128), 1) < HID, bias, 0.0)
        total = jnp.zeros((8, D), f32)
        for i in range(8):
            part = jnp.concatenate([bias[8 * i : 8 * i + 8], jnp.zeros((8, D - 128), f32)], 1)
            total = total + (pltpu.roll(part, HID * i, 1) if i else part)
        for h in range(2):
            b_in[j, h] = jnp.concatenate([total[2 * h : 2 * h + 1], total[2 * h + 1 : 2 * h + 2]], 1)

    def spectrum_of(j, i, big):
        sv = sv_large[j, i] if big else sv_small[j, i]
        h, period = (FLP, FLP) if big else (QF, FS)
        re, im = sv[:h] * gains[j, 0:1, :], sv[h:] * gains[j, 0:1, :]
        mean = first_row(GL if big else GS) * shift[j, 0]
        parts = []
        for n in range(0, h, period):
            parts += [re[n : n + 8] + mean, re[n + 8 : n + period]]
        f = pack[j].reshape(SPEC, D).astype(f32) if big else filt_s[j]
        return sv, jnp.concatenate(parts, 0), im, f[:h], f[h:]

    def from_spectrum(j, which=BOTH):
        def body(o, i, big):
            _, re, im, fr, fi = spectrum_of(j, i, big)
            out = jnp.concatenate([re * fr - im * fi, re * fi + im * fr], 0)
            xs[o, :] = xs[o, :] + apply_table(t_inv[...] if big else t_sinv[...], out)
        crop_loops(body, which)

    def tiles(body):
        for t in range(rows // TILE):
            body(pl.ds(t * TILE, TILE))

    def expand(j, h, first):
        def body(o):
            if first:
                vh, r = standardize(xs[o, :])
                vh2[j, o, :] = vh
                r2[j, o, :] = spread_rows(r)
                s = (vh * gains[j, 1:2, :] + shift[j, 1]).astype(bf16)
                second[j, o, :] = s
            else:
                s = second[j, o, :]
            pre = mm_nt(s, w_in[j, pl.ds(2 * h, 2)].reshape(FF // 2, D)) + b_in[j, h]
            phi = 0.5 + 0.5 * lax.erf(pre * (1 / math.sqrt(2)))
            active[j, h, o, :] = (pre * phi).astype(bf16)
            slope[j, h, o, :] = (phi + pre * (jnp.exp(-0.5 * pre * pre) * (1 / math.sqrt(2 * math.pi)))).astype(bf16)
        tiles(body)

    def contract(j):
        def body(o):
            s = xs[o, :] + shift[j, 2]
            for h in range(2):
                s = s + mm(active[j, h, o, :], w_out[j, 2 * h : 2 * h + 2].reshape(FF // 2, D))
            xs[o, :] = s
        tiles(body)

    def z_offset(k):
        zz = z_of(k)
        return lax.div(zz, 2), pl.ds(aligned(lax.rem(zz, 2) * (FF // 4), 128), FF // 4)

    def back_hidden(j, h, last):
        def body(o):
            w = w_out[j, pl.ds(2 * h, 2)].reshape(FF // 2, D)
            pg = mm_nt(grad_low[o, :], w) * slope[j, h, o, :].astype(f32)
            bacc[j, h] += fold(pg)
            p = pg.astype(bf16)
            slope[j, h, o, :] = p
            sg = mm(p, w_in[j, pl.ds(2 * h, 2)].reshape(FF // 2, D))
            if not last:
                back[o, :] = sg
            else:
                sg = sg + back[o, :]
                vh = vh2[j, o, :]
                vacc[j, 1] += fold(sg * vh)
                vacc[j, 3] += fold(sg)
                xs[o, :] = xs[o, :] + norm_back(vh, wide_rows(r2[j, o, :]), sg * gains[j, 1:2, :])
        tiles(body)

    def weight_in(j, k):
        h, lanes = z_offset(k)
        return mm_tn(slope[j, h, :, lanes], second[j])

    def weight_out(j, k):
        h, lanes = z_offset(k)
        return mm_tn(active[j, h, :, lanes], grad_low[...])

    def back_spectrum(j, which):
        if which == ("small",):
            sacc[...] = jnp.zeros_like(sacc)
            gacc[...] = jnp.zeros_like(gacc)
        else:
            facc[j] = jnp.zeros(facc.shape[1:], f32)

        def body(o, i, big):
            sv, re, im, fr, fi = spectrum_of(j, i, big)
            h, period = (FLP, FLP) if big else (QF, FS)
            sg = apply_table(t_fwd[...] if big else t_sfwd[...], xs[o, :])
            gr, gi = sg[:h], sg[h:]
            d_re, d_im = re * gr + im * gi, re * gi - im * gr
            if big:
                facc[j] += jnp.concatenate([d_re, d_im], 0).reshape(4, 2, 2, 2, 8, D)
            else:
                sacc[...] += jnp.concatenate([d_re, d_im], 0)
            n_re, n_im = gr * fr + gi * fi, gi * fr - gr * fi
            first = 0 if big else FLP
            gacc[first : first + h] += n_re * sv[:h] + n_im * sv[h:]
            mean = n_re[:8]
            for n in range(period, h, period):
                mean = mean + n_re[n : n + 8]
            vacc[j, 2] += mean * first_row(GL if big else GS)
            n = jnp.concatenate([n_re, n_im], 0)
            if big:
                sv_large[j, i] = n
            else:
                sv_small[j, i] = n
        crop_loops(body, which)

    def back_filters(j):
        w, ws = column_weights(True), column_weights(False)
        vacc[j, 0] = fold(gacc[:FLP] * w) + fold(gacc[FLP:] * ws)
        for h in range(2):
            s = sacc[h * QF : (h + 1) * QF] * ws
            s = s[:FS] + s[FS : 2 * FS] + s[2 * FS : 3 * FS] + s[3 * FS :]
            total = facc[j, 2 * h : 2 * h + 2].reshape(FLP, D) * w + apply_table(t_shrink_t[...], s)
            facc[j, 2 * h : 2 * h + 2] = total.reshape(2, 2, 2, 2, 8, D)
        row = [jnp.sum(bacc[j, h], 0, keepdims=True) for h in range(2)]
        row = jnp.concatenate([row[0][:, :D], row[0][:, D:], row[1][:, :D], row[1][:, D:], jnp.zeros((4, D), f32)], 0)
        mine = lax.broadcasted_iota(jnp.int32, (8, 128), 1) < HID
        for i in range(8):
            part = jnp.where(mine, (pltpu.roll(row, D - HID * i, 1) if i else row)[:, :128], 0.0)
            for g in range(4):
                facc[j, g, i // 4, i // 2 % 2, i % 2, 7:8, :128] = part[g : g + 1]

    def back_rows(j, which=BOTH):
        def body(o, i, big):
            n = sv_large[j, i] if big else sv_small[j, i]
            ng = apply_table(t_inv[...] if big else t_sinv[...], n)
            xs[o, :] = xs[o, :] + norm_back(vh1[j, o, :].astype(f32), wide_rows(r1[j, o, :]), ng * gains[j, 0:1, :])
        crop_loops(body, which)

    i0, o0 = gather_ops(0, "in"), gather_ops(0, "out")
    i1, o1 = gather_ops(1, "in"), gather_ops(1, "out")
    barrier = pltpu.get_barrier_semaphore()
    for to in peer.values():
        pl.semaphore_signal(barrier, 1, device_id=to, device_id_type=MESH_ID)
    for d in fetches:
        d.start()
    fetched(0, 1, 2)
    own_pieces()
    pl.semaphore_wait(barrier, len(peer))

    pack_z(0)
    i0["p"](0)
    i0["z"]()
    bacc[...] = jnp.zeros_like(bacc)
    vacc[...] = jnp.zeros_like(vacc)
    fetched(3, 4, 5, 6)
    load_rows(xs, large_rows, small_rows)

    def forward(j, _):
        first, then = (lambda f: pl.when(j == 0)(f)), (lambda f: pl.when(j == 1)(f))
        to_spectrum(j, ("big",))

        @first
        def _():
            pack_plane(0)
            i0["zw"](True)
            i0["p"](1)
            o0["z"]()
        to_spectrum(j, ("small",))

        @first
        def _():
            i0["zw"](False)
            i0["p"](2, 3)
            o0["p"](0)
            pack_z(1)
            fetched(*range(7, N_IN))
            for l in range(BLOCKS):
                for i in range(3):
                    shift[l, i] = biases[i, l : l + 1, :]
            load_rows(grad_low, cot_large, cot_small)

            def cot_sum(o):
                vacc[1, 4] += fold(grad_low[o, :].astype(f32))
            tiles(cot_sum)
            pack_core(0)
            i1["z"]()
            pack_wait(0)

        @then
        def _():
            pack_wait(1)
        unpack_filters(j)

        @then
        def _():
            i1["sw"](0, 1, 2, 3)
            i1["c"](True)
            i1["c"](False)
            o1["s"](0, 1)
        from_spectrum(j, ("big",))

        @first
        def _():
            i0["pw"](0, 1)
            i0["c"](True)
            o0["zw"](True)
            o0["p"](1)
        from_spectrum(j, ("small",))

        @first
        def _():
            o0["zw"](False)
            o0["p"](2, 3)
            i1["f"](0)
            o1["z"]()
            i0["pw"](2, 3)
            i0["c"](False)
            i0["cw"](True)

        @then
        def _():
            o1["s"](2, 3)
            i1["cw"](True)
        expand(j, half_z, True)

        @first
        def _():
            pack_plane(1)
            i1["zw"](True)
            i1["zw"](False)
            i1["f"](1, 2, 3)
            i0["cw"](False)
            o0["pw"](0, 1)
            o0["c"](True)

        @then
        def _():
            i1["cw"](False)
            o1["sw"](0, 1, 2, 3)
            o1["c"](True)
            o1["c"](False)
        expand(j, 1 - half_z, False)

        @first
        def _():
            o0["pw"](2, 3)
            o0["c"](False)
            o1["f"](0)
            i1["s"](0, 1, 2, 3)
            o0["cw"](True)
            o0["cw"](False)

        @then
        def _():
            o1["cw"](True)
            o1["cw"](False)
        contract(j)

        @first
        def _():
            o1["zw"](True)
            o1["zw"](False)
            o1["f"](1, 2, 3)
            pack_core(1)
        return 0

    lax.fori_loop(0, BLOCKS, forward, 0)
    store_large(large_rows)
    put(0, large_rows)
    store_small(small_rows)
    put(1, small_rows)

    def weights(j, a, k):
        reduce_core(j, a, k, (weight_out if a else weight_in)(j, k))

    def plane(j, a, *ks):
        for k in ks:
            reduce_plane(j, a, k)

    def along_z(j, a, *ks):
        for k in ks:
            reduce_z(j, a, k)

    def backward(t, _):
        j = BLOCKS - 1 - t
        first, then = (lambda f: pl.when(j == 1)(f)), (lambda f: pl.when(j == 0)(f))

        @first
        def _():
            def start(o):
                xs[o, :] = grad_low[o, :].astype(f32)
            tiles(start)

        @then
        def _():
            def low(o):
                g = xs[o, :]
                vacc[0, 4] += fold(g)
                grad_low[o, :] = g.astype(bf16)
            tiles(low)
            plane(1, 0, 0)
        for k in (2, 3, 1):
            weights(j, 1, k)
        plane(j, 1, 2, 3)

        @then
        def _():
            along_z(1, 0, 1)
        back_hidden(j, 1 - half_z, False)
        plane(j, 1, 1)

        @then
        def _():
            along_z(1, 1, 0)
            small_z(1)
            along_z(1, 0, 0)
        for k in (2, 3):
            weights(j, 0, k)
        along_z(j, 1, 2)
        back_hidden(j, half_z, True)
        plane(j, 0, 2, 3)
        along_z(j, 1, 3, 1)

        @then
        def _():
            small_end(1)
            reduce_end(1, 1)
            reduce_end(1, 0)
        back_spectrum(j, ("small",))
        back_spectrum(j, ("big",))
        back_filters(j)
        small_core(j)
        weights(j, 0, 1)
        small_plane(j)
        weights(j, 1, 0)
        plane(j, 0, 1)
        weights(j, 0, 0)
        along_z(j, 0, 2, 3)
        back_rows(j, ("small",))
        plane(j, 1, 0)

        @then
        def _():
            store_small(grad_small)
            put(3, grad_small)
        back_rows(j, ("big",))
        return 0

    lax.fori_loop(0, BLOCKS, backward, 0)
    plane(0, 0, 0)
    small_z(0)
    along_z(0, 0, 1)
    store_large(grad_large)
    put(2, grad_large)
    along_z(0, 1, 0)
    reduce_end(0, 1)
    put(6, g_w_out)
    along_z(0, 0, 0)
    reduce_end(0, 0)
    small_end(0)
    put(4, g_filters)
    put(5, g_w_in)
    put(7, g_gains)
    put(8, g_biases)
    for n in range(len(made)):
        pltpu.make_async_copy(stores[n], made[n], out_sem.at[n]).wait()
    for ops in (i0, o0, i1, o1):
        ops["e"]()
    for j in range(BLOCKS):
        pack_sent(j)
        small_sent(j)
    for a in range(2):
        for key, view in (("rc%d", s_core), ("rp%d", s_plane), ("rz%d", s_z)):
            sent(0, key % a, view.at[a])
    assert 2 * len(sending) == N_SEND and 2 * len(receiving) == N_RECEIVE, (len(sending), len(receiving))


def hand_over_kernel(*refs):
    sources, targets, between = refs[:N_OUT], refs[N_OUT : 2 * N_OUT], refs[2 * N_OUT : 3 * N_OUT]
    in_sem, out_sem = refs[3 * N_OUT :]
    largest_first = (2, 3, 0, 1, 6, 5, 4, 7, 8)
    ins = [pltpu.make_async_copy(sources[n], between[n], in_sem.at[n]) for n in largest_first]
    outs = [pltpu.make_async_copy(between[n], targets[n], out_sem.at[n]) for n in largest_first]
    for d in ins:
        d.start()
    for a, b in zip(ins, outs):
        a.wait()
        b.start()
    for d in outs:
        d.wait()


def fused(large_in, small_in, large_cot, small_cot, filters, w_in, w_out, gains, biases):
    large, small = large_in.shape[0], small_in.shape[0]
    rows = -(-(large * LP + small * PS) // TILE) * TILE
    early, late = [[jnp.asarray(t) for t in part] for part in constant_tables()]
    args = [jnp.swapaxes(w_in, 1, 2), w_out, filters, small_in, jnp.swapaxes(large_in, 0, 1), *early,
            jnp.swapaxes(large_cot, 0, 1), small_cot, gains, jnp.swapaxes(biases, 0, 1), *late]
    V = pltpu.VMEM
    patch_major = (large_in.shape[1], large, D)
    outs = [(patch_major, bf16), (small_in.shape, bf16), (patch_major, f32), (small_in.shape, f32), (filters.shape, f32),
            ((BLOCKS, HID, D + 1), f32), ((BLOCKS, HID, D), f32), (gains.shape, f32), ((3, BLOCKS, D), f32)]
    grid8 = (4, 2, 2, 2)
    scratch = [V(a.shape, a.dtype) for a in args] + [V(shape, dtype) for shape, dtype in outs[2:]] + [
        V((rows, D), f32), V((BLOCKS, rows, D), bf16), V((BLOCKS, rows, 128), f32), V((BLOCKS, rows, D), f32),
        V((BLOCKS, rows, 128), f32), V((BLOCKS, rows, D), bf16), V((BLOCKS, 2, rows, FF // 2), bf16),
        V((BLOCKS, 2, rows, FF // 2), bf16), V((BLOCKS, large, SPEC, D), f32), V((BLOCKS, small // Q, 2 * QF, D), f32),
        V((rows, D), bf16),
        V((BLOCKS, *grid8, HID, D), bf16), V((BLOCKS, *grid8, HID, D), bf16), V((BLOCKS, *grid8, 8, D), bf16),
        V((BLOCKS, 2 * QF, D), f32), V((BLOCKS, 2, 1, FF // 2), f32), V((BLOCKS, 3, 1, D), f32), V((rows, D), f32),
        V((BLOCKS, *grid8, 8, D), f32), V((2 * QF, D), f32), V((FLP + QF, D), f32), V((BLOCKS, 2, 8, FF // 2), f32), V((BLOCKS, 5, 8, D), f32),
        V((2, 4, 2, 2, HID, D), f32),
        V((2, 4, 2, 2, HID, D), bf16), V((2, 4, 3, HID, D), bf16), V((2, 3, HID, D), bf16),
        V((BLOCKS, 2, 4, 2, 2, HID, D), bf16), V((BLOCKS, 2, 4, 3, HID, D), bf16), V((BLOCKS, 2, 3, HID, D), bf16),
        V((BLOCKS, 4, 2, 2, 8, D), bf16), V((BLOCKS, 4, 2, 2, 8, D), bf16), V((BLOCKS, 2, 2, 4, 8, D), f32),
        V((BLOCKS, 3, 4, 8, D), bf16), V((BLOCKS, 3, 4, 8, D), bf16), V((BLOCKS, 3, 8, D), bf16), V((BLOCKS, 3, 8, D), bf16),
        V((BLOCKS, 8, D), f32), V((BLOCKS, 8, D), f32), V((BLOCKS, 2, 2, 8, D), f32), V((BLOCKS, 4, 8, D), f32),
        pltpu.SemaphoreType.DMA((N_SEND,)), pltpu.SemaphoreType.DMA((N_RECEIVE,)),
        pltpu.SemaphoreType.DMA((N_IN,)), pltpu.SemaphoreType.DMA((N_OUT,)),
    ]
    anywhere = pl.BlockSpec(memory_space=pl.ANY)
    out_shape = [jax.ShapeDtypeStruct(shape, dtype) for shape, dtype in outs]
    result = pl.pallas_call(
        partial(fused_kernel, large, small),
        out_shape=out_shape,
        in_specs=[anywhere] * N_IN,
        out_specs=[anywhere] * N_OUT,
        scratch_shapes=scratch,
        compiler_params=pltpu.CompilerParams(collective_id=0, has_side_effects=True, vmem_limit_bytes=VMEM_BYTES),
        name="gfnet_step",
    )(*args)
    out_large, out_small, grad_large, grad_small, g_filters, g_in, g_out, g_gains, g_biases = pl.pallas_call(
        hand_over_kernel,
        out_shape=out_shape,
        in_specs=[anywhere] * N_OUT,
        out_specs=[anywhere] * N_OUT,
        scratch_shapes=[V(shape, dtype) for shape, dtype in outs] + [pltpu.SemaphoreType.DMA((N_OUT,))] * 2,
        compiler_params=pltpu.CompilerParams(vmem_limit_bytes=VMEM_BYTES),
        name="hand_over",
    )(*result)
    return (jnp.swapaxes(out_large, 0, 1), out_small, jnp.swapaxes(grad_large, 0, 1), grad_small, g_filters,
            jnp.swapaxes(g_in, 1, 2), g_out, g_gains, jnp.swapaxes(g_biases, 0, 1))


def solution(mesh):
    in_specs = (
        P(("wide", "narrow"), None, None),
        P(("wide", "narrow"), None, None),
        P(("wide", "narrow"), None, None),
        P(("wide", "narrow"), None, None),
        P(None, ("wide", "narrow")),
        P(None, None, ("wide", "narrow")),
        P(None, ("wide", "narrow"), None),
        P(),
        P(),
    )
    out_specs = (
        P(("wide", "narrow"), None, None),
        P(("wide", "narrow"), None, None),
        P(("wide", "narrow"), None, None),
        P(("wide", "narrow"), None, None),
        P(None, ("wide", "narrow")),
        P(None, None, ("wide", "narrow")),
        P(None, ("wide", "narrow"), None),
        P(),
        P(),
    )
    body = fused if dict(mesh.shape) == {"wide": 8, "narrow": 4} else per_device
    return jax.shard_map(
        body, mesh=mesh, in_specs=in_specs, out_specs=out_specs, check_vma=False
    )
```
